32 devices in a mesh: dp: 8 (over z, x), tensor: 4 (over y, core).
Axes of the slice: x: 2, y: 2, z: 4, core: 2. Of those that a mesh axis runs over, the one named last changes fastest.
Arguments:
- codons: int32 [32, 1024], P(('dp', 'tensor')), may hold values from 0 to 69
- segments: int32 [32, 1024], P('dp'), may hold values from 0 to 3, never falling along the last dimension, each value on 1 to 512 neighbouring positions
- targets: int32 [32, 1024], P(('dp', 'tensor')), may hold values from 0 to 69
- loss_mask: int32 [32, 1024], P(('dp', 'tensor')), may hold values 0 or 1
- owner_map: int32 [192], replicated, may hold values from 0 to 191, as said below
- step_count: int32 [], replicated, may hold values from 2 to 20
- block_weight: float32 [4, 192, 96, 96], P('tensor', 'dp')
- block_left: float32 [4, 192, 96, 96], P('tensor', 'dp'), as said below
- block_right: float32 [4, 192, 96, 96], P('tensor', 'dp'), as said below
- block_left_root: float32 [4, 192, 96, 96], P('tensor', 'dp'), as said below
- block_right_root: float32 [4, 192, 96, 96], P('tensor', 'dp'), as said below
- embedding_weight: float32 [128, 768], replicated, may hold values from -0.4375 to 0.4375
- table_left: float32 [128, 128], replicated, as said below
- table_right: float32 [768, 768], replicated, as said below
- table_left_root: float32 [128, 128], replicated, as said below
- table_right_root: float32 [768, 768], replicated, as said below
- norm_params: float32 [6, 768], replicated, as said below
- norm_moment: float32 [6, 768], replicated, may hold values from -1.1444092e-05 to 1.1444092e-05
- norm_second: float32 [6, 768], replicated, may hold values from 5.57041e-14 to 2.228164e-13
Outputs:
- loss_value: float32 [], replicated
- grad_norm: float32 [], replicated
- block_grad: float32 [4, 192, 96, 96], P('tensor', 'dp')
- new_block_left: float32 [4, 192, 96, 96], P('tensor', 'dp')
- new_block_right: float32 [4, 192, 96, 96], P('tensor', 'dp')
- new_block_weight: float32 [4, 192, 96, 96], P('tensor', 'dp')
- embedding_clipped_gradient: float32 [128, 768], replicated
- new_table_left: float32 [128, 128], replicated
- new_table_right: float32 [768, 768], replicated
- new_table_weight: float32 [128, 768], replicated
- norm_clipped_gradient: float32 [6, 768], replicated
- new_norm_moment: float32 [6, 768], replicated
- new_norm_second: float32 [6, 768], replicated
- new_norm_params: float32 [6, 768], replicated
The draws below stay inside these ranges and needn't reach their ends.
Inputs may be any that keep to these rules, and one draw needn't show every extreme that they name: owner_map is a permutation. `block_left`: symmetric. `block_right`: symmetric. `block_left_root`: symmetric positive definite. `block_right_root`: symmetric positive definite. `table_left`: symmetric. `table_right`: symmetric. `table_left_root`: symmetric positive definite. `table_right_root`: symmetric positive definite. `norm_params`: rows 0, 2, 4 are gains, rows 1, 3, 5 biases.
All inputs are finite; a program needn't handle non-finite values. No bound on the sum of `loss_mask` on one device may be relied on, other than what follows from the above.
Results may differ from the reference program's by a relative error of at most 0.0013.
The reference program's roundings to bfloat16 on the way count: a program that leaves them out, or rounds other values in their place, can miss the bound.
Values may be sent and summed in bfloat16 or wider, within the bound.
A program may use at most 256 MiB of HBM per device.

```python
import math
import jax
import jax.numpy as jnp
import numpy as np
from jax import lax

D = 768
FF = 3072
HS = 64
VOCAB = 128
LEN = 1024
BS = 96
SEQS_DEV = 1
SHARDS = 4
SHARD_WIDTH = 192
SHARD_FF = 768
SEQS = 32
BLOCKS = 192
NPARAMS = 7180800


def slot_blocks(key):
    return jax.random.permutation(jax.random.fold_in(key, 11), BLOCKS)


def draw_owner_map(key, part):
    return slot_blocks(key).astype(jnp.int32)


def block_scales():
    model_blocks = D // BS
    project_end = model_blocks * (3 * SHARD_WIDTH // BS)
    output_end = project_end + SHARD_WIDTH // BS * model_blocks
    expand_end = output_end + model_blocks * (SHARD_FF // BS)
    block_index = jnp.arange(BLOCKS)
    return jnp.where(block_index < project_end, D ** (-0.5), jnp.where(block_index < output_end, 8.0 * D ** (-0.5), jnp.where(block_index < expand_end, D ** (-0.5), 3.0 * FF ** (-0.5)))).astype(jnp.float32)


def draw_block_weight(key, part):
    slot_map = slot_blocks(key)
    holder = jnp.argsort(slot_map)
    block_scale = block_scales()[holder]
    normal_draw = jax.random.normal(jax.random.fold_in(key, 12), (SHARDS, BLOCKS, BS, BS), jnp.float32)
    return normal_draw * block_scale[None, :, None, None]


def statistic(key, leading, order, level, low_factor, high_factor):
    factor = jnp.exp(jax.random.uniform(jax.random.fold_in(key, 1), leading + (1, 1), jnp.float32, math.log(low_factor), math.log(high_factor)))
    normal_draw = jax.random.normal(jax.random.fold_in(key, 2), leading + (order, order), jnp.float32)
    symmetric = (normal_draw + jnp.swapaxes(normal_draw, -1, -2)) * (0.4 / math.sqrt(2.0 * order))
    return level * factor * (jnp.eye(order, dtype=jnp.float32) + symmetric)


def square_level():
    return 0.005 ** 2 / NPARAMS


def draw_block_left(key, part):
    return statistic(jax.random.fold_in(key, 21), (SHARDS, BLOCKS), BS, BS * square_level(), 1.0, 4.0)


def draw_block_right(key, part):
    return statistic(jax.random.fold_in(key, 22), (SHARDS, BLOCKS), BS, BS * square_level(), 1.0, 4.0)


def draw_block_left_root(key, part):
    return statistic(jax.random.fold_in(key, 23), (SHARDS, BLOCKS), BS, (BS * square_level()) ** (-0.25), 0.7, 1.4)


def draw_block_right_root(key, part):
    return statistic(jax.random.fold_in(key, 24), (SHARDS, BLOCKS), BS, (BS * square_level()) ** (-0.25), 0.7, 1.4)


def draw_table_left(key, part):
    return statistic(jax.random.fold_in(key, 25), (), VOCAB, D * square_level(), 1.0, 4.0)


def draw_table_right(key, part):
    return statistic(jax.random.fold_in(key, 26), (), D, VOCAB * square_level(), 1.0, 4.0)


def draw_table_left_root(key, part):
    return statistic(jax.random.fold_in(key, 27), (), VOCAB, (D * square_level()) ** (-0.25), 0.7, 1.4)


def draw_table_right_root(key, part):
    return statistic(jax.random.fold_in(key, 28), (), D, (VOCAB * square_level()) ** (-0.25), 0.7, 1.4)


def draw_norm_params(key, part):
    gains = jax.random.uniform(jax.random.fold_in(key, 31), (3, D), jnp.float32, 0.5, 1.5)
    biases = 0.2 * jax.random.normal(jax.random.fold_in(key, 32), (3, D), jnp.float32)
    return jnp.stack([gains, biases], 1).reshape(6, D)


def plant(values, rng, smallest, largest):
    dims = values.shape
    place = [jax.random.randint(jax.random.fold_in(rng, axis), (), 0, dims[axis]) for axis in range(len(dims))]
    values = values.at[tuple(place)].set(smallest)
    longest = dims.index(max(dims))
    place[longest] = (place[longest] + 1) % dims[longest]
    return values.at[tuple(place)].set(largest)


def split_up(amount, total, reach, skew):
    weights = [(1 << 20) // math.isqrt(standing ** skew) + 1 for standing in range(2, amount + 1)]
    rest, given = total - reach - (amount - 1), [1] * (amount - 1)
    while rest > 0:
        movable = [i for i in range(amount - 1) if given[i] < reach]
        pool, left = sum([weights[i] for i in movable]), rest
        for i in movable:
            more = min(reach - given[i], max(1, left * weights[i] // pool), rest)
            given[i] = given[i] + more
            rest = rest - more
    return np.array([reach] + given)


def uneven_parts(key, number_of, total, limit, skew):
    if number_of == 2:
        one = jax.random.randint(key, (), max(1, total - limit), min(limit, total - 1) + 1)
        return jnp.stack([one, total - one])
    sizes = jnp.asarray(split_up(number_of, total, limit, skew), jnp.int32)
    couples = (number_of - 1) // 2
    donor, taker = sizes[1:1 + 2 * couples:2], sizes[2:2 + 2 * couples:2]
    room = jnp.minimum(donor - 1, limit - taker)
    shifted = jax.random.randint(jax.random.fold_in(key, 1), (couples,), 0, 1 << 20) % (room + 1)
    sizes = sizes.at[1:1 + 2 * couples:2].set(donor - shifted).at[2:2 + 2 * couples:2].set(taker + shifted)
    return sizes[jax.random.permutation(jax.random.fold_in(key, 2), number_of)]


def scatter_about(own_key, shape, deviation, reach, held_as=jnp.bfloat16):
    array = deviation * jax.random.normal(own_key, shape, jnp.float32)
    return jnp.clip(array, min=-reach, max=reach).astype(held_as)


def setup_inputs(seed: int = 0) -> dict:
    seeds = jax.random.split(jax.random.key(seed), 20)
    return {
        "codons": plant(jax.random.randint(seeds[0], (SEQS, LEN), 0, 70), jax.random.fold_in(seeds[0], 1), 0, 69).astype(jnp.int32),
        "segments": jax.vmap(lambda own: jnp.searchsorted(jnp.cumsum(uneven_parts(own, 4, LEN, LEN // 2, 0)), jnp.arange(LEN), side="right"))(jax.random.split(seeds[1], SEQS)).reshape((SEQS, LEN)).astype(jnp.int32),
        "targets": plant(jax.random.randint(seeds[2], (SEQS, LEN), 0, 70), jax.random.fold_in(seeds[2], 1), 0, 69).astype(jnp.int32),
        "loss_mask": plant((jax.random.randint(seeds[3], (SEQS, LEN), 0, 20) < 3).astype(jnp.int32), jax.random.fold_in(seeds[3], 1), 0, 1),
        "owner_map": draw_owner_map(jax.random.fold_in(seeds[19], 71), 0),
        "step_count": jax.random.randint(seeds[5], (), 2, 21).astype(jnp.int32),
        "block_weight": draw_block_weight(jax.random.fold_in(seeds[19], 71), 0),
        "block_left": draw_block_left(jax.random.fold_in(seeds[19], 71), 0),
        "block_right": draw_block_right(jax.random.fold_in(seeds[19], 71), 0),
        "block_left_root": draw_block_left_root(jax.random.fold_in(seeds[19], 71), 0),
        "block_right_root": draw_block_right_root(jax.random.fold_in(seeds[19], 71), 0),
        "embedding_weight": scatter_about(seeds[11], (VOCAB, D), (D // 4) ** -0.5, 0.4375, jnp.float32),
        "table_left": draw_table_left(jax.random.fold_in(seeds[19], 71), 0),
        "table_right": draw_table_right(jax.random.fold_in(seeds[19], 71), 0),
        "table_left_root": draw_table_left_root(jax.random.fold_in(seeds[19], 71), 0),
        "table_right_root": draw_table_right_root(jax.random.fold_in(seeds[19], 71), 0),
        "norm_params": draw_norm_params(jax.random.fold_in(seeds[19], 71), 0),
        "norm_moment": scatter_about(seeds[17], (6, D), (0.11 * 0.02 / NPARAMS ** 0.5), 1.1444091796875e-05, jnp.float32),
        "norm_second": jnp.clip(jnp.exp(jax.random.uniform(seeds[18], (6, D), jnp.float32, math.log(5.570409856037878e-14), math.log(2.2281639424151511e-13))), 5.570409856037878e-14, 2.2281639424151511e-13),
    }


CLIP_LEVEL = 0.005
STAT_DECAY = 0.5
MATRIX_RATE = 0.03
WEIGHT_DECAY = 0.01
VECTOR_RATE = 0.2
FIRST_BETA = 0.9
SECOND_BETA = 0.999
ADAM_EPSILON = 1e-08
NORM_EPSILON = 1e-05
ROOT_EPSILON = 1e-06
MASK_VALUE = -1e+30
ROTARY_BASE = 10000.0
TOP_PRECISION = lax.Precision.HIGHEST

@jax.custom_vjp
def low(v):
    return lax.optimization_barrier(v.astype(jnp.bfloat16)).astype(jnp.float32)

@jax.custom_vjp
def low_back(v):
    return v

def low_keep(v):
    return (low(v), None)

def low_pass(kept, grad):
    return (grad,)

def back_keep(v):
    return (v, None)

def back_low(kept, grad):
    return (low(grad),)
low.defvjp(low_keep, low_pass)
low_back.defvjp(back_keep, back_low)

def layer_norm(values, gain_row, bias_row):
    center = values - lax.optimization_barrier(jnp.mean(values, -1, keepdims=True))
    spread = lax.optimization_barrier(jnp.mean(center * center, -1, keepdims=True))
    return center * lax.rsqrt(spread + NORM_EPSILON) * gain_row + bias_row

def rotary_tables(length, width):
    half_width = width // 2
    freqs = jnp.exp(-math.log(ROTARY_BASE) * (2.0 * jnp.arange(half_width, dtype=jnp.float32) / width))
    angles = jnp.arange(length, dtype=jnp.float32)[:, None] * freqs[None, :]
    return (jnp.cos(angles), jnp.sin(angles))

def rotate(values, cosine, sine):
    half_width = values.shape[-1] // 2
    front = values[..., :half_width]
    behind = values[..., half_width:]
    cos_col = cosine[:, None, :]
    sin_col = sine[:, None, :]
    return jnp.concatenate([front * cos_col - behind * sin_col, behind * cos_col + front * sin_col], -1)

def tile_blocks(blocks, block_rows, block_columns):
    leading = blocks.shape[0]
    block_edge = blocks.shape[-1]
    shaped = blocks.reshape(leading, block_rows, block_columns, block_edge, block_edge)
    return shaped.transpose(0, 1, 3, 2, 4).reshape(leading, block_rows * block_edge, block_columns * block_edge)

def split_matrices(blocks):
    block_edge = blocks.shape[-1]
    model_blocks = D // block_edge
    layout = [(model_blocks, 3 * SHARD_WIDTH // block_edge), (SHARD_WIDTH // block_edge, model_blocks), (model_blocks, SHARD_FF // block_edge), (SHARD_FF // block_edge, model_blocks)]
    matrices = []
    offset = 0
    for block_rows, block_columns in layout:
        matrices.append(tile_blocks(blocks[:, offset:offset + block_rows * block_columns], block_rows, block_columns))
        offset = offset + block_rows * block_columns
    return matrices

def attend_sequence(packed):
    query, keys, values, segment = packed
    scores = low_back(jnp.einsum('qhd,khd->hqk', query, keys, precision=TOP_PRECISION))
    same = segment[:, None] == segment[None, :]
    scores = jnp.where(same[None], scores, MASK_VALUE)
    top_score = lax.optimization_barrier(jnp.max(scores, -1, keepdims=True))
    weights = jnp.exp(scores - top_score)
    probs = weights / lax.optimization_barrier(jnp.sum(weights, -1, keepdims=True))
    return jnp.einsum('hqk,khd->qhd', low(probs), values, precision=TOP_PRECISION)

def sequence_group(shared, batch_data):
    projection_weight, output_matrix, expansion_weight, contract_weight, table, vectors = shared
    tokens, segment_rows, target_rows, mask_rows = batch_data
    group = tokens.shape[0]
    length = tokens.shape[1]
    shards = projection_weight.shape[0]
    heads_shard = SHARD_WIDTH // HS
    embedded = math.sqrt(D) * table[tokens]
    normed = low(layer_norm(embedded, vectors[0], vectors[1]))
    projection_output = low_back(jnp.einsum('gld,tde->glte', normed, projection_weight, precision=TOP_PRECISION))
    projection_output = projection_output.reshape(group, length, shards, 3, heads_shard, HS)
    cosine, sine = rotary_tables(length, HS)

    def heads_of(component):
        return projection_output[:, :, :, component].reshape(group, length, shards * heads_shard, HS)
    query = low(rotate(heads_of(0), cosine, sine) * HS ** (-0.5))
    keys = low(rotate(heads_of(1), cosine, sine))
    values = low(heads_of(2))
    attention_output = lax.map(jax.checkpoint(attend_sequence), (query, keys, values, segment_rows))
    attention_output = low(low_back(attention_output)).reshape(group, length, shards, SHARD_WIDTH)
    branch = low_back(jnp.einsum('glte,ted->gld', attention_output, output_matrix, precision=TOP_PRECISION))
    middle = embedded + branch
    normed_two = low(layer_norm(middle, vectors[2], vectors[3]))
    hidden_state = low_back(jnp.einsum('gld,tdf->gltf', normed_two, expansion_weight, precision=TOP_PRECISION))
    active_units = low(jax.nn.gelu(hidden_state, approximate=False))
    branch_two = low_back(jnp.einsum('gltf,tfd->gld', active_units, contract_weight, precision=TOP_PRECISION))
    final = layer_norm(middle + branch_two, vectors[4], vectors[5])
    output_scores = low_back(jnp.einsum('gld,vd->glv', low(final), low(table), precision=TOP_PRECISION))
    log_probs = jax.nn.log_softmax(output_scores, -1)
    picked = jnp.take_along_axis(log_probs, target_rows[..., None], -1)[..., 0]
    return -jnp.sum(mask_rows.astype(jnp.float32) * picked)

def shampoo(grad, left, right, left_root, right_root, weight):
    new_left = STAT_DECAY * left + (1.0 - STAT_DECAY) * jnp.einsum('...ij,...kj->...ik', grad, grad, precision=TOP_PRECISION)
    new_right = STAT_DECAY * right + (1.0 - STAT_DECAY) * jnp.einsum('...ji,...jk->...ik', grad, grad, precision=TOP_PRECISION)
    partial_left = jnp.einsum('...ij,...jk->...ik', left_root, grad, precision=TOP_PRECISION)
    precond = jnp.einsum('...ij,...jk->...ik', partial_left, right_root, precision=TOP_PRECISION)
    scale_back = lax.rsqrt(lax.optimization_barrier(jnp.mean(precond * precond, axis=(-2, -1), keepdims=True)) + ROOT_EPSILON)
    new_weight = weight * (1.0 - MATRIX_RATE * WEIGHT_DECAY) - MATRIX_RATE * precond * scale_back
    return (new_left, new_right, new_weight)

def adamw(grad, moment, second, weight, step_value):
    new_moment = FIRST_BETA * moment + (1.0 - FIRST_BETA) * grad
    new_second = SECOND_BETA * second + (1.0 - SECOND_BETA) * grad * grad
    corrected_one = new_moment / (1.0 - FIRST_BETA ** step_value)
    corrected_two = new_second / (1.0 - SECOND_BETA ** step_value)
    new_weight = weight - VECTOR_RATE * (corrected_one / (jnp.sqrt(corrected_two) + ADAM_EPSILON) + WEIGHT_DECAY * weight)
    return (new_moment, new_second, new_weight)

def reference(codons, segments, targets, loss_mask, owner_map, step_count, block_weight, block_left, block_right, block_left_root, block_right_root, embedding_weight, table_left, table_right, table_left_root, table_right_root, norm_params, norm_moment, norm_second):
    group = SEQS_DEV * SHARDS
    batches = tuple((source.reshape(SEQS // group, group, LEN) for source in (codons, segments, targets, loss_mask)))
    token_count = jnp.maximum(jnp.sum(loss_mask.astype(jnp.float32)), 1.0)

    def total_loss(params):
        weights_slot, table, vectors = params
        ordered = low(weights_slot)[:, owner_map]
        projection_weight, output_matrix, expansion_weight, contract_weight = split_matrices(ordered)
        shared = (projection_weight, output_matrix, expansion_weight, contract_weight, table, vectors)

        def scan_step(running, batch_data):
            return (running + jax.checkpoint(sequence_group)(shared, batch_data), None)
        summed, _ = lax.scan(scan_step, jnp.zeros((), jnp.float32), batches)
        return summed / token_count
    loss_value, pullback = jax.vjp(total_loss, (block_weight, embedding_weight, norm_params))
    raw_blocks, raw_table, raw_norms = pullback(jnp.ones((), jnp.float32))[0]
    grad_norm = jnp.sqrt(jnp.sum(raw_blocks * raw_blocks) + jnp.sum(raw_table * raw_table) + jnp.sum(raw_norms * raw_norms))
    factor = CLIP_LEVEL / jnp.maximum(grad_norm, CLIP_LEVEL)
    block_grad = raw_blocks * factor
    embedding_clipped_gradient = raw_table * factor
    norm_clipped_gradient = raw_norms * factor
    new_block_left, new_block_right, new_block_weight = shampoo(block_grad, block_left, block_right, block_left_root, block_right_root, block_weight)
    new_table_left, new_table_right, new_table_weight = shampoo(embedding_clipped_gradient, table_left, table_right, table_left_root, table_right_root, embedding_weight)
    new_norm_moment, new_norm_second, new_norm_params = adamw(norm_clipped_gradient, norm_moment, norm_second, norm_params, step_count.astype(jnp.float32))
    return (loss_value, grad_norm, block_grad, new_block_left, new_block_right, new_block_weight, embedding_clipped_gradient, new_table_left, new_table_right, new_table_weight, norm_clipped_gradient, new_norm_moment, new_norm_second, new_norm_params)
```

```python
import math

import jax
import jax.numpy as jnp
from jax import lax
from jax.sharding import PartitionSpec as P

FF = 3072
HS = 64


CLIP_LEVEL = 0.005
STAT_DECAY = 0.5
MATRIX_RATE = 0.03
WEIGHT_DECAY = 0.01
VECTOR_RATE = 0.2
FIRST_BETA = 0.9
SECOND_BETA = 0.999
ADAM_EPSILON = 1e-08
NORM_EPSILON = 1e-05
ROOT_EPSILON = 1e-06
MASK_VALUE = -1e30
ROTARY_BASE = 10000.0
TOP_PRECISION = lax.Precision.HIGHEST


def layer_norm(values, gain_row, bias_row):
    center = values - jnp.mean(values, -1, keepdims=True)
    spread = jnp.mean(center * center, -1, keepdims=True)
    return center * lax.rsqrt(spread + NORM_EPSILON) * gain_row + bias_row


def exact_gelu(values):
    return jax.nn.gelu(values, approximate=False)


def rotary_tables(length, width):
    half_width = width // 2
    freqs = jnp.exp(
        -math.log(ROTARY_BASE) * (2.0 * jnp.arange(half_width, dtype=jnp.float32) / width)
    )
    angles = jnp.arange(length, dtype=jnp.float32)[:, None] * freqs[None, :]
    return (jnp.cos(angles), jnp.sin(angles))


def rotate(values, cosine, sine):
    half_width = values.shape[-1] // 2
    front = values[..., :half_width]
    behind = values[..., half_width:]
    cos_col = cosine[:, None, :]
    sin_col = sine[:, None, :]
    return jnp.concatenate(
        [front * cos_col - behind * sin_col, behind * cos_col + front * sin_col], -1
    )


def block_parts(ordered, width, shard_width, shard_ff, edge):
    shards = ordered.shape[0]
    model = width // edge
    wide = shard_width // edge
    tall = shard_ff // edge
    ends = [3 * wide * model, wide * model, model * tall, tall * model]
    pieces = []
    offset = 0
    for count in ends:
        pieces.append(ordered[:, offset : offset + count])
        offset += count
    project = pieces[0].reshape(shards, model, 3, wide, edge, edge)
    project = project.transpose(1, 4, 2, 0, 3, 5).reshape(width, 3 * shards * shard_width)
    outward = pieces[1].reshape(shards, wide, model, edge, edge)
    outward = outward.transpose(0, 1, 3, 2, 4).reshape(shards * shard_width, width)
    expand = pieces[2].reshape(shards, model, tall, edge, edge)
    expand = expand.transpose(1, 3, 0, 2, 4).reshape(width, shards * shard_ff)
    contract = pieces[3].reshape(shards, tall, model, edge, edge)
    contract = contract.transpose(0, 1, 3, 2, 4).reshape(shards * shard_ff, width)
    return project, outward, expand, contract


def parts_to_blocks(parts, width, shards, shard_width, shard_ff, edge):
    model = width // edge
    wide = shard_width // edge
    tall = shard_ff // edge
    project, outward, expand, contract = parts
    project = project.reshape(model, edge, 3, shards, wide, edge).transpose(3, 0, 2, 4, 1, 5)
    outward = outward.reshape(shards, wide, edge, model, edge).transpose(0, 1, 3, 2, 4)
    expand = expand.reshape(model, edge, shards, tall, edge).transpose(2, 0, 3, 1, 4)
    contract = contract.reshape(shards, tall, edge, model, edge).transpose(0, 1, 3, 2, 4)
    return jnp.concatenate(
        [piece.reshape(shards, -1, edge, edge) for piece in (project, outward, expand, contract)], 1
    )


def masked_scores(chosen, keys, segment, offset, block_rows):
    same = segment[offset : offset + block_rows, None] == segment[None, :]
    scores = jnp.einsum("qhd,khd->hqk", chosen, keys, preferred_element_type=jnp.float32)
    return jnp.where(same[None], scores, MASK_VALUE)


def attend_forward(query, keys, values, segment):
    length = query.shape[0]
    block_rows = min(512, length)
    outputs = []
    totals = []
    for offset in range(0, length, block_rows):
        scores = masked_scores(
            query[offset : offset + block_rows], keys, segment, offset, block_rows
        )
        top_score = jnp.max(scores, -1, keepdims=True)
        weights = jnp.exp(scores - top_score)
        summed = jnp.sum(weights, -1, keepdims=True)
        probs = weights / summed
        outputs.append(
            jnp.einsum(
                "hqk,khd->qhd",
                probs.astype(jnp.bfloat16),
                values,
                preferred_element_type=jnp.float32,
            )
        )
        totals.append((top_score + jnp.log(summed))[..., 0])
    return (jnp.concatenate(outputs, 0), jnp.concatenate(totals, 1))


def attend_backward(query, keys, values, segment, grad_out, log_total):
    length = query.shape[0]
    block_rows = min(512, length)
    query_parts = []
    key_grad = jnp.zeros(keys.shape, jnp.float32)
    value_grad = jnp.zeros(values.shape, jnp.float32)
    for offset in range(0, length, block_rows):
        chosen = query[offset : offset + block_rows]
        grad_block = grad_out[offset : offset + block_rows]
        scores = masked_scores(chosen, keys, segment, offset, block_rows)
        probs = jnp.exp(scores - log_total[:, offset : offset + block_rows, None])
        grad_probs = jnp.einsum(
            "qhd,khd->hqk", grad_block, values, preferred_element_type=jnp.float32
        )
        delta = jnp.sum(probs * grad_probs, -1, keepdims=True)
        grad_scores = (probs * (grad_probs - delta)).astype(jnp.bfloat16)
        query_parts.append(
            jnp.einsum("hqk,khd->qhd", grad_scores, keys, preferred_element_type=jnp.float32)
        )
        key_grad = key_grad + jnp.einsum(
            "hqk,qhd->khd", grad_scores, chosen, preferred_element_type=jnp.float32
        )
        value_grad = value_grad + jnp.einsum(
            "hqk,qhd->khd",
            probs.astype(jnp.bfloat16),
            grad_block,
            preferred_element_type=jnp.float32,
        )
    return (jnp.concatenate(query_parts, 0), key_grad, value_grad)


def shampoo(grad, left, right, left_root, right_root, weight):
    new_left = STAT_DECAY * left + (1.0 - STAT_DECAY) * jnp.einsum(
        "...ij,...kj->...ik", grad, grad, precision=TOP_PRECISION
    )
    new_right = STAT_DECAY * right + (1.0 - STAT_DECAY) * jnp.einsum(
        "...ji,...jk->...ik", grad, grad, precision=TOP_PRECISION
    )
    partial_left = jnp.einsum("...ij,...jk->...ik", left_root, grad, precision=TOP_PRECISION)
    precond = jnp.einsum("...ij,...jk->...ik", partial_left, right_root, precision=TOP_PRECISION)
    scale_back = lax.rsqrt(jnp.mean(precond * precond, axis=(-2, -1), keepdims=True) + ROOT_EPSILON)
    new_weight = weight * (1.0 - MATRIX_RATE * WEIGHT_DECAY) - MATRIX_RATE * precond * scale_back
    return (new_left, new_right, new_weight)


def adamw(grad, moment, second, weight, step_value):
    new_moment = FIRST_BETA * moment + (1.0 - FIRST_BETA) * grad
    new_second = SECOND_BETA * second + (1.0 - SECOND_BETA) * grad * grad
    corrected_one = new_moment / (1.0 - FIRST_BETA**step_value)
    corrected_two = new_second / (1.0 - SECOND_BETA**step_value)
    new_weight = weight - VECTOR_RATE * (
        corrected_one / (jnp.sqrt(corrected_two) + ADAM_EPSILON) + WEIGHT_DECAY * weight
    )
    return (new_moment, new_second, new_weight)


def body(
    codons,
    segments,
    targets,
    loss_mask,
    owner_map,
    step_count,
    block_weight,
    block_left,
    block_right,
    block_left_root,
    block_right_root,
    embedding_weight,
    table_left,
    table_right,
    table_left_root,
    table_right_root,
    norm_params,
    norm_moment,
    norm_second,
):
    width = embedding_weight.shape[1]
    vocab_size = embedding_weight.shape[0]
    shards = lax.axis_size("tensor")
    owners = lax.axis_size("dp")
    shard_width = width // shards
    shard_ff = FF // shards
    block_edge = block_weight.shape[-1]
    slot_count = block_weight.shape[1]
    block_total = owner_map.shape[0]
    heads = width // HS
    length = codons.shape[1]
    bf16 = jnp.bfloat16
    single_float = jnp.float32

    gathered = lax.all_gather(block_weight[0].astype(bf16), ("dp", "tensor"), axis=0, tiled=False)
    gathered = gathered.reshape(owners, shards, slot_count, block_edge, block_edge)
    by_shard = gathered.transpose(1, 0, 2, 3, 4).reshape(shards, block_total, block_edge, block_edge)
    ordered = by_shard[:, owner_map]
    parts = block_parts(ordered, width, shard_width, shard_ff, block_edge)
    project, outward, expand, contract = parts

    vocab_index = jnp.arange(vocab_size, dtype=jnp.int32)
    codon_hot = (codons[0][:, None] == vocab_index).astype(single_float)
    embed_scale = math.sqrt(width)
    embedded = embed_scale * jnp.dot(codon_hot, embedding_weight, precision=TOP_PRECISION)
    normed = layer_norm(embedded, norm_params[0], norm_params[1]).astype(bf16)
    projected = jnp.dot(normed, project, preferred_element_type=single_float)
    cosine, sine = rotary_tables(length, HS)

    def heads_of(component):
        return projected[:, component * width : (component + 1) * width].reshape(length, heads, HS)

    query = (rotate(heads_of(0), cosine, sine) * HS ** (-0.5)).astype(bf16)
    keys = rotate(heads_of(1), cosine, sine).astype(bf16)
    values = heads_of(2).astype(bf16)
    row_index = lax.axis_index("tensor")
    segment = lax.dynamic_index_in_dim(segments, row_index, 0, keepdims=False)
    attended, log_total = attend_forward(query, keys, values, segment)
    attended = attended.astype(bf16).reshape(length, width)
    middle = embedded + jnp.dot(attended, outward, preferred_element_type=single_float)
    normed_two = layer_norm(middle, norm_params[2], norm_params[3]).astype(bf16)
    hidden = jnp.dot(normed_two, expand, preferred_element_type=single_float)
    active = exact_gelu(hidden).astype(bf16)
    final_in = middle + jnp.dot(active, contract, preferred_element_type=single_float)
    final = layer_norm(final_in, norm_params[4], norm_params[5])
    final_low = final.astype(bf16)
    table_low = embedding_weight.astype(bf16)
    scores = jnp.einsum("xt,qt->xq", final_low, table_low, preferred_element_type=single_float)
    shifted = scores - jnp.max(scores, -1, keepdims=True)
    log_probs = shifted - jnp.log(jnp.sum(jnp.exp(shifted), -1, keepdims=True))
    target_hot = (targets[0][:, None] == vocab_index).astype(single_float)
    mask_values = loss_mask[0].astype(single_float)
    picked = jnp.sum(target_hot * log_probs, -1)
    loss_sum, mask_total = lax.psum(
        (-jnp.sum(mask_values * picked), jnp.sum(mask_values)), ("dp", "tensor")
    )
    token_count = jnp.maximum(mask_total, 1.0)
    loss_value = loss_sum / token_count
    logit_grad = (
        (jnp.exp(log_probs) - target_hot) * (mask_values / token_count)[:, None]
    ).astype(bf16)
    table_grad = jnp.einsum("ux,up->xp", logit_grad, final_low, preferred_element_type=single_float)
    final_grad = jnp.dot(logit_grad, table_low, preferred_element_type=single_float)
    _, final_back = jax.vjp(layer_norm, final_in, norm_params[4], norm_params[5])
    grad_final_in, gain_five, bias_five = final_back(final_grad)
    d_two = grad_final_in.astype(bf16)
    contract_grad = jnp.einsum("lk,le->ke", active, d_two, preferred_element_type=single_float)
    grad_active = jnp.einsum("le,ke->lk", d_two, contract, preferred_element_type=single_float)
    _, gelu_back = jax.vjp(exact_gelu, hidden)
    hidden_grad = gelu_back(grad_active)[0].astype(bf16)
    expand_grad = jnp.einsum("lz,lx->zx", normed_two, hidden_grad, preferred_element_type=single_float)
    grad_normed_two = jnp.einsum(
        "lx,zx->lz", hidden_grad, expand, preferred_element_type=single_float
    )
    _, second_back = jax.vjp(layer_norm, middle, norm_params[2], norm_params[3])
    grad_middle_norm, gain_three, bias_three = second_back(grad_normed_two)
    grad_middle = grad_final_in + grad_middle_norm
    d_one = grad_middle.astype(bf16)
    outward_grad = jnp.einsum("lk,lx->kx", attended, d_one, preferred_element_type=single_float)
    grad_attended = jnp.einsum("lc,vc->lv", d_one, outward, preferred_element_type=single_float)
    grad_attended = grad_attended.astype(bf16).reshape(length, heads, HS)
    grad_query, grad_keys, grad_values = attend_backward(
        query, keys, values, segment, grad_attended, log_total
    )
    grad_projected = jnp.concatenate(
        [
            rotate(grad_query * HS ** (-0.5), cosine, -sine).reshape(length, width),
            rotate(grad_keys, cosine, -sine).reshape(length, width),
            grad_values.reshape(length, width),
        ],
        -1,
    ).astype(bf16)
    project_grad = jnp.einsum(
        "lh,lf->hf", normed, grad_projected, preferred_element_type=single_float
    )
    grad_normed = jnp.einsum(
        "lf,hf->lh", grad_projected, project, preferred_element_type=single_float
    )
    _, first_back = jax.vjp(layer_norm, embedded, norm_params[0], norm_params[1])
    grad_embed_norm, gain_one, bias_one = first_back(grad_normed)
    embedded_grad = grad_middle + grad_embed_norm
    table_grad = table_grad + embed_scale * jnp.einsum(
        "ux,up->xp", codon_hot, embedded_grad, precision=TOP_PRECISION
    )
    norm_grad = jnp.stack([gain_one, bias_one, gain_three, bias_three, gain_five, bias_five])
    table_grad, norm_grad = lax.psum((table_grad, norm_grad), ("dp", "tensor"))
    block_grads = parts_to_blocks(
        (project_grad, outward_grad, expand_grad, contract_grad),
        width, shards, shard_width, shard_ff, block_edge,
    )
    slot_order = (
        jnp.zeros((block_total,), jnp.int32)
        .at[owner_map]
        .set(jnp.arange(block_total, dtype=jnp.int32))
    )
    slot_grads = block_grads[:, slot_order].reshape(
        shards, owners, slot_count, block_edge, block_edge
    )
    slot_grads = slot_grads.transpose(1, 0, 2, 3, 4).reshape(
        owners * shards * slot_count, block_edge, block_edge
    )
    owned = lax.psum_scatter(slot_grads, ("dp", "tensor"), scatter_dimension=0, tiled=True)
    embedding_clipped_gradient = table_grad
    square_sum = lax.psum(jnp.sum(owned * owned), ("dp", "tensor"))
    square_sum = (
        square_sum
        + jnp.sum(embedding_clipped_gradient * embedding_clipped_gradient)
        + jnp.sum(norm_grad * norm_grad)
    )
    grad_norm = jnp.sqrt(square_sum)
    factor = CLIP_LEVEL / jnp.maximum(grad_norm, CLIP_LEVEL)
    block_grad = owned * factor
    new_left, new_right, new_weight = shampoo(
        block_grad,
        block_left[0],
        block_right[0],
        block_left_root[0],
        block_right_root[0],
        block_weight[0],
    )
    table_clipped = embedding_clipped_gradient * factor
    table_left_new, table_right_new, table_weight_new = shampoo(
        table_clipped, table_left, table_right, table_left_root, table_right_root, embedding_weight
    )
    norm_clipped = norm_grad * factor
    moment_new, second_new, params_new = adamw(
        norm_clipped, norm_moment, norm_second, norm_params, step_count.astype(single_float)
    )
    return (
        loss_value,
        grad_norm,
        block_grad[None],
        new_left[None],
        new_right[None],
        new_weight[None],
        table_clipped,
        table_left_new,
        table_right_new,
        table_weight_new,
        norm_clipped,
        moment_new,
        second_new,
        params_new,
    )


def solution(mesh):
    in_specs = (
        P(("dp", "tensor"), None),
        P("dp", None),
        P(("dp", "tensor"), None),
        P(("dp", "tensor"), None),
        P(),
        P(),
        P("tensor", "dp", None, None),
        P("tensor", "dp", None, None),
        P("tensor", "dp", None, None),
        P("tensor", "dp", None, None),
        P("tensor", "dp", None, None),
        P(),
        P(),
        P(),
        P(),
        P(),
        P(),
        P(),
        P(),
    )
    out_specs = (
        P(),
        P(),
        P("tensor", "dp", None, None),
        P("tensor", "dp", None, None),
        P("tensor", "dp", None, None),
        P("tensor", "dp", None, None),
        P(),
        P(),
        P(),
        P(),
        P(),
        P(),
        P(),
        P(),
    )
    return jax.shard_map(body, mesh=mesh, in_specs=in_specs, out_specs=out_specs, check_vma=False)
```

```python
import functools
import math

import jax
import jax.numpy as jnp
from jax import lax
from jax.experimental import pallas as pl
from jax.experimental.pallas import tpu as pltpu
from jax.sharding import PartitionSpec as P

FF = 3072
HS = 64

CLIP_LEVEL = 0.005
STAT_DECAY = 0.5
MATRIX_RATE = 0.03
WEIGHT_DECAY = 0.01
VECTOR_RATE = 0.2
FIRST_BETA = 0.9
SECOND_BETA = 0.999
ADAM_EPSILON = 1e-08
NORM_EPSILON = 1e-05
ROOT_EPSILON = 1e-06
MASK_VALUE = -1e30
ROTARY_BASE = 10000.0
TOP_PRECISION = lax.Precision.HIGHEST

LANES = 128
PACK = 4
VMEM_LIMIT = 60 * 1024 * 1024
BF16 = jnp.bfloat16
F32 = jnp.float32


def dot(left, right):
    return lax.dot_general(left, right, (((1,), (0,)), ((), ())), preferred_element_type=F32)


def dot_nt(left, right):
    return lax.dot_general(left, right, (((1,), (1,)), ((), ())), preferred_element_type=F32)


def dot_tn(left, right):
    return lax.dot_general(left, right, (((0,), (0,)), ((), ())), preferred_element_type=F32)


def split_three(values):
    high = values.astype(BF16)
    rest = values - high.astype(F32)
    middle = rest.astype(BF16)
    low = (rest - middle.astype(F32)).astype(BF16)
    return high, middle, low


def params(**more):
    return pltpu.CompilerParams(vmem_limit_bytes=VMEM_LIMIT, **more)


def whole(shape):
    return pl.BlockSpec(shape, lambda *_: (0,) * len(shape))


def unpack_group(group, edge):
    return [group[:, edge * j : edge * (j + 1)] for j in range(PACK)]


def assemble_kernel(
    place_ref, in_ref, project_ref, outward_ref, expand_ref, contract_ref, store, *, load_steps
):
    step = pl.program_id(0)
    per_step, edge, _ = in_ref.shape

    @pl.when(step < load_steps)
    def _():
        def unpack(g, carry):
            pieces = unpack_group(in_ref[g], edge)
            for j in range(PACK):
                store[(step * per_step + g) * PACK + j, :, :edge] = pieces[j]
            return carry

        lax.fori_loop(0, per_step, unpack, 0)

    @pl.when(step >= load_steps)
    def _():
        row = step - load_steps
        strip = PACK * edge

        def fill(out_ref, rows, base):
            strips = out_ref.shape[1] // strip

            def body(k, carry):
                r = k // strips
                c = k - r * strips
                first = base + k * PACK
                blocks = [store[place_ref[first + j]][:, :edge] for j in range(PACK)]
                out_ref[pl.ds(pl.multiple_of(r * edge, edge), edge), pl.ds(pl.multiple_of(c * strip, strip), strip)] = (
                    jnp.concatenate(blocks, axis=1)
                )
                return carry

            lax.fori_loop(0, rows * strips, body, 0)
            return rows * strips * PACK

        steps = pl.num_programs(0) - load_steps
        offset = 0
        for out_ref in (project_ref, outward_ref, expand_ref, contract_ref):
            rows = out_ref.shape[0] // edge
            count = rows * (out_ref.shape[1] // strip) * PACK
            fill(out_ref, rows, offset + row * count)
            offset = offset + count * steps


def assemble(place, packed, width, hidden_width):
    groups, edge, strip = packed.shape
    per_step = 16
    load_steps = groups // per_step
    fill_steps = width // edge
    tall = hidden_width // fill_steps

    def late(step, *_):
        return (jnp.maximum(step - load_steps, 0), 0)

    return pl.pallas_call(
        functools.partial(assemble_kernel, load_steps=load_steps),
        out_shape=(
            jax.ShapeDtypeStruct((width, 3 * width), BF16),
            jax.ShapeDtypeStruct((width, width), BF16),
            jax.ShapeDtypeStruct((width, hidden_width), BF16),
            jax.ShapeDtypeStruct((hidden_width, width), BF16),
        ),
        grid_spec=pltpu.PrefetchScalarGridSpec(
            num_scalar_prefetch=1,
            grid=(load_steps + fill_steps,),
            in_specs=[
                pl.BlockSpec(
                    (per_step, edge, strip), lambda s, *_: (jnp.minimum(s, load_steps - 1), 0, 0)
                )
            ],
            out_specs=[
                pl.BlockSpec((edge, 3 * width), late),
                pl.BlockSpec((edge, width), late),
                pl.BlockSpec((edge, hidden_width), late),
                pl.BlockSpec((tall, width), late),
            ],
            scratch_shapes=[pltpu.VMEM((groups * PACK, edge, LANES), BF16)],
        ),
        compiler_params=params(),
        name="assemble_weights",
    )(place, packed)


def block_tables(slot_place, width, shard_width, hidden_width, edge):
    shards = slot_place.shape[0]
    model = width // edge
    wide = shard_width // edge
    tall = hidden_width // shards // edge
    ends = [3 * wide * model, wide * model, model * tall, tall * model]
    pieces = []
    offset = 0
    for count in ends:
        pieces.append(slot_place[:, offset : offset + count])
        offset += count
    project = pieces[0].reshape(shards, model, 3, wide).transpose(1, 2, 0, 3)
    outward = pieces[1].reshape(shards * wide, model)
    expand = pieces[2].reshape(shards, model, tall).transpose(1, 0, 2)
    contract = pieces[3].reshape(shards * tall, model)
    return [piece.reshape(-1) for piece in (project, outward, expand, contract)]


def norm_parts(values):
    scale = 1.0 / values.shape[-1]
    center = values - jnp.sum(values, -1, keepdims=True) * scale
    spread = jnp.sum(center * center, -1, keepdims=True) * scale
    inverse = lax.rsqrt(spread + NORM_EPSILON)
    return center * inverse, inverse


def norm_back(grad, unit, inverse, gain):
    scale = 1.0 / grad.shape[-1]
    inner = grad * gain
    mean_one = jnp.sum(inner, -1, keepdims=True) * scale
    mean_two = jnp.sum(inner * unit, -1, keepdims=True) * scale
    return (inner - mean_one - unit * mean_two) * inverse


def turn(values, cosine, sine):
    lane = lax.broadcasted_iota(jnp.int32, values.shape, 1)
    half = HS // 2
    ahead = pltpu.roll(values, LANES - half, 1)
    behind = pltpu.roll(values, half, 1)
    other = jnp.where(lane % HS < half, ahead, behind)
    return values * cosine + other * sine


def front_kernel(
    codon_ref, table_ref, norm_ref, project_ref, cos_ref, sin_ref, x_ref, h_ref, q_ref, k_ref, v_ref
):
    rows = codon_ref.shape[0]
    vocab, width = table_ref.shape
    index = lax.broadcasted_iota(jnp.int32, (rows, vocab), 1)
    hot = jnp.where(codon_ref[...] == index, 1.0, 0.0).astype(BF16)
    high, middle, low = split_three(table_ref[...])
    embedded = (dot(hot, high) + dot(hot, middle)) + dot(hot, low)
    embedded = embedded * math.sqrt(width)
    x_ref[...] = embedded
    unit, _ = norm_parts(embedded)
    normed = (unit * norm_ref[0:1, :] + norm_ref[1:2, :]).astype(BF16)
    h_ref[...] = normed
    cosine = cos_ref[...]
    sine = sin_ref[...]
    for part, out_ref in ((0, q_ref), (1, k_ref), (2, v_ref)):
        values = dot(normed, project_ref[:, part * width : (part + 1) * width])
        for c in range(width // LANES):
            piece = values[:, c * LANES : (c + 1) * LANES]
            if part < 2:
                piece = turn(piece, cosine, sine)
            if part == 0:
                piece = piece * HS ** (-0.5)
            out_ref[:, c * LANES : (c + 1) * LANES] = piece.astype(BF16)


def front(codon_column, table, norm_params, project, cosine, sine):
    length = codon_column.shape[0]
    vocab, width = table.shape
    rows = 256
    spec = pl.BlockSpec((rows, width), lambda i: (i, 0))
    low = jax.ShapeDtypeStruct((length, width), BF16)
    return pl.pallas_call(
        front_kernel,
        out_shape=(jax.ShapeDtypeStruct((length, width), F32), low, low, low, low),
        grid=(length // rows,),
        in_specs=[
            pl.BlockSpec((rows, 1), lambda i: (i, 0)),
            whole(table.shape),
            whole(norm_params.shape),
            whole(project.shape),
            pl.BlockSpec((rows, LANES), lambda i: (i, 0)),
            pl.BlockSpec((rows, LANES), lambda i: (i, 0)),
        ],
        out_specs=(spec, spec, spec, spec, spec),
        compiler_params=params(),
        name="embed_project",
    )(codon_column, table, norm_params, project, cosine, sine)


TILE = 256


def head_masks(rows):
    lane = lax.broadcasted_iota(jnp.int32, (rows, LANES), 1)
    return [lane // HS == h for h in range(LANES // HS)]


def attend_kernel(low_ref, high_ref, q_ref, k_ref, v_ref, seg_col_ref, seg_row_ref, o_ref, lse_ref, scores):
    tile = pl.program_id(1)
    first, last = low_ref[tile], high_ref[tile]
    query = q_ref[...]
    masks = head_masks(TILE)
    zero = jnp.zeros_like(query)
    parts = [jnp.where(mask, query, zero) for mask in masks]
    seg_col = seg_col_ref[...]

    def score(j, tops):
        start = pl.multiple_of(j * TILE, TILE)
        keys = k_ref[pl.ds(start, TILE), :]
        same = seg_col == seg_row_ref[j]
        new = []
        for h, part in enumerate(parts):
            s = jnp.where(same, dot_nt(part, keys), MASK_VALUE)
            scores[h, j] = s
            top = tops[h]
            for c in range(TILE // LANES):
                top = jnp.maximum(top, s[:, c * LANES : (c + 1) * LANES])
            new.append(top)
        return tuple(new)

    begin = jnp.full((TILE, LANES), -jnp.inf, F32)
    tops = lax.fori_loop(first, last, score, (begin,) * len(parts))
    tops = [jnp.max(top, -1, keepdims=True) for top in tops]

    def total(j, sums):
        new = []
        for h in range(len(parts)):
            e = jnp.exp(scores[h, j] - tops[h])
            scores[h, j] = e
            acc = sums[h]
            for c in range(TILE // LANES):
                acc = acc + e[:, c * LANES : (c + 1) * LANES]
            new.append(acc)
        return tuple(new)

    sums = lax.fori_loop(first, last, total, (jnp.zeros((TILE, LANES), F32),) * len(parts))
    sums = [jnp.sum(acc, -1, keepdims=True) for acc in sums]
    inverse = [1.0 / acc for acc in sums]

    def gather(j, outs):
        start = pl.multiple_of(j * TILE, TILE)
        values = v_ref[pl.ds(start, TILE), :]
        return tuple(
            out + dot((scores[h, j] * inverse[h]).astype(BF16), values) for h, out in enumerate(outs)
        )

    outs = lax.fori_loop(first, last, gather, (jnp.zeros((TILE, LANES), F32),) * len(parts))
    o_ref[...] = jnp.where(masks[0], outs[0], outs[1]).astype(BF16)
    logs = [top + jnp.log(acc) for top, acc in zip(tops, sums)]
    lse_ref[...] = jnp.where(masks[0], logs[0], logs[1])


def attend(low, high, query, keys, values, seg_col, seg_row):
    length, width = query.shape
    tiles = length // TILE
    pairs = width // LANES
    column = pl.BlockSpec((TILE, LANES), lambda p, i, *_: (i, p))
    full = pl.BlockSpec((length, LANES), lambda p, i, *_: (0, p))
    return pl.pallas_call(
        attend_kernel,
        out_shape=(
            jax.ShapeDtypeStruct((length, width), BF16),
            jax.ShapeDtypeStruct((length, width), F32),
        ),
        grid_spec=pltpu.PrefetchScalarGridSpec(
            num_scalar_prefetch=2,
            grid=(pairs, tiles),
            in_specs=[
                column,
                full,
                full,
                pl.BlockSpec((TILE, 1), lambda p, i, *_: (i, 0)),
                whole((tiles, 1, TILE)),
            ],
            out_specs=(column, column),
            scratch_shapes=[pltpu.VMEM((LANES // HS, tiles, TILE, TILE), F32)],
        ),
        compiler_params=params(),
        name="attend_forward",
    )(low, high, query, keys, values, seg_col, seg_row)


def attend_back_kernel(
    low_ref, high_ref, q_ref, k_ref, v_ref, g_ref, lse_ref, seg_col_ref, seg_row_ref, cos_ref, sin_ref,
    dq_ref, dk_ref, dv_ref, prob_buf, grad_buf, dk_acc, dv_acc,
):
    tile = pl.program_id(1)
    tiles = pl.num_programs(1)
    heads = LANES // HS

    @pl.when(tile == 0)
    def _():
        dk_acc[...] = jnp.zeros_like(dk_acc)
        dv_acc[...] = jnp.zeros_like(dv_acc)

    first, last = low_ref[tile], high_ref[tile]
    query = q_ref[...]
    grad = g_ref[...]
    masks = head_masks(TILE)
    zero = jnp.zeros_like(query)
    queries = [jnp.where(mask, query, zero) for mask in masks]
    grads = [jnp.where(mask, grad, zero) for mask in masks]
    query_turned = [part.T for part in queries]
    grad_turned = [part.T for part in grads]
    seg_col = seg_col_ref[...]
    logs = [lse_ref[:, h * HS : h * HS + 1] for h in range(heads)]

    def probe(j, deltas):
        start = pl.multiple_of(j * TILE, TILE)
        keys = k_ref[pl.ds(start, TILE), :]
        values = v_ref[pl.ds(start, TILE), :]
        same = seg_col == seg_row_ref[j]
        new = []
        for h in range(heads):
            s = jnp.where(same, dot_nt(queries[h], keys), MASK_VALUE)
            p = jnp.exp(s - logs[h])
            gp = dot_nt(grads[h], values)
            prob_buf[h, j] = p
            grad_buf[h, j] = gp
            product = p * gp
            acc = deltas[h]
            for c in range(TILE // LANES):
                acc = acc + product[:, c * LANES : (c + 1) * LANES]
            new.append(acc)
        return tuple(new)

    deltas = lax.fori_loop(first, last, probe, (jnp.zeros((TILE, LANES), F32),) * heads)
    deltas = [jnp.sum(acc, -1, keepdims=True) for acc in deltas]

    def push(j, dq):
        start = pl.multiple_of(j * TILE, TILE)
        keys = k_ref[pl.ds(start, TILE), :]
        dk = dk_acc[j]
        dv = dv_acc[j]
        outs = []
        for h in range(heads):
            p = prob_buf[h, j]
            gs = (p * (grad_buf[h, j] - deltas[h])).astype(BF16)
            outs.append(dq[h] + dot(gs, keys))
            dk = dk + dot(query_turned[h], gs)
            dv = dv + dot(grad_turned[h], p.astype(BF16))
        dk_acc[j] = dk
        dv_acc[j] = dv
        return tuple(outs)

    dq = lax.fori_loop(first, last, push, (jnp.zeros((TILE, LANES), F32),) * heads)
    dq = jnp.where(masks[0], dq[0], dq[1]) * HS ** (-0.5)
    start = pl.multiple_of(tile * TILE, TILE)
    rows = pl.ds(start, TILE)
    dq_ref[rows, :] = turn(dq, cos_ref[rows, :], -sin_ref[rows, :]).astype(BF16)

    @pl.when(tile == tiles - 1)
    def _():
        for j in range(dk_acc.shape[0]):
            rows = slice(j * TILE, (j + 1) * TILE)
            dk = dk_acc[j].T
            dk_ref[rows, :] = turn(dk, cos_ref[rows, :], -sin_ref[rows, :]).astype(BF16)
            dv_ref[rows, :] = dv_acc[j].T.astype(BF16)


def attend_back(low, high, query, keys, values, grad, lse, seg_col, seg_row, cosine, sine):
    length, width = query.shape
    tiles = length // TILE
    pairs = width // LANES
    heads = LANES // HS
    column = pl.BlockSpec((TILE, LANES), lambda p, i, *_: (i, p))
    full = pl.BlockSpec((length, LANES), lambda p, i, *_: (0, p))
    low_out = jax.ShapeDtypeStruct((length, width), BF16)
    return pl.pallas_call(
        attend_back_kernel,
        out_shape=(low_out, low_out, low_out),
        grid_spec=pltpu.PrefetchScalarGridSpec(
            num_scalar_prefetch=2,
            grid=(pairs, tiles),
            in_specs=[
                column,
                full,
                full,
                column,
                column,
                pl.BlockSpec((TILE, 1), lambda p, i, *_: (i, 0)),
                whole((tiles, 1, TILE)),
                whole((length, LANES)),
                whole((length, LANES)),
            ],
            out_specs=(full, full, full),
            scratch_shapes=[
                pltpu.VMEM((heads, tiles, TILE, TILE), F32),
                pltpu.VMEM((heads, tiles, TILE, TILE), F32),
                pltpu.VMEM((tiles, LANES, TILE), F32),
                pltpu.VMEM((tiles, LANES, TILE), F32),
            ],
        ),
        compiler_params=params(),
        name="attend_backward",
    )(low, high, query, keys, values, grad, lse, seg_col, seg_row, cosine, sine)


INV_SQRT_TWO = 2.0 ** (-0.5)
INV_SQRT_TWO_PI = (2.0 * math.pi) ** (-0.5)


def middle_kernel(
    x_ref, att_ref, target_ref, mask_ref, count_ref, norm_ref, table_ref,
    outward_ref, expand_ref, contract_ref,
    h_ref, active_ref, d_two_ref, ghid_ref, d_one_ref, gatt_ref, gx_ref, head_ref, norm_grad_ref,
    slope,
):
    step = pl.program_id(0)
    rows, width = x_ref.shape
    vocab = table_ref.shape[0]
    ff = expand_ref.shape[1]
    part = width

    @pl.when(step == 0)
    def _():
        head_ref[...] = jnp.zeros_like(head_ref)
        norm_grad_ref[...] = jnp.zeros_like(norm_grad_ref)

    middle = x_ref[...] + dot(att_ref[...], outward_ref[...])
    unit_two, inverse_two = norm_parts(middle)
    gain_two = norm_ref[2:3, :]
    normed_two = (unit_two * gain_two + norm_ref[3:4, :]).astype(BF16)
    h_ref[...] = normed_two

    def forward(c, total):
        cols = pl.ds(pl.multiple_of(c * part, part), part)
        hidden = dot(normed_two, expand_ref[:, cols])
        cumulative = 0.5 + 0.5 * lax.erf(hidden * INV_SQRT_TWO)
        active = (hidden * cumulative).astype(BF16)
        density = jnp.exp(-0.5 * hidden * hidden) * INV_SQRT_TWO_PI
        slope[:, cols] = cumulative + hidden * density
        active_ref[:, cols] = active
        return total + dot(active, contract_ref[cols, :])

    branch = lax.fori_loop(0, ff // part, forward, jnp.zeros((rows, width), F32))
    unit, inverse = norm_parts(middle + branch)
    gain = norm_ref[4:5, :]
    final = (unit * gain + norm_ref[5:6, :]).astype(BF16)
    table = table_ref[...].astype(BF16)
    logits = dot_nt(final, table)
    shifted = logits - jnp.max(logits, -1, keepdims=True)
    exps = jnp.exp(shifted)
    sums = jnp.sum(exps, -1, keepdims=True)
    hot = target_ref[...] == lax.broadcasted_iota(jnp.int32, (rows, vocab), 1)
    mask = mask_ref[...]
    log_probs = shifted - jnp.log(sums)
    picked = jnp.sum(jnp.where(hot, log_probs, 0.0) * mask, 0, keepdims=True)
    norm_grad_ref[6:7, 0:vocab] -= picked
    glogits = ((jnp.exp(log_probs) - jnp.where(hot, 1.0, 0.0)) * (mask / count_ref[...])).astype(BF16)
    head_ref[...] += dot_tn(glogits, final)
    gfinal = dot(glogits, table)
    norm_grad_ref[4:5, :] += jnp.sum(gfinal * unit, 0, keepdims=True)
    norm_grad_ref[5:6, :] += jnp.sum(gfinal, 0, keepdims=True)
    gx_two = norm_back(gfinal, unit, inverse, gain)
    d_two = gx_two.astype(BF16)
    d_two_ref[...] = d_two

    def backward(c, total):
        cols = pl.ds(pl.multiple_of(c * part, part), part)
        gactive = dot_nt(d_two, contract_ref[cols, :])
        ghid = (gactive * slope[:, cols]).astype(BF16)
        ghid_ref[:, cols] = ghid
        return total + dot_nt(ghid, expand_ref[:, cols])

    gh = lax.fori_loop(0, ff // part, backward, jnp.zeros((rows, width), F32))
    norm_grad_ref[2:3, :] += jnp.sum(gh * unit_two, 0, keepdims=True)
    norm_grad_ref[3:4, :] += jnp.sum(gh, 0, keepdims=True)
    gx_one = gx_two + norm_back(gh, unit_two, inverse_two, gain_two)
    gx_ref[...] = gx_one
    d_one = gx_one.astype(BF16)
    d_one_ref[...] = d_one
    gatt_ref[...] = dot_nt(d_one, outward_ref[...]).astype(BF16)


def middle_rows(x, att, target_col, mask_col, count, norm_params, table, outward, expand, contract):
    length, width = x.shape
    vocab = table.shape[0]
    ff = expand.shape[1]
    rows = 256
    narrow = pl.BlockSpec((rows, width), lambda i: (i, 0))
    broad = pl.BlockSpec((rows, ff), lambda i: (i, 0))
    column = pl.BlockSpec((rows, 1), lambda i: (i, 0))
    low = jax.ShapeDtypeStruct((length, width), BF16)
    low_broad = jax.ShapeDtypeStruct((length, ff), BF16)
    return pl.pallas_call(
        middle_kernel,
        out_shape=(
            low, low_broad, low, low_broad, low, low,
            jax.ShapeDtypeStruct((length, width), F32),
            jax.ShapeDtypeStruct((vocab, width), F32),
            jax.ShapeDtypeStruct((8, width), F32),
        ),
        grid=(length // rows,),
        in_specs=[
            narrow, narrow, column, column, whole((1, 1)), whole(norm_params.shape), whole(table.shape),
            whole(outward.shape), whole(expand.shape), whole(contract.shape),
        ],
        out_specs=(
            narrow, broad, narrow, broad, narrow, narrow, narrow,
            whole((vocab, width)), whole((8, width)),
        ),
        scratch_shapes=[pltpu.VMEM((rows, ff), F32)],
        compiler_params=params(),
        name="middle_rows",
    )(x, att, target_col, mask_col, count, norm_params, table, outward, expand, contract)


def tail_kernel(
    codon_ref, x_ref, gx_ref, dq_ref, dk_ref, dv_ref, norm_ref, project_ref, head_ref, norm_in_ref,
    table_grad_ref, norm_grad_ref,
):
    step = pl.program_id(0)
    rows, width = x_ref.shape
    vocab = head_ref.shape[0]

    @pl.when(step == 0)
    def _():
        table_grad_ref[...] = head_ref[...]
        norm_grad_ref[...] = norm_in_ref[...]

    gh = dot_nt(dq_ref[...], project_ref[:, 0:width])
    gh = gh + dot_nt(dk_ref[...], project_ref[:, width : 2 * width])
    gh = gh + dot_nt(dv_ref[...], project_ref[:, 2 * width : 3 * width])
    unit, inverse = norm_parts(x_ref[...])
    norm_grad_ref[0:1, :] += jnp.sum(gh * unit, 0, keepdims=True)
    norm_grad_ref[1:2, :] += jnp.sum(gh, 0, keepdims=True)
    gx = gx_ref[...] + norm_back(gh, unit, inverse, norm_ref[0:1, :])
    hot = jnp.where(codon_ref[...] == lax.broadcasted_iota(jnp.int32, (rows, vocab), 1), 1.0, 0.0)
    hot = hot.T.astype(BF16)
    high, middle, low = split_three(gx)
    total = dot(hot, high) + (dot(hot, middle) + dot(hot, low))
    table_grad_ref[...] += total * math.sqrt(width)


def tail_rows(codon_col, x, gx, dq, dk, dv, norm_params, project, head, norm_in):
    length, width = x.shape
    rows = 256
    narrow = pl.BlockSpec((rows, width), lambda i: (i, 0))
    return pl.pallas_call(
        tail_kernel,
        out_shape=(
            jax.ShapeDtypeStruct(head.shape, F32),
            jax.ShapeDtypeStruct(norm_in.shape, F32),
        ),
        grid=(length // rows,),
        in_specs=[
            pl.BlockSpec((rows, 1), lambda i: (i, 0)),
            narrow, narrow, narrow, narrow, narrow,
            whole(norm_params.shape), whole(project.shape), whole(head.shape), whole(norm_in.shape),
        ],
        out_specs=(whole(head.shape), whole(norm_in.shape)),
        compiler_params=params(),
        name="tail_rows",
    )(codon_col, x, gx, dq, dk, dv, norm_params, project, head, norm_in)


def weight_grad_kernel(place_ref, left_ref, right_ref, *rest, edge):
    out_ref, buf, sem = rest[-3:]
    step = pl.program_id(0) * pl.num_programs(1) + pl.program_id(1)
    steps = pl.num_programs(0) * pl.num_programs(1)
    count = buf.shape[1]
    slot = lax.rem(step, 2)
    strip = PACK * edge
    block_rows = count // PACK

    def drain(which):
        pltpu.make_async_copy(buf.at[which], out_ref.at[pl.ds(0, count)], sem.at[which]).wait()

    @pl.when(step >= 2)
    def _():
        drain(slot)

    right = right_ref[...]
    left = left_ref[...]
    result = dot_tn(left, right)
    for r in range(block_rows):
        pieces = unpack_group(result[r * edge : (r + 1) * edge, :], edge)
        for j in range(PACK):
            buf[slot, r * PACK + j, :, :edge] = pieces[j]

    def send(k, carry):
        target = place_ref[step * count + k]
        pltpu.make_async_copy(buf.at[slot, k], out_ref.at[target], sem.at[slot]).start()
        return carry

    lax.fori_loop(0, count, send, 0)

    @pl.when(step == steps - 1)
    def _():
        @pl.when(step >= 1)
        def _():
            drain(1 - slot)

        drain(slot)


def weight_grad(place, left, right, into, blocks, edge, left_cols, name):
    length, tall = left.shape
    broad = right.shape[1]
    strip = PACK * edge
    grid = (tall // left_cols, broad // strip)
    count = left_cols // edge * PACK
    operands = [place, left, right]
    in_specs = [
        pl.BlockSpec((length, left_cols), lambda a, b, *_: (0, a)),
        pl.BlockSpec((length, strip), lambda a, b, *_: (0, b)),
    ]
    aliases = {}
    if into is not None:
        operands.append(into)
        in_specs.append(pl.BlockSpec(memory_space=pl.ANY))
        aliases = {3: 0}
    return pl.pallas_call(
        functools.partial(weight_grad_kernel, edge=edge),
        out_shape=jax.ShapeDtypeStruct((blocks, edge, LANES), F32),
        grid_spec=pltpu.PrefetchScalarGridSpec(
            num_scalar_prefetch=1,
            grid=grid,
            in_specs=in_specs,
            out_specs=pl.BlockSpec(memory_space=pl.ANY),
            scratch_shapes=[
                pltpu.VMEM((2, count, edge, LANES), F32),
                pltpu.SemaphoreType.DMA((2,)),
            ],
        ),
        input_output_aliases=aliases,
        compiler_params=params(),
        name=name,
    )(*operands)


def by_strips(table, rows, cols, chunk):
    shaped = table.reshape(rows // chunk, chunk, cols // PACK, PACK)
    return shaped.transpose(0, 2, 1, 3).reshape(-1)


CORE, NEAR_Y, NEAR_X, NEAR_Z, FAR_Z = range(5)
AXIS_STRIDE = {CORE: 1, NEAR_Y: 2, NEAR_X: 4, NEAR_Z: 8, FAR_Z: 16}
CHUNK_AXES = (
    (NEAR_X, NEAR_Y, NEAR_Z, FAR_Z),
    (NEAR_Y, NEAR_X, NEAR_Z, FAR_Z),
    (NEAR_Z, NEAR_X, NEAR_Y, FAR_Z),
    (NEAR_X, NEAR_Y, NEAR_Z, FAR_Z),
    (NEAR_Y, NEAR_X, NEAR_Z, FAR_Z),
    (NEAR_Z, NEAR_Y, NEAR_X, FAR_Z),
)
SUM_ORDER = (
    (0, 0), (0, 1), (1, 0), (1, 1), (0, 2), (0, 3), (1, 2), (1, 3), (0, 4), (0, 5), (2, 0), (1, 4), (2, 1),
    (1, 5), (2, 2), (3, 0), (2, 3), (3, 1), (2, 5), (2, 4), (4, 0), (3, 2), (4, 1), (3, 3), (5, 0), (5, 1),
    (3, 4), (4, 3), (3, 5), (4, 4), (5, 3), (4, 2), (4, 5), (5, 4), (5, 2), (5, 5),
)
SMALL_ROWS = 1024
SMALL_AXES = (CORE, NEAR_X, NEAR_Y, NEAR_Z, FAR_Z)
MESH = pl.DeviceIdType.MESH


def on_known_slice(owners, shards, slots):
    return owners == 8 and shards == 4 and slots % PACK == 0 and slots // PACK == len(CHUNK_AXES)


def own_bits():
    owner, shard = lax.axis_index("dp"), lax.axis_index("tensor")
    return owner, shard, {
        CORE: shard % 2,
        NEAR_Y: shard // 2,
        NEAR_X: owner % 2,
        NEAR_Z: owner // 2 % 2,
        FAR_Z: owner // 4,
    }


def partner_of(axis, owner, shard, bits):
    if axis == CORE:
        return (owner, shard + 1 - 2 * bits[CORE])
    if axis == NEAR_Y:
        return (owner, shard + 2 - 4 * bits[NEAR_Y])
    step = {NEAR_X: 1, NEAR_Z: 2, FAR_Z: 4}[axis]
    return (owner + step - 2 * step * bits[axis], shard)


def meet_partners(owner, shard, bits):
    barrier = pltpu.get_barrier_semaphore()
    for axis in range(5):
        pl.semaphore_signal(
            barrier, inc=1, device_id=partner_of(axis, owner, shard, bits), device_id_type=MESH
        )
    pl.semaphore_wait(barrier, 5)


def sum_kernel(
    grads_ref, table_ref, norm_ref, owned_ref, table_out, norm_out, square_out,
    inbuf, stage, r0, r1, r2, r3, r4, small, s0, s1, s2, s3, s4, spread, square, squares,
    in_sem, send_sem, recv_sem, small_send, small_recv, square_send, square_recv,
):
    owner, shard, bits = own_bits()
    edge = grads_ref.shape[3]
    strip = PACK * edge
    chunks = len(CHUNK_AXES)
    received = (r0, r1, r2, r3, r4)

    def fetch(g):
        return pltpu.make_async_copy(grads_ref.at[g], inbuf.at[g % 2], in_sem.at[g % 2])

    fetch(0).start()
    fetch(1).start()
    meet_partners(owner, shard, bits)

    def send(source, target, axis, g, k):
        return pltpu.make_async_remote_copy(
            src_ref=source,
            dst_ref=target,
            send_sem=send_sem.at[g, k],
            recv_sem=recv_sem.at[g, k],
            device_id=partner_of(axis, owner, shard, bits),
            device_id_type=MESH,
        )

    def chunk_send(g, k):
        if k == 0:
            return send(stage.at[g % 2], r0.at[g], CORE, g, 0)
        axis = CHUNK_AXES[g][k - 1]
        half = received[k - 1].shape[1] // 2
        return send(
            received[k - 1].at[g, pl.ds(half * (1 - bits[axis]), half)], received[k].at[g], axis, g, k
        )

    def packed(g, e, core):
        d = core
        for k, axis in enumerate(CHUNK_AXES[g]):
            d = d + e // (8 >> k) % 2 * AXIS_STRIDE[axis]
        blocks = [inbuf[g % 2, d, j][:, :edge] for j in range(PACK)]
        return jnp.concatenate(blocks, axis=1)

    def pack(g):
        fetch(g).wait()
        if g >= 2:
            chunk_send(g - 2, 0).wait_send()

        def body(e, carry):
            stage[g % 2, e] = packed(g, e, 1 - bits[CORE])
            return carry

        lax.fori_loop(0, 16, body, 0)
        chunk_send(g, 0).start()

    def merge_own(g):
        chunk_send(g, 0).wait_recv()

        def body(e, carry):
            r0[g, e] = r0[g, e] + packed(g, e, bits[CORE])
            return carry

        lax.fori_loop(0, 16, body, 0)
        chunk_send(g, 1).start()
        if g + 2 < chunks:
            fetch(g + 2).start()

    def merge(g, k):
        chunk_send(g, k).wait_recv()
        axis = CHUNK_AXES[g][k - 1]
        half = received[k].shape[1]
        base = half * bits[axis]

        def body(e, carry):
            received[k][g, e] = received[k][g, e] + received[k - 1][g, base + e]
            return carry

        lax.fori_loop(0, half, body, 0)
        if k < 4:
            chunk_send(g, k + 1).start()
        else:
            group = r4[g, 0]
            pieces = unpack_group(group, edge)
            for j in range(PACK):
                owned_ref[PACK * g + j] = pieces[j]
            parts = group * group
            line = parts[:, :LANES]
            for c in range(1, strip // LANES):
                line = line + parts[:, c * LANES : (c + 1) * LANES]
            total = square[...]
            for r in range(edge // 8):
                total = total + line[r * 8 : (r + 1) * 8]
            square[...] = total

    vocab, width = table_ref.shape
    vectors = norm_ref.shape[0]
    columns = width // LANES
    small_parts = (s0, s1, s2, s3, s4)

    def small_fill():
        for c in range(columns):
            lanes = slice(c * LANES, (c + 1) * LANES)
            small[c * vocab : (c + 1) * vocab] = table_ref[:, lanes]
            start = columns * vocab + c * vectors
            small[start : start + vectors] = norm_ref[:, lanes]
        used = columns * (vocab + vectors)
        small[used:] = jnp.zeros((SMALL_ROWS - used, LANES), F32)

    def small_base(k):
        base = 0
        for i in range(k):
            base = base + (SMALL_ROWS >> (i + 1)) * bits[SMALL_AXES[i]]
        return base

    def small_copy(k):
        rows = SMALL_ROWS >> (k + 1)
        start = pl.multiple_of(small_base(k) + rows * (1 - bits[SMALL_AXES[k]]), 8)
        return pltpu.make_async_remote_copy(
            src_ref=small.at[pl.ds(start, rows)],
            dst_ref=small_parts[k],
            send_sem=small_send.at[k],
            recv_sem=small_recv.at[k],
            device_id=partner_of(SMALL_AXES[k], owner, shard, bits),
            device_id_type=MESH,
        )

    def small_merge(k):
        small_copy(k).wait_recv()
        rows = SMALL_ROWS >> (k + 1)
        mine = pl.ds(pl.multiple_of(small_base(k + 1), 8), rows)
        if k < 4:
            small[mine, :] = small[mine, :] + small_parts[k][...]
            small_copy(k + 1).start()
        else:
            spread[mine, :] = small[mine, :] + small_parts[k][...]
            spread_copy(4).start()

    def spread_copy(k):
        rows = SMALL_ROWS >> (k + 1)
        here = pl.ds(pl.multiple_of(small_base(k + 1), 8), rows)
        return pltpu.make_async_remote_copy(
            src_ref=spread.at[here],
            dst_ref=spread.at[here],
            send_sem=small_send.at[5 + k],
            recv_sem=small_recv.at[5 + k],
            device_id=partner_of(SMALL_AXES[k], owner, shard, bits),
            device_id_type=MESH,
        )

    def spread_next(k):
        spread_copy(k).wait_recv()
        if k > 0:
            spread_copy(k - 1).start()
        else:
            for c in range(columns):
                lanes = slice(c * LANES, (c + 1) * LANES)
                table_out[:, lanes] = spread[c * vocab : (c + 1) * vocab]
                start = columns * vocab + c * vectors
                norm_out[:, lanes] = spread[start : start + vectors]

    square[...] = jnp.zeros_like(square)
    small_fill()
    small_copy(0).start()
    extra = [functools.partial(small_merge, k) for k in range(5)]
    extra += [functools.partial(spread_next, k) for k in range(4, -1, -1)]
    for position, (k, g) in enumerate(SUM_ORDER):
        if k == 0:
            pack(g)
        elif k == 1:
            merge_own(g)
        else:
            merge(g, k - 1)
        if position >= 9 and (position - 9) % 2 == 0 and extra:
            extra.pop(0)()
    while extra:
        extra.pop(0)()

    def square_copy(k):
        return pltpu.make_async_remote_copy(
            src_ref=squares.at[k],
            dst_ref=squares.at[5 + k],
            send_sem=square_send.at[k],
            recv_sem=square_recv.at[k],
            device_id=partner_of(SMALL_AXES[k], owner, shard, bits),
            device_id_type=MESH,
        )

    value = square[...]
    for k in range(5):
        squares[k] = value
        square_copy(k).start()
        square_copy(k).wait_recv()
        value = squares[k] + squares[5 + k]
    square_out[...] = value

    for g in range(chunks):
        for k in range(5):
            if k > 0 or g >= chunks - 2:
                chunk_send(g, k).wait_send()
    for k in range(5):
        small_copy(k).wait_send()
        spread_copy(k).wait_send()
        square_copy(k).wait_send()


def sum_everywhere(grads, table_grad, norm_grad):
    chunks, devices, _, edge, _ = grads.shape
    strip = PACK * edge
    group = lambda count: pltpu.VMEM((chunks, count, edge, strip), F32)
    small = lambda rows: pltpu.VMEM((rows, LANES), F32)
    return pl.pallas_call(
        sum_kernel,
        out_shape=(
            jax.ShapeDtypeStruct((chunks * PACK, edge, edge), F32),
            jax.ShapeDtypeStruct(table_grad.shape, F32),
            jax.ShapeDtypeStruct(norm_grad.shape, F32),
            jax.ShapeDtypeStruct((8, LANES), F32),
        ),
        in_specs=[
            pl.BlockSpec(memory_space=pl.ANY),
            pl.BlockSpec(memory_space=pltpu.VMEM),
            pl.BlockSpec(memory_space=pltpu.VMEM),
        ],
        out_specs=(pl.BlockSpec(memory_space=pltpu.VMEM),) * 4,
        scratch_shapes=[
            pltpu.VMEM((2, devices, PACK, edge, LANES), F32),
            pltpu.VMEM((2, devices // 2, edge, strip), F32),
            group(16), group(8), group(4), group(2), group(1),
            small(SMALL_ROWS), small(512), small(256), small(128), small(64), small(32), small(SMALL_ROWS),
            pltpu.VMEM((8, LANES), F32),
            pltpu.VMEM((10, 8, LANES), F32),
            pltpu.SemaphoreType.DMA((2,)),
            pltpu.SemaphoreType.DMA((chunks, 5)),
            pltpu.SemaphoreType.DMA((chunks, 5)),
            pltpu.SemaphoreType.DMA((10,)),
            pltpu.SemaphoreType.DMA((10,)),
            pltpu.SemaphoreType.DMA((5,)),
            pltpu.SemaphoreType.DMA((5,)),
        ],
        compiler_params=pltpu.CompilerParams(
            vmem_limit_bytes=66_000_000, collective_id=1, has_side_effects=True
        ),
        name="sum_gradients",
    )(grads, table_grad, norm_grad)


def shampoo(grad, left, right, left_root, right_root, weight):
    new_left = STAT_DECAY * left + (1.0 - STAT_DECAY) * jnp.einsum(
        "...ij,...kj->...ik", grad, grad, precision=TOP_PRECISION
    )
    new_right = STAT_DECAY * right + (1.0 - STAT_DECAY) * jnp.einsum(
        "...ji,...jk->...ik", grad, grad, precision=TOP_PRECISION
    )
    partial_left = jnp.einsum("...ij,...jk->...ik", left_root, grad, precision=TOP_PRECISION)
    precond = jnp.einsum("...ij,...jk->...ik", partial_left, right_root, precision=TOP_PRECISION)
    scale_back = lax.rsqrt(jnp.mean(precond * precond, axis=(-2, -1), keepdims=True) + ROOT_EPSILON)
    new_weight = weight * (1.0 - MATRIX_RATE * WEIGHT_DECAY) - MATRIX_RATE * precond * scale_back
    return (new_left, new_right, new_weight)


def adamw(grad, moment, second, weight, step_value):
    new_moment = FIRST_BETA * moment + (1.0 - FIRST_BETA) * grad
    new_second = SECOND_BETA * second + (1.0 - SECOND_BETA) * grad * grad
    corrected_one = new_moment / (1.0 - FIRST_BETA**step_value)
    corrected_two = new_second / (1.0 - SECOND_BETA**step_value)
    new_weight = weight - VECTOR_RATE * (
        corrected_one / (jnp.sqrt(corrected_two) + ADAM_EPSILON) + WEIGHT_DECAY * weight
    )
    return (new_moment, new_second, new_weight)


def rotary_tables(length):
    half = HS // 2
    freqs = jnp.exp(-math.log(ROTARY_BASE) * (2.0 * jnp.arange(half, dtype=F32) / HS))
    angles = jnp.arange(length, dtype=F32)[:, None] * freqs[None, :]
    cosine, sine = jnp.cos(angles), jnp.sin(angles)
    repeats = LANES // HS
    return (
        jnp.concatenate([cosine, cosine] * repeats, -1),
        jnp.concatenate([-sine, sine] * repeats, -1),
    )


def pack_blocks(blocks):
    count, edge, _ = blocks.shape
    groups = blocks.reshape(count // PACK, PACK, edge, edge).transpose(0, 2, 1, 3)
    return groups.reshape(count // PACK, edge, PACK * edge)


def gather_weights(own):
    everyone = ("dp", "tensor")
    slots, edge, _ = own.shape
    if slots % PACK == 0:
        packed = lax.all_gather(pack_blocks(own), everyone, axis=0, tiled=True)
    else:
        packed = pack_blocks(lax.all_gather(own, everyone, axis=0, tiled=True))
    return packed, lambda device, slot: device * slots + slot


def body(
    codons,
    segments,
    targets,
    loss_mask,
    owner_map,
    step_count,
    block_weight,
    block_left,
    block_right,
    block_left_root,
    block_right_root,
    embedding_weight,
    table_left,
    table_right,
    table_left_root,
    table_right_root,
    norm_params,
    norm_moment,
    norm_second,
):
    everyone = ("dp", "tensor")
    vocab, width = embedding_weight.shape
    shards = lax.axis_size("tensor")
    owners = lax.axis_size("dp")
    slots = block_weight.shape[1]
    edge = block_weight.shape[-1]
    blocks = owner_map.shape[0]
    length = codons.shape[1]
    shard_width = width // shards

    packed, place_of = gather_weights(block_weight[0].astype(BF16))
    owner, slot = owner_map // slots, owner_map % slots
    device = owner[None, :] * shards + jnp.arange(shards, dtype=jnp.int32)[:, None]
    slot = jnp.broadcast_to(slot[None, :], device.shape)
    place = jnp.concatenate(block_tables(place_of(device, slot), width, shard_width, FF, edge))
    project, outward, expand, contract = assemble(place, packed, width, FF)

    mask_col = loss_mask.reshape(length, 1).astype(F32)
    count = jnp.maximum(lax.psum(jnp.sum(mask_col), everyone), 1.0)
    codon_col = codons.reshape(length, 1)
    target_col = targets.reshape(length, 1)
    segment = lax.dynamic_index_in_dim(segments, lax.axis_index("tensor"), 0, keepdims=False)
    tiles = length // TILE
    seg_col = segment.reshape(length, 1)
    seg_row = segment.reshape(tiles, 1, TILE)
    tiled = segment.reshape(tiles, TILE)
    before = jnp.sum((segment[None, :] < tiled[:, :1]).astype(jnp.int32), -1)
    until = jnp.sum((segment[None, :] <= tiled[:, -1:]).astype(jnp.int32), -1)
    low, high = before // TILE, (until + TILE - 1) // TILE
    cosine, sine = rotary_tables(length)

    x0, h1, query, keys, values = front(codon_col, embedding_weight, norm_params, project, cosine, sine)
    attended, lse = attend(low, high, query, keys, values, seg_col, seg_row)
    (h2, active, d_two, ghid, d_one, gatt, gx, head_grad, norm_grad) = middle_rows(
        x0, attended, target_col, mask_col, count.reshape(1, 1), norm_params, embedding_weight,
        outward, expand, contract,
    )
    dq, dk, dv = attend_back(
        low, high, query, keys, values, gatt, lse, seg_col, seg_row, cosine, sine
    )
    table_grad, norm_grad = tail_rows(
        codon_col, x0, gx, dq, dk, dv, norm_params, project, head_grad, norm_grad
    )

    known = on_known_slice(owners, shards, slots)
    if known:
        home = (slot // PACK * (owners * shards) + device) * PACK + slot % PACK
    else:
        home = device * slots + slot
    home = block_tables(home, width, shard_width, FF, edge)
    model = width // edge
    total = shards * blocks
    strips_p = by_strips(home[0], model, 3 * model, model).reshape(3, -1)
    grads = None
    for part, right in enumerate((dq, dk, dv)):
        grads = weight_grad(strips_p[part], h1, right, grads, total, edge, width, "grad_project")
    grads = weight_grad(by_strips(home[1], model, model, model), attended, d_one, grads, total, edge, width, "grad_outward")
    grads = weight_grad(by_strips(home[2], model, FF // edge, model), h2, ghid, grads, total, edge, width, "grad_expand")
    grads = weight_grad(by_strips(home[3], FF // edge, model, model), active, d_two, grads, total, edge, width, "grad_contract")
    if known:
        owned, table_grad, norm_grad, square_sum = sum_everywhere(
            grads.reshape(slots // PACK, owners * shards, PACK, edge, LANES), table_grad, norm_grad
        )
        square_sum = jnp.sum(square_sum)
    else:
        owned = lax.psum_scatter(grads[:, :, :edge], everyone, scatter_dimension=0, tiled=True)
        table_grad, norm_grad, square_sum = lax.psum((table_grad, norm_grad), everyone) + (
            lax.psum(jnp.sum(owned * owned), everyone),
        )
    loss_value = jnp.sum(norm_grad[6]) / count
    norm_grad = norm_grad[:6]
    square_sum = square_sum + jnp.sum(table_grad * table_grad) + jnp.sum(norm_grad * norm_grad)
    grad_norm = jnp.sqrt(square_sum)
    factor = CLIP_LEVEL / jnp.maximum(grad_norm, CLIP_LEVEL)
    block_grad = owned * factor
    new_left, new_right, new_weight = shampoo(
        block_grad,
        block_left[0],
        block_right[0],
        block_left_root[0],
        block_right_root[0],
        block_weight[0],
    )
    table_clipped = table_grad * factor
    table_left_new, table_right_new, table_weight_new = shampoo(
        table_clipped, table_left, table_right, table_left_root, table_right_root, embedding_weight
    )
    norm_clipped = norm_grad * factor
    moment_new, second_new, params_new = adamw(
        norm_clipped, norm_moment, norm_second, norm_params, step_count.astype(F32)
    )
    return (
        loss_value,
        grad_norm,
        block_grad[None],
        new_left[None],
        new_right[None],
        new_weight[None],
        table_clipped,
        table_left_new,
        table_right_new,
        table_weight_new,
        norm_clipped,
        moment_new,
        second_new,
        params_new,
    )


def solution(mesh):
    in_specs = (
        P(("dp", "tensor"), None),
        P("dp", None),
        P(("dp", "tensor"), None),
        P(("dp", "tensor"), None),
        P(),
        P(),
        P("tensor", "dp", None, None),
        P("tensor", "dp", None, None),
        P("tensor", "dp", None, None),
        P("tensor", "dp", None, None),
        P("tensor", "dp", None, None),
        P(),
        P(),
        P(),
        P(),
        P(),
        P(),
        P(),
        P(),
    )
    out_specs = (
        P(),
        P(),
        P("tensor", "dp", None, None),
        P("tensor", "dp", None, None),
        P("tensor", "dp", None, None),
        P("tensor", "dp", None, None),
        P(),
        P(),
        P(),
        P(),
        P(),
        P(),
        P(),
        P(),
    )
    return jax.shard_map(body, mesh=mesh, in_specs=in_specs, out_specs=out_specs, check_vma=False)
```

```python
import functools
import math

import jax
import jax.numpy as jnp
from jax import lax
from jax.experimental import pallas as pl
from jax.experimental.pallas import tpu as pltpu
from jax.sharding import PartitionSpec as P

FF = 3072
HS = 64

CLIP_LEVEL = 0.005
STAT_DECAY = 0.5
MATRIX_RATE = 0.03
WEIGHT_DECAY = 0.01
VECTOR_RATE = 0.2
FIRST_BETA = 0.9
SECOND_BETA = 0.999
ADAM_EPSILON = 1e-08
NORM_EPSILON = 1e-05
ROOT_EPSILON = 1e-06
MASK_VALUE = -1e30
ROTARY_BASE = 10000.0
TOP_PRECISION = lax.Precision.HIGHEST

LANES = 128
PACK = 4
VMEM_LIMIT = 60 * 1024 * 1024
BF16 = jnp.bfloat16
F32 = jnp.float32


def dot(left, right):
    return lax.dot_general(left, right, (((1,), (0,)), ((), ())), preferred_element_type=F32)


def dot_nt(left, right):
    return lax.dot_general(left, right, (((1,), (1,)), ((), ())), preferred_element_type=F32)


def dot_tn(left, right):
    return lax.dot_general(left, right, (((0,), (0,)), ((), ())), preferred_element_type=F32)


def split_three(values):
    high = values.astype(BF16)
    rest = values - high.astype(F32)
    middle = rest.astype(BF16)
    low = (rest - middle.astype(F32)).astype(BF16)
    return high, middle, low


def params(**more):
    return pltpu.CompilerParams(vmem_limit_bytes=VMEM_LIMIT, **more)


def whole(shape):
    return pl.BlockSpec(shape, lambda *_: (0,) * len(shape))


def unpack_group(group, edge):
    return [group[:, edge * j : edge * (j + 1)] for j in range(PACK)]


def assemble_kernel(
    place_ref, in_ref, project_ref, outward_ref, expand_ref, contract_ref, store, *, load_steps
):
    step = pl.program_id(0)
    halves, per_step, part, strip_width = in_ref.shape
    edge = strip_width // PACK

    @pl.when(step < load_steps)
    def _():
        def unpack(g, carry):
            for h in range(halves):
                pieces = unpack_group(in_ref[h, g], edge)
                for j in range(PACK):
                    store[(step * per_step + g) * PACK + j, h * part : (h + 1) * part, :edge] = pieces[j]
            return carry

        lax.fori_loop(0, per_step, unpack, 0, unroll=4)

    @pl.when(step >= load_steps)
    def _():
        row = step - load_steps
        strip = PACK * edge

        def fill(out_ref, rows, base):
            strips = out_ref.shape[1] // strip

            def body(k, carry):
                r = k // strips
                c = k - r * strips
                first = base + k * PACK
                blocks = [store[place_ref[first + j]][:, :edge] for j in range(PACK)]
                out_ref[pl.ds(pl.multiple_of(r * edge, edge), edge), pl.ds(pl.multiple_of(c * strip, strip), strip)] = (
                    jnp.concatenate(blocks, axis=1)
                )
                return carry

            lax.fori_loop(0, rows * strips, body, 0, unroll=2)
            return rows * strips * PACK

        steps = pl.num_programs(0) - load_steps
        offset = 0
        for out_ref in (project_ref, outward_ref, expand_ref, contract_ref):
            rows = out_ref.shape[0] // edge
            count = rows * (out_ref.shape[1] // strip) * PACK
            fill(out_ref, rows, offset + row * count)
            offset = offset + count * steps


def assemble(place, packed, width, hidden_width):
    halves, groups, part, strip = packed.shape
    edge = halves * part
    per_step = 16
    load_steps = groups // per_step
    fill_steps = width // edge
    tall = hidden_width // fill_steps

    def late(step, *_):
        return (jnp.maximum(step - load_steps, 0), 0)

    return pl.pallas_call(
        functools.partial(assemble_kernel, load_steps=load_steps),
        out_shape=(
            jax.ShapeDtypeStruct((width, 3 * width), BF16),
            jax.ShapeDtypeStruct((width, width), BF16),
            jax.ShapeDtypeStruct((width, hidden_width), BF16),
            jax.ShapeDtypeStruct((hidden_width, width), BF16),
        ),
        grid_spec=pltpu.PrefetchScalarGridSpec(
            num_scalar_prefetch=1,
            grid=(load_steps + fill_steps,),
            in_specs=[
                pl.BlockSpec(
                    (halves, per_step, part, strip),
                    lambda s, *_: (0, jnp.minimum(s, load_steps - 1), 0, 0),
                )
            ],
            out_specs=[
                pl.BlockSpec((edge, 3 * width), late),
                pl.BlockSpec((edge, width), late),
                pl.BlockSpec((edge, hidden_width), late),
                pl.BlockSpec((tall, width), late),
            ],
            scratch_shapes=[pltpu.VMEM((groups * PACK, edge, LANES), BF16)],
        ),
        compiler_params=params(),
        name="assemble_weights",
    )(place, packed)


def block_tables(slot_place, width, shard_width, hidden_width, edge):
    shards = slot_place.shape[0]
    model = width // edge
    wide = shard_width // edge
    tall = hidden_width // shards // edge
    ends = [3 * wide * model, wide * model, model * tall, tall * model]
    pieces = []
    offset = 0
    for count in ends:
        pieces.append(slot_place[:, offset : offset + count])
        offset += count
    project = pieces[0].reshape(shards, model, 3, wide).transpose(1, 2, 0, 3)
    outward = pieces[1].reshape(shards * wide, model)
    expand = pieces[2].reshape(shards, model, tall).transpose(1, 0, 2)
    contract = pieces[3].reshape(shards * tall, model)
    return [piece.reshape(-1) for piece in (project, outward, expand, contract)]


def norm_parts(values):
    scale = 1.0 / values.shape[-1]
    center = values - jnp.sum(values, -1, keepdims=True) * scale
    spread = jnp.sum(center * center, -1, keepdims=True) * scale
    inverse = lax.rsqrt(spread + NORM_EPSILON)
    return center * inverse, inverse


def norm_back(grad, unit, inverse, gain):
    scale = 1.0 / grad.shape[-1]
    inner = grad * gain
    mean_one = jnp.sum(inner, -1, keepdims=True) * scale
    mean_two = jnp.sum(inner * unit, -1, keepdims=True) * scale
    return (inner - mean_one - unit * mean_two) * inverse


def turn(values, cosine, sine):
    lane = lax.broadcasted_iota(jnp.int32, values.shape, 1)
    half = HS // 2
    ahead = pltpu.roll(values, LANES - half, 1)
    behind = pltpu.roll(values, half, 1)
    other = jnp.where(lane % HS < half, ahead, behind)
    return values * cosine + other * sine


def front_kernel(
    codon_ref, table_ref, norm_ref, project_ref, cos_ref, sin_ref, x_ref, h_ref, q_ref, k_ref, v_ref
):
    rows = codon_ref.shape[0]
    vocab, width = table_ref.shape
    index = lax.broadcasted_iota(jnp.int32, (rows, vocab), 1)
    hot = jnp.where(codon_ref[...] == index, 1.0, 0.0).astype(BF16)
    high, middle, low = split_three(table_ref[...])
    embedded = (dot(hot, high) + dot(hot, middle)) + dot(hot, low)
    embedded = embedded * math.sqrt(width)
    x_ref[...] = embedded
    unit, _ = norm_parts(embedded)
    normed = (unit * norm_ref[0:1, :] + norm_ref[1:2, :]).astype(BF16)
    h_ref[...] = normed
    cosine = cos_ref[...]
    sine = sin_ref[...]
    for part, out_ref in ((0, q_ref), (1, k_ref), (2, v_ref)):
        values = dot(normed, project_ref[:, part * width : (part + 1) * width])
        for c in range(width // LANES):
            piece = values[:, c * LANES : (c + 1) * LANES]
            if part < 2:
                piece = turn(piece, cosine, sine)
            if part == 0:
                piece = piece * HS ** (-0.5)
            out_ref[:, c * LANES : (c + 1) * LANES] = piece.astype(BF16)


def front(codon_column, table, norm_params, project, cosine, sine):
    length = codon_column.shape[0]
    vocab, width = table.shape
    rows = 256
    spec = pl.BlockSpec((rows, width), lambda i: (i, 0))
    low = jax.ShapeDtypeStruct((length, width), BF16)
    return pl.pallas_call(
        front_kernel,
        out_shape=(jax.ShapeDtypeStruct((length, width), F32), low, low, low, low),
        grid=(length // rows,),
        in_specs=[
            pl.BlockSpec((rows, 1), lambda i: (i, 0)),
            whole(table.shape),
            whole(norm_params.shape),
            whole(project.shape),
            pl.BlockSpec((rows, LANES), lambda i: (i, 0)),
            pl.BlockSpec((rows, LANES), lambda i: (i, 0)),
        ],
        out_specs=(spec, spec, spec, spec, spec),
        compiler_params=params(),
        name="embed_project",
    )(codon_column, table, norm_params, project, cosine, sine)


ROWS = 256
TILE = 128


def head_masks(rows):
    lane = lax.broadcasted_iota(jnp.int32, (rows, LANES), 1)
    return [lane // HS == h for h in range(LANES // HS)]


def same_segment(seg_col, seg_row_ref, first, count):
    row = jnp.concatenate([seg_row_ref[first + i] for i in range(count)], axis=1)
    return seg_col == row


def attend_kernel(low_ref, high_ref, q_ref, k_ref, v_ref, seg_col_ref, seg_row_ref, o_ref, lse_ref):
    part = pl.program_id(1)
    first, last = low_ref[part], high_ref[part]
    masks = head_masks(ROWS)

    def run(count):
        query = q_ref[...]
        zero = jnp.zeros_like(query)
        span = pl.ds(pl.multiple_of(first * TILE, TILE), count * TILE)
        keys = k_ref[span, :]
        values = v_ref[span, :]
        same = same_segment(seg_col_ref[...], seg_row_ref, first, count)
        outs, logs = [], []
        for mask in masks:
            scores = jnp.where(same, dot_nt(jnp.where(mask, query, zero), keys), MASK_VALUE)
            top = jnp.max(scores, -1, keepdims=True)
            exps = jnp.exp(scores - top)
            total = jnp.sum(exps, -1, keepdims=True)
            probs = (exps * (1.0 / total)).astype(BF16)
            outs.append(dot(probs, values))
            logs.append(top + jnp.log(total))
        o_ref[...] = jnp.where(masks[0], outs[0], outs[1]).astype(BF16)
        lse_ref[...] = jnp.where(masks[0], logs[0], logs[1])

    for count in range(1, k_ref.shape[0] // TILE + 1):
        pl.when(last - first == count)(functools.partial(run, count))


def attend(low, high, query, keys, values, seg_col, seg_row):
    length, width = query.shape
    tiles = length // TILE
    pairs = width // LANES
    column = pl.BlockSpec((ROWS, LANES), lambda p, i, *_: (i, p))
    full = pl.BlockSpec((length, LANES), lambda p, i, *_: (0, p))
    return pl.pallas_call(
        attend_kernel,
        out_shape=(
            jax.ShapeDtypeStruct((length, width), BF16),
            jax.ShapeDtypeStruct((length, width), F32),
        ),
        grid_spec=pltpu.PrefetchScalarGridSpec(
            num_scalar_prefetch=2,
            grid=(pairs, length // ROWS),
            in_specs=[
                column,
                full,
                full,
                pl.BlockSpec((ROWS, 1), lambda p, i, *_: (i, 0)),
                whole((tiles, 1, TILE)),
            ],
            out_specs=(column, column),
        ),
        compiler_params=params(),
        name="attend_forward",
    )(low, high, query, keys, values, seg_col, seg_row)


def attend_back_kernel(
    low_ref, high_ref, q_ref, k_ref, v_ref, g_ref, lse_ref, seg_col_ref, seg_row_ref, cos_ref, sin_ref,
    out_ref, dk_acc, dv_acc,
):
    part = pl.program_id(1)
    parts = pl.num_programs(1)
    heads = LANES // HS
    first, last = low_ref[part], high_ref[part]
    masks = head_masks(ROWS)

    @pl.when(part == 0)
    def _():
        dk_acc[...] = jnp.zeros_like(dk_acc)
        dv_acc[...] = jnp.zeros_like(dv_acc)

    def run(count):
        query = q_ref[...]
        grad = g_ref[...]
        zero = jnp.zeros_like(query)
        span = pl.ds(pl.multiple_of(first * TILE, TILE), count * TILE)
        keys = k_ref[span, :]
        values = v_ref[span, :]
        same = same_segment(seg_col_ref[...], seg_row_ref, first, count)
        dq = []
        dk = dv = None
        for h, mask in enumerate(masks):
            own_query = jnp.where(mask, query, zero)
            own_grad = jnp.where(mask, grad, zero)
            scores = jnp.where(same, dot_nt(own_query, keys), MASK_VALUE)
            probs = jnp.exp(scores - lse_ref[:, h * HS : h * HS + 1])
            grad_probs = dot_nt(own_grad, values)
            delta = jnp.sum(probs * grad_probs, -1, keepdims=True)
            grad_scores = (probs * (grad_probs - delta)).astype(BF16)
            dq.append(dot(grad_scores, keys))
            more_dk = dot(own_query.T, grad_scores)
            more_dv = dot(own_grad.T, probs.astype(BF16))
            dk = more_dk if dk is None else dk + more_dk
            dv = more_dv if dv is None else dv + more_dv
        for i in range(count):
            lanes = slice(i * TILE, (i + 1) * TILE)
            dk_acc[first + i] += dk[:, lanes]
            dv_acc[first + i] += dv[:, lanes]
        rows = pl.ds(pl.multiple_of(part * ROWS, ROWS), ROWS)
        turned = turn(
            jnp.where(masks[0], dq[0], dq[1]) * HS ** (-0.5), cos_ref[rows, :], -sin_ref[rows, :]
        )
        out_ref[0, rows, :] = turned.astype(BF16)

    for count in range(1, k_ref.shape[0] // TILE + 1):
        pl.when(last - first == count)(functools.partial(run, count))

    @pl.when(part == parts - 1)
    def _():
        for j in range(dk_acc.shape[0]):
            rows = slice(j * TILE, (j + 1) * TILE)
            out_ref[1, rows, :] = turn(dk_acc[j].T, cos_ref[rows, :], -sin_ref[rows, :]).astype(BF16)
            out_ref[2, rows, :] = dv_acc[j].T.astype(BF16)


def attend_back(low, high, query, keys, values, grad, lse, seg_col, seg_row, cosine, sine):
    length, width = query.shape
    tiles = length // TILE
    pairs = width // LANES
    column = pl.BlockSpec((ROWS, LANES), lambda p, i, *_: (i, p))
    full = pl.BlockSpec((length, LANES), lambda p, i, *_: (0, p))
    return pl.pallas_call(
        attend_back_kernel,
        out_shape=jax.ShapeDtypeStruct((3, length, width), BF16),
        grid_spec=pltpu.PrefetchScalarGridSpec(
            num_scalar_prefetch=2,
            grid=(pairs, length // ROWS),
            in_specs=[
                column,
                full,
                full,
                column,
                column,
                pl.BlockSpec((ROWS, 1), lambda p, i, *_: (i, 0)),
                whole((tiles, 1, TILE)),
                whole((length, LANES)),
                whole((length, LANES)),
            ],
            out_specs=pl.BlockSpec((3, length, LANES), lambda p, i, *_: (0, 0, p)),
            scratch_shapes=[
                pltpu.VMEM((tiles, LANES, TILE), F32),
                pltpu.VMEM((tiles, LANES, TILE), F32),
            ],
        ),
        compiler_params=params(),
        name="attend_backward",
    )(low, high, query, keys, values, grad, lse, seg_col, seg_row, cosine, sine)


INV_SQRT_TWO = 2.0 ** (-0.5)
INV_SQRT_TWO_PI = (2.0 * math.pi) ** (-0.5)


def middle_kernel(
    x_ref, att_ref, target_ref, mask_ref, count_ref, norm_ref, table_ref,
    outward_ref, expand_ref, contract_ref,
    h_ref, active_ref, d_two_ref, ghid_ref, d_one_ref, gatt_ref, gx_ref, head_ref, norm_grad_ref,
    slope,
):
    step = pl.program_id(0)
    rows, width = x_ref.shape
    vocab = table_ref.shape[0]
    ff = expand_ref.shape[1]
    part = width

    @pl.when(step == 0)
    def _():
        head_ref[...] = jnp.zeros_like(head_ref)
        norm_grad_ref[...] = jnp.zeros_like(norm_grad_ref)

    middle = x_ref[...] + dot(att_ref[...], outward_ref[...])
    unit_two, inverse_two = norm_parts(middle)
    gain_two = norm_ref[2:3, :]
    normed_two = (unit_two * gain_two + norm_ref[3:4, :]).astype(BF16)
    h_ref[...] = normed_two

    def forward(c, total):
        cols = pl.ds(pl.multiple_of(c * part, part), part)
        hidden = dot(normed_two, expand_ref[:, cols])
        cumulative = 0.5 + 0.5 * lax.erf(hidden * INV_SQRT_TWO)
        active = (hidden * cumulative).astype(BF16)
        density = jnp.exp(-0.5 * hidden * hidden) * INV_SQRT_TWO_PI
        slope[:, cols] = cumulative + hidden * density
        active_ref[:, cols] = active
        return total + dot(active, contract_ref[cols, :])

    branch = lax.fori_loop(0, ff // part, forward, jnp.zeros((rows, width), F32))
    unit, inverse = norm_parts(middle + branch)
    gain = norm_ref[4:5, :]
    final = (unit * gain + norm_ref[5:6, :]).astype(BF16)
    table = table_ref[...].astype(BF16)
    logits = dot_nt(final, table)
    shifted = logits - jnp.max(logits, -1, keepdims=True)
    exps = jnp.exp(shifted)
    sums = jnp.sum(exps, -1, keepdims=True)
    hot = target_ref[...] == lax.broadcasted_iota(jnp.int32, (rows, vocab), 1)
    mask = mask_ref[...]
    log_probs = shifted - jnp.log(sums)
    picked = jnp.sum(jnp.where(hot, log_probs, 0.0) * mask, 0, keepdims=True)
    norm_grad_ref[6:7, 0:vocab] -= picked
    glogits = ((jnp.exp(log_probs) - jnp.where(hot, 1.0, 0.0)) * (mask / count_ref[...])).astype(BF16)
    head_ref[...] += dot_tn(glogits, final)
    gfinal = dot(glogits, table)
    norm_grad_ref[4:5, :] += jnp.sum(gfinal * unit, 0, keepdims=True)
    norm_grad_ref[5:6, :] += jnp.sum(gfinal, 0, keepdims=True)
    gx_two = norm_back(gfinal, unit, inverse, gain)
    d_two = gx_two.astype(BF16)
    d_two_ref[...] = d_two

    def backward(c, total):
        cols = pl.ds(pl.multiple_of(c * part, part), part)
        gactive = dot_nt(d_two, contract_ref[cols, :])
        ghid = (gactive * slope[:, cols]).astype(BF16)
        ghid_ref[:, cols] = ghid
        return total + dot_nt(ghid, expand_ref[:, cols])

    gh = lax.fori_loop(0, ff // part, backward, jnp.zeros((rows, width), F32))
    norm_grad_ref[2:3, :] += jnp.sum(gh * unit_two, 0, keepdims=True)
    norm_grad_ref[3:4, :] += jnp.sum(gh, 0, keepdims=True)
    gx_one = gx_two + norm_back(gh, unit_two, inverse_two, gain_two)
    gx_ref[...] = gx_one
    d_one = gx_one.astype(BF16)
    d_one_ref[...] = d_one
    gatt_ref[...] = dot_nt(d_one, outward_ref[...]).astype(BF16)


def middle_rows(x, att, target_col, mask_col, count, norm_params, table, outward, expand, contract):
    length, width = x.shape
    vocab = table.shape[0]
    ff = expand.shape[1]
    rows = 256
    narrow = pl.BlockSpec((rows, width), lambda i: (i, 0))
    broad = pl.BlockSpec((rows, ff), lambda i: (i, 0))
    column = pl.BlockSpec((rows, 1), lambda i: (i, 0))
    low = jax.ShapeDtypeStruct((length, width), BF16)
    low_broad = jax.ShapeDtypeStruct((length, ff), BF16)
    return pl.pallas_call(
        middle_kernel,
        out_shape=(
            low, low_broad, low, low_broad, low, low,
            jax.ShapeDtypeStruct((length, width), F32),
            jax.ShapeDtypeStruct((vocab, width), F32),
            jax.ShapeDtypeStruct((8, width), F32),
        ),
        grid=(length // rows,),
        in_specs=[
            narrow, narrow, column, column, whole((1, 1)), whole(norm_params.shape), whole(table.shape),
            whole(outward.shape), whole(expand.shape), whole(contract.shape),
        ],
        out_specs=(
            narrow, broad, narrow, broad, narrow, narrow, narrow,
            whole((vocab, width)), whole((8, width)),
        ),
        scratch_shapes=[pltpu.VMEM((rows, ff), F32)],
        compiler_params=params(),
        name="middle_rows",
    )(x, att, target_col, mask_col, count, norm_params, table, outward, expand, contract)


def tail_kernel(
    codon_ref, x_ref, gx_ref, gproj_ref, norm_ref, project_ref, head_ref, norm_in_ref,
    table_grad_ref, norm_grad_ref,
):
    step = pl.program_id(0)
    rows, width = x_ref.shape
    vocab = head_ref.shape[0]

    @pl.when(step == 0)
    def _():
        table_grad_ref[...] = head_ref[...]
        norm_grad_ref[...] = norm_in_ref[...]

    gh = dot_nt(gproj_ref[0], project_ref[:, 0:width])
    gh = gh + dot_nt(gproj_ref[1], project_ref[:, width : 2 * width])
    gh = gh + dot_nt(gproj_ref[2], project_ref[:, 2 * width : 3 * width])
    unit, inverse = norm_parts(x_ref[...])
    norm_grad_ref[0:1, :] += jnp.sum(gh * unit, 0, keepdims=True)
    norm_grad_ref[1:2, :] += jnp.sum(gh, 0, keepdims=True)
    gx = gx_ref[...] + norm_back(gh, unit, inverse, norm_ref[0:1, :])
    hot = jnp.where(codon_ref[...] == lax.broadcasted_iota(jnp.int32, (rows, vocab), 1), 1.0, 0.0)
    hot = hot.T.astype(BF16)
    high, middle, low = split_three(gx)
    total = dot(hot, high) + (dot(hot, middle) + dot(hot, low))
    table_grad_ref[...] += total * math.sqrt(width)


def tail_rows(codon_col, x, gx, gproj, norm_params, project, head, norm_in):
    length, width = x.shape
    rows = 256
    narrow = pl.BlockSpec((rows, width), lambda i: (i, 0))
    return pl.pallas_call(
        tail_kernel,
        out_shape=(
            jax.ShapeDtypeStruct(head.shape, F32),
            jax.ShapeDtypeStruct(norm_in.shape, F32),
        ),
        grid=(length // rows,),
        in_specs=[
            pl.BlockSpec((rows, 1), lambda i: (i, 0)),
            narrow, narrow, pl.BlockSpec((3, rows, width), lambda i: (0, i, 0)),
            whole(norm_params.shape), whole(project.shape), whole(head.shape), whole(norm_in.shape),
        ],
        out_specs=(whole(head.shape), whole(norm_in.shape)),
        compiler_params=params(),
        name="tail_rows",
    )(codon_col, x, gx, gproj, norm_params, project, head, norm_in)


def weight_grad_kernel(place_ref, left_ref, right_ref, *rest, edge):
    out_ref, buf, turned, sem = rest[-4:]
    strip_index = pl.program_id(1)
    step = pl.program_id(0) * pl.num_programs(1) + strip_index
    steps = pl.num_programs(0) * pl.num_programs(1)
    count = buf.shape[1]
    slot = lax.rem(step, 2)
    block_rows = count // PACK

    def drain(which):
        pltpu.make_async_copy(buf.at[which], out_ref.at[pl.ds(0, count)], sem.at[which]).wait()

    @pl.when(strip_index == 0)
    def _():
        turned[...] = left_ref[...].T

    @pl.when(step >= 2)
    def _():
        drain(slot)

    right = right_ref[...]
    for r in range(block_rows):
        result = dot(turned[r * edge : (r + 1) * edge, :], right)
        pieces = unpack_group(result, edge)
        for j in range(PACK):
            buf[slot, r * PACK + j, :, :edge] = pieces[j]
        for j in range(PACK):
            k = r * PACK + j
            target = place_ref[step * count + k]
            pltpu.make_async_copy(buf.at[slot, k], out_ref.at[target], sem.at[slot]).start()

    @pl.when(step == steps - 1)
    def _():
        @pl.when(step >= 1)
        def _():
            drain(1 - slot)

        drain(slot)


def weight_grad(place, left, right, into, blocks, edge, left_cols, name):
    length, tall = left.shape
    strip = PACK * edge
    count = left_cols // edge * PACK
    if right.ndim == 3:
        strips = right.shape[2] // strip
        right_spec = pl.BlockSpec((None, length, strip), lambda a, b, *_: (b // strips, 0, b % strips))
        grid = (tall // left_cols, right.shape[0] * strips)
    else:
        right_spec = pl.BlockSpec((length, strip), lambda a, b, *_: (0, b))
        grid = (tall // left_cols, right.shape[1] // strip)
    operands = [place, left, right]
    in_specs = [pl.BlockSpec((length, left_cols), lambda a, b, *_: (0, a)), right_spec]
    aliases = {}
    if into is not None:
        operands.append(into)
        in_specs.append(pl.BlockSpec(memory_space=pl.ANY))
        aliases = {3: 0}
    return pl.pallas_call(
        functools.partial(weight_grad_kernel, edge=edge),
        out_shape=jax.ShapeDtypeStruct((blocks, edge, LANES), F32),
        grid_spec=pltpu.PrefetchScalarGridSpec(
            num_scalar_prefetch=1,
            grid=grid,
            in_specs=in_specs,
            out_specs=pl.BlockSpec(memory_space=pl.ANY),
            scratch_shapes=[
                pltpu.VMEM((2, count, edge, LANES), F32),
                pltpu.VMEM((left_cols, length), BF16),
                pltpu.SemaphoreType.DMA((2,)),
            ],
        ),
        input_output_aliases=aliases,
        compiler_params=params(),
        name=name,
    )(*operands)


def by_strips(table, rows, cols, chunk):
    shaped = table.reshape(rows // chunk, chunk, cols // PACK, PACK)
    return shaped.transpose(0, 2, 1, 3).reshape(-1)


CORE, NEAR_Y, NEAR_X, NEAR_Z, FAR_Z = range(5)
AXIS_STRIDE = {CORE: 1, NEAR_Y: 2, NEAR_X: 4, NEAR_Z: 8, FAR_Z: 16}
CHUNK_AXES = (
    (NEAR_X, NEAR_Y, NEAR_Z, FAR_Z),
    (NEAR_Y, NEAR_X, NEAR_Z, FAR_Z),
    (NEAR_X, NEAR_Y, NEAR_Z, FAR_Z),
    (NEAR_Y, NEAR_X, NEAR_Z, FAR_Z),
    (NEAR_Z, NEAR_X, NEAR_Y, FAR_Z),
    (NEAR_Z, NEAR_Y, NEAR_X, FAR_Z),
)
PACK_GROUPS = 6
QUARTERS = 4
SUM_CHUNKS = PACK_GROUPS * QUARTERS
SUM_SLOTS = 3
SUM_ORDER = (
    0, 2000, 10, 2010, 20, 2020, 1000, 2001, 1010, 2011, 1020, 2021, 30, 2030, 40, 2040, 50, 2050, 1030, 2031, 1040,
    2041, 1050, 2051, 60, 2060, 70, 2070, 1011, 80, 2012, 2080, 1001, 2002, 1060, 2061, 1070, 1080, 2071, 90, 2090,
    1021, 100, 2100, 1031, 2032, 110, 2110, 2022, 1012, 1090, 2013, 1002, 1100, 2003, 120, 2120, 1041, 1110, 2101,
    1051, 130, 2130, 2042, 140, 2140, 2111, 1013, 2052, 2014, 1120, 1032, 1003, 2081, 2004, 1022, 150, 2150, 1130,
    2091, 1061, 1014, 1140, 160, 2160, 1004, 1071, 2072, 1150, 2062, 170, 2170, 1042, 180, 2180, 1052, 1160, 190,
    2190, 2023, 1170, 1180, 2053, 1101, 200, 2200, 2043, 2033, 210, 2210, 2102, 2161, 1072, 1190, 1062, 1023, 2024,
    1111, 2121, 2112, 1081, 2063, 220, 2220, 2082, 1200, 1053, 2054, 1033, 2034, 1091, 1043, 1210, 1024, 2073, 230,
    2230, 1220, 2092, 2044, 1063, 2064, 1102, 2103, 1054, 2171, 1034, 1230, 2131, 1112, 1073, 2074, 1082, 2151,
    1044, 1064, 1103, 2104, 2083, 2113, 1074, 2141, 1161, 1092, 1121, 2093, 1104, 2162, 1083, 2084, 1113, 2114,
    2221, 1093, 2094, 2231, 1084, 2122, 1114, 2181, 1171, 2172, 1131, 1094, 1162, 1151, 2132, 1141, 2142, 2163,
    1122, 1172, 2123, 2191, 2152, 1221, 1163, 2164, 1132, 2133, 2211, 2173, 1231, 1123, 2124, 1142, 2143, 1181,
    1164, 1133, 2134, 2201, 2222, 1124, 1143, 2144, 1173, 2174, 1152, 2153, 1134, 1153, 2154, 1144, 1174, 2182,
    1191, 2192, 1222, 2223, 1154, 1211, 2212, 1201, 2202, 2232, 1223, 2224, 1182, 2183, 1192, 2193, 1224, 1212,
    2213, 1183, 2184, 1202, 2203, 1193, 2194, 1232, 2233, 1184, 1213, 2214, 1203, 2204, 1233, 2234, 1194, 1214,
    1204, 1234,
)
SMALL_ROWS = 1024
SMALL_AXES = (CORE, NEAR_X, NEAR_Y, NEAR_Z, FAR_Z)
MESH = pl.DeviceIdType.MESH


def on_known_slice(owners, shards, slots):
    return owners == 8 and shards == 4 and slots % PACK == 0 and slots == PACK * PACK_GROUPS


def bits_of(owner, shard):
    return {
        CORE: shard % 2,
        NEAR_Y: shard // 2,
        NEAR_X: owner % 2,
        NEAR_Z: owner // 2 % 2,
        FAR_Z: owner // 4,
    }


def own_bits():
    owner, shard = lax.axis_index("dp"), lax.axis_index("tensor")
    return owner, shard, bits_of(owner, shard)


def partner_of(axis, owner, shard, bits):
    if axis == CORE:
        return (owner, shard + 1 - 2 * bits[CORE])
    if axis == NEAR_Y:
        return (owner, shard + 2 - 4 * bits[NEAR_Y])
    step = {NEAR_X: 1, NEAR_Z: 2, FAR_Z: 4}[axis]
    return (owner + step - 2 * step * bits[axis], shard)


def meet_partners(owner, shard, bits):
    barrier = pltpu.get_barrier_semaphore()
    for axis in range(5):
        pl.semaphore_signal(
            barrier, inc=1, device_id=partner_of(axis, owner, shard, bits), device_id_type=MESH
        )
    pl.semaphore_wait(barrier, 5)


def total_of(values):
    return jnp.sum(jnp.sum(values, 1, keepdims=True), 0, keepdims=True)


def statistics(square_sum, loss_sum, count):
    norm = jnp.sqrt(square_sum)
    factor = CLIP_LEVEL / jnp.maximum(norm, CLIP_LEVEL)
    row = lax.broadcasted_iota(jnp.int32, (8, LANES), 0)
    return jnp.where(row == 0, factor, jnp.where(row == 1, norm, loss_sum / count))


def sum_kernel(
    grads_ref, table_ref, norm_ref, count_ref, owned_ref, table_out, norm_out, stats_out,
    inbuf, stage, r0, r1, r2, r3, r4, small, s0, s1, s2, s3, s4, spread, square, squares,
    in_sem, send_sem, recv_sem, small_send, small_recv, square_send, square_recv,
):
    owner, shard, bits = own_bits()
    edge = grads_ref.shape[3]
    strip = PACK * edge
    part = edge // QUARTERS
    received = (r0, r1, r2, r3, r4)

    def axes_of(c):
        return CHUNK_AXES[c % len(CHUNK_AXES)]

    def fetch(c):
        rows = pl.ds(c % QUARTERS * part, part)
        slot = c % SUM_SLOTS
        return pltpu.make_async_copy(
            grads_ref.at[c // QUARTERS, :, :, rows], inbuf.at[slot], in_sem.at[slot]
        )

    for c in range(SUM_SLOTS):
        fetch(c).start()
    meet_partners(owner, shard, bits)

    def chunk_send(c, k):
        if k == 0:
            axis, source = CORE, stage.at[c % SUM_SLOTS]
        else:
            axis = axes_of(c)[k - 1]
            half = received[k - 1].shape[1] // 2
            source = received[k - 1].at[c, pl.ds(half * (1 - bits[axis]), half)]
        return pltpu.make_async_remote_copy(
            src_ref=source,
            dst_ref=received[k].at[c],
            send_sem=send_sem.at[c, k],
            recv_sem=recv_sem.at[c, k],
            device_id=partner_of(axis, owner, shard, bits),
            device_id_type=MESH,
        )

    def packed(c, e, core):
        d = core
        for k, axis in enumerate(axes_of(c)):
            d = d + e // (8 >> k) % 2 * AXIS_STRIDE[axis]
        blocks = [inbuf[c % SUM_SLOTS, d, j][:, :edge] for j in range(PACK)]
        return jnp.concatenate(blocks, axis=1)

    def pack(c):
        fetch(c).wait()
        if c >= SUM_SLOTS:
            chunk_send(c - SUM_SLOTS, 0).wait_send()

        def body(e, carry):
            stage[c % SUM_SLOTS, e] = packed(c, e, 1 - bits[CORE])
            return carry

        lax.fori_loop(0, 16, body, 0, unroll=4)

    def merge(c, k):
        chunk_send(c, k).wait_recv()
        if k == 0:

            def body(e, carry):
                r0[c, e] = r0[c, e] + packed(c, e, bits[CORE])
                return carry

            lax.fori_loop(0, 16, body, 0, unroll=4)
            if c + SUM_SLOTS < SUM_CHUNKS:
                fetch(c + SUM_SLOTS).start()
            return
        axis = axes_of(c)[k - 1]
        half = received[k].shape[1]
        base = half * bits[axis]

        def body(e, carry):
            received[k][c, e] = received[k][c, e] + received[k - 1][c, base + e]
            return carry

        if k < 4:
            lax.fori_loop(0, half, body, 0, unroll=2)
            return
        group = r4[c, 0] + r3[c, base]
        pieces = unpack_group(group, edge)
        rows = slice(c % QUARTERS * part, (c % QUARTERS + 1) * part)
        for j in range(PACK):
            owned_ref[PACK * (c // QUARTERS) + j, rows, :] = pieces[j]
        parts = group * group
        line = parts[:, :LANES]
        for i in range(1, strip // LANES):
            line = line + parts[:, i * LANES : (i + 1) * LANES]
        total = square[...]
        for r in range(part // 8):
            total = total + line[r * 8 : (r + 1) * 8]
        square[...] = total

    vocab, width = table_ref.shape
    vectors = norm_ref.shape[0]
    columns = width // LANES
    small_parts = (s0, s1, s2, s3, s4)

    def small_fill():
        for c in range(columns):
            lanes = slice(c * LANES, (c + 1) * LANES)
            small[c * vocab : (c + 1) * vocab] = table_ref[:, lanes]
            start = columns * vocab + c * vectors
            small[start : start + vectors] = norm_ref[:, lanes]
        used = columns * (vocab + vectors)
        small[used:] = jnp.zeros((SMALL_ROWS - used, LANES), F32)

    def small_base(k):
        base = 0
        for i in range(k):
            base = base + (SMALL_ROWS >> (i + 1)) * bits[SMALL_AXES[i]]
        return base

    def small_copy(k):
        rows = SMALL_ROWS >> (k + 1)
        start = pl.multiple_of(small_base(k) + rows * (1 - bits[SMALL_AXES[k]]), 8)
        return pltpu.make_async_remote_copy(
            src_ref=small.at[pl.ds(start, rows)],
            dst_ref=small_parts[k],
            send_sem=small_send.at[k],
            recv_sem=small_recv.at[k],
            device_id=partner_of(SMALL_AXES[k], owner, shard, bits),
            device_id_type=MESH,
        )

    def small_merge(k):
        small_copy(k).wait_recv()
        rows = SMALL_ROWS >> (k + 1)
        mine = pl.ds(pl.multiple_of(small_base(k + 1), 8), rows)
        if k < 4:
            small[mine, :] = small[mine, :] + small_parts[k][...]
            small_copy(k + 1).start()
        else:
            spread[mine, :] = small[mine, :] + small_parts[k][...]
            spread_copy(4).start()

    def spread_copy(k):
        rows = SMALL_ROWS >> (k + 1)
        here = pl.ds(pl.multiple_of(small_base(k + 1), 8), rows)
        return pltpu.make_async_remote_copy(
            src_ref=spread.at[here],
            dst_ref=spread.at[here],
            send_sem=small_send.at[5 + k],
            recv_sem=small_recv.at[5 + k],
            device_id=partner_of(SMALL_AXES[k], owner, shard, bits),
            device_id_type=MESH,
        )

    def spread_next(k):
        spread_copy(k).wait_recv()
        if k > 0:
            spread_copy(k - 1).start()
        else:
            for c in range(columns):
                lanes = slice(c * LANES, (c + 1) * LANES)
                table_out[:, lanes] = spread[c * vocab : (c + 1) * vocab]
                start = columns * vocab + c * vectors
                norm_out[:, lanes] = spread[start : start + vectors]

    square[...] = jnp.zeros_like(square)
    small_fill()
    small_copy(0).start()
    extra = [functools.partial(small_merge, k) for k in range(5)]
    extra += [functools.partial(spread_next, k) for k in range(4, -1, -1)]
    for position, code in enumerate(SUM_ORDER):
        c, k = code % 1000 // 10, code % 10
        if code < 1000:
            pack(c)
        elif code < 2000:
            merge(c, k)
        else:
            chunk_send(c, k).start()
        if position >= 60 and position % 12 == 0 and extra:
            extra.pop(0)()
    while extra:
        extra.pop(0)()

    def square_copy(k):
        return pltpu.make_async_remote_copy(
            src_ref=squares.at[k],
            dst_ref=squares.at[5 + k],
            send_sem=square_send.at[k],
            recv_sem=square_recv.at[k],
            device_id=partner_of(SMALL_AXES[k], owner, shard, bits),
            device_id_type=MESH,
        )

    value = square[...]
    for k in range(5):
        squares[k] = value
        square_copy(k).start()
        square_copy(k).wait_recv()
        value = squares[k] + squares[5 + k]
    table_sum, vectors_sum = table_out[...], norm_out[0:6, :]
    stats_out[...] = statistics(
        total_of(value) + total_of(table_sum * table_sum) + total_of(vectors_sum * vectors_sum),
        total_of(norm_out[6:7, :]),
        count_ref[0:1, 0:1],
    )

    for c in range(SUM_CHUNKS):
        for k in range(5):
            if k > 0 or c >= SUM_CHUNKS - SUM_SLOTS:
                chunk_send(c, k).wait_send()
    for k in range(5):
        small_copy(k).wait_send()
        spread_copy(k).wait_send()
        square_copy(k).wait_send()


def sum_everywhere(grads, table_grad, norm_grad, count):
    groups, devices, _, edge, _ = grads.shape
    strip = PACK * edge
    part = edge // QUARTERS
    group = lambda count: pltpu.VMEM((SUM_CHUNKS, count, part, strip), F32)
    small = lambda rows: pltpu.VMEM((rows, LANES), F32)
    return pl.pallas_call(
        sum_kernel,
        out_shape=(
            jax.ShapeDtypeStruct((groups * PACK, edge, edge), F32),
            jax.ShapeDtypeStruct(table_grad.shape, F32),
            jax.ShapeDtypeStruct(norm_grad.shape, F32),
            jax.ShapeDtypeStruct((8, LANES), F32),
        ),
        in_specs=[
            pl.BlockSpec(memory_space=pl.ANY),
            pl.BlockSpec(memory_space=pltpu.VMEM),
            pl.BlockSpec(memory_space=pltpu.VMEM),
            pl.BlockSpec(memory_space=pltpu.VMEM),
        ],
        out_specs=(pl.BlockSpec(memory_space=pltpu.VMEM),) * 4,
        scratch_shapes=[
            pltpu.VMEM((SUM_SLOTS, devices, PACK, part, LANES), F32),
            pltpu.VMEM((SUM_SLOTS, devices // 2, part, strip), F32),
            group(16), group(8), group(4), group(2), group(1),
            small(SMALL_ROWS), small(512), small(256), small(128), small(64), small(32), small(SMALL_ROWS),
            pltpu.VMEM((8, LANES), F32),
            pltpu.VMEM((10, 8, LANES), F32),
            pltpu.SemaphoreType.DMA((SUM_SLOTS,)),
            pltpu.SemaphoreType.DMA((SUM_CHUNKS, 5)),
            pltpu.SemaphoreType.DMA((SUM_CHUNKS, 5)),
            pltpu.SemaphoreType.DMA((10,)),
            pltpu.SemaphoreType.DMA((10,)),
            pltpu.SemaphoreType.DMA((5,)),
            pltpu.SemaphoreType.DMA((5,)),
        ],
        compiler_params=pltpu.CompilerParams(
            vmem_limit_bytes=66_000_000, collective_id=1, has_side_effects=True
        ),
        name="sum_gradients",
    )(grads, table_grad, norm_grad, count)


GATHER_AXES = (
    (NEAR_Z, NEAR_X, NEAR_Y),
    (NEAR_Z, NEAR_Y, NEAR_X),
    (NEAR_X, NEAR_Y, NEAR_Z),
    (NEAR_Y, NEAR_X, NEAR_Z),
    (NEAR_X, NEAR_Y, NEAR_Z),
    (NEAR_Y, NEAR_X, NEAR_Z),
)
HALVES = 2
GATHER_CHUNKS = PACK_GROUPS * HALVES
GATHER_ORDER = (
    2000, 2010, 2020, 2030, 1000, 2001, 1010, 2011, 2040, 2050, 1020, 2021, 1030, 1001, 2002, 1011, 2012, 2060,
    2070, 2031, 1040, 2041, 1050, 1021, 2022, 2080, 2090, 2051, 1031, 2032, 1002, 1012, 1060, 1070, 2003, 1041,
    2061, 2100, 2110, 2071, 2042, 1051, 1022, 1080, 1090, 2052, 1032, 1061, 2033, 1071, 1100, 1110, 2081, 2062,
    1042, 2091, 1003, 2004, 1052, 2101, 2023, 1081, 2111, 2072, 1091, 1004, 1062, 2013, 1101, 1033, 2034, 1111,
    2082, 2092, 1034, 1072, 2102, 1023, 2024, 2063, 2112, 1082, 2053, 1013, 2014, 1092, 1024, 2043, 1102, 1014,
    1112, 2073, 2093, 1063, 2064, 2083, 1053, 2054, 1043, 2044, 1064, 1054, 2113, 1073, 2074, 1044, 2103, 1093,
    2094, 1074, 1083, 2084, 1094, 1084, 1113, 2114, 1103, 2104, 1114, 1104,
)


def gather_entry(group, bits):
    first, second, third = GATHER_AXES[group]
    return 16 * bits[CORE] + 8 * bits[first] + 4 * bits[second] + 2 * bits[third] + bits[FAR_Z]


def gather_kernel(own_ref, mask_ref, out_ref, count_ref, counts, own_sem, send_sem, recv_sem, count_send, count_recv):
    owner, shard, bits = own_bits()
    rows = own_ref.shape[1] // HALVES

    def place(c):
        return gather_entry(c % PACK_GROUPS, bits)

    def keep(c):
        part = pl.ds(c // PACK_GROUPS * rows, rows)
        return pltpu.make_async_copy(
            own_ref.at[c % PACK_GROUPS, part], out_ref.at[c, place(c)], own_sem.at[c]
        )

    def move(c, k):
        if k == 0:
            axis = FAR_Z
            source = own_ref.at[c % PACK_GROUPS, pl.ds(c // PACK_GROUPS * rows, rows)]
            target = out_ref.at[c, place(c)]
        else:
            axis = CORE if k == 4 else GATHER_AXES[c % PACK_GROUPS][3 - k]
            size = 1 << k
            base = place(c) // size * size
            source = out_ref.at[c, pl.ds(base, size)]
            target = source
        return pltpu.make_async_remote_copy(
            src_ref=source,
            dst_ref=target,
            send_sem=send_sem.at[c, k],
            recv_sem=recv_sem.at[c, k],
            device_id=partner_of(axis, owner, shard, bits),
            device_id_type=MESH,
        )

    def count_copy(k):
        return pltpu.make_async_remote_copy(
            src_ref=counts.at[k],
            dst_ref=counts.at[5 + k],
            send_sem=count_send.at[k],
            recv_sem=count_recv.at[k],
            device_id=partner_of(SMALL_AXES[k], owner, shard, bits),
            device_id_type=MESH,
        )

    for c in range(GATHER_CHUNKS):
        keep(c).start()
    total = jnp.broadcast_to(jnp.sum(mask_ref[...].astype(F32), keepdims=True), count_ref.shape)
    counts[0] = total
    meet_partners(owner, shard, bits)
    stage = 0
    for position, code in enumerate(GATHER_ORDER):
        c, k = code % 1000 // 10, code % 10
        if code < 2000:
            move(c, k).wait_recv()
        else:
            if k == 1:
                keep(c).wait()
            move(c, k).start()
        if position == 0:
            count_copy(0).start()
        elif position % 12 == 0 and stage < 5:
            count_copy(stage).wait_recv()
            total = counts[stage] + counts[5 + stage]
            stage += 1
            if stage < 5:
                counts[stage] = total
                count_copy(stage).start()
    count_ref[...] = jnp.maximum(total, 1.0)
    for c in range(GATHER_CHUNKS):
        for k in range(5):
            move(c, k).wait_send()
    for k in range(5):
        count_copy(k).wait_send()


def gather_everywhere(own, mask):
    groups, edge, strip = own.shape
    return pl.pallas_call(
        gather_kernel,
        out_shape=(
            jax.ShapeDtypeStruct((GATHER_CHUNKS, 32, edge // HALVES, strip), own.dtype),
            jax.ShapeDtypeStruct((8, LANES), F32),
        ),
        in_specs=[pl.BlockSpec(memory_space=pltpu.VMEM)] * 2,
        out_specs=(pl.BlockSpec(memory_space=pl.ANY), pl.BlockSpec(memory_space=pltpu.VMEM)),
        scratch_shapes=[
            pltpu.VMEM((10, 8, LANES), F32),
            pltpu.SemaphoreType.DMA((GATHER_CHUNKS,)),
            pltpu.SemaphoreType.DMA((GATHER_CHUNKS, 5)),
            pltpu.SemaphoreType.DMA((GATHER_CHUNKS, 5)),
            pltpu.SemaphoreType.DMA((5,)),
            pltpu.SemaphoreType.DMA((5,)),
        ],
        compiler_params=pltpu.CompilerParams(collective_id=2, has_side_effects=True),
        name="gather_weights",
    )(own, mask)


def dot_top(left, right, dims):
    return lax.dot_general(
        left, right, (dims, ((), ())), precision=TOP_PRECISION, preferred_element_type=F32
    )


def shampoo_parts(grad, left, right, left_root, right_root, weight):
    new_left = STAT_DECAY * left + (1.0 - STAT_DECAY) * dot_top(grad, grad, ((1,), (1,)))
    new_right = STAT_DECAY * right + (1.0 - STAT_DECAY) * dot_top(grad, grad, ((0,), (0,)))
    precond = dot_top(dot_top(left_root, grad, ((1,), (0,))), right_root, ((1,), (0,)))
    scale = 1.0 / (grad.shape[0] * grad.shape[1])
    mean = jnp.sum(jnp.sum(precond * precond, 1, keepdims=True), 0, keepdims=True) * scale
    scale_back = lax.rsqrt(mean + ROOT_EPSILON)
    new_weight = weight * (1.0 - MATRIX_RATE * WEIGHT_DECAY) - MATRIX_RATE * precond * scale_back
    return new_left, new_right, new_weight


def block_update_kernel(
    stats_ref, grad_ref, left_ref, right_ref, left_root_ref, right_root_ref, weight_ref,
    grad_out, left_out, right_out, weight_out,
):
    factor = stats_ref[0:1, 0:1]
    for b in range(grad_ref.shape[0]):
        grad = grad_ref[b] * factor
        grad_out[b] = grad
        left_out[b], right_out[b], weight_out[b] = shampoo_parts(
            grad, left_ref[b], right_ref[b], left_root_ref[b], right_root_ref[b], weight_ref[b]
        )


def update_blocks(stats, grads, left, right, left_root, right_root, weight):
    count, edge, _ = grads.shape
    per_step = PACK if count % PACK == 0 else 1
    spec = pl.BlockSpec((per_step, edge, edge), lambda i: (i, 0, 0))
    out = jax.ShapeDtypeStruct(grads.shape, F32)
    return pl.pallas_call(
        block_update_kernel,
        out_shape=(out,) * 4,
        grid=(count // per_step,),
        in_specs=[whole(stats.shape)] + [spec] * 6,
        out_specs=(spec,) * 4,
        compiler_params=params(),
        name="update_blocks",
    )(stats, grads, left, right, left_root, right_root, weight)


def table_update_kernel(
    step_ref, stats_ref, grad_ref, left_ref, right_ref, left_root_ref, right_root_ref, weight_ref,
    norm_grad_ref, moment_ref, second_ref, norm_ref,
    grad_out, left_out, right_out, weight_out, norm_grad_out, moment_out, second_out, norm_out,
):
    factor = stats_ref[0:1, 0:1]
    grad = grad_ref[...] * factor
    grad_out[...] = grad
    left_out[...], right_out[...], weight_out[...] = shampoo_parts(
        grad, left_ref[...], right_ref[...], left_root_ref[...], right_root_ref[...], weight_ref[...]
    )
    rows = norm_ref.shape[0]
    clipped = norm_grad_ref[0:rows, :] * factor
    norm_grad_out[...] = clipped
    moment = FIRST_BETA * moment_ref[...] + (1.0 - FIRST_BETA) * clipped
    second = SECOND_BETA * second_ref[...] + (1.0 - SECOND_BETA) * clipped * clipped
    moment_out[...] = moment
    second_out[...] = second
    one = moment / step_ref[0:1, 0:1]
    two = second / step_ref[0:1, 1:2]
    weight = norm_ref[...]
    norm_out[...] = weight - VECTOR_RATE * (one / (jnp.sqrt(two) + ADAM_EPSILON) + WEIGHT_DECAY * weight)


def update_table(corrections, stats, grad, left, right, left_root, right_root, weight, norm_grad, moment, second, norms):
    like = lambda array: jax.ShapeDtypeStruct(array.shape, F32)
    return pl.pallas_call(
        table_update_kernel,
        out_shape=(like(grad), like(left), like(right), like(weight)) + (like(norms),) * 4,
        compiler_params=params(),
        name="update_table",
    )(corrections, stats, grad, left, right, left_root, right_root, weight, norm_grad, moment, second, norms)


def rotary_tables(length):
    half = HS // 2
    freqs = jnp.exp(-math.log(ROTARY_BASE) * (2.0 * jnp.arange(half, dtype=F32) / HS))
    angles = jnp.arange(length, dtype=F32)[:, None] * freqs[None, :]
    cosine, sine = jnp.cos(angles), jnp.sin(angles)
    repeats = LANES // HS
    return (
        jnp.concatenate([cosine, cosine] * repeats, -1),
        jnp.concatenate([-sine, sine] * repeats, -1),
    )


def pack_blocks(blocks):
    count, edge, _ = blocks.shape
    groups = blocks.reshape(count // PACK, PACK, edge, edge).transpose(0, 2, 1, 3)
    return groups.reshape(count // PACK, edge, PACK * edge)


def gather_weights(own, mask, known):
    everyone = ("dp", "tensor")
    slots, edge, _ = own.shape
    strip = PACK * edge
    if known:
        packed, count = gather_everywhere(pack_blocks(own), mask)
        packed = packed.reshape(HALVES, -1, edge // HALVES, strip)

        def place_of(owner, shard, slot):
            bits = bits_of(owner, shard)
            group = slot // PACK
            entry = gather_entry(0, bits)
            for g in range(1, PACK_GROUPS):
                entry = jnp.where(group == g, gather_entry(g, bits), entry)
            return (group * 32 + entry) * PACK + slot % PACK

        return packed, place_of, count
    packed = pack_blocks(lax.all_gather(own, everyone, axis=0, tiled=True))
    packed = packed.reshape(-1, HALVES, edge // HALVES, strip).transpose(1, 0, 2, 3)
    shards = lax.axis_size("tensor")
    count = jnp.maximum(lax.psum(jnp.sum(mask.astype(F32)), everyone), 1.0)
    return (
        packed,
        lambda owner, shard, slot: (owner * shards + shard) * slots + slot,
        jnp.broadcast_to(count, (8, LANES)),
    )


def body(
    codons,
    segments,
    targets,
    loss_mask,
    owner_map,
    step_count,
    block_weight,
    block_left,
    block_right,
    block_left_root,
    block_right_root,
    embedding_weight,
    table_left,
    table_right,
    table_left_root,
    table_right_root,
    norm_params,
    norm_moment,
    norm_second,
):
    everyone = ("dp", "tensor")
    vocab, width = embedding_weight.shape
    shards = lax.axis_size("tensor")
    owners = lax.axis_size("dp")
    slots = block_weight.shape[1]
    edge = block_weight.shape[-1]
    blocks = owner_map.shape[0]
    length = codons.shape[1]
    shard_width = width // shards

    known = on_known_slice(owners, shards, slots)
    packed, place_of, count = gather_weights(block_weight[0].astype(BF16), loss_mask, known)
    owner = jnp.broadcast_to((owner_map // slots)[None, :], (shards, blocks))
    slot = jnp.broadcast_to((owner_map % slots)[None, :], (shards, blocks))
    shard = jnp.broadcast_to(jnp.arange(shards, dtype=jnp.int32)[:, None], (shards, blocks))
    device = owner * shards + shard
    place = jnp.concatenate(block_tables(place_of(owner, shard, slot), width, shard_width, FF, edge))
    project, outward, expand, contract = assemble(place, packed, width, FF)

    mask_col = loss_mask.reshape(length, 1).astype(F32)
    codon_col = codons.reshape(length, 1)
    target_col = targets.reshape(length, 1)
    segment = lax.dynamic_index_in_dim(segments, lax.axis_index("tensor"), 0, keepdims=False)
    tiles = length // TILE
    seg_col = segment.reshape(length, 1)
    seg_row = segment.reshape(tiles, 1, TILE)
    tiled = segment.reshape(length // ROWS, ROWS)
    before = jnp.sum((segment[None, :] < tiled[:, :1]).astype(jnp.int32), -1)
    until = jnp.sum((segment[None, :] <= tiled[:, -1:]).astype(jnp.int32), -1)
    low, high = before // TILE, (until + TILE - 1) // TILE
    cosine, sine = rotary_tables(length)

    x0, h1, query, keys, values = front(codon_col, embedding_weight, norm_params, project, cosine, sine)
    attended, lse = attend(low, high, query, keys, values, seg_col, seg_row)
    (h2, active, d_two, ghid, d_one, gatt, gx, head_grad, norm_grad) = middle_rows(
        x0, attended, target_col, mask_col, count[:1, :1], norm_params, embedding_weight,
        outward, expand, contract,
    )
    gproj = attend_back(
        low, high, query, keys, values, gatt, lse, seg_col, seg_row, cosine, sine
    )
    table_grad, norm_grad = tail_rows(
        codon_col, x0, gx, gproj, norm_params, project, head_grad, norm_grad
    )

    if known:
        home = (slot // PACK * (owners * shards) + device) * PACK + slot % PACK
    else:
        home = device * slots + slot
    home = block_tables(home, width, shard_width, FF, edge)
    model = width // edge
    total = shards * blocks
    grads = weight_grad(by_strips(home[0], model, 3 * model, model), h1, gproj, None, total, edge, width, "grad_project")
    grads = weight_grad(by_strips(home[1], model, model, model), attended, d_one, grads, total, edge, width, "grad_outward")
    grads = weight_grad(by_strips(home[2], model, FF // edge, model), h2, ghid, grads, total, edge, width, "grad_expand")
    grads = weight_grad(by_strips(home[3], FF // edge, model, model), active, d_two, grads, total, edge, width, "grad_contract")
    if known:
        owned, table_grad, norm_grad, stats = sum_everywhere(
            grads.reshape(slots // PACK, owners * shards, PACK, edge, LANES), table_grad, norm_grad, count
        )
    else:
        owned = lax.psum_scatter(grads[:, :, :edge], everyone, scatter_dimension=0, tiled=True)
        table_grad, norm_grad, square_sum = lax.psum((table_grad, norm_grad), everyone) + (
            lax.psum(jnp.sum(owned * owned), everyone),
        )
        vectors = norm_grad[:6]
        square_sum = square_sum + jnp.sum(table_grad * table_grad) + jnp.sum(vectors * vectors)
        stats = statistics(square_sum, jnp.sum(norm_grad[6]), count[:1, :1])
    loss_value, grad_norm = stats[2, 0], stats[1, 0]
    step_value = step_count.astype(F32)
    corrections = jnp.stack([1.0 - FIRST_BETA**step_value, 1.0 - SECOND_BETA**step_value]).reshape(1, 2)
    block_grad, new_left, new_right, new_weight = update_blocks(
        stats, owned, block_left[0], block_right[0], block_left_root[0], block_right_root[0], block_weight[0]
    )
    (
        table_clipped, table_left_new, table_right_new, table_weight_new,
        norm_clipped, moment_new, second_new, params_new,
    ) = update_table(
        corrections, stats, table_grad, table_left, table_right, table_left_root, table_right_root,
        embedding_weight, norm_grad, norm_moment, norm_second, norm_params,
    )
    return (
        loss_value,
        grad_norm,
        block_grad[None],
        new_left[None],
        new_right[None],
        new_weight[None],
        table_clipped,
        table_left_new,
        table_right_new,
        table_weight_new,
        norm_clipped,
        moment_new,
        second_new,
        params_new,
    )


def solution(mesh):
    in_specs = (
        P(("dp", "tensor"), None),
        P("dp", None),
        P(("dp", "tensor"), None),
        P(("dp", "tensor"), None),
        P(),
        P(),
        P("tensor", "dp", None, None),
        P("tensor", "dp", None, None),
        P("tensor", "dp", None, None),
        P("tensor", "dp", None, None),
        P("tensor", "dp", None, None),
        P(),
        P(),
        P(),
        P(),
        P(),
        P(),
        P(),
        P(),
    )
    out_specs = (
        P(),
        P(),
        P("tensor", "dp", None, None),
        P("tensor", "dp", None, None),
        P("tensor", "dp", None, None),
        P("tensor", "dp", None, None),
        P(),
        P(),
        P(),
        P(),
        P(),
        P(),
        P(),
        P(),
    )
    return jax.shard_map(body, mesh=mesh, in_specs=in_specs, out_specs=out_specs, check_vma=False)
```

```python
import functools
import math

import jax
import jax.numpy as jnp
from jax import lax
from jax.experimental import pallas as pl
from jax.experimental.pallas import tpu as pltpu
from jax.sharding import PartitionSpec as P

FF = 3072
HS = 64

CLIP_LEVEL = 0.005
STAT_DECAY = 0.5
MATRIX_RATE = 0.03
WEIGHT_DECAY = 0.01
VECTOR_RATE = 0.2
FIRST_BETA = 0.9
SECOND_BETA = 0.999
ADAM_EPSILON = 1e-08
NORM_EPSILON = 1e-05
ROOT_EPSILON = 1e-06
MASK_VALUE = -1e30
ROTARY_BASE = 10000.0
TOP_PRECISION = lax.Precision.HIGHEST

LANES = 128
PACK = 4
VMEM_LIMIT = 60 * 1024 * 1024
BF16 = jnp.bfloat16
F32 = jnp.float32


def dot(left, right):
    return lax.dot_general(left, right, (((1,), (0,)), ((), ())), preferred_element_type=F32)


def dot_nt(left, right):
    return lax.dot_general(left, right, (((1,), (1,)), ((), ())), preferred_element_type=F32)


def dot_tn(left, right):
    return lax.dot_general(left, right, (((0,), (0,)), ((), ())), preferred_element_type=F32)


def split_three(values):
    high = values.astype(BF16)
    rest = values - high.astype(F32)
    middle = rest.astype(BF16)
    low = (rest - middle.astype(F32)).astype(BF16)
    return high, middle, low


def params(**more):
    return pltpu.CompilerParams(vmem_limit_bytes=VMEM_LIMIT, **more)


def whole(shape):
    return pl.BlockSpec(shape, lambda *_: (0,) * len(shape))


def unpack_group(group, edge):
    return [group[:, edge * j : edge * (j + 1)] for j in range(PACK)]


def block_index(shard, block, blocks):
    return shard * blocks + block


def matrix_rows(row, width, shards, shard_width, hidden_width, edge):
    model = width // edge
    wide = shard_width // edge
    tall = hidden_width // shards // edge
    starts = [0, 3 * wide * model, 4 * wide * model, 4 * wide * model + model * tall]
    blocks = starts[3] + tall * model
    project = [
        block_index(c % (shards * wide) // wide, row * 3 * wide + c // (shards * wide) * wide + c % wide, blocks)
        for c in range(3 * model)
    ]
    outward = [
        block_index(row // wide, starts[1] + row % wide * model + c, blocks) for c in range(model)
    ]
    expand = [
        block_index(c // tall, starts[2] + row * tall + c % tall, blocks) for c in range(shards * tall)
    ]
    steps = model
    each = shards * tall // steps
    contract = []
    for q in range(each):
        r = row * each + q
        contract.append(
            [block_index(r // tall, starts[3] + r % tall * model + c, blocks) for c in range(model)]
        )
    return [project], [outward], [expand], contract


def assemble_rows(tables, place_ref, store, targets, edge):
    strip = PACK * edge
    for block_rows, target in zip(tables, targets):
        for r, places in enumerate(block_rows):
            for c in range(len(places) // PACK):
                blocks = [store[place_ref[places[c * PACK + j]]][:, :edge] for j in range(PACK)]
                target[r * edge : (r + 1) * edge, c * strip : (c + 1) * strip] = jnp.concatenate(
                    blocks, axis=1
                )


def unpack_rows(store, first, group, offset, edge):
    pieces = unpack_group(group, edge)
    for j in range(PACK):
        store[first + j, offset : offset + group.shape[0], :edge] = pieces[j]


def assemble_kernel(
    place_ref, in_ref, project_ref, outward_ref, expand_ref, contract_ref, store, *, load_steps, sizes
):
    step = pl.program_id(0)
    per_step, edge, _ = in_ref.shape

    @pl.when(step < load_steps)
    def _():
        def unpack(g, carry):
            unpack_rows(store, (step * per_step + g) * PACK, in_ref[g], 0, edge)
            return carry

        lax.fori_loop(0, per_step, unpack, 0)

    @pl.when(step >= load_steps)
    def _():
        tables = matrix_rows(step - load_steps, *sizes, edge)
        assemble_rows(tables, place_ref, store, (project_ref, outward_ref, expand_ref, contract_ref), edge)


def matrix_shapes(width, hidden_width):
    return (
        jax.ShapeDtypeStruct((width, 3 * width), BF16),
        jax.ShapeDtypeStruct((width, width), BF16),
        jax.ShapeDtypeStruct((width, hidden_width), BF16),
        jax.ShapeDtypeStruct((hidden_width, width), BF16),
    )


def assemble(place, packed, sizes):
    groups, edge, strip = packed.shape
    width, _, _, hidden_width = sizes
    per_step = 16
    load_steps = groups // per_step
    fill_steps = width // edge
    tall = hidden_width // fill_steps

    def late(step, *_):
        return (jnp.maximum(step - load_steps, 0), 0)

    return pl.pallas_call(
        functools.partial(assemble_kernel, load_steps=load_steps, sizes=sizes),
        out_shape=matrix_shapes(width, hidden_width),
        grid_spec=pltpu.PrefetchScalarGridSpec(
            num_scalar_prefetch=1,
            grid=(load_steps + fill_steps,),
            in_specs=[
                pl.BlockSpec(
                    (per_step, edge, strip), lambda s, *_: (jnp.minimum(s, load_steps - 1), 0, 0)
                )
            ],
            out_specs=[
                pl.BlockSpec((edge, 3 * width), late),
                pl.BlockSpec((edge, width), late),
                pl.BlockSpec((edge, hidden_width), late),
                pl.BlockSpec((tall, width), late),
            ],
            scratch_shapes=[pltpu.VMEM((groups * PACK, edge, LANES), BF16)],
        ),
        compiler_params=params(),
        name="assemble_weights",
    )(place, packed)


def norm_parts(values):
    scale = 1.0 / values.shape[-1]
    center = values - jnp.sum(values, -1, keepdims=True) * scale
    spread = jnp.sum(center * center, -1, keepdims=True) * scale
    inverse = lax.rsqrt(spread + NORM_EPSILON)
    return center * inverse, inverse


def norm_back(grad, unit, inverse, gain):
    scale = 1.0 / grad.shape[-1]
    inner = grad * gain
    mean_one = jnp.sum(inner, -1, keepdims=True) * scale
    mean_two = jnp.sum(inner * unit, -1, keepdims=True) * scale
    return (inner - mean_one - unit * mean_two) * inverse


def turn(values, cosine, sine):
    lane = lax.broadcasted_iota(jnp.int32, values.shape, 1)
    half = HS // 2
    ahead = pltpu.roll(values, LANES - half, 1)
    behind = pltpu.roll(values, half, 1)
    other = jnp.where(lane % HS < half, ahead, behind)
    return values * cosine + other * sine


def front_kernel(
    column_ref, table_ref, norm_ref, project_ref, cos_ref, sin_ref, x_ref, h_ref, q_ref, k_ref, v_ref
):
    rows = column_ref.shape[0]
    vocab, width = table_ref.shape
    index = lax.broadcasted_iota(jnp.int32, (rows, vocab), 1)
    hot = jnp.where(column_ref[:, 0:1] == index, 1.0, 0.0).astype(BF16)
    high, middle, low = split_three(table_ref[...])
    embedded = (dot(hot, high) + dot(hot, middle)) + dot(hot, low)
    embedded = embedded * math.sqrt(width)
    x_ref[...] = embedded
    unit, _ = norm_parts(embedded)
    normed = (unit * norm_ref[0:1, :] + norm_ref[1:2, :]).astype(BF16)
    h_ref[...] = normed
    cosine = cos_ref[...]
    sine = sin_ref[...]
    for part, out_ref in ((0, q_ref), (1, k_ref), (2, v_ref)):
        values = dot(normed, project_ref[:, part * width : (part + 1) * width])
        for c in range(width // LANES):
            piece = values[:, c * LANES : (c + 1) * LANES]
            if part < 2:
                piece = turn(piece, cosine, sine)
            if part == 0:
                piece = piece * HS ** (-0.5)
            out_ref[:, c * LANES : (c + 1) * LANES] = piece.astype(BF16)


def front(columns, table, norm_params, project, cosine, sine):
    length, kinds = columns.shape
    vocab, width = table.shape
    rows = 256
    spec = pl.BlockSpec((rows, width), lambda i: (i, 0))
    low = jax.ShapeDtypeStruct((length, width), BF16)
    return pl.pallas_call(
        front_kernel,
        out_shape=(jax.ShapeDtypeStruct((length, width), F32), low, low, low, low),
        grid=(length // rows,),
        in_specs=[
            pl.BlockSpec((rows, kinds), lambda i: (i, 0)),
            whole(table.shape),
            whole(norm_params.shape),
            whole(project.shape),
            pl.BlockSpec((rows, LANES), lambda i: (i, 0)),
            pl.BlockSpec((rows, LANES), lambda i: (i, 0)),
        ],
        out_specs=(spec, spec, spec, spec, spec),
        compiler_params=params(),
        name="embed_project",
    )(columns, table, norm_params, project, cosine, sine)


ROWS = 256
TILE = 128


def head_masks(rows):
    lane = lax.broadcasted_iota(jnp.int32, (rows, LANES), 1)
    return [lane // HS == h for h in range(LANES // HS)]


def same_segment(seg_col, seg_row_ref, first, count):
    row = jnp.concatenate([seg_row_ref[first + i] for i in range(count)], axis=1)
    return seg_col == row


def attend_kernel(low_ref, high_ref, q_ref, k_ref, v_ref, column_ref, seg_row_ref, o_ref, lse_ref):
    part = pl.program_id(1)
    first, last = low_ref[part], high_ref[part]
    masks = head_masks(ROWS)

    def run(count):
        query = q_ref[...]
        zero = jnp.zeros_like(query)
        span = pl.ds(pl.multiple_of(first * TILE, TILE), count * TILE)
        keys = k_ref[span, :]
        values = v_ref[span, :]
        same = same_segment(column_ref[:, 3:4], seg_row_ref, first, count)
        outs, logs = [], []
        for mask in masks:
            scores = jnp.where(same, dot_nt(jnp.where(mask, query, zero), keys), MASK_VALUE)
            top = jnp.max(scores, -1, keepdims=True)
            exps = jnp.exp(scores - top)
            total = jnp.sum(exps, -1, keepdims=True)
            probs = (exps * (1.0 / total)).astype(BF16)
            outs.append(dot(probs, values))
            logs.append(top + jnp.log(total))
        o_ref[...] = jnp.where(masks[0], outs[0], outs[1]).astype(BF16)
        lse_ref[...] = jnp.where(masks[0], logs[0], logs[1])

    for count in range(1, k_ref.shape[0] // TILE + 1):
        pl.when(last - first == count)(functools.partial(run, count))


def attend(low, high, query, keys, values, columns, seg_row):
    length, width = query.shape
    tiles = length // TILE
    pairs = width // LANES
    column = pl.BlockSpec((ROWS, LANES), lambda p, i, *_: (i, p))
    full = pl.BlockSpec((length, LANES), lambda p, i, *_: (0, p))
    return pl.pallas_call(
        attend_kernel,
        out_shape=(
            jax.ShapeDtypeStruct((length, width), BF16),
            jax.ShapeDtypeStruct((length, width), F32),
        ),
        grid_spec=pltpu.PrefetchScalarGridSpec(
            num_scalar_prefetch=2,
            grid=(pairs, length // ROWS),
            in_specs=[
                column,
                full,
                full,
                pl.BlockSpec((ROWS, columns.shape[1]), lambda p, i, *_: (i, 0)),
                whole((tiles, 1, TILE)),
            ],
            out_specs=(column, column),
        ),
        compiler_params=params(),
        name="attend_forward",
    )(low, high, query, keys, values, columns, seg_row)


def attend_back_kernel(
    low_ref, high_ref, q_ref, k_ref, v_ref, g_ref, lse_ref, column_ref, seg_row_ref, cos_ref, sin_ref,
    out_ref, dk_acc, dv_acc,
):
    part = pl.program_id(1)
    parts = pl.num_programs(1)
    heads = LANES // HS
    first, last = low_ref[part], high_ref[part]
    masks = head_masks(ROWS)

    @pl.when(part == 0)
    def _():
        dk_acc[...] = jnp.zeros_like(dk_acc)
        dv_acc[...] = jnp.zeros_like(dv_acc)

    def run(count):
        query = q_ref[...]
        grad = g_ref[...]
        zero = jnp.zeros_like(query)
        span = pl.ds(pl.multiple_of(first * TILE, TILE), count * TILE)
        keys = k_ref[span, :]
        values = v_ref[span, :]
        same = same_segment(column_ref[:, 3:4], seg_row_ref, first, count)
        dq = []
        dk = dv = None
        for h, mask in enumerate(masks):
            own_query = jnp.where(mask, query, zero)
            own_grad = jnp.where(mask, grad, zero)
            scores = jnp.where(same, dot_nt(own_query, keys), MASK_VALUE)
            probs = jnp.exp(scores - lse_ref[:, h * HS : h * HS + 1])
            grad_probs = dot_nt(own_grad, values)
            delta = jnp.sum(probs * grad_probs, -1, keepdims=True)
            grad_scores = (probs * (grad_probs - delta)).astype(BF16)
            dq.append(dot(grad_scores, keys))
            more_dk = dot(own_query.T, grad_scores)
            more_dv = dot(own_grad.T, probs.astype(BF16))
            dk = more_dk if dk is None else dk + more_dk
            dv = more_dv if dv is None else dv + more_dv
        for i in range(count):
            lanes = slice(i * TILE, (i + 1) * TILE)
            dk_acc[first + i] += dk[:, lanes]
            dv_acc[first + i] += dv[:, lanes]
        rows = pl.ds(pl.multiple_of(part * ROWS, ROWS), ROWS)
        turned = turn(
            jnp.where(masks[0], dq[0], dq[1]) * HS ** (-0.5), cos_ref[rows, :], -sin_ref[rows, :]
        )
        out_ref[0, rows, :] = turned.astype(BF16)

    for count in range(1, k_ref.shape[0] // TILE + 1):
        pl.when(last - first == count)(functools.partial(run, count))

    @pl.when(part == parts - 1)
    def _():
        for j in range(dk_acc.shape[0]):
            rows = slice(j * TILE, (j + 1) * TILE)
            out_ref[1, rows, :] = turn(dk_acc[j].T, cos_ref[rows, :], -sin_ref[rows, :]).astype(BF16)
            out_ref[2, rows, :] = dv_acc[j].T.astype(BF16)


def attend_back(low, high, query, keys, values, grad, lse, columns, seg_row, cosine, sine):
    length, width = query.shape
    tiles = length // TILE
    pairs = width // LANES
    column = pl.BlockSpec((ROWS, LANES), lambda p, i, *_: (i, p))
    full = pl.BlockSpec((length, LANES), lambda p, i, *_: (0, p))
    return pl.pallas_call(
        attend_back_kernel,
        out_shape=jax.ShapeDtypeStruct((3, length, width), BF16),
        grid_spec=pltpu.PrefetchScalarGridSpec(
            num_scalar_prefetch=2,
            grid=(pairs, length // ROWS),
            in_specs=[
                column,
                full,
                full,
                column,
                column,
                pl.BlockSpec((ROWS, columns.shape[1]), lambda p, i, *_: (i, 0)),
                whole((tiles, 1, TILE)),
                whole((length, LANES)),
                whole((length, LANES)),
            ],
            out_specs=pl.BlockSpec((3, length, LANES), lambda p, i, *_: (0, 0, p)),
            scratch_shapes=[
                pltpu.VMEM((tiles, LANES, TILE), F32),
                pltpu.VMEM((tiles, LANES, TILE), F32),
            ],
        ),
        compiler_params=params(),
        name="attend_backward",
    )(low, high, query, keys, values, grad, lse, columns, seg_row, cosine, sine)


INV_SQRT_TWO = 2.0 ** (-0.5)
INV_SQRT_TWO_PI = (2.0 * math.pi) ** (-0.5)


def middle_kernel(
    x_ref, att_ref, column_ref, count_ref, norm_ref, table_ref,
    outward_ref, expand_ref, contract_ref,
    h_ref, active_ref, d_two_ref, ghid_ref, d_one_ref, gatt_ref, gx_ref, head_ref, norm_grad_ref,
    slope,
):
    step = pl.program_id(0)
    rows, width = x_ref.shape
    vocab = table_ref.shape[0]
    ff = expand_ref.shape[1]
    part = width

    @pl.when(step == 0)
    def _():
        head_ref[...] = jnp.zeros_like(head_ref)
        norm_grad_ref[...] = jnp.zeros_like(norm_grad_ref)

    middle = x_ref[...] + dot(att_ref[...], outward_ref[...])
    unit_two, inverse_two = norm_parts(middle)
    gain_two = norm_ref[2:3, :]
    normed_two = (unit_two * gain_two + norm_ref[3:4, :]).astype(BF16)
    h_ref[...] = normed_two

    def forward(c, total):
        cols = pl.ds(pl.multiple_of(c * part, part), part)
        hidden = dot(normed_two, expand_ref[:, cols])
        cumulative = 0.5 + 0.5 * lax.erf(hidden * INV_SQRT_TWO)
        active = (hidden * cumulative).astype(BF16)
        density = jnp.exp(-0.5 * hidden * hidden) * INV_SQRT_TWO_PI
        slope[:, cols] = cumulative + hidden * density
        active_ref[:, cols] = active
        return total + dot(active, contract_ref[cols, :])

    branch = lax.fori_loop(0, ff // part, forward, jnp.zeros((rows, width), F32))
    unit, inverse = norm_parts(middle + branch)
    gain = norm_ref[4:5, :]
    final = (unit * gain + norm_ref[5:6, :]).astype(BF16)
    table = table_ref[...].astype(BF16)
    logits = dot_nt(final, table)
    shifted = logits - jnp.max(logits, -1, keepdims=True)
    exps = jnp.exp(shifted)
    sums = jnp.sum(exps, -1, keepdims=True)
    hot = column_ref[:, 1:2] == lax.broadcasted_iota(jnp.int32, (rows, vocab), 1)
    mask = column_ref[:, 2:3].astype(F32)
    log_probs = shifted - jnp.log(sums)
    picked = jnp.sum(jnp.where(hot, log_probs, 0.0) * mask, 0, keepdims=True)
    norm_grad_ref[6:7, 0:vocab] -= picked
    glogits = ((jnp.exp(log_probs) - jnp.where(hot, 1.0, 0.0)) * (mask / count_ref[0:1, 0:1])).astype(BF16)
    head_ref[...] += dot_tn(glogits, final)
    gfinal = dot(glogits, table)
    norm_grad_ref[4:5, :] += jnp.sum(gfinal * unit, 0, keepdims=True)
    norm_grad_ref[5:6, :] += jnp.sum(gfinal, 0, keepdims=True)
    gx_two = norm_back(gfinal, unit, inverse, gain)
    d_two = gx_two.astype(BF16)
    d_two_ref[...] = d_two

    def backward(c, total):
        cols = pl.ds(pl.multiple_of(c * part, part), part)
        gactive = dot_nt(d_two, contract_ref[cols, :])
        ghid = (gactive * slope[:, cols]).astype(BF16)
        ghid_ref[:, cols] = ghid
        return total + dot_nt(ghid, expand_ref[:, cols])

    gh = lax.fori_loop(0, ff // part, backward, jnp.zeros((rows, width), F32))
    norm_grad_ref[2:3, :] += jnp.sum(gh * unit_two, 0, keepdims=True)
    norm_grad_ref[3:4, :] += jnp.sum(gh, 0, keepdims=True)
    gx_one = gx_two + norm_back(gh, unit_two, inverse_two, gain_two)
    gx_ref[...] = gx_one
    d_one = gx_one.astype(BF16)
    d_one_ref[...] = d_one
    gatt_ref[...] = dot_nt(d_one, outward_ref[...]).astype(BF16)


def middle_rows(x, att, columns, count, norm_params, table, outward, expand, contract):
    length, width = x.shape
    vocab = table.shape[0]
    ff = expand.shape[1]
    rows = 512
    narrow = pl.BlockSpec((rows, width), lambda i: (i, 0))
    broad = pl.BlockSpec((rows, ff), lambda i: (i, 0))
    column = pl.BlockSpec((rows, columns.shape[1]), lambda i: (i, 0))
    low = jax.ShapeDtypeStruct((length, width), BF16)
    low_broad = jax.ShapeDtypeStruct((length, ff), BF16)
    return pl.pallas_call(
        middle_kernel,
        out_shape=(
            low, low_broad, low, low_broad, low, low,
            jax.ShapeDtypeStruct((length, width), F32),
            jax.ShapeDtypeStruct((vocab, width), F32),
            jax.ShapeDtypeStruct((8, width), F32),
        ),
        grid=(length // rows,),
        in_specs=[
            narrow, narrow, column, whole(count.shape), whole(norm_params.shape), whole(table.shape),
            whole(outward.shape), whole(expand.shape), whole(contract.shape),
        ],
        out_specs=(
            narrow, broad, narrow, broad, narrow, narrow, narrow,
            whole((vocab, width)), whole((8, width)),
        ),
        scratch_shapes=[pltpu.VMEM((rows, ff), F32)],
        compiler_params=params(),
        name="middle_rows",
    )(x, att, columns, count, norm_params, table, outward, expand, contract)


def tail_kernel(
    column_ref, x_ref, gx_ref, gproj_ref, norm_ref, project_ref, head_ref, norm_in_ref,
    table_grad_ref, norm_grad_ref,
):
    step = pl.program_id(0)
    rows, width = x_ref.shape
    vocab = head_ref.shape[0]

    @pl.when(step == 0)
    def _():
        table_grad_ref[...] = head_ref[...]
        norm_grad_ref[...] = norm_in_ref[...]

    gh = dot_nt(gproj_ref[0], project_ref[:, 0:width])
    gh = gh + dot_nt(gproj_ref[1], project_ref[:, width : 2 * width])
    gh = gh + dot_nt(gproj_ref[2], project_ref[:, 2 * width : 3 * width])
    unit, inverse = norm_parts(x_ref[...])
    norm_grad_ref[0:1, :] += jnp.sum(gh * unit, 0, keepdims=True)
    norm_grad_ref[1:2, :] += jnp.sum(gh, 0, keepdims=True)
    gx = gx_ref[...] + norm_back(gh, unit, inverse, norm_ref[0:1, :])
    hot = jnp.where(column_ref[:, 0:1] == lax.broadcasted_iota(jnp.int32, (rows, vocab), 1), 1.0, 0.0)
    hot = hot.T.astype(BF16)
    high, middle, low = split_three(gx)
    total = dot(hot, high) + (dot(hot, middle) + dot(hot, low))
    table_grad_ref[...] += total * math.sqrt(width)


def tail_rows(columns, x, gx, gproj, norm_params, project, head, norm_in):
    length, width = x.shape
    rows = 256
    narrow = pl.BlockSpec((rows, width), lambda i: (i, 0))
    return pl.pallas_call(
        tail_kernel,
        out_shape=(
            jax.ShapeDtypeStruct(head.shape, F32),
            jax.ShapeDtypeStruct(norm_in.shape, F32),
        ),
        grid=(length // rows,),
        in_specs=[
            pl.BlockSpec((rows, columns.shape[1]), lambda i: (i, 0)),
            narrow, narrow, pl.BlockSpec((3, rows, width), lambda i: (0, i, 0)),
            whole(norm_params.shape), whole(project.shape), whole(head.shape), whole(norm_in.shape),
        ],
        out_specs=(whole(head.shape), whole(norm_in.shape)),
        compiler_params=params(),
        name="tail_rows",
    )(columns, x, gx, gproj, norm_params, project, head, norm_in)


def weight_grad_kernel(
    place_ref, h_one, att, h_two, active, gproj, d_one, ghid, d_two, out_ref,
    left, right, turned, buf, left_sem, right_sem, out_sem, *, sizes, edge,
):
    width, shards, shard_width, hidden_width = sizes
    model = width // edge
    wide = shard_width // edge
    tall = hidden_width // shards // edge
    starts = [0, 3 * wide * model, 4 * wide * model, 4 * wide * model + model * tall]
    blocks = starts[3] + tall * model
    part = hidden_width // shards
    columns = lambda ref, t: ref.at[:, pl.ds(t * part, part)]
    lefts = [h_one, att, h_two] + [columns(active, t) for t in range(shards)]
    rights = [gproj.at[i] for i in range(3)] + [d_one] + [columns(ghid, t) for t in range(shards)] + [d_two]
    plan = [(0, 0), (0, 1), (0, 2), (1, 3)]
    plan += [(2, 4 + t) for t in range(shards)]
    plan += [(3 + t, 4 + shards) for t in range(shards)]
    step = pl.program_id(0)
    slot = step % 2
    count = buf.shape[1]

    def fetches(n):
        found = []
        if n == 0 or plan[n][0] != plan[n - 1][0]:
            which = plan[n][0] % 2
            found.append(pltpu.make_async_copy(lefts[plan[n][0]], left.at[which], left_sem.at[which]))
        if n == 0 or plan[n][1] != plan[n - 1][1]:
            which = plan[n][1] % 2
            found.append(pltpu.make_async_copy(rights[plan[n][1]], right.at[which], right_sem.at[which]))
        return found

    def drain(which):
        pltpu.make_async_copy(buf.at[which], out_ref.at[pl.ds(0, count)], out_sem.at[which]).wait()

    for n in range(len(plan)):

        @pl.when(step == n)
        def _():
            if n == 0:
                for copy in fetches(0):
                    copy.start()
            for copy in fetches(n):
                copy.wait()
            if n + 1 < len(plan):
                for copy in fetches(n + 1):
                    copy.start()
            if n == 0 or plan[n][0] != plan[n - 1][0]:
                turned[...] = left[plan[n][0] % 2].T

    @pl.when(step >= 2)
    def _():
        drain(slot)

    which = jnp.minimum(step, 4 + shards) % 2
    rows = turned.shape[0] // 2
    for half in range(2):
        result = dot(turned[half * rows : (half + 1) * rows], right[which])
        for i in range(rows // edge):
            r = half * (rows // edge) + i
            for c in range(model // PACK):
                pieces = unpack_group(
                    result[i * edge : (i + 1) * edge, c * PACK * edge : (c + 1) * PACK * edge], edge
                )
                for j in range(PACK):
                    buf[slot, r * model + c * PACK + j, :, :edge] = pieces[j]
            for c in range(model):
                index = block_index(c // wide, r * 3 * wide + step * wide + c % wide, blocks)
                index = jnp.where(
                    step == 3, block_index(r // wide, starts[1] + r % wide * model + c, blocks), index
                )
                index = jnp.where(
                    step >= 4, block_index(step - 4, starts[2] + r * tall + c, blocks), index
                )
                index = jnp.where(
                    step >= 4 + shards,
                    block_index(step - 4 - shards, starts[3] + r * model + c, blocks),
                    index,
                )
                k = r * model + c
                pltpu.make_async_copy(
                    buf.at[slot, k], out_ref.at[place_ref[index]], out_sem.at[slot]
                ).start()

    @pl.when(step == len(plan) - 1)
    def _():
        drain(1 - slot)
        drain(slot)


def weight_grads(place, h_one, att, h_two, active, gproj, d_one, ghid, d_two, sizes, blocks, edge):
    length, width = h_one.shape
    shards = sizes[1]
    count = (width // edge) ** 2
    anywhere = pl.BlockSpec(memory_space=pl.ANY)
    return pl.pallas_call(
        functools.partial(weight_grad_kernel, sizes=sizes, edge=edge),
        out_shape=jax.ShapeDtypeStruct((blocks, edge, LANES), F32),
        grid_spec=pltpu.PrefetchScalarGridSpec(
            num_scalar_prefetch=1,
            grid=(4 + 2 * shards,),
            in_specs=[anywhere] * 8,
            out_specs=anywhere,
            scratch_shapes=[
                pltpu.VMEM((2, length, width), BF16),
                pltpu.VMEM((2, length, width), BF16),
                pltpu.VMEM((width, length), BF16),
                pltpu.VMEM((2, count, edge, LANES), F32),
                pltpu.SemaphoreType.DMA((2,)),
                pltpu.SemaphoreType.DMA((2,)),
                pltpu.SemaphoreType.DMA((2,)),
            ],
        ),
        compiler_params=params(),
        name="weight_gradients",
    )(place, h_one, att, h_two, active, gproj, d_one, ghid, d_two)


CORE, NEAR_Y, NEAR_X, NEAR_Z, FAR_Z = range(5)
AXIS_STRIDE = {CORE: 1, NEAR_Y: 2, NEAR_X: 4, NEAR_Z: 8, FAR_Z: 16}
CHUNK_AXES = (
    (NEAR_X, NEAR_Y, NEAR_Z, FAR_Z),
    (NEAR_Y, NEAR_X, NEAR_Z, FAR_Z),
    (NEAR_X, NEAR_Y, NEAR_Z, FAR_Z),
    (NEAR_Y, NEAR_X, NEAR_Z, FAR_Z),
    (NEAR_Z, NEAR_X, NEAR_Y, FAR_Z),
    (NEAR_Z, NEAR_Y, NEAR_X, FAR_Z),
)
PACK_GROUPS = 6
QUARTERS = 4
SUM_CHUNKS = PACK_GROUPS * QUARTERS
SUM_SLOTS = 3
SUM_ORDER = (
    0, 2000, 10, 2010, 20, 2020, 1000, 2001, 1010, 2011, 1020, 2021, 30, 2030, 40, 2040, 50, 2050, 1030, 2031, 1040,
    2041, 1050, 2051, 60, 2060, 70, 2070, 1011, 80, 2012, 2080, 1001, 2002, 1060, 2061, 1070, 1080, 2071, 90, 2090,
    1021, 100, 2100, 1031, 2032, 110, 2110, 2022, 1012, 1090, 2013, 1002, 1100, 2003, 120, 2120, 1041, 1110, 2101,
    1051, 130, 2130, 2042, 140, 2140, 2111, 1013, 2052, 2014, 1120, 1032, 1003, 2081, 2004, 1022, 150, 2150, 1130,
    2091, 1061, 1014, 1140, 160, 2160, 1004, 1071, 2072, 1150, 2062, 170, 2170, 1042, 180, 2180, 1052, 1160, 190,
    2190, 2023, 1170, 1180, 2053, 1101, 200, 2200, 2043, 2033, 210, 2210, 2102, 2161, 1072, 1190, 1062, 1023, 2024,
    1111, 2121, 2112, 1081, 2063, 220, 2220, 2082, 1200, 1053, 2054, 1033, 2034, 1091, 1043, 1210, 1024, 2073, 230,
    2230, 1220, 2092, 2044, 1063, 2064, 1102, 2103, 1054, 2171, 1034, 1230, 2131, 1112, 1073, 2074, 1082, 2151,
    1044, 1064, 1103, 2104, 2083, 2113, 1074, 2141, 1161, 1092, 1121, 2093, 1104, 2162, 1083, 2084, 1113, 2114,
    2221, 1093, 2094, 2231, 1084, 2122, 1114, 2181, 1171, 2172, 1131, 1094, 1162, 1151, 2132, 1141, 2142, 2163,
    1122, 1172, 2123, 2191, 2152, 1221, 1163, 2164, 1132, 2133, 2211, 2173, 1231, 1123, 2124, 1142, 2143, 1181,
    1164, 1133, 2134, 2201, 2222, 1124, 1143, 2144, 1173, 2174, 1152, 2153, 1134, 1153, 2154, 1144, 1174, 2182,
    1191, 2192, 1222, 2223, 1154, 1211, 2212, 1201, 2202, 2232, 1223, 2224, 1182, 2183, 1192, 2193, 1224, 1212,
    2213, 1183, 2184, 1202, 2203, 1193, 2194, 1232, 2233, 1184, 1213, 2214, 1203, 2204, 1233, 2234, 1194, 1214,
    1204, 1234,
)
SMALL_ROWS = 1024
SMALL_AXES = (CORE, NEAR_X, NEAR_Y, NEAR_Z, FAR_Z)
MESH = pl.DeviceIdType.MESH


def on_known_slice(owners, shards, slots):
    return owners == 8 and shards == 4 and slots % PACK == 0 and slots == PACK * PACK_GROUPS


def bits_of(owner, shard):
    return {
        CORE: shard % 2,
        NEAR_Y: shard // 2,
        NEAR_X: owner % 2,
        NEAR_Z: owner // 2 % 2,
        FAR_Z: owner // 4,
    }


def own_bits():
    owner, shard = lax.axis_index("dp"), lax.axis_index("tensor")
    return owner, shard, bits_of(owner, shard)


def partner_of(axis, owner, shard, bits):
    if axis == CORE:
        return (owner, shard + 1 - 2 * bits[CORE])
    if axis == NEAR_Y:
        return (owner, shard + 2 - 4 * bits[NEAR_Y])
    step = {NEAR_X: 1, NEAR_Z: 2, FAR_Z: 4}[axis]
    return (owner + step - 2 * step * bits[axis], shard)


def greet_partners(owner, shard, bits):
    barrier = pltpu.get_barrier_semaphore()
    for axis in range(5):
        pl.semaphore_signal(
            barrier, inc=1, device_id=partner_of(axis, owner, shard, bits), device_id_type=MESH
        )


def await_partners():
    pl.semaphore_wait(pltpu.get_barrier_semaphore(), 5)


def total_of(values):
    return jnp.sum(jnp.sum(values, 1, keepdims=True), 0, keepdims=True)


def statistics(square_sum, loss_sum, count):
    norm = jnp.sqrt(square_sum)
    factor = CLIP_LEVEL / jnp.maximum(norm, CLIP_LEVEL)
    row = lax.broadcasted_iota(jnp.int32, (8, LANES), 0)
    return jnp.where(row == 0, factor, jnp.where(row == 1, norm, loss_sum / count))


def sum_kernel(
    grads_ref, table_ref, norm_ref, count_ref, owned_ref, table_out, norm_out, stats_out,
    inbuf, stage, r0, r1, r2, r3, r4, small, s0, s1, s2, s3, s4, spread, square, squares,
    in_sem, send_sem, recv_sem, small_send, small_recv, square_send, square_recv,
):
    owner, shard, bits = own_bits()
    edge = grads_ref.shape[3]
    strip = PACK * edge
    part = edge // QUARTERS
    received = (r0, r1, r2, r3, r4)

    def axes_of(c):
        return CHUNK_AXES[c % len(CHUNK_AXES)]

    def fetch(c):
        rows = pl.ds(c % QUARTERS * part, part)
        slot = c % SUM_SLOTS
        return pltpu.make_async_copy(
            grads_ref.at[c // QUARTERS, :, :, rows], inbuf.at[slot], in_sem.at[slot]
        )

    for c in range(SUM_SLOTS):
        fetch(c).start()
    greet_partners(owner, shard, bits)
    await_partners()

    def chunk_send(c, k):
        if k == 0:
            axis, source = CORE, stage.at[c % SUM_SLOTS]
        else:
            axis = axes_of(c)[k - 1]
            half = received[k - 1].shape[1] // 2
            source = received[k - 1].at[c, pl.ds(half * (1 - bits[axis]), half)]
        return pltpu.make_async_remote_copy(
            src_ref=source,
            dst_ref=received[k].at[c],
            send_sem=send_sem.at[c, k],
            recv_sem=recv_sem.at[c, k],
            device_id=partner_of(axis, owner, shard, bits),
            device_id_type=MESH,
        )

    def packed(c, e, core):
        d = core
        for k, axis in enumerate(axes_of(c)):
            d = d + e // (8 >> k) % 2 * AXIS_STRIDE[axis]
        blocks = [inbuf[c % SUM_SLOTS, d, j][:, :edge] for j in range(PACK)]
        return jnp.concatenate(blocks, axis=1)

    def pack(c):
        fetch(c).wait()
        if c >= SUM_SLOTS:
            chunk_send(c - SUM_SLOTS, 0).wait_send()

        def body(e, carry):
            stage[c % SUM_SLOTS, e] = packed(c, e, 1 - bits[CORE])
            return carry

        lax.fori_loop(0, 16, body, 0, unroll=4)

    def merge(c, k):
        chunk_send(c, k).wait_recv()
        if k == 0:

            def body(e, carry):
                r0[c, e] = r0[c, e] + packed(c, e, bits[CORE])
                return carry

            lax.fori_loop(0, 16, body, 0, unroll=4)
            if c + SUM_SLOTS < SUM_CHUNKS:
                fetch(c + SUM_SLOTS).start()
            return
        axis = axes_of(c)[k - 1]
        half = received[k].shape[1]
        base = half * bits[axis]

        def body(e, carry):
            received[k][c, e] = received[k][c, e] + received[k - 1][c, base + e]
            return carry

        if k < 4:
            lax.fori_loop(0, half, body, 0, unroll=2)
            return
        group = r4[c, 0] + r3[c, base]
        pieces = unpack_group(group, edge)
        rows = slice(c % QUARTERS * part, (c % QUARTERS + 1) * part)
        for j in range(PACK):
            owned_ref[PACK * (c // QUARTERS) + j, rows, :] = pieces[j]
        parts = group * group
        line = parts[:, :LANES]
        for i in range(1, strip // LANES):
            line = line + parts[:, i * LANES : (i + 1) * LANES]
        total = square[...]
        for r in range(part // 8):
            total = total + line[r * 8 : (r + 1) * 8]
        square[...] = total

    vocab, width = table_ref.shape
    vectors = norm_ref.shape[0]
    columns = width // LANES
    small_parts = (s0, s1, s2, s3, s4)

    def small_fill():
        for c in range(columns):
            lanes = slice(c * LANES, (c + 1) * LANES)
            small[c * vocab : (c + 1) * vocab] = table_ref[:, lanes]
            start = columns * vocab + c * vectors
            small[start : start + vectors] = norm_ref[:, lanes]
        used = columns * (vocab + vectors)
        small[used:] = jnp.zeros((SMALL_ROWS - used, LANES), F32)

    def small_base(k):
        base = 0
        for i in range(k):
            base = base + (SMALL_ROWS >> (i + 1)) * bits[SMALL_AXES[i]]
        return base

    def small_copy(k):
        rows = SMALL_ROWS >> (k + 1)
        start = pl.multiple_of(small_base(k) + rows * (1 - bits[SMALL_AXES[k]]), 8)
        return pltpu.make_async_remote_copy(
            src_ref=small.at[pl.ds(start, rows)],
            dst_ref=small_parts[k],
            send_sem=small_send.at[k],
            recv_sem=small_recv.at[k],
            device_id=partner_of(SMALL_AXES[k], owner, shard, bits),
            device_id_type=MESH,
        )

    def small_merge(k):
        small_copy(k).wait_recv()
        rows = SMALL_ROWS >> (k + 1)
        mine = pl.ds(pl.multiple_of(small_base(k + 1), 8), rows)
        if k < 4:
            small[mine, :] = small[mine, :] + small_parts[k][...]
            small_copy(k + 1).start()
        else:
            spread[mine, :] = small[mine, :] + small_parts[k][...]
            spread_copy(4).start()

    def spread_copy(k):
        rows = SMALL_ROWS >> (k + 1)
        here = pl.ds(pl.multiple_of(small_base(k + 1), 8), rows)
        return pltpu.make_async_remote_copy(
            src_ref=spread.at[here],
            dst_ref=spread.at[here],
            send_sem=small_send.at[5 + k],
            recv_sem=small_recv.at[5 + k],
            device_id=partner_of(SMALL_AXES[k], owner, shard, bits),
            device_id_type=MESH,
        )

    def spread_next(k):
        spread_copy(k).wait_recv()
        if k > 0:
            spread_copy(k - 1).start()
        else:
            for c in range(columns):
                lanes = slice(c * LANES, (c + 1) * LANES)
                table_out[:, lanes] = spread[c * vocab : (c + 1) * vocab]
                start = columns * vocab + c * vectors
                norm_out[:, lanes] = spread[start : start + vectors]

    square[...] = jnp.zeros_like(square)
    small_fill()
    small_copy(0).start()
    extra = [functools.partial(small_merge, k) for k in range(5)]
    extra += [functools.partial(spread_next, k) for k in range(4, -1, -1)]
    for position, code in enumerate(SUM_ORDER):
        c, k = code % 1000 // 10, code % 10
        if code < 1000:
            pack(c)
        elif code < 2000:
            merge(c, k)
        else:
            chunk_send(c, k).start()
        if position >= 60 and position % 12 == 0 and extra:
            extra.pop(0)()
    while extra:
        extra.pop(0)()

    def square_copy(k):
        return pltpu.make_async_remote_copy(
            src_ref=squares.at[k],
            dst_ref=squares.at[5 + k],
            send_sem=square_send.at[k],
            recv_sem=square_recv.at[k],
            device_id=partner_of(SMALL_AXES[k], owner, shard, bits),
            device_id_type=MESH,
        )

    value = square[...]
    for k in range(5):
        squares[k] = value
        square_copy(k).start()
        square_copy(k).wait_recv()
        value = squares[k] + squares[5 + k]
    table_sum, vectors_sum = table_out[...], norm_out[0:6, :]
    stats_out[...] = statistics(
        total_of(value) + total_of(table_sum * table_sum) + total_of(vectors_sum * vectors_sum),
        total_of(norm_out[6:7, :]),
        count_ref[0:1, 0:1],
    )

    for c in range(SUM_CHUNKS):
        for k in range(5):
            if k > 0 or c >= SUM_CHUNKS - SUM_SLOTS:
                chunk_send(c, k).wait_send()
    for k in range(5):
        small_copy(k).wait_send()
        spread_copy(k).wait_send()
        square_copy(k).wait_send()


def sum_everywhere(grads, table_grad, norm_grad, count):
    groups, devices, _, edge, _ = grads.shape
    strip = PACK * edge
    part = edge // QUARTERS
    group = lambda count: pltpu.VMEM((SUM_CHUNKS, count, part, strip), F32)
    small = lambda rows: pltpu.VMEM((rows, LANES), F32)
    return pl.pallas_call(
        sum_kernel,
        out_shape=(
            jax.ShapeDtypeStruct((groups * PACK, edge, edge), F32),
            jax.ShapeDtypeStruct(table_grad.shape, F32),
            jax.ShapeDtypeStruct(norm_grad.shape, F32),
            jax.ShapeDtypeStruct((8, LANES), F32),
        ),
        in_specs=[
            pl.BlockSpec(memory_space=pl.ANY),
            pl.BlockSpec(memory_space=pltpu.VMEM),
            pl.BlockSpec(memory_space=pltpu.VMEM),
            pl.BlockSpec(memory_space=pltpu.VMEM),
        ],
        out_specs=(pl.BlockSpec(memory_space=pltpu.VMEM),) * 4,
        scratch_shapes=[
            pltpu.VMEM((SUM_SLOTS, devices, PACK, part, LANES), F32),
            pltpu.VMEM((SUM_SLOTS, devices // 2, part, strip), F32),
            group(16), group(8), group(4), group(2), group(1),
            small(SMALL_ROWS), small(512), small(256), small(128), small(64), small(32), small(SMALL_ROWS),
            pltpu.VMEM((8, LANES), F32),
            pltpu.VMEM((10, 8, LANES), F32),
            pltpu.SemaphoreType.DMA((SUM_SLOTS,)),
            pltpu.SemaphoreType.DMA((SUM_CHUNKS, 5)),
            pltpu.SemaphoreType.DMA((SUM_CHUNKS, 5)),
            pltpu.SemaphoreType.DMA((10,)),
            pltpu.SemaphoreType.DMA((10,)),
            pltpu.SemaphoreType.DMA((5,)),
            pltpu.SemaphoreType.DMA((5,)),
        ],
        compiler_params=pltpu.CompilerParams(
            vmem_limit_bytes=66_000_000, collective_id=1, has_side_effects=True
        ),
        name="sum_gradients",
    )(grads, table_grad, norm_grad, count)


GATHER_AXES = (
    (NEAR_Z, NEAR_Y, NEAR_X, FAR_Z),
    (NEAR_X, NEAR_Y, NEAR_Z, FAR_Z),
    (NEAR_Y, NEAR_X, FAR_Z, NEAR_Z),
    (NEAR_Z, NEAR_Y, FAR_Z, NEAR_X),
    (NEAR_X, NEAR_Z, FAR_Z, NEAR_Y),
    (NEAR_Y, NEAR_X, FAR_Z, NEAR_Z),
)
HALVES = 2
GATHER_CHUNKS = PACK_GROUPS * HALVES
GATHER_ORDER = (
    2030, 2090, 2100, 2040, 2080, 2060, 2020, 2070, 2110, 2010, 1080, 1030, 1100, 1090, 1040, 1060, 2061, 2050,
    2081, 1020, 1070, 2071, 1110, 1010, 2021, 1061, 2062, 1050, 2011, 1081, 2082, 2031, 1071, 2072, 1062, 2063,
    1021, 2022, 2101, 1011, 2012, 1082, 2083, 1072, 2073, 1031, 2032, 2111, 1022, 1101, 2000, 2023, 2091, 1012,
    2013, 1111, 2112, 1000, 2001, 2041, 1073, 2074, 2102, 1063, 2064, 1091, 2092, 1074, 2051, 1032, 1064, 1041,
    1001, 2033, 1112, 2113, 1102, 2103, 1051, 2052, 1083, 2084, 1013, 2014, 2002, 1084, 2042, 1092, 1014, 1033,
    2034, 1023, 2024, 2093, 1052, 2053, 1034, 1042, 2043, 1024, 1103, 2104, 1002, 2003, 1104, 1093, 2094, 1113,
    2114, 1043, 2044, 1094, 1114, 1053, 2054, 1044, 1003, 2004, 1054, 1004,
)


def gather_entry(group, bits):
    first, second, third, fourth = GATHER_AXES[group]
    return 16 * bits[CORE] + 8 * bits[first] + 4 * bits[second] + 2 * bits[third] + bits[fourth]


def gather_kernel(
    place_ref, own_ref, mask_ref, project_out, outward_out, expand_out, contract_out, count_ref,
    packed, held, store, project, outward, expand, contract, counts,
    own_sem, send_sem, recv_sem, count_send, count_recv, out_sem, *, sizes,
):
    owner, shard, bits = own_bits()
    edge = own_ref.shape[1]
    rows = edge // HALVES
    devices = held.shape[1]

    def place(c):
        return gather_entry(c % PACK_GROUPS, bits)

    def own_part(c):
        return packed.at[c % PACK_GROUPS, pl.ds(c // PACK_GROUPS * rows, rows)]

    def keep(c):
        return pltpu.make_async_copy(own_part(c), held.at[c, place(c)], own_sem.at[c])

    def move(c, k):
        axis = CORE if k == 4 else GATHER_AXES[c % PACK_GROUPS][3 - k]
        if k == 0:
            source = own_part(c)
            target = held.at[c, place(c)]
        else:
            size = 1 << k
            base = place(c) // size * size
            source = held.at[c, pl.ds(base, size)]
            target = source
        return pltpu.make_async_remote_copy(
            src_ref=source,
            dst_ref=target,
            send_sem=send_sem.at[c, k],
            recv_sem=recv_sem.at[c, k],
            device_id=partner_of(axis, owner, shard, bits),
            device_id_type=MESH,
        )

    def count_copy(k):
        return pltpu.make_async_remote_copy(
            src_ref=counts.at[k],
            dst_ref=counts.at[5 + k],
            send_sem=count_send.at[k],
            recv_sem=count_recv.at[k],
            device_id=partner_of(SMALL_AXES[k], owner, shard, bits),
            device_id_type=MESH,
        )

    greet_partners(owner, shard, bits)
    for g in range(PACK_GROUPS):
        blocks = [own_ref[g * PACK + b].astype(BF16) for b in range(PACK)]
        packed[g] = jnp.concatenate(blocks, axis=1)
    total = jnp.broadcast_to(jnp.sum(mask_ref[...].astype(F32), keepdims=True), count_ref.shape)
    counts[0] = total
    await_partners()
    for c in range(GATHER_CHUNKS):
        keep(c).start()

    def unpack(c):
        group = c % PACK_GROUPS
        offset = c // PACK_GROUPS * rows

        def body(e, carry):
            unpack_rows(store, (group * devices + e) * PACK, held[c, e], offset, edge)
            return carry

        lax.fori_loop(0, devices, body, 0, unroll=2)

    stage = 0
    for position, code in enumerate(GATHER_ORDER):
        c, k = code % 1000 // 10, code % 10
        if code >= 2000:
            if k == 1:
                keep(c).wait()
            move(c, k).start()
        else:
            move(c, k).wait_recv()
            if k == 4:
                unpack(c)
        if position == 0:
            count_copy(0).start()
        elif position % 12 == 0 and stage < 5:
            count_copy(stage).wait_recv()
            total = counts[stage] + counts[5 + stage]
            stage += 1
            if stage < 5:
                counts[stage] = total
                count_copy(stage).start()
    count_ref[...] = jnp.maximum(total, 1.0)

    steps = project.shape[0] // edge
    staged = ((project, project_out), (outward, outward_out), (expand, expand_out), (contract, contract_out))

    def body(row, carry):
        tables = matrix_rows(row, *sizes, edge)
        targets, copies = [], []
        for n, (inside, outside) in enumerate(staged):
            size = inside.shape[0] // steps
            part = pl.ds(pl.multiple_of(row * size, size), size)
            targets.append(inside.at[part])
            copies.append(pltpu.make_async_copy(inside.at[part], outside.at[part], out_sem.at[n]))
        assemble_rows(tables, place_ref, store, targets, edge)
        for copy in copies:
            copy.start()
        return carry

    lax.fori_loop(0, steps, body, 0)
    for c in range(GATHER_CHUNKS):
        for k in range(5):
            move(c, k).wait_send()
    for k in range(5):
        count_copy(k).wait_send()
    for n, (inside, outside) in enumerate(staged):
        pltpu.make_async_copy(inside, outside, out_sem.at[n]).wait()


def gather_everywhere(place, own, mask, devices, sizes):
    slots, edge, _ = own.shape
    width, _, _, hidden_width = sizes
    strip = PACK * edge
    shapes = matrix_shapes(width, hidden_width)
    return pl.pallas_call(
        functools.partial(gather_kernel, sizes=sizes),
        out_shape=shapes + (jax.ShapeDtypeStruct((8, LANES), F32),),
        in_specs=[
            pl.BlockSpec(memory_space=pltpu.SMEM),
            pl.BlockSpec(memory_space=pltpu.VMEM),
            pl.BlockSpec(memory_space=pltpu.VMEM),
        ],
        out_specs=(pl.BlockSpec(memory_space=pl.ANY),) * 4 + (pl.BlockSpec(memory_space=pltpu.VMEM),),
        scratch_shapes=[
            pltpu.VMEM((PACK_GROUPS, edge, strip), BF16),
            pltpu.VMEM((GATHER_CHUNKS, devices, edge // HALVES, strip), BF16),
            pltpu.VMEM((devices * slots, edge, LANES), BF16),
            *[pltpu.VMEM(shape.shape, shape.dtype) for shape in shapes],
            pltpu.VMEM((10, 8, LANES), F32),
            pltpu.SemaphoreType.DMA((GATHER_CHUNKS,)),
            pltpu.SemaphoreType.DMA((GATHER_CHUNKS, 5)),
            pltpu.SemaphoreType.DMA((GATHER_CHUNKS, 5)),
            pltpu.SemaphoreType.DMA((5,)),
            pltpu.SemaphoreType.DMA((5,)),
            pltpu.SemaphoreType.DMA((4,)),
        ],
        compiler_params=params(collective_id=2, has_side_effects=True),
        name="gather_weights",
    )(place, own, mask)


def dot_top(left, right, dims):
    return lax.dot_general(
        left, right, (dims, ((), ())), precision=TOP_PRECISION, preferred_element_type=F32
    )


def shampoo_parts(grad, left, right, left_root, right_root, weight):
    new_left = STAT_DECAY * left + (1.0 - STAT_DECAY) * dot_top(grad, grad, ((1,), (1,)))
    new_right = STAT_DECAY * right + (1.0 - STAT_DECAY) * dot_top(grad, grad, ((0,), (0,)))
    precond = dot_top(dot_top(left_root, grad, ((1,), (0,))), right_root, ((1,), (0,)))
    scale = 1.0 / (grad.shape[0] * grad.shape[1])
    mean = jnp.sum(jnp.sum(precond * precond, 1, keepdims=True), 0, keepdims=True) * scale
    scale_back = lax.rsqrt(mean + ROOT_EPSILON)
    new_weight = weight * (1.0 - MATRIX_RATE * WEIGHT_DECAY) - MATRIX_RATE * precond * scale_back
    return new_left, new_right, new_weight


def block_update_kernel(
    stats_ref, grad_ref, left_ref, right_ref, left_root_ref, right_root_ref, weight_ref,
    grad_out, left_out, right_out, weight_out,
):
    factor = stats_ref[0:1, 0:1]
    for b in range(grad_ref.shape[0]):
        grad = grad_ref[b] * factor
        grad_out[b] = grad
        left_out[b], right_out[b], weight_out[b] = shampoo_parts(
            grad, left_ref[b], right_ref[b], left_root_ref[b], right_root_ref[b], weight_ref[b]
        )


def update_blocks(stats, grads, left, right, left_root, right_root, weight):
    count, edge, _ = grads.shape
    per_step = PACK if count % PACK == 0 else 1
    spec = pl.BlockSpec((per_step, edge, edge), lambda i: (i, 0, 0))
    out = jax.ShapeDtypeStruct(grads.shape, F32)
    return pl.pallas_call(
        block_update_kernel,
        out_shape=(out,) * 4,
        grid=(count // per_step,),
        in_specs=[whole(stats.shape)] + [spec] * 6,
        out_specs=(spec,) * 4,
        compiler_params=params(),
        name="update_blocks",
    )(stats, grads, left, right, left_root, right_root, weight)


def table_update_kernel(
    step_ref, stats_ref, grad_ref, left_ref, right_ref, left_root_ref, right_root_ref, weight_ref,
    norm_grad_ref, moment_ref, second_ref, norm_ref,
    grad_out, left_out, right_out, weight_out, norm_grad_out, moment_out, second_out, norm_out,
):
    factor = stats_ref[0:1, 0:1]
    grad = grad_ref[...] * factor
    grad_out[...] = grad
    left_out[...], right_out[...], weight_out[...] = shampoo_parts(
        grad, left_ref[...], right_ref[...], left_root_ref[...], right_root_ref[...], weight_ref[...]
    )
    rows = norm_ref.shape[0]
    clipped = norm_grad_ref[0:rows, :] * factor
    norm_grad_out[...] = clipped
    moment = FIRST_BETA * moment_ref[...] + (1.0 - FIRST_BETA) * clipped
    second = SECOND_BETA * second_ref[...] + (1.0 - SECOND_BETA) * clipped * clipped
    moment_out[...] = moment
    second_out[...] = second
    one = moment / step_ref[0:1, 0:1]
    two = second / step_ref[0:1, 1:2]
    weight = norm_ref[...]
    norm_out[...] = weight - VECTOR_RATE * (one / (jnp.sqrt(two) + ADAM_EPSILON) + WEIGHT_DECAY * weight)


def update_table(corrections, stats, grad, left, right, left_root, right_root, weight, norm_grad, moment, second, norms):
    like = lambda array: jax.ShapeDtypeStruct(array.shape, F32)
    return pl.pallas_call(
        table_update_kernel,
        out_shape=(like(grad), like(left), like(right), like(weight)) + (like(norms),) * 4,
        compiler_params=params(),
        name="update_table",
    )(corrections, stats, grad, left, right, left_root, right_root, weight, norm_grad, moment, second, norms)


def rotary_tables(length):
    lane = jnp.arange(LANES, dtype=jnp.int32)[None, :]
    half = HS // 2
    freqs = jnp.exp(-math.log(ROTARY_BASE) * (2.0 * (lane % half).astype(F32) / HS))
    angles = jnp.arange(length, dtype=F32)[:, None] * freqs
    sine = jnp.sin(angles)
    return jnp.cos(angles), jnp.where(lane % HS < half, -sine, sine)


def pack_blocks(blocks):
    count, edge, _ = blocks.shape
    groups = blocks.reshape(count // PACK, PACK, edge, edge).transpose(0, 2, 1, 3)
    return groups.reshape(count // PACK, edge, PACK * edge)


def gather_weights(own, mask, owner_map, known, sizes):
    everyone = ("dp", "tensor")
    slots, edge, _ = own.shape
    shards = sizes[1]
    owner, slot = owner_map[None, :] // slots, owner_map[None, :] % slots
    shard = jnp.arange(shards, dtype=jnp.int32)[:, None]
    if known:
        bits = bits_of(owner, shard)
        group = slot // PACK
        entry = gather_entry(0, bits)
        for g in range(1, PACK_GROUPS):
            entry = jnp.where(group == g, gather_entry(g, bits), entry)
        place = ((group * 32 + entry) * PACK + slot % PACK).reshape(-1)
        return gather_everywhere(place, own, mask, 32, sizes)
    packed = pack_blocks(lax.all_gather(own.astype(BF16), everyone, axis=0, tiled=True))
    count = jnp.maximum(lax.psum(jnp.sum(mask.astype(F32)), everyone), 1.0)
    place = ((owner * shards + shard) * slots + slot).reshape(-1)
    return assemble(place, packed, sizes) + (jnp.broadcast_to(count, (8, LANES)),)


def body(
    codons,
    segments,
    targets,
    loss_mask,
    owner_map,
    step_count,
    block_weight,
    block_left,
    block_right,
    block_left_root,
    block_right_root,
    embedding_weight,
    table_left,
    table_right,
    table_left_root,
    table_right_root,
    norm_params,
    norm_moment,
    norm_second,
):
    everyone = ("dp", "tensor")
    vocab, width = embedding_weight.shape
    shards = lax.axis_size("tensor")
    owners = lax.axis_size("dp")
    slots = block_weight.shape[1]
    edge = block_weight.shape[-1]
    blocks = owner_map.shape[0]
    length = codons.shape[1]
    shard_width = width // shards

    known = on_known_slice(owners, shards, slots)
    sizes = (width, shards, shard_width, FF)
    project, outward, expand, contract, count = gather_weights(
        block_weight[0], loss_mask, owner_map, known, sizes
    )
    segment = lax.dynamic_index_in_dim(segments, lax.axis_index("tensor"), 0, keepdims=False)
    tiles = length // TILE
    columns = jnp.stack([codons[0], targets[0], loss_mask[0], segment], 1)
    seg_row = segment.reshape(tiles, 1, TILE)
    tiled = segment.reshape(length // ROWS, ROWS)
    before = jnp.sum((segment[None, :] < tiled[:, :1]).astype(jnp.int32), -1)
    until = jnp.sum((segment[None, :] <= tiled[:, -1:]).astype(jnp.int32), -1)
    low, high = before // TILE, (until + TILE - 1) // TILE
    cosine, sine = rotary_tables(length)

    x0, h1, query, keys, values = front(columns, embedding_weight, norm_params, project, cosine, sine)
    attended, lse = attend(low, high, query, keys, values, columns, seg_row)
    (h2, active, d_two, ghid, d_one, gatt, gx, head_grad, norm_grad) = middle_rows(
        x0, attended, columns, count, norm_params, embedding_weight,
        outward, expand, contract,
    )
    gproj = attend_back(
        low, high, query, keys, values, gatt, lse, columns, seg_row, cosine, sine
    )
    table_grad, norm_grad = tail_rows(
        columns, x0, gx, gproj, norm_params, project, head_grad, norm_grad
    )

    owner, slot = owner_map[None, :] // slots, owner_map[None, :] % slots
    device = owner * shards + jnp.arange(shards, dtype=jnp.int32)[:, None]
    if known:
        home = (slot // PACK * (owners * shards) + device) * PACK + slot % PACK
    else:
        home = device * slots + slot
    grads = weight_grads(
        home.reshape(-1), h1, attended, h2, active, gproj, d_one, ghid, d_two, sizes, shards * blocks, edge
    )
    if known:
        owned, table_grad, norm_grad, stats = sum_everywhere(
            grads.reshape(slots // PACK, owners * shards, PACK, edge, LANES), table_grad, norm_grad, count
        )
    else:
        owned = lax.psum_scatter(grads[:, :, :edge], everyone, scatter_dimension=0, tiled=True)
        table_grad, norm_grad, square_sum = lax.psum((table_grad, norm_grad), everyone) + (
            lax.psum(jnp.sum(owned * owned), everyone),
        )
        vectors = norm_grad[:6]
        square_sum = square_sum + jnp.sum(table_grad * table_grad) + jnp.sum(vectors * vectors)
        stats = statistics(square_sum, jnp.sum(norm_grad[6]), count[:1, :1])
    loss_value, grad_norm = stats[2, 0], stats[1, 0]
    step_value = step_count.astype(F32)
    corrections = jnp.stack([1.0 - FIRST_BETA**step_value, 1.0 - SECOND_BETA**step_value]).reshape(1, 2)
    block_grad, new_left, new_right, new_weight = update_blocks(
        stats, owned, block_left[0], block_right[0], block_left_root[0], block_right_root[0], block_weight[0]
    )
    (
        table_clipped, table_left_new, table_right_new, table_weight_new,
        norm_clipped, moment_new, second_new, params_new,
    ) = update_table(
        corrections, stats, table_grad, table_left, table_right, table_left_root, table_right_root,
        embedding_weight, norm_grad, norm_moment, norm_second, norm_params,
    )
    return (
        loss_value,
        grad_norm,
        block_grad[None],
        new_left[None],
        new_right[None],
        new_weight[None],
        table_clipped,
        table_left_new,
        table_right_new,
        table_weight_new,
        norm_clipped,
        moment_new,
        second_new,
        params_new,
    )


def solution(mesh):
    in_specs = (
        P(("dp", "tensor"), None),
        P("dp", None),
        P(("dp", "tensor"), None),
        P(("dp", "tensor"), None),
        P(),
        P(),
        P("tensor", "dp", None, None),
        P("tensor", "dp", None, None),
        P("tensor", "dp", None, None),
        P("tensor", "dp", None, None),
        P("tensor", "dp", None, None),
        P(),
        P(),
        P(),
        P(),
        P(),
        P(),
        P(),
        P(),
    )
    out_specs = (
        P(),
        P(),
        P("tensor", "dp", None, None),
        P("tensor", "dp", None, None),
        P("tensor", "dp", None, None),
        P("tensor", "dp", None, None),
        P(),
        P(),
        P(),
        P(),
        P(),
        P(),
        P(),
        P(),
    )
    return jax.shard_map(body, mesh=mesh, in_specs=in_specs, out_specs=out_specs, check_vma=False)
```

```python
import functools
import math

import jax
import jax.numpy as jnp
from jax import lax
from jax.experimental import pallas as pl
from jax.experimental.pallas import tpu as pltpu
from jax.sharding import PartitionSpec as P

FF = 3072
HS = 64

CLIP_LEVEL = 0.005
STAT_DECAY = 0.5
MATRIX_RATE = 0.03
WEIGHT_DECAY = 0.01
VECTOR_RATE = 0.2
FIRST_BETA = 0.9
SECOND_BETA = 0.999
ADAM_EPSILON = 1e-08
NORM_EPSILON = 1e-05
ROOT_EPSILON = 1e-06
MASK_VALUE = -1e30
ROTARY_BASE = 10000.0

LANES = 128
PACK = 4
VMEM_LIMIT = 60 * 1024 * 1024
BF16 = jnp.bfloat16
F32 = jnp.float32


def dot(left, right):
    return lax.dot_general(left, right, (((1,), (0,)), ((), ())), preferred_element_type=F32)


def dot_nt(left, right):
    return lax.dot_general(left, right, (((1,), (1,)), ((), ())), preferred_element_type=F32)


def dot_tn(left, right):
    return lax.dot_general(left, right, (((0,), (0,)), ((), ())), preferred_element_type=F32)


def split_three(values):
    high = values.astype(BF16)
    rest = values - high.astype(F32)
    middle = rest.astype(BF16)
    low = (rest - middle.astype(F32)).astype(BF16)
    return high, middle, low


def params(**more):
    return pltpu.CompilerParams(vmem_limit_bytes=VMEM_LIMIT, **more)


def whole(shape):
    return pl.BlockSpec(shape, lambda *_: (0,) * len(shape))


def dense_rows(edge):
    return edge * edge // LANES


def to_dense(block):
    half, quarter = block.shape[0] // 2, block.shape[0] // 4
    wide, slim = LANES // 2, LANES // 4
    return (
        jnp.concatenate([block[:half, :wide], block[half:, :wide]], axis=1),
        jnp.concatenate(
            [block[i * quarter : (i + 1) * quarter, wide : wide + slim] for i in range(4)], axis=1
        ),
    )


def from_dense(dense):
    half = dense.shape[0] * 2 // 3
    quarter = half // 2
    wide, slim = LANES // 2, LANES // 4
    quarters = []
    for i in range(4):
        start = i % 2 * quarter
        lanes = slice(i // 2 * wide, (i // 2 + 1) * wide)
        quarters.append(
            jnp.concatenate(
                [dense[start : start + quarter, lanes], dense[half:, i * slim : (i + 1) * slim]], axis=1
            )
        )
    return quarters


def unpack_group(group, edge):
    return [group[:, edge * j : edge * (j + 1)] for j in range(PACK)]


def block_index(shard, block, blocks):
    return shard * blocks + block


def matrix_rows(row, width, shards, shard_width, hidden_width, edge):
    model = width // edge
    wide = shard_width // edge
    tall = hidden_width // shards // edge
    starts = [0, 3 * wide * model, 4 * wide * model, 4 * wide * model + model * tall]
    blocks = starts[3] + tall * model
    project = [
        block_index(c % (shards * wide) // wide, row * 3 * wide + c // (shards * wide) * wide + c % wide, blocks)
        for c in range(3 * model)
    ]
    outward = [
        block_index(row // wide, starts[1] + row % wide * model + c, blocks) for c in range(model)
    ]
    expand = [
        block_index(c // tall, starts[2] + row * tall + c % tall, blocks) for c in range(shards * tall)
    ]
    steps = model
    each = shards * tall // steps
    contract = []
    for q in range(each):
        r = row * each + q
        contract.append(
            [block_index(r // tall, starts[3] + r % tall * model + c, blocks) for c in range(model)]
        )
    return [project], [outward], [expand], contract


def assemble_rows(tables, place_ref, store, targets, edge):
    strip = PACK * edge
    for block_rows, target in zip(tables, targets):
        for r, places in enumerate(block_rows):
            for c in range(len(places) // PACK):
                blocks = [store[place_ref[places[c * PACK + j]]][:, :edge] for j in range(PACK)]
                target[r * edge : (r + 1) * edge, c * strip : (c + 1) * strip] = jnp.concatenate(
                    blocks, axis=1
                )


def unpack_rows(store, first, group, offset, edge):
    pieces = unpack_group(group, edge)
    for j in range(PACK):
        store[first + j, offset : offset + group.shape[0], :edge] = pieces[j]


def assemble_kernel(
    place_ref, in_ref, project_ref, outward_ref, expand_ref, contract_ref, store, *, load_steps, sizes
):
    step = pl.program_id(0)
    per_step, edge, _ = in_ref.shape

    @pl.when(step < load_steps)
    def _():
        def unpack(g, carry):
            unpack_rows(store, (step * per_step + g) * PACK, in_ref[g], 0, edge)
            return carry

        lax.fori_loop(0, per_step, unpack, 0)

    @pl.when(step >= load_steps)
    def _():
        tables = matrix_rows(step - load_steps, *sizes, edge)
        assemble_rows(tables, place_ref, store, (project_ref, outward_ref, expand_ref, contract_ref), edge)


def matrix_shapes(width, hidden_width):
    return (
        jax.ShapeDtypeStruct((width, 3 * width), BF16),
        jax.ShapeDtypeStruct((width, width), BF16),
        jax.ShapeDtypeStruct((width, hidden_width), BF16),
        jax.ShapeDtypeStruct((hidden_width, width), BF16),
    )


def assemble(place, packed, sizes):
    groups, edge, strip = packed.shape
    width, _, _, hidden_width = sizes
    per_step = 16
    load_steps = groups // per_step
    fill_steps = width // edge
    tall = hidden_width // fill_steps

    def late(step, *_):
        return (jnp.maximum(step - load_steps, 0), 0)

    return pl.pallas_call(
        functools.partial(assemble_kernel, load_steps=load_steps, sizes=sizes),
        out_shape=matrix_shapes(width, hidden_width),
        grid_spec=pltpu.PrefetchScalarGridSpec(
            num_scalar_prefetch=1,
            grid=(load_steps + fill_steps,),
            in_specs=[
                pl.BlockSpec(
                    (per_step, edge, strip), lambda s, *_: (jnp.minimum(s, load_steps - 1), 0, 0)
                )
            ],
            out_specs=[
                pl.BlockSpec((edge, 3 * width), late),
                pl.BlockSpec((edge, width), late),
                pl.BlockSpec((edge, hidden_width), late),
                pl.BlockSpec((tall, width), late),
            ],
            scratch_shapes=[pltpu.VMEM((groups * PACK, edge, LANES), BF16)],
        ),
        compiler_params=params(),
        name="assemble_weights",
    )(place, packed)


def norm_parts(values):
    scale = 1.0 / values.shape[-1]
    center = values - jnp.sum(values, -1, keepdims=True) * scale
    spread = jnp.sum(center * center, -1, keepdims=True) * scale
    inverse = lax.rsqrt(spread + NORM_EPSILON)
    return center * inverse, inverse


def norm_back(grad, unit, inverse, gain):
    scale = 1.0 / grad.shape[-1]
    inner = grad * gain
    mean_one = jnp.sum(inner, -1, keepdims=True) * scale
    mean_two = jnp.sum(inner * unit, -1, keepdims=True) * scale
    return (inner - mean_one - unit * mean_two) * inverse


def turn(values, cosine, sine):
    lane = lax.broadcasted_iota(jnp.int32, values.shape, 1)
    half = HS // 2
    ahead = pltpu.roll(values, LANES - half, 1)
    behind = pltpu.roll(values, half, 1)
    other = jnp.where(lane % HS < half, ahead, behind)
    return values * cosine + other * sine


def front_kernel(
    column_ref, table_ref, norm_ref, project_ref, cos_ref, sin_ref, x_ref, h_ref, q_ref, k_ref, v_ref
):
    rows = column_ref.shape[0]
    vocab, width = table_ref.shape
    index = lax.broadcasted_iota(jnp.int32, (rows, vocab), 1)
    hot = jnp.where(column_ref[:, 0:1] == index, 1.0, 0.0).astype(BF16)
    high, middle, low = split_three(table_ref[...])
    embedded = (dot(hot, high) + dot(hot, middle)) + dot(hot, low)
    embedded = embedded * math.sqrt(width)
    x_ref[...] = embedded
    unit, _ = norm_parts(embedded)
    normed = (unit * norm_ref[0:1, :] + norm_ref[1:2, :]).astype(BF16)
    h_ref[...] = normed
    cosine = cos_ref[...]
    sine = sin_ref[...]
    for part, out_ref in ((0, q_ref), (1, k_ref), (2, v_ref)):
        values = dot(normed, project_ref[:, part * width : (part + 1) * width])
        for c in range(width // LANES):
            piece = values[:, c * LANES : (c + 1) * LANES]
            if part < 2:
                piece = turn(piece, cosine, sine)
            if part == 0:
                piece = piece * HS ** (-0.5)
            out_ref[:, c * LANES : (c + 1) * LANES] = piece.astype(BF16)


def front(columns, table, norm_params, project, cosine, sine):
    length, kinds = columns.shape
    vocab, width = table.shape
    rows = 256
    spec = pl.BlockSpec((rows, width), lambda i: (i, 0))
    low = jax.ShapeDtypeStruct((length, width), BF16)
    return pl.pallas_call(
        front_kernel,
        out_shape=(jax.ShapeDtypeStruct((length, width), F32), low, low, low, low),
        grid=(length // rows,),
        in_specs=[
            pl.BlockSpec((rows, kinds), lambda i: (i, 0)),
            whole(table.shape),
            whole(norm_params.shape),
            whole(project.shape),
            pl.BlockSpec((rows, LANES), lambda i: (i, 0)),
            pl.BlockSpec((rows, LANES), lambda i: (i, 0)),
        ],
        out_specs=(spec, spec, spec, spec, spec),
        compiler_params=params(),
        name="embed_project",
    )(columns, table, norm_params, project, cosine, sine)


ROWS = 256
TILE = 128


def head_masks(rows):
    lane = lax.broadcasted_iota(jnp.int32, (rows, LANES), 1)
    return [lane // HS == h for h in range(LANES // HS)]


def same_segment(seg_col, seg_row_ref, first, count):
    row = jnp.concatenate([seg_row_ref[first + i] for i in range(count)], axis=1)
    return seg_col == row


def attend_kernel(low_ref, half_ref, q_ref, k_ref, v_ref, column_ref, seg_row_ref, o_ref, lse_ref):
    part = pl.program_id(1)
    first, half = low_ref[part], half_ref[part]
    masks = head_masks(ROWS)

    def run(count):
        query = q_ref[...]
        zero = jnp.zeros_like(query)
        span = pl.ds(pl.multiple_of(first * TILE, TILE), count * TILE)
        keys = k_ref[span, :]
        values = v_ref[span, :]
        same = same_segment(column_ref[:, 3:4], seg_row_ref, first, count)
        outs, logs = [], []
        for mask in masks:
            scores = jnp.where(same, dot_nt(jnp.where(mask, query, zero), keys), MASK_VALUE)
            top = jnp.max(scores, -1, keepdims=True)
            exps = jnp.exp(scores - top)
            total = jnp.sum(exps, -1, keepdims=True)
            probs = (exps * (1.0 / total)).astype(BF16)
            outs.append(dot(probs, values))
            logs.append(top + jnp.log(total))
        o_ref[...] = jnp.where(masks[0], outs[0], outs[1]).astype(BF16)
        lse_ref[...] = jnp.where(masks[0], logs[0], logs[1])

    for n in range(1, k_ref.shape[0] // TILE // 2 + 1):
        pl.when(half == n)(functools.partial(run, 2 * n))


def attend(low, half, query, keys, values, columns, seg_row):
    length, width = query.shape
    tiles = length // TILE
    pairs = width // LANES
    column = pl.BlockSpec((ROWS, LANES), lambda p, i, *_: (i, p))
    full = pl.BlockSpec((length, LANES), lambda p, i, *_: (0, p))
    return pl.pallas_call(
        attend_kernel,
        out_shape=(
            jax.ShapeDtypeStruct((length, width), BF16),
            jax.ShapeDtypeStruct((length, width), F32),
        ),
        grid_spec=pltpu.PrefetchScalarGridSpec(
            num_scalar_prefetch=2,
            grid=(pairs, length // ROWS),
            in_specs=[
                column,
                full,
                full,
                pl.BlockSpec((ROWS, columns.shape[1]), lambda p, i, *_: (i, 0)),
                whole((tiles, 1, TILE)),
            ],
            out_specs=(column, column),
        ),
        compiler_params=params(),
        name="attend_forward",
    )(low, half, query, keys, values, columns, seg_row)


def attend_back_kernel(
    low_ref, half_ref, q_ref, k_ref, v_ref, g_ref, lse_ref, column_ref, seg_row_ref, cos_ref, sin_ref,
    out_ref, dk_acc, dv_acc,
):
    part = pl.program_id(1)
    parts = pl.num_programs(1)
    heads = LANES // HS
    first, half = low_ref[part], half_ref[part]
    masks = head_masks(ROWS)

    @pl.when(part == 0)
    def _():
        dk_acc[...] = jnp.zeros_like(dk_acc)
        dv_acc[...] = jnp.zeros_like(dv_acc)

    def run(count):
        query = q_ref[...]
        grad = g_ref[...]
        zero = jnp.zeros_like(query)
        span = pl.ds(pl.multiple_of(first * TILE, TILE), count * TILE)
        keys = k_ref[span, :]
        values = v_ref[span, :]
        same = same_segment(column_ref[:, 3:4], seg_row_ref, first, count)
        dq = []
        dk = dv = None
        for h, mask in enumerate(masks):
            own_query = jnp.where(mask, query, zero)
            own_grad = jnp.where(mask, grad, zero)
            scores = jnp.where(same, dot_nt(own_query, keys), MASK_VALUE)
            probs = jnp.exp(scores - lse_ref[:, h * HS : h * HS + 1])
            grad_probs = dot_nt(own_grad, values)
            delta = jnp.sum(probs * grad_probs, -1, keepdims=True)
            grad_scores = (probs * (grad_probs - delta)).astype(BF16)
            dq.append(dot(grad_scores, keys))
            more_dk = dot(own_query.T, grad_scores)
            more_dv = dot(own_grad.T, probs.astype(BF16))
            dk = more_dk if dk is None else dk + more_dk
            dv = more_dv if dv is None else dv + more_dv
        for i in range(count):
            lanes = slice(i * TILE, (i + 1) * TILE)
            dk_acc[first + i] += dk[:, lanes]
            dv_acc[first + i] += dv[:, lanes]
        rows = pl.ds(pl.multiple_of(part * ROWS, ROWS), ROWS)
        turned = turn(
            jnp.where(masks[0], dq[0], dq[1]) * HS ** (-0.5), cos_ref[rows, :], -sin_ref[rows, :]
        )
        out_ref[0, rows, :] = turned.astype(BF16)

    for n in range(1, k_ref.shape[0] // TILE // 2 + 1):
        pl.when(half == n)(functools.partial(run, 2 * n))

    @pl.when(part == parts - 1)
    def _():
        for j in range(dk_acc.shape[0]):
            rows = slice(j * TILE, (j + 1) * TILE)
            out_ref[1, rows, :] = turn(dk_acc[j].T, cos_ref[rows, :], -sin_ref[rows, :]).astype(BF16)
            out_ref[2, rows, :] = dv_acc[j].T.astype(BF16)


def attend_back(low, half, query, keys, values, grad, lse, columns, seg_row, cosine, sine):
    length, width = query.shape
    tiles = length // TILE
    pairs = width // LANES
    column = pl.BlockSpec((ROWS, LANES), lambda p, i, *_: (i, p))
    full = pl.BlockSpec((length, LANES), lambda p, i, *_: (0, p))
    return pl.pallas_call(
        attend_back_kernel,
        out_shape=jax.ShapeDtypeStruct((3, length, width), BF16),
        grid_spec=pltpu.PrefetchScalarGridSpec(
            num_scalar_prefetch=2,
            grid=(pairs, length // ROWS),
            in_specs=[
                column,
                full,
                full,
                column,
                column,
                pl.BlockSpec((ROWS, columns.shape[1]), lambda p, i, *_: (i, 0)),
                whole((tiles, 1, TILE)),
                whole((length, LANES)),
                whole((length, LANES)),
            ],
            out_specs=pl.BlockSpec((3, length, LANES), lambda p, i, *_: (0, 0, p)),
            scratch_shapes=[
                pltpu.VMEM((tiles, LANES, TILE), F32),
                pltpu.VMEM((tiles, LANES, TILE), F32),
            ],
        ),
        compiler_params=params(),
        name="attend_backward",
    )(low, half, query, keys, values, grad, lse, columns, seg_row, cosine, sine)


INV_SQRT_TWO = 2.0 ** (-0.5)
INV_SQRT_TWO_PI = (2.0 * math.pi) ** (-0.5)


def middle_kernel(
    x_ref, att_ref, column_ref, count_ref, norm_ref, table_ref,
    outward_ref, expand_ref, contract_ref,
    h_ref, active_ref, d_two_ref, ghid_ref, d_one_ref, gatt_ref, gx_ref, head_ref, norm_grad_ref,
    slope,
):
    step = pl.program_id(0)
    rows, width = x_ref.shape
    vocab = table_ref.shape[0]
    ff = expand_ref.shape[1]
    part = width

    @pl.when(step == 0)
    def _():
        head_ref[...] = jnp.zeros_like(head_ref)
        norm_grad_ref[...] = jnp.zeros_like(norm_grad_ref)

    middle = x_ref[...] + dot(att_ref[...], outward_ref[...])
    unit_two, inverse_two = norm_parts(middle)
    gain_two = norm_ref[2:3, :]
    normed_two = (unit_two * gain_two + norm_ref[3:4, :]).astype(BF16)
    h_ref[...] = normed_two

    def forward(c, total):
        cols = pl.ds(pl.multiple_of(c * part, part), part)
        hidden = dot(normed_two, expand_ref[:, cols])
        cumulative = 0.5 + 0.5 * lax.erf(hidden * INV_SQRT_TWO)
        active = (hidden * cumulative).astype(BF16)
        density = jnp.exp(-0.5 * hidden * hidden) * INV_SQRT_TWO_PI
        slope[:, cols] = cumulative + hidden * density
        active_ref[:, cols] = active
        return total + dot(active, contract_ref[cols, :])

    branch = lax.fori_loop(0, ff // part, forward, jnp.zeros((rows, width), F32))
    unit, inverse = norm_parts(middle + branch)
    gain = norm_ref[4:5, :]
    final = (unit * gain + norm_ref[5:6, :]).astype(BF16)
    table = table_ref[...].astype(BF16)
    logits = dot_nt(final, table)
    shifted = logits - jnp.max(logits, -1, keepdims=True)
    exps = jnp.exp(shifted)
    sums = jnp.sum(exps, -1, keepdims=True)
    hot = column_ref[:, 1:2] == lax.broadcasted_iota(jnp.int32, (rows, vocab), 1)
    mask = column_ref[:, 2:3].astype(F32)
    log_probs = shifted - jnp.log(sums)
    picked = jnp.sum(jnp.where(hot, log_probs, 0.0) * mask, 0, keepdims=True)
    norm_grad_ref[6:7, 0:vocab] -= picked
    glogits = ((jnp.exp(log_probs) - jnp.where(hot, 1.0, 0.0)) * (mask / count_ref[0:1, 0:1])).astype(BF16)
    head_ref[...] += dot_tn(glogits, final)
    gfinal = dot(glogits, table)
    norm_grad_ref[4:5, :] += jnp.sum(gfinal * unit, 0, keepdims=True)
    norm_grad_ref[5:6, :] += jnp.sum(gfinal, 0, keepdims=True)
    gx_two = norm_back(gfinal, unit, inverse, gain)
    d_two = gx_two.astype(BF16)
    d_two_ref[...] = d_two

    def backward(c, total):
        cols = pl.ds(pl.multiple_of(c * part, part), part)
        gactive = dot_nt(d_two, contract_ref[cols, :])
        ghid = (gactive * slope[:, cols]).astype(BF16)
        ghid_ref[:, cols] = ghid
        return total + dot_nt(ghid, expand_ref[:, cols])

    gh = lax.fori_loop(0, ff // part, backward, jnp.zeros((rows, width), F32))
    norm_grad_ref[2:3, :] += jnp.sum(gh * unit_two, 0, keepdims=True)
    norm_grad_ref[3:4, :] += jnp.sum(gh, 0, keepdims=True)
    gx_one = gx_two + norm_back(gh, unit_two, inverse_two, gain_two)
    gx_ref[...] = gx_one
    d_one = gx_one.astype(BF16)
    d_one_ref[...] = d_one
    gatt_ref[...] = dot_nt(d_one, outward_ref[...]).astype(BF16)


def middle_rows(x, att, columns, count, norm_params, table, outward, expand, contract):
    length, width = x.shape
    vocab = table.shape[0]
    ff = expand.shape[1]
    rows = 512
    narrow = pl.BlockSpec((rows, width), lambda i: (i, 0))
    broad = pl.BlockSpec((rows, ff), lambda i: (i, 0))
    column = pl.BlockSpec((rows, columns.shape[1]), lambda i: (i, 0))
    low = jax.ShapeDtypeStruct((length, width), BF16)
    low_broad = jax.ShapeDtypeStruct((length, ff), BF16)
    return pl.pallas_call(
        middle_kernel,
        out_shape=(
            low, low_broad, low, low_broad, low, low,
            jax.ShapeDtypeStruct((length, width), F32),
            jax.ShapeDtypeStruct((vocab, width), F32),
            jax.ShapeDtypeStruct((8, width), F32),
        ),
        grid=(length // rows,),
        in_specs=[
            narrow, narrow, column, whole(count.shape), whole(norm_params.shape), whole(table.shape),
            whole(outward.shape), whole(expand.shape), whole(contract.shape),
        ],
        out_specs=(
            narrow, broad, narrow, broad, narrow, narrow, narrow,
            whole((vocab, width)), whole((8, width)),
        ),
        scratch_shapes=[pltpu.VMEM((rows, ff), F32)],
        compiler_params=params(),
        name="middle_rows",
    )(x, att, columns, count, norm_params, table, outward, expand, contract)


def tail_part(codon_col, x, gx, gprojs, norm_params, project, table_acc, norm_acc):
    rows, width = x.shape
    vocab = table_acc.shape[0]
    gh = dot_nt(gprojs[0], project[:, 0:width])
    gh = gh + dot_nt(gprojs[1], project[:, width : 2 * width])
    gh = gh + dot_nt(gprojs[2], project[:, 2 * width : 3 * width])
    unit, inverse = norm_parts(x)
    norm_acc[0:1, :] += jnp.sum(gh * unit, 0, keepdims=True)
    norm_acc[1:2, :] += jnp.sum(gh, 0, keepdims=True)
    gx = gx + norm_back(gh, unit, inverse, norm_params[0:1, :])
    hot = jnp.where(codon_col == lax.broadcasted_iota(jnp.int32, (rows, vocab), 1), 1.0, 0.0)
    hot = hot.T.astype(BF16)
    high, middle, low = split_three(gx)
    total = dot(hot, high) + (dot(hot, middle) + dot(hot, low))
    table_acc[...] += total * math.sqrt(width)


def tail_kernel(
    column_ref, x_ref, gx_ref, gproj_ref, norm_ref, project_ref, head_ref, norm_in_ref,
    table_grad_ref, norm_grad_ref,
):
    @pl.when(pl.program_id(0) == 0)
    def _():
        table_grad_ref[...] = head_ref[...]
        norm_grad_ref[...] = norm_in_ref[...]

    tail_part(
        column_ref[:, 0:1], x_ref[...], gx_ref[...], gproj_ref, norm_ref, project_ref,
        table_grad_ref, norm_grad_ref,
    )


def tail_rows(columns, x, gx, gproj, norm_params, project, head, norm_in):
    length, width = x.shape
    rows = 256
    narrow = pl.BlockSpec((rows, width), lambda i: (i, 0))
    return pl.pallas_call(
        tail_kernel,
        out_shape=(
            jax.ShapeDtypeStruct(head.shape, F32),
            jax.ShapeDtypeStruct(norm_in.shape, F32),
        ),
        grid=(length // rows,),
        in_specs=[
            pl.BlockSpec((rows, columns.shape[1]), lambda i: (i, 0)),
            narrow, narrow, pl.BlockSpec((3, rows, width), lambda i: (0, i, 0)),
            whole(norm_params.shape), whole(project.shape), whole(head.shape), whole(norm_in.shape),
        ],
        out_specs=(whole(head.shape), whole(norm_in.shape)),
        compiler_params=params(),
        name="tail_rows",
    )(columns, x, gx, gproj, norm_params, project, head, norm_in)


def weight_grad_kernel(
    place_ref, h_one, att, h_two, active, gproj, d_one, ghid, d_two, out_ref,
    left, right, turned, buf, left_sem, right_sem, out_sem, *, sizes, edge,
):
    width, shards, shard_width, hidden_width = sizes
    model = width // edge
    wide = shard_width // edge
    tall = hidden_width // shards // edge
    starts = [0, 3 * wide * model, 4 * wide * model, 4 * wide * model + model * tall]
    blocks = starts[3] + tall * model
    part = hidden_width // shards
    columns = lambda ref, t: ref.at[:, pl.ds(t * part, part)]
    lefts = [h_one, att, h_two] + [columns(active, t) for t in range(shards)]
    rights = [gproj.at[i] for i in range(3)] + [d_one] + [columns(ghid, t) for t in range(shards)] + [d_two]
    plan = [(0, 0), (0, 1), (0, 2), (1, 3)]
    plan += [(2, 4 + t) for t in range(shards)]
    plan += [(3 + t, 4 + shards) for t in range(shards)]
    step = pl.program_id(0)
    slot = step % 2
    count = buf.shape[1]

    def fetches(n):
        found = []
        if n == 0 or plan[n][0] != plan[n - 1][0]:
            which = plan[n][0] % 2
            found.append(pltpu.make_async_copy(lefts[plan[n][0]], left.at[which], left_sem.at[which]))
        if n == 0 or plan[n][1] != plan[n - 1][1]:
            which = plan[n][1] % 2
            found.append(pltpu.make_async_copy(rights[plan[n][1]], right.at[which], right_sem.at[which]))
        return found

    def drain(which):
        pltpu.make_async_copy(buf.at[which], out_ref.at[pl.ds(0, count)], out_sem.at[which]).wait()

    for n in range(len(plan)):

        @pl.when(step == n)
        def _():
            if n == 0:
                for copy in fetches(0):
                    copy.start()
            for copy in fetches(n):
                copy.wait()
            if n + 1 < len(plan):
                for copy in fetches(n + 1):
                    copy.start()
            if n == 0 or plan[n][0] != plan[n - 1][0]:
                turned[...] = left[plan[n][0] % 2].T

    @pl.when(step >= 2)
    def _():
        drain(slot)

    which = jnp.minimum(step, 4 + shards) % 2
    rows = turned.shape[0] // 2
    for half in range(2):
        result = dot(turned[half * rows : (half + 1) * rows], right[which])
        for i in range(rows // edge):
            r = half * (rows // edge) + i
            for c in range(model):
                block = result[i * edge : (i + 1) * edge, c * edge : (c + 1) * edge]
                upper, lower = to_dense(block)
                buf[slot, r * model + c, : edge // 2] = upper
                buf[slot, r * model + c, edge // 2 :] = lower
            for c in range(model):
                index = block_index(c // wide, r * 3 * wide + step * wide + c % wide, blocks)
                index = jnp.where(
                    step == 3, block_index(r // wide, starts[1] + r % wide * model + c, blocks), index
                )
                index = jnp.where(
                    step >= 4, block_index(step - 4, starts[2] + r * tall + c, blocks), index
                )
                index = jnp.where(
                    step >= 4 + shards,
                    block_index(step - 4 - shards, starts[3] + r * model + c, blocks),
                    index,
                )
                k = r * model + c
                pltpu.make_async_copy(
                    buf.at[slot, k], out_ref.at[place_ref[index]], out_sem.at[slot]
                ).start()

    @pl.when(step == len(plan) - 1)
    def _():
        drain(1 - slot)
        drain(slot)


def weight_grads(place, h_one, att, h_two, active, gproj, d_one, ghid, d_two, sizes, blocks, edge):
    length, width = h_one.shape
    shards = sizes[1]
    count = (width // edge) ** 2
    anywhere = pl.BlockSpec(memory_space=pl.ANY)
    return pl.pallas_call(
        functools.partial(weight_grad_kernel, sizes=sizes, edge=edge),
        out_shape=jax.ShapeDtypeStruct((blocks, dense_rows(edge), LANES), F32),
        grid_spec=pltpu.PrefetchScalarGridSpec(
            num_scalar_prefetch=1,
            grid=(4 + 2 * shards,),
            in_specs=[anywhere] * 8,
            out_specs=anywhere,
            scratch_shapes=[
                pltpu.VMEM((2, length, width), BF16),
                pltpu.VMEM((2, length, width), BF16),
                pltpu.VMEM((width, length), BF16),
                pltpu.VMEM((2, count, dense_rows(edge), LANES), F32),
                pltpu.SemaphoreType.DMA((2,)),
                pltpu.SemaphoreType.DMA((2,)),
                pltpu.SemaphoreType.DMA((2,)),
            ],
        ),
        compiler_params=params(),
        name="weight_gradients",
    )(place, h_one, att, h_two, active, gproj, d_one, ghid, d_two)


CORE, NEAR_Y, NEAR_X, NEAR_Z, FAR_Z = range(5)
AXIS_STRIDE = {CORE: 1, NEAR_Y: 2, NEAR_X: 4, NEAR_Z: 8, FAR_Z: 16}
NATURAL = (FAR_Z, NEAR_Z, NEAR_X, NEAR_Y)
CHUNK_AXES = (
    (NEAR_X, NEAR_Y, NEAR_Z, FAR_Z),
    (NEAR_Y, NEAR_X, NEAR_Z, FAR_Z),
    (NEAR_X, NEAR_Y, NEAR_Z, FAR_Z),
    (NEAR_Y, NEAR_X, NEAR_Z, FAR_Z),
    (NEAR_Z, NEAR_X, NEAR_Y, FAR_Z),
    (NEAR_Z, NEAR_Y, NEAR_X, FAR_Z),
)
PACK_GROUPS = 6
SUM_CHUNKS = PACK_GROUPS * PACK
SUM_SLOTS = 6
SUM_ORDER = (
    0, 2000, 10, 20, 2010, 30, 40, 50, 2020, 1000, 2001, 2030, 60, 1010, 2011, 2040, 70, 1020, 2021, 2050, 80, 1030,
    2031, 2060, 90, 1040, 2041, 2070, 100, 1050, 2051, 2080, 110, 1060, 2090, 120, 1070, 2100, 130, 1080, 2061,
    2110, 140, 1090, 2071, 2120, 150, 1100, 1001, 2130, 160, 1110, 1011, 2140, 170, 2012, 1120, 2150, 180, 2002,
    1130, 2101, 2160, 190, 1140, 1021, 2170, 200, 2111, 1150, 1031, 1041, 2180, 210, 1160, 2190, 220, 2032, 1170,
    1051, 2200, 230, 2022, 1180, 2042, 2210, 1190, 2052, 1012, 2220, 1200, 1002, 1061, 2230, 1210, 1071, 2072, 1220,
    2062, 1230, 2081, 2003, 1032, 2091, 2013, 1022, 1101, 1042, 2023, 1052, 2053, 1111, 2033, 2043, 1003, 2004,
    2161, 1072, 2102, 1013, 2014, 1062, 2112, 1023, 2024, 2063, 1053, 2054, 1004, 1043, 2044, 2121, 1033, 2034,
    2131, 2141, 1014, 2151, 1081, 1024, 2073, 1091, 1102, 1054, 1112, 1063, 2064, 1044, 2171, 1034, 1073, 2074,
    1064, 2221, 2092, 2082, 2113, 2103, 1161, 1121, 1074, 1131, 1141, 2132, 1151, 2122, 2152, 1113, 2114, 2142,
    1103, 2104, 1092, 2093, 1082, 2162, 2191, 1171, 2181, 2083, 1114, 1132, 2172, 2133, 1104, 1122, 1152, 1093,
    2094, 2123, 1142, 1221, 2201, 2143, 1083, 2084, 1162, 2163, 1133, 2134, 2153, 1094, 2231, 1172, 2211, 1123,
    2124, 1084, 2173, 1143, 2144, 1163, 2164, 1134, 1191, 1181, 2182, 2192, 1153, 2154, 2222, 1124, 1173, 2174,
    1144, 1201, 2202, 1164, 1154, 1211, 2212, 1231, 2232, 1182, 2183, 1174, 1192, 2193, 1222, 2223, 1202, 2203,
    1212, 2213, 1183, 2184, 1193, 2194, 1223, 1232, 2233, 2224, 1203, 1213, 2204, 2214, 1184, 1233, 2234, 1194,
    1224, 1204, 1214, 1234,
)
SMALL_ROWS = 1024
SMALL_AXES = (CORE, NEAR_X, NEAR_Y, NEAR_Z, FAR_Z)
MESH = pl.DeviceIdType.MESH


def on_known_slice(owners, shards, slots):
    return owners == 8 and shards == 4 and slots % PACK == 0 and slots == PACK * PACK_GROUPS


def bits_of(owner, shard):
    return {
        CORE: shard % 2,
        NEAR_Y: shard // 2,
        NEAR_X: owner % 2,
        NEAR_Z: owner // 2 % 2,
        FAR_Z: owner // 4,
    }


def own_bits():
    owner, shard = lax.axis_index("dp"), lax.axis_index("tensor")
    return owner, shard, bits_of(owner, shard)


def partner_of(axis, owner, shard, bits):
    if axis == CORE:
        return (owner, shard + 1 - 2 * bits[CORE])
    if axis == NEAR_Y:
        return (owner, shard + 2 - 4 * bits[NEAR_Y])
    step = {NEAR_X: 1, NEAR_Z: 2, FAR_Z: 4}[axis]
    return (owner + step - 2 * step * bits[axis], shard)


def axis_partners(owner, shard, bits):
    return [partner_of(axis, owner, shard, bits) for axis in range(5)]


def group_partners(owner, shard):
    same_owner = [(owner, (shard + i) % 4) for i in range(1, 4)]
    same_shard = [((owner + i) % 8, shard) for i in range(1, 8)]
    return same_owner, same_shard


def greet(partners):
    for partner in partners:
        pl.semaphore_signal(
            pltpu.get_barrier_semaphore(), inc=1, device_id=partner, device_id_type=MESH
        )


def await_greetings(count):
    pl.semaphore_wait(pltpu.get_barrier_semaphore(), count)


def total_of(values):
    return jnp.sum(jnp.sum(values, 1, keepdims=True), 0, keepdims=True)


def statistics(square_sum, loss_sum, count):
    norm = jnp.sqrt(square_sum)
    factor = CLIP_LEVEL / jnp.maximum(norm, CLIP_LEVEL)
    row = lax.broadcasted_iota(jnp.int32, (8, LANES), 0)
    return jnp.where(row == 0, factor, jnp.where(row == 1, norm, loss_sum / count))


def sum_kernel(
    grads_ref, table_ref, norm_ref, count_ref,
    owned_ref, table_out, norm_out, stats_out,
    inbuf, r0, r1, r2, r3, r4, small, s0, s1, s2, s3, s4, spread, square, near_squares, far_squares,
    in_sem, send_sem, recv_sem, small_send, small_recv, square_send, square_recv,
):
    owner, shard, bits = own_bits()
    received = (r0, r1, r2, r3, r4)

    def axes_of(c):
        return CHUNK_AXES[c % len(CHUNK_AXES)]

    def half_of(ref, c, k, bit):
        left = [axis for axis in NATURAL if axis not in axes_of(c)[:k]]
        place = left.index(axes_of(c)[k])
        return ref.at[(c,) + (slice(None),) * place + (bit,)]

    def fetch(c):
        slot = c % SUM_SLOTS
        return pltpu.make_async_copy(
            grads_ref.at[c, :, :, :, :, bits[CORE]], inbuf.at[slot], in_sem.at[slot]
        )

    same_owner, same_shard = group_partners(owner, shard)
    greet(same_owner + same_shard)
    await_greetings(len(same_owner) + len(same_shard))

    def chunk_send(c, k):
        if k == 0:
            axis, source = CORE, grads_ref.at[c, :, :, :, :, 1 - bits[CORE]]
        else:
            axis = axes_of(c)[k - 1]
            source = half_of(received[k - 1], c, k - 1, 1 - bits[axis])
        return pltpu.make_async_remote_copy(
            src_ref=source,
            dst_ref=received[k].at[c],
            send_sem=send_sem.at[c, k],
            recv_sem=recv_sem.at[c, k],
            device_id=partner_of(axis, owner, shard, bits),
            device_id_type=MESH,
        )

    def merge(c, k):
        chunk_send(c, k).wait_recv()
        if k == 0:
            fetch(c).wait()
            r0[c] = r0[c] + inbuf[c % SUM_SLOTS]
            return
        own = half_of(received[k - 1], c, k - 1, bits[axes_of(c)[k - 1]])[...]
        if k < 4:
            received[k][c] = received[k][c] + own
            return
        dense = r4[c] + own
        quarter = owned_ref.shape[1] // 4
        for i, rows in enumerate(from_dense(dense)):
            owned_ref[c, i * quarter : (i + 1) * quarter, :] = rows
        parts = dense * dense
        total = square[...]
        for r in range(dense.shape[0] // 8):
            total = total + parts[r * 8 : (r + 1) * 8]
        square[...] = total

    vocab, width = table_ref.shape
    vectors = norm_ref.shape[0]
    columns = width // LANES
    small_parts = (s0, s1, s2, s3, s4)

    def small_fill():
        for c in range(columns):
            lanes = slice(c * LANES, (c + 1) * LANES)
            small[c * vocab : (c + 1) * vocab] = table_ref[:, lanes]
            start = columns * vocab + c * vectors
            small[start : start + vectors] = norm_ref[:, lanes]
        used = columns * (vocab + vectors)
        small[used:] = jnp.zeros((SMALL_ROWS - used, LANES), F32)

    def small_base(k):
        base = 0
        for i in range(k):
            base = base + (SMALL_ROWS >> (i + 1)) * bits[SMALL_AXES[i]]
        return base

    def small_copy(k):
        rows = SMALL_ROWS >> (k + 1)
        start = pl.multiple_of(small_base(k) + rows * (1 - bits[SMALL_AXES[k]]), 8)
        return pltpu.make_async_remote_copy(
            src_ref=small.at[pl.ds(start, rows)],
            dst_ref=small_parts[k],
            send_sem=small_send.at[k],
            recv_sem=small_recv.at[k],
            device_id=partner_of(SMALL_AXES[k], owner, shard, bits),
            device_id_type=MESH,
        )

    def small_merge(k):
        small_copy(k).wait_recv()
        rows = SMALL_ROWS >> (k + 1)
        mine = pl.ds(pl.multiple_of(small_base(k + 1), 8), rows)
        if k < 4:
            small[mine, :] = small[mine, :] + small_parts[k][...]
            small_copy(k + 1).start()
        else:
            spread[mine, :] = small[mine, :] + small_parts[k][...]
            spread_copy(4).start()

    def spread_copy(k):
        rows = SMALL_ROWS >> (k + 1)
        here = pl.ds(pl.multiple_of(small_base(k + 1), 8), rows)
        return pltpu.make_async_remote_copy(
            src_ref=spread.at[here],
            dst_ref=spread.at[here],
            send_sem=small_send.at[5 + k],
            recv_sem=small_recv.at[5 + k],
            device_id=partner_of(SMALL_AXES[k], owner, shard, bits),
            device_id_type=MESH,
        )

    def spread_next(k):
        spread_copy(k).wait_recv()
        if k > 0:
            spread_copy(k - 1).start()
        else:
            for c in range(columns):
                lanes = slice(c * LANES, (c + 1) * LANES)
                table_out[:, lanes] = spread[c * vocab : (c + 1) * vocab]
                start = columns * vocab + c * vectors
                norm_out[:, lanes] = spread[start : start + vectors]

    square[...] = jnp.zeros_like(square)
    small_fill()
    small_copy(0).start()
    extra = []
    extra += [functools.partial(small_merge, k) for k in range(5)]
    extra += [functools.partial(spread_next, k) for k in range(4, -1, -1)]
    for position, code in enumerate(SUM_ORDER):
        c, k = code % 1000 // 10, code % 10
        if code < 1000:
            fetch(c).start()
        elif code < 2000:
            merge(c, k)
        else:
            chunk_send(c, k).start()
        if position >= 70 and position % 16 == 0 and extra:
            extra.pop(0)()
    while extra:
        extra.pop(0)()

    def exchange(partners, mine, slots, first):
        slots[mine] = square[...]
        copies = [
            pltpu.make_async_remote_copy(
                src_ref=square,
                dst_ref=slots.at[mine],
                send_sem=square_send.at[first + i],
                recv_sem=square_recv.at[first + i],
                device_id=partner,
                device_id_type=MESH,
            )
            for i, partner in enumerate(partners)
        ]
        for copy in copies:
            copy.start()
        for copy in copies:
            copy.wait()
        value = slots[0]
        for i in range(1, slots.shape[0]):
            value = value + slots[i]
        return value

    square[...] = exchange(same_owner, shard, near_squares, 0)
    value = exchange(same_shard, owner, far_squares, 3)
    table_sum, vectors_sum = table_out[...], norm_out[0:6, :]
    stats_out[...] = statistics(
        total_of(value) + total_of(table_sum * table_sum) + total_of(vectors_sum * vectors_sum),
        total_of(norm_out[6:7, :]),
        count_ref[0:1, 0:1],
    )

    for c in range(SUM_CHUNKS):
        for k in range(5):
            chunk_send(c, k).wait_send()
    for k in range(5):
        small_copy(k).wait_send()
        spread_copy(k).wait_send()


def sum_everywhere(grads, table_grad, norm_grad, count):
    chunks = grads.shape[0]
    block = grads.shape[-2:]
    edge = math.isqrt(block[0] * block[1])
    group = lambda count: pltpu.VMEM((chunks,) + (2,) * count + block, F32)
    small = lambda rows: pltpu.VMEM((rows, LANES), F32)
    anywhere, inside = pl.BlockSpec(memory_space=pl.ANY), pl.BlockSpec(memory_space=pltpu.VMEM)
    return pl.pallas_call(
        sum_kernel,
        out_shape=(
            jax.ShapeDtypeStruct((chunks, edge, edge), F32),
            jax.ShapeDtypeStruct(table_grad.shape, F32),
            jax.ShapeDtypeStruct(norm_grad.shape, F32),
            jax.ShapeDtypeStruct((8, LANES), F32),
        ),
        in_specs=[anywhere, inside, inside, inside],
        out_specs=(inside,) * 4,
        scratch_shapes=[
            pltpu.VMEM((SUM_SLOTS,) + (2,) * 4 + block, F32),
            group(4), group(3), group(2), group(1), group(0),
            small(SMALL_ROWS), small(512), small(256), small(128), small(64), small(32), small(SMALL_ROWS),
            pltpu.VMEM((8, LANES), F32),
            pltpu.VMEM((4, 8, LANES), F32),
            pltpu.VMEM((8, 8, LANES), F32),
            pltpu.SemaphoreType.DMA((SUM_SLOTS,)),
            pltpu.SemaphoreType.DMA((SUM_CHUNKS, 5)),
            pltpu.SemaphoreType.DMA((SUM_CHUNKS, 5)),
            pltpu.SemaphoreType.DMA((10,)),
            pltpu.SemaphoreType.DMA((10,)),
            pltpu.SemaphoreType.DMA((10,)),
            pltpu.SemaphoreType.DMA((10,)),
        ],
        compiler_params=pltpu.CompilerParams(
            vmem_limit_bytes=66_000_000, collective_id=1, has_side_effects=True
        ),
        name="sum_gradients",
    )(grads, table_grad, norm_grad, count)


GATHER_AXES = (
    (NEAR_Z, NEAR_Y, NEAR_X, FAR_Z),
    (NEAR_X, NEAR_Y, NEAR_Z, FAR_Z),
    (NEAR_Y, NEAR_X, FAR_Z, NEAR_Z),
    (NEAR_Z, NEAR_Y, FAR_Z, NEAR_X),
    (NEAR_X, NEAR_Z, FAR_Z, NEAR_Y),
    (NEAR_Y, NEAR_X, FAR_Z, NEAR_Z),
)
HALVES = 2
GATHER_CHUNKS = PACK_GROUPS * HALVES
GATHER_ORDER = (
    2030, 2090, 2100, 2040, 2080, 2060, 2020, 2070, 2110, 2010, 1080, 1030, 1100, 1090, 1040, 1060, 2061, 2050,
    2081, 1020, 1070, 2071, 1110, 1010, 2021, 1061, 2062, 1050, 2011, 1081, 2082, 2031, 1071, 2072, 1062, 2063,
    1021, 2022, 2101, 1011, 2012, 1082, 2083, 1072, 2073, 1031, 2032, 2111, 1022, 1101, 2000, 2023, 2091, 1012,
    2013, 1111, 2112, 1000, 2001, 2041, 1073, 2074, 2102, 1063, 2064, 1091, 2092, 1074, 2051, 1032, 1064, 1041,
    1001, 2033, 1112, 2113, 1102, 2103, 1051, 2052, 1083, 2084, 1013, 2014, 2002, 1084, 2042, 1092, 1014, 1033,
    2034, 1023, 2024, 2093, 1052, 2053, 1034, 1042, 2043, 1024, 1103, 2104, 1002, 2003, 1104, 1093, 2094, 1113,
    2114, 1043, 2044, 1094, 1114, 1053, 2054, 1044, 1003, 2004, 1054, 1004,
)


def gather_entry(group, bits):
    first, second, third, fourth = GATHER_AXES[group]
    return 16 * bits[CORE] + 8 * bits[first] + 4 * bits[second] + 2 * bits[third] + bits[fourth]


def gather_kernel(
    place_ref, own_ref, mask_ref, project_out, outward_out, expand_out, contract_out, count_ref,
    packed, held, store, project, outward, expand, contract, counts,
    own_sem, send_sem, recv_sem, count_send, count_recv, out_sem, *, sizes,
):
    owner, shard, bits = own_bits()
    edge = own_ref.shape[1]
    rows = edge // HALVES
    devices = held.shape[1]

    def place(c):
        return gather_entry(c % PACK_GROUPS, bits)

    def own_part(c):
        return packed.at[c % PACK_GROUPS, pl.ds(c // PACK_GROUPS * rows, rows)]

    def keep(c):
        return pltpu.make_async_copy(own_part(c), held.at[c, place(c)], own_sem.at[c])

    def move(c, k):
        axis = CORE if k == 4 else GATHER_AXES[c % PACK_GROUPS][3 - k]
        if k == 0:
            source = own_part(c)
            target = held.at[c, place(c)]
        else:
            size = 1 << k
            base = place(c) // size * size
            source = held.at[c, pl.ds(base, size)]
            target = source
        return pltpu.make_async_remote_copy(
            src_ref=source,
            dst_ref=target,
            send_sem=send_sem.at[c, k],
            recv_sem=recv_sem.at[c, k],
            device_id=partner_of(axis, owner, shard, bits),
            device_id_type=MESH,
        )

    def count_copy(k):
        return pltpu.make_async_remote_copy(
            src_ref=counts.at[k],
            dst_ref=counts.at[5 + k],
            send_sem=count_send.at[k],
            recv_sem=count_recv.at[k],
            device_id=partner_of(SMALL_AXES[k], owner, shard, bits),
            device_id_type=MESH,
        )

    greet(axis_partners(owner, shard, bits))
    for g in range(PACK_GROUPS):
        blocks = [own_ref[g * PACK + b].astype(BF16) for b in range(PACK)]
        packed[g] = jnp.concatenate(blocks, axis=1)
    total = jnp.broadcast_to(jnp.sum(mask_ref[...].astype(F32), keepdims=True), count_ref.shape)
    counts[0] = total
    await_greetings(5)
    for c in range(GATHER_CHUNKS):
        keep(c).start()

    def unpack(c):
        group = c % PACK_GROUPS
        offset = c // PACK_GROUPS * rows

        def body(e, carry):
            unpack_rows(store, (group * devices + e) * PACK, held[c, e], offset, edge)
            return carry

        lax.fori_loop(0, devices, body, 0, unroll=2)

    stage = 0
    for position, code in enumerate(GATHER_ORDER):
        c, k = code % 1000 // 10, code % 10
        if code >= 2000:
            if k == 1:
                keep(c).wait()
            move(c, k).start()
        else:
            move(c, k).wait_recv()
            if k == 4:
                unpack(c)
        if position == 0:
            count_copy(0).start()
        elif position % 12 == 0 and stage < 5:
            count_copy(stage).wait_recv()
            total = counts[stage] + counts[5 + stage]
            stage += 1
            if stage < 5:
                counts[stage] = total
                count_copy(stage).start()
    count_ref[...] = jnp.maximum(total, 1.0)

    steps = project.shape[0] // edge
    staged = ((project, project_out), (outward, outward_out), (expand, expand_out), (contract, contract_out))

    def body(row, carry):
        tables = matrix_rows(row, *sizes, edge)
        targets, copies = [], []
        for n, (inside, outside) in enumerate(staged):
            size = inside.shape[0] // steps
            part = pl.ds(pl.multiple_of(row * size, size), size)
            targets.append(inside.at[part])
            copies.append(pltpu.make_async_copy(inside.at[part], outside.at[part], out_sem.at[n]))
        assemble_rows(tables, place_ref, store, targets, edge)
        for copy in copies:
            copy.start()
        return carry

    lax.fori_loop(0, steps, body, 0)
    for c in range(GATHER_CHUNKS):
        for k in range(5):
            move(c, k).wait_send()
    for k in range(5):
        count_copy(k).wait_send()
    for n, (inside, outside) in enumerate(staged):
        pltpu.make_async_copy(inside, outside, out_sem.at[n]).wait()


def gather_everywhere(place, own, mask, devices, sizes):
    slots, edge, _ = own.shape
    width, _, _, hidden_width = sizes
    strip = PACK * edge
    shapes = matrix_shapes(width, hidden_width)
    return pl.pallas_call(
        functools.partial(gather_kernel, sizes=sizes),
        out_shape=shapes + (jax.ShapeDtypeStruct((8, LANES), F32),),
        in_specs=[
            pl.BlockSpec(memory_space=pltpu.SMEM),
            pl.BlockSpec(memory_space=pltpu.VMEM),
            pl.BlockSpec(memory_space=pltpu.VMEM),
        ],
        out_specs=(pl.BlockSpec(memory_space=pl.ANY),) * 4 + (pl.BlockSpec(memory_space=pltpu.VMEM),),
        scratch_shapes=[
            pltpu.VMEM((PACK_GROUPS, edge, strip), BF16),
            pltpu.VMEM((GATHER_CHUNKS, devices, edge // HALVES, strip), BF16),
            pltpu.VMEM((devices * slots, edge, LANES), BF16),
            *[pltpu.VMEM(shape.shape, shape.dtype) for shape in shapes],
            pltpu.VMEM((10, 8, LANES), F32),
            pltpu.SemaphoreType.DMA((GATHER_CHUNKS,)),
            pltpu.SemaphoreType.DMA((GATHER_CHUNKS, 5)),
            pltpu.SemaphoreType.DMA((GATHER_CHUNKS, 5)),
            pltpu.SemaphoreType.DMA((5,)),
            pltpu.SemaphoreType.DMA((5,)),
            pltpu.SemaphoreType.DMA((4,)),
        ],
        compiler_params=params(collective_id=2, has_side_effects=True),
        name="gather_weights",
    )(place, own, mask)


def split_two(values):
    high = values.astype(BF16)
    return high, (values - high.astype(F32)).astype(BF16)


def dot_split(left, right, dims):
    product = lambda a, b: lax.dot_general(a, b, (dims, ((), ())), preferred_element_type=F32)
    return product(left[0], right[0]) + (product(left[0], right[1]) + product(left[1], right[0]))


def shampoo_parts(grad, left, right, left_root, right_root, weight):
    parts = split_two(grad)
    new_left = STAT_DECAY * left + (1.0 - STAT_DECAY) * dot_split(parts, parts, ((1,), (1,)))
    new_right = STAT_DECAY * right + (1.0 - STAT_DECAY) * dot_split(parts, parts, ((0,), (0,)))
    half = dot_split(split_two(left_root), parts, ((1,), (0,)))
    precond = dot_split(split_two(half), split_two(right_root), ((1,), (0,)))
    scale = 1.0 / (grad.shape[0] * grad.shape[1])
    mean = jnp.sum(jnp.sum(precond * precond, 1, keepdims=True), 0, keepdims=True) * scale
    scale_back = lax.rsqrt(mean + ROOT_EPSILON)
    new_weight = weight * (1.0 - MATRIX_RATE * WEIGHT_DECAY) - MATRIX_RATE * precond * scale_back
    return new_left, new_right, new_weight


def block_update_kernel(
    stats_ref, grad_ref, left_ref, right_ref, left_root_ref, right_root_ref, weight_ref,
    grad_out, left_out, right_out, weight_out,
):
    factor = stats_ref[0:1, 0:1]
    for b in range(grad_ref.shape[0]):
        grad = grad_ref[b] * factor
        grad_out[b] = grad
        left_out[b], right_out[b], weight_out[b] = shampoo_parts(
            grad, left_ref[b], right_ref[b], left_root_ref[b], right_root_ref[b], weight_ref[b]
        )


def update_blocks(stats, grads, left, right, left_root, right_root, weight):
    count, edge, _ = grads.shape
    per_step = PACK if count % PACK == 0 else 1
    spec = pl.BlockSpec((per_step, edge, edge), lambda i: (i, 0, 0))
    out = jax.ShapeDtypeStruct(grads.shape, F32)
    return pl.pallas_call(
        block_update_kernel,
        out_shape=(out,) * 4,
        grid=(count // per_step,),
        in_specs=[whole(stats.shape)] + [spec] * 6,
        out_specs=(spec,) * 4,
        compiler_params=params(),
        name="update_blocks",
    )(stats, grads, left, right, left_root, right_root, weight)


def table_update_kernel(
    step_ref, stats_ref, grad_ref, left_ref, right_ref, left_root_ref, right_root_ref, weight_ref,
    norm_grad_ref, moment_ref, second_ref, norm_ref,
    grad_out, left_out, right_out, weight_out, norm_grad_out, moment_out, second_out, norm_out,
    grad_parts, precond,
):
    factor = stats_ref[0:1, 0:1]
    grad = grad_ref[...] * factor
    grad_out[...] = grad
    parts = split_two(grad)
    left_out[...] = STAT_DECAY * left_ref[...] + (1.0 - STAT_DECAY) * dot_split(parts, parts, ((1,), (1,)))
    half = split_two(dot_split(split_two(left_root_ref[...]), parts, ((1,), (0,))))
    for n in range(2):
        grad_parts[n] = parts[n]
    width = grad.shape[1]
    strip = width // 3

    def strip_body(i, carry):
        cols = pl.ds(pl.multiple_of(i * strip, strip), strip)
        own = (grad_parts[0, :, cols], grad_parts[1, :, cols])
        right_out[cols, :] = STAT_DECAY * right_ref[cols, :] + (1.0 - STAT_DECAY) * dot_split(
            own, parts, ((0,), (0,))
        )
        precond[:, cols] = dot_split(half, split_two(right_root_ref[:, cols]), ((1,), (0,)))
        return carry

    lax.fori_loop(0, 3, strip_body, 0)
    turned = precond[...]
    mean = total_of(turned * turned) * (1.0 / (grad.shape[0] * width))
    weight_out[...] = weight_ref[...] * (1.0 - MATRIX_RATE * WEIGHT_DECAY) - MATRIX_RATE * turned * lax.rsqrt(
        mean + ROOT_EPSILON
    )
    rows = norm_ref.shape[0]
    clipped = norm_grad_ref[0:rows, :] * factor
    norm_grad_out[...] = clipped
    moment = FIRST_BETA * moment_ref[...] + (1.0 - FIRST_BETA) * clipped
    second = SECOND_BETA * second_ref[...] + (1.0 - SECOND_BETA) * clipped * clipped
    moment_out[...] = moment
    second_out[...] = second
    one = moment / step_ref[0:1, 0:1]
    two = second / step_ref[0:1, 1:2]
    weight = norm_ref[...]
    norm_out[...] = weight - VECTOR_RATE * (one / (jnp.sqrt(two) + ADAM_EPSILON) + WEIGHT_DECAY * weight)


def update_table(corrections, stats, grad, left, right, left_root, right_root, weight, norm_grad, moment, second, norms):
    like = lambda array: jax.ShapeDtypeStruct(array.shape, F32)
    return pl.pallas_call(
        table_update_kernel,
        out_shape=(like(grad), like(left), like(right), like(weight)) + (like(norms),) * 4,
        scratch_shapes=[pltpu.VMEM((2,) + grad.shape, BF16), pltpu.VMEM(grad.shape, F32)],
        compiler_params=params(),
        name="update_table",
    )(corrections, stats, grad, left, right, left_root, right_root, weight, norm_grad, moment, second, norms)


def rotary_tables(length):
    lane = jnp.arange(LANES, dtype=jnp.int32)[None, :]
    half = HS // 2
    freqs = jnp.exp(-math.log(ROTARY_BASE) * (2.0 * (lane % half).astype(F32) / HS))
    angles = jnp.arange(length, dtype=F32)[:, None] * freqs
    sine = jnp.sin(angles)
    return jnp.cos(angles), jnp.where(lane % HS < half, -sine, sine)


def pack_blocks(blocks):
    count, edge, _ = blocks.shape
    groups = blocks.reshape(count // PACK, PACK, edge, edge).transpose(0, 2, 1, 3)
    return groups.reshape(count // PACK, edge, PACK * edge)


def gather_weights(own, mask, owner_map, known, sizes):
    everyone = ("dp", "tensor")
    slots, edge, _ = own.shape
    shards = sizes[1]
    owner, slot = owner_map[None, :] // slots, owner_map[None, :] % slots
    shard = jnp.arange(shards, dtype=jnp.int32)[:, None]
    if known:
        bits = bits_of(owner, shard)
        group = slot // PACK
        entry = gather_entry(0, bits)
        for g in range(1, PACK_GROUPS):
            entry = jnp.where(group == g, gather_entry(g, bits), entry)
        place = ((group * 32 + entry) * PACK + slot % PACK).reshape(-1)
        return gather_everywhere(place, own, mask, 32, sizes)
    packed = pack_blocks(lax.all_gather(own.astype(BF16), everyone, axis=0, tiled=True))
    count = jnp.maximum(lax.psum(jnp.sum(mask.astype(F32)), everyone), 1.0)
    place = ((owner * shards + shard) * slots + slot).reshape(-1)
    return assemble(place, packed, sizes) + (jnp.broadcast_to(count, (8, LANES)),)


def body(
    codons,
    segments,
    targets,
    loss_mask,
    owner_map,
    step_count,
    block_weight,
    block_left,
    block_right,
    block_left_root,
    block_right_root,
    embedding_weight,
    table_left,
    table_right,
    table_left_root,
    table_right_root,
    norm_params,
    norm_moment,
    norm_second,
):
    everyone = ("dp", "tensor")
    vocab, width = embedding_weight.shape
    shards = lax.axis_size("tensor")
    owners = lax.axis_size("dp")
    slots = block_weight.shape[1]
    edge = block_weight.shape[-1]
    blocks = owner_map.shape[0]
    length = codons.shape[1]
    shard_width = width // shards

    known = on_known_slice(owners, shards, slots)
    sizes = (width, shards, shard_width, FF)
    project, outward, expand, contract, count = gather_weights(
        block_weight[0], loss_mask, owner_map, known, sizes
    )
    segment = lax.dynamic_index_in_dim(segments, lax.axis_index("tensor"), 0, keepdims=False)
    tiles = length // TILE
    columns = jnp.stack([codons[0], targets[0], loss_mask[0], segment], 1)
    seg_row = segment.reshape(tiles, 1, TILE)
    tiled = segment.reshape(length // ROWS, ROWS)
    before = jnp.sum((segment[None, :] < tiled[:, :1]).astype(jnp.int32), -1)
    until = jnp.sum((segment[None, :] <= tiled[:, -1:]).astype(jnp.int32), -1)
    low, high = before // TILE, (until + TILE - 1) // TILE
    half = (high - low + 1) // 2
    low = jnp.minimum(low, tiles - 2 * half)
    cosine, sine = rotary_tables(length)

    x0, h1, query, keys, values = front(columns, embedding_weight, norm_params, project, cosine, sine)
    attended, lse = attend(low, half, query, keys, values, columns, seg_row)
    (h2, active, d_two, ghid, d_one, gatt, gx, head_grad, norm_grad) = middle_rows(
        x0, attended, columns, count, norm_params, embedding_weight,
        outward, expand, contract,
    )
    gproj = attend_back(
        low, half, query, keys, values, gatt, lse, columns, seg_row, cosine, sine
    )
    table_grad, norm_grad = tail_rows(
        columns, x0, gx, gproj, norm_params, project, head_grad, norm_grad
    )
    owner, slot = owner_map[None, :] // slots, owner_map[None, :] % slots
    device = owner * shards + jnp.arange(shards, dtype=jnp.int32)[:, None]
    if known:
        home = slot * (owners * shards) + device
    else:
        home = device * slots + slot
    grads = weight_grads(
        home.reshape(-1), h1, attended, h2, active, gproj, d_one, ghid, d_two, sizes, shards * blocks, edge
    )
    if known:
        owned, table_grad, norm_grad, stats = sum_everywhere(
            grads.reshape((slots,) + (2,) * 5 + grads.shape[1:]),
            table_grad, norm_grad, count,
        )
    else:
        owned = lax.psum_scatter(grads, everyone, scatter_dimension=0, tiled=True)
        owned = jnp.stack([jnp.concatenate(from_dense(owned[b]), 0) for b in range(slots)])
        table_grad, norm_grad, square_sum = lax.psum((table_grad, norm_grad), everyone) + (
            lax.psum(jnp.sum(owned * owned), everyone),
        )
        vectors = norm_grad[:6]
        square_sum = square_sum + jnp.sum(table_grad * table_grad) + jnp.sum(vectors * vectors)
        stats = statistics(square_sum, jnp.sum(norm_grad[6]), count[:1, :1])
    loss_value, grad_norm = stats[2, 0], stats[1, 0]
    step_value = step_count.astype(F32)
    corrections = jnp.stack([1.0 - FIRST_BETA**step_value, 1.0 - SECOND_BETA**step_value]).reshape(1, 2)
    block_grad, new_left, new_right, new_weight = update_blocks(
        stats, owned, block_left[0], block_right[0], block_left_root[0], block_right_root[0], block_weight[0]
    )
    (
        table_clipped, table_left_new, table_right_new, table_weight_new,
        norm_clipped, moment_new, second_new, params_new,
    ) = update_table(
        corrections, stats, table_grad, table_left, table_right, table_left_root, table_right_root,
        embedding_weight, norm_grad, norm_moment, norm_second, norm_params,
    )
    return (
        loss_value,
        grad_norm,
        block_grad[None],
        new_left[None],
        new_right[None],
        new_weight[None],
        table_clipped,
        table_left_new,
        table_right_new,
        table_weight_new,
        norm_clipped,
        moment_new,
        second_new,
        params_new,
    )


def solution(mesh):
    in_specs = (
        P(("dp", "tensor"), None),
        P("dp", None),
        P(("dp", "tensor"), None),
        P(("dp", "tensor"), None),
        P(),
        P(),
        P("tensor", "dp", None, None),
        P("tensor", "dp", None, None),
        P("tensor", "dp", None, None),
        P("tensor", "dp", None, None),
        P("tensor", "dp", None, None),
        P(),
        P(),
        P(),
        P(),
        P(),
        P(),
        P(),
        P(),
    )
    out_specs = (
        P(),
        P(),
        P("tensor", "dp", None, None),
        P("tensor", "dp", None, None),
        P("tensor", "dp", None, None),
        P("tensor", "dp", None, None),
        P(),
        P(),
        P(),
        P(),
        P(),
        P(),
        P(),
        P(),
    )
    return jax.shard_map(body, mesh=mesh, in_specs=in_specs, out_specs=out_specs, check_vma=False)
```

```python
import functools
import math

import jax
import jax.numpy as jnp
from jax import lax
from jax.experimental import pallas as pl
from jax.experimental.pallas import tpu as pltpu
from jax.sharding import PartitionSpec as P

FF = 3072
HS = 64

CLIP_LEVEL = 0.005
STAT_DECAY = 0.5
MATRIX_RATE = 0.03
WEIGHT_DECAY = 0.01
VECTOR_RATE = 0.2
FIRST_BETA = 0.9
SECOND_BETA = 0.999
ADAM_EPSILON = 1e-08
NORM_EPSILON = 1e-05
ROOT_EPSILON = 1e-06
MASK_VALUE = -1e30
ROTARY_BASE = 10000.0

LANES = 128
PACK = 4
VMEM_LIMIT = 60 * 1024 * 1024
BF16 = jnp.bfloat16
F32 = jnp.float32


def dot(left, right):
    return lax.dot_general(left, right, (((1,), (0,)), ((), ())), preferred_element_type=F32)


def dot_nt(left, right):
    return lax.dot_general(left, right, (((1,), (1,)), ((), ())), preferred_element_type=F32)


def dot_tn(left, right):
    return lax.dot_general(left, right, (((0,), (0,)), ((), ())), preferred_element_type=F32)


def split_three(values):
    high = values.astype(BF16)
    rest = values - high.astype(F32)
    middle = rest.astype(BF16)
    low = (rest - middle.astype(F32)).astype(BF16)
    return high, middle, low


def params(**more):
    return pltpu.CompilerParams(vmem_limit_bytes=VMEM_LIMIT, **more)


def whole(shape):
    return pl.BlockSpec(shape, lambda *_: (0,) * len(shape))


def dense_rows(edge):
    return edge * edge // LANES


def to_dense(block):
    half, quarter = block.shape[0] // 2, block.shape[0] // 4
    wide, slim = LANES // 2, LANES // 4
    return (
        jnp.concatenate([block[:half, :wide], block[half:, :wide]], axis=1),
        jnp.concatenate(
            [block[i * quarter : (i + 1) * quarter, wide : wide + slim] for i in range(4)], axis=1
        ),
    )


def from_dense(dense):
    half = dense.shape[0] * 2 // 3
    quarter = half // 2
    wide, slim = LANES // 2, LANES // 4
    quarters = []
    for i in range(4):
        start = i % 2 * quarter
        lanes = slice(i // 2 * wide, (i // 2 + 1) * wide)
        quarters.append(
            jnp.concatenate(
                [dense[start : start + quarter, lanes], dense[half:, i * slim : (i + 1) * slim]], axis=1
            )
        )
    return quarters


def unpack_group(group, edge):
    return [group[:, edge * j : edge * (j + 1)] for j in range(PACK)]


def block_index(shard, block, blocks):
    return shard * blocks + block


def matrix_rows(row, width, shards, shard_width, hidden_width, edge):
    model = width // edge
    wide = shard_width // edge
    tall = hidden_width // shards // edge
    starts = [0, 3 * wide * model, 4 * wide * model, 4 * wide * model + model * tall]
    blocks = starts[3] + tall * model
    project = [
        block_index(c % (shards * wide) // wide, row * 3 * wide + c // (shards * wide) * wide + c % wide, blocks)
        for c in range(3 * model)
    ]
    outward = [
        block_index(row // wide, starts[1] + row % wide * model + c, blocks) for c in range(model)
    ]
    expand = [
        block_index(c // tall, starts[2] + row * tall + c % tall, blocks) for c in range(shards * tall)
    ]
    steps = model
    each = shards * tall // steps
    contract = []
    for q in range(each):
        r = row * each + q
        contract.append(
            [block_index(r // tall, starts[3] + r % tall * model + c, blocks) for c in range(model)]
        )
    return [project], [outward], [expand], contract


def assemble_rows(tables, place_ref, store, targets, edge):
    strip = PACK * edge
    for block_rows, target in zip(tables, targets):
        for r, places in enumerate(block_rows):
            for c in range(len(places) // PACK):
                blocks = [store[place_ref[places[c * PACK + j]]][:, :edge] for j in range(PACK)]
                target[r * edge : (r + 1) * edge, c * strip : (c + 1) * strip] = jnp.concatenate(
                    blocks, axis=1
                )


def unpack_rows(store, first, group, offset, edge):
    pieces = unpack_group(group, edge)
    for j in range(PACK):
        store[first + j, offset : offset + group.shape[0], :edge] = pieces[j]


def assemble_kernel(
    place_ref, in_ref, project_ref, outward_ref, expand_ref, contract_ref, store, *, load_steps, sizes
):
    step = pl.program_id(0)
    per_step, edge, _ = in_ref.shape

    @pl.when(step < load_steps)
    def _():
        def unpack(g, carry):
            unpack_rows(store, (step * per_step + g) * PACK, in_ref[g], 0, edge)
            return carry

        lax.fori_loop(0, per_step, unpack, 0)

    @pl.when(step >= load_steps)
    def _():
        tables = matrix_rows(step - load_steps, *sizes, edge)
        assemble_rows(tables, place_ref, store, (project_ref, outward_ref, expand_ref, contract_ref), edge)


def matrix_shapes(width, hidden_width):
    return (
        jax.ShapeDtypeStruct((width, 3 * width), BF16),
        jax.ShapeDtypeStruct((width, width), BF16),
        jax.ShapeDtypeStruct((width, hidden_width), BF16),
        jax.ShapeDtypeStruct((hidden_width, width), BF16),
    )


def assemble(place, packed, sizes):
    groups, edge, strip = packed.shape
    width, _, _, hidden_width = sizes
    per_step = 16
    load_steps = groups // per_step
    fill_steps = width // edge
    tall = hidden_width // fill_steps

    def late(step, *_):
        return (jnp.maximum(step - load_steps, 0), 0)

    return pl.pallas_call(
        functools.partial(assemble_kernel, load_steps=load_steps, sizes=sizes),
        out_shape=matrix_shapes(width, hidden_width),
        grid_spec=pltpu.PrefetchScalarGridSpec(
            num_scalar_prefetch=1,
            grid=(load_steps + fill_steps,),
            in_specs=[
                pl.BlockSpec(
                    (per_step, edge, strip), lambda s, *_: (jnp.minimum(s, load_steps - 1), 0, 0)
                )
            ],
            out_specs=[
                pl.BlockSpec((edge, 3 * width), late),
                pl.BlockSpec((edge, width), late),
                pl.BlockSpec((edge, hidden_width), late),
                pl.BlockSpec((tall, width), late),
            ],
            scratch_shapes=[pltpu.VMEM((groups * PACK, edge, LANES), BF16)],
        ),
        compiler_params=params(),
        name="assemble_weights",
    )(place, packed)


def norm_parts(values):
    scale = 1.0 / values.shape[-1]
    center = values - jnp.sum(values, -1, keepdims=True) * scale
    spread = jnp.sum(center * center, -1, keepdims=True) * scale
    inverse = lax.rsqrt(spread + NORM_EPSILON)
    return center * inverse, inverse


def norm_back(grad, unit, inverse, gain):
    scale = 1.0 / grad.shape[-1]
    inner = grad * gain
    mean_one = jnp.sum(inner, -1, keepdims=True) * scale
    mean_two = jnp.sum(inner * unit, -1, keepdims=True) * scale
    return (inner - mean_one - unit * mean_two) * inverse


def turn(values, cosine, sine):
    lane = lax.broadcasted_iota(jnp.int32, values.shape, 1)
    half = HS // 2
    ahead = pltpu.roll(values, LANES - half, 1)
    behind = pltpu.roll(values, half, 1)
    other = jnp.where(lane % HS < half, ahead, behind)
    return values * cosine + other * sine


def front_kernel(
    column_ref, table_ref, norm_ref, project_ref, cos_ref, sin_ref, x_ref, h_ref, q_ref, k_ref, v_ref
):
    rows = column_ref.shape[0]
    vocab, width = table_ref.shape
    index = lax.broadcasted_iota(jnp.int32, (rows, vocab), 1)
    hot = jnp.where(column_ref[:, 0:1] == index, 1.0, 0.0).astype(BF16)
    high, middle, low = split_three(table_ref[...])
    embedded = (dot(hot, high) + dot(hot, middle)) + dot(hot, low)
    embedded = embedded * math.sqrt(width)
    x_ref[...] = embedded
    unit, _ = norm_parts(embedded)
    normed = (unit * norm_ref[0:1, :] + norm_ref[1:2, :]).astype(BF16)
    h_ref[...] = normed
    cosine = cos_ref[...]
    sine = sin_ref[...]
    for part, out_ref in ((0, q_ref), (1, k_ref), (2, v_ref)):
        values = dot(normed, project_ref[:, part * width : (part + 1) * width])
        for c in range(width // LANES):
            piece = values[:, c * LANES : (c + 1) * LANES]
            if part < 2:
                piece = turn(piece, cosine, sine)
            if part == 0:
                piece = piece * HS ** (-0.5)
            out_ref[:, c * LANES : (c + 1) * LANES] = piece.astype(BF16)


def front(columns, table, norm_params, project, cosine, sine):
    length, kinds = columns.shape
    vocab, width = table.shape
    rows = 256
    spec = pl.BlockSpec((rows, width), lambda i: (i, 0))
    low = jax.ShapeDtypeStruct((length, width), BF16)
    return pl.pallas_call(
        front_kernel,
        out_shape=(jax.ShapeDtypeStruct((length, width), F32), low, low, low, low),
        grid=(length // rows,),
        in_specs=[
            pl.BlockSpec((rows, kinds), lambda i: (i, 0)),
            whole(table.shape),
            whole(norm_params.shape),
            whole(project.shape),
            pl.BlockSpec((rows, LANES), lambda i: (i, 0)),
            pl.BlockSpec((rows, LANES), lambda i: (i, 0)),
        ],
        out_specs=(spec, spec, spec, spec, spec),
        compiler_params=params(),
        name="embed_project",
    )(columns, table, norm_params, project, cosine, sine)


ROWS = 512
TILE = 128
SHORTEST = 3


def head_masks(rows):
    lane = lax.broadcasted_iota(jnp.int32, (rows, LANES), 1)
    return [lane // HS == h for h in range(LANES // HS)]


def same_segment(seg_col, seg_row_ref, first, count):
    row = jnp.concatenate([seg_row_ref[first + i] for i in range(count)], axis=1)
    return seg_col == row


def attend_kernel(low_ref, half_ref, q_ref, k_ref, v_ref, column_ref, seg_row_ref, o_ref, lse_ref):
    part = pl.program_id(1)
    first, half = low_ref[part], half_ref[part]
    masks = head_masks(ROWS)

    def run(count):
        query = q_ref[...]
        zero = jnp.zeros_like(query)
        span = pl.ds(pl.multiple_of(first * TILE, TILE), count * TILE)
        keys = k_ref[span, :]
        values = v_ref[span, :]
        same = same_segment(column_ref[:, 3:4], seg_row_ref, first, count)
        outs, logs = [], []
        for mask in masks:
            scores = jnp.where(same, dot_nt(jnp.where(mask, query, zero), keys), MASK_VALUE)
            top = jnp.max(scores, -1, keepdims=True)
            exps = jnp.exp(scores - top)
            total = jnp.sum(exps, -1, keepdims=True)
            probs = (exps * (1.0 / total)).astype(BF16)
            outs.append(dot(probs, values))
            logs.append(top + jnp.log(total))
        o_ref[...] = jnp.where(masks[0], outs[0], outs[1]).astype(BF16)
        lse_ref[...] = jnp.where(masks[0], logs[0], logs[1])

    for n in range(SHORTEST, k_ref.shape[0] // TILE // 2 + 1):
        pl.when(half == n)(functools.partial(run, 2 * n))


def attend(low, half, query, keys, values, columns, seg_row):
    length, width = query.shape
    tiles = length // TILE
    pairs = width // LANES
    column = pl.BlockSpec((ROWS, LANES), lambda p, i, *_: (i, p))
    full = pl.BlockSpec((length, LANES), lambda p, i, *_: (0, p))
    return pl.pallas_call(
        attend_kernel,
        out_shape=(
            jax.ShapeDtypeStruct((length, width), BF16),
            jax.ShapeDtypeStruct((length, width), F32),
        ),
        grid_spec=pltpu.PrefetchScalarGridSpec(
            num_scalar_prefetch=2,
            grid=(pairs, length // ROWS),
            in_specs=[
                column,
                full,
                full,
                pl.BlockSpec((ROWS, columns.shape[1]), lambda p, i, *_: (i, 0)),
                whole((tiles, 1, TILE)),
            ],
            out_specs=(column, column),
        ),
        compiler_params=params(),
        name="attend_forward",
    )(low, half, query, keys, values, columns, seg_row)


def attend_back_kernel(
    low_ref, half_ref, q_ref, k_ref, v_ref, g_ref, lse_ref, column_ref, seg_row_ref, cos_ref, sin_ref,
    out_ref, dk_acc, dv_acc,
):
    part = pl.program_id(1)
    parts = pl.num_programs(1)
    heads = LANES // HS
    first, half = low_ref[part], half_ref[part]
    masks = head_masks(ROWS)

    @pl.when(part == 0)
    def _():
        dk_acc[...] = jnp.zeros_like(dk_acc)
        dv_acc[...] = jnp.zeros_like(dv_acc)

    def run(count):
        query = q_ref[...]
        grad = g_ref[...]
        zero = jnp.zeros_like(query)
        span = pl.ds(pl.multiple_of(first * TILE, TILE), count * TILE)
        keys = k_ref[span, :]
        values = v_ref[span, :]
        same = same_segment(column_ref[:, 3:4], seg_row_ref, first, count)
        dq, dk, dv = [], [], []
        query_turned, grad_turned = query.T, grad.T
        for h, mask in enumerate(masks):
            own_query = jnp.where(mask, query, zero)
            own_grad = jnp.where(mask, grad, zero)
            scores = jnp.where(same, dot_nt(own_query, keys), MASK_VALUE)
            probs = jnp.exp(scores - lse_ref[:, h * HS : h * HS + 1])
            grad_probs = dot_nt(own_grad, values)
            delta = jnp.sum(probs * grad_probs, -1, keepdims=True)
            grad_scores = (probs * (grad_probs - delta)).astype(BF16)
            dq.append(dot(grad_scores, keys))
            rows = slice(h * HS, (h + 1) * HS)
            dk.append(dot(query_turned[rows], grad_scores))
            dv.append(dot(grad_turned[rows], probs.astype(BF16)))
        dk, dv = jnp.concatenate(dk, axis=0), jnp.concatenate(dv, axis=0)
        for i in range(count):
            lanes = slice(i * TILE, (i + 1) * TILE)
            dk_acc[first + i] += dk[:, lanes]
            dv_acc[first + i] += dv[:, lanes]
        rows = pl.ds(pl.multiple_of(part * ROWS, ROWS), ROWS)
        turned = turn(
            jnp.where(masks[0], dq[0], dq[1]) * HS ** (-0.5), cos_ref[rows, :], -sin_ref[rows, :]
        )
        out_ref[0, rows, :] = turned.astype(BF16)

    for n in range(SHORTEST, k_ref.shape[0] // TILE // 2 + 1):
        pl.when(half == n)(functools.partial(run, 2 * n))

    @pl.when(part == parts - 1)
    def _():
        for j in range(dk_acc.shape[0]):
            rows = slice(j * TILE, (j + 1) * TILE)
            out_ref[1, rows, :] = turn(dk_acc[j].T, cos_ref[rows, :], -sin_ref[rows, :]).astype(BF16)
            out_ref[2, rows, :] = dv_acc[j].T.astype(BF16)


def attend_back(low, half, query, keys, values, grad, lse, columns, seg_row, cosine, sine):
    length, width = query.shape
    tiles = length // TILE
    pairs = width // LANES
    column = pl.BlockSpec((ROWS, LANES), lambda p, i, *_: (i, p))
    full = pl.BlockSpec((length, LANES), lambda p, i, *_: (0, p))
    return pl.pallas_call(
        attend_back_kernel,
        out_shape=jax.ShapeDtypeStruct((3, length, width), BF16),
        grid_spec=pltpu.PrefetchScalarGridSpec(
            num_scalar_prefetch=2,
            grid=(pairs, length // ROWS),
            in_specs=[
                column,
                full,
                full,
                column,
                column,
                pl.BlockSpec((ROWS, columns.shape[1]), lambda p, i, *_: (i, 0)),
                whole((tiles, 1, TILE)),
                whole((length, LANES)),
                whole((length, LANES)),
            ],
            out_specs=pl.BlockSpec((3, length, LANES), lambda p, i, *_: (0, 0, p)),
            scratch_shapes=[
                pltpu.VMEM((tiles, LANES, TILE), F32),
                pltpu.VMEM((tiles, LANES, TILE), F32),
            ],
        ),
        compiler_params=params(),
        name="attend_backward",
    )(low, half, query, keys, values, grad, lse, columns, seg_row, cosine, sine)


INV_SQRT_TWO = 2.0 ** (-0.5)
INV_SQRT_TWO_PI = (2.0 * math.pi) ** (-0.5)


def middle_kernel(
    x_ref, att_ref, column_ref, count_ref, norm_ref, table_ref,
    outward_ref, expand_ref, contract_ref,
    h_ref, active_ref, d_two_ref, ghid_ref, d_one_ref, gatt_ref, gx_ref, head_ref, norm_grad_ref,
    slope,
):
    step = pl.program_id(0)
    rows, width = x_ref.shape
    vocab = table_ref.shape[0]
    ff = expand_ref.shape[1]
    part = width

    @pl.when(step == 0)
    def _():
        head_ref[...] = jnp.zeros_like(head_ref)
        norm_grad_ref[...] = jnp.zeros_like(norm_grad_ref)

    middle = x_ref[...] + dot(att_ref[...], outward_ref[...])
    unit_two, inverse_two = norm_parts(middle)
    gain_two = norm_ref[2:3, :]
    normed_two = (unit_two * gain_two + norm_ref[3:4, :]).astype(BF16)
    h_ref[...] = normed_two

    def forward(c, total):
        cols = pl.ds(pl.multiple_of(c * part, part), part)
        hidden = dot(normed_two, expand_ref[:, cols])
        cumulative = 0.5 + 0.5 * lax.erf(hidden * INV_SQRT_TWO)
        active = (hidden * cumulative).astype(BF16)
        density = jnp.exp(-0.5 * hidden * hidden) * INV_SQRT_TWO_PI
        slope[:, cols] = cumulative + hidden * density
        active_ref[:, cols] = active
        return total + dot(active, contract_ref[cols, :])

    branch = lax.fori_loop(0, ff // part, forward, jnp.zeros((rows, width), F32))
    unit, inverse = norm_parts(middle + branch)
    gain = norm_ref[4:5, :]
    final = (unit * gain + norm_ref[5:6, :]).astype(BF16)
    table = table_ref[...].astype(BF16)
    logits = dot_nt(final, table)
    shifted = logits - jnp.max(logits, -1, keepdims=True)
    exps = jnp.exp(shifted)
    sums = jnp.sum(exps, -1, keepdims=True)
    hot = column_ref[:, 1:2] == lax.broadcasted_iota(jnp.int32, (rows, vocab), 1)
    mask = column_ref[:, 2:3].astype(F32)
    log_probs = shifted - jnp.log(sums)
    picked = jnp.sum(jnp.where(hot, log_probs, 0.0) * mask, 0, keepdims=True)
    norm_grad_ref[6:7, 0:vocab] -= picked
    glogits = ((jnp.exp(log_probs) - jnp.where(hot, 1.0, 0.0)) * (mask / count_ref[0:1, 0:1])).astype(BF16)
    head_ref[...] += dot_tn(glogits, final)
    gfinal = dot(glogits, table)
    norm_grad_ref[4:5, :] += jnp.sum(gfinal * unit, 0, keepdims=True)
    norm_grad_ref[5:6, :] += jnp.sum(gfinal, 0, keepdims=True)
    gx_two = norm_back(gfinal, unit, inverse, gain)
    d_two = gx_two.astype(BF16)
    d_two_ref[...] = d_two

    def backward(c, total):
        cols = pl.ds(pl.multiple_of(c * part, part), part)
        gactive = dot_nt(d_two, contract_ref[cols, :])
        ghid = (gactive * slope[:, cols]).astype(BF16)
        ghid_ref[:, cols] = ghid
        return total + dot_nt(ghid, expand_ref[:, cols])

    gh = lax.fori_loop(0, ff // part, backward, jnp.zeros((rows, width), F32))
    norm_grad_ref[2:3, :] += jnp.sum(gh * unit_two, 0, keepdims=True)
    norm_grad_ref[3:4, :] += jnp.sum(gh, 0, keepdims=True)
    gx_one = gx_two + norm_back(gh, unit_two, inverse_two, gain_two)
    gx_ref[...] = gx_one
    d_one = gx_one.astype(BF16)
    d_one_ref[...] = d_one
    gatt_ref[...] = dot_nt(d_one, outward_ref[...]).astype(BF16)


def middle_rows(x, att, columns, count, norm_params, table, outward, expand, contract):
    length, width = x.shape
    vocab = table.shape[0]
    ff = expand.shape[1]
    rows = 512
    narrow = pl.BlockSpec((rows, width), lambda i: (i, 0))
    broad = pl.BlockSpec((rows, ff), lambda i: (i, 0))
    column = pl.BlockSpec((rows, columns.shape[1]), lambda i: (i, 0))
    low = jax.ShapeDtypeStruct((length, width), BF16)
    low_broad = jax.ShapeDtypeStruct((length, ff), BF16)
    return pl.pallas_call(
        middle_kernel,
        out_shape=(
            low, low_broad, low, low_broad, low, low,
            jax.ShapeDtypeStruct((length, width), F32),
            jax.ShapeDtypeStruct((vocab, width), F32),
            jax.ShapeDtypeStruct((8, width), F32),
        ),
        grid=(length // rows,),
        in_specs=[
            narrow, narrow, column, whole(count.shape), whole(norm_params.shape), whole(table.shape),
            whole(outward.shape), whole(expand.shape), whole(contract.shape),
        ],
        out_specs=(
            narrow, broad, narrow, broad, narrow, narrow, narrow,
            whole((vocab, width)), whole((8, width)),
        ),
        scratch_shapes=[pltpu.VMEM((rows, ff), F32)],
        compiler_params=params(),
        name="middle_rows",
    )(x, att, columns, count, norm_params, table, outward, expand, contract)


def tail_part(codon_col, x, gx, gprojs, norm_params, project, table_acc, norm_acc):
    rows, width = x.shape
    vocab = table_acc.shape[0]
    gh = dot_nt(gprojs[0], project[:, 0:width])
    gh = gh + dot_nt(gprojs[1], project[:, width : 2 * width])
    gh = gh + dot_nt(gprojs[2], project[:, 2 * width : 3 * width])
    unit, inverse = norm_parts(x)
    norm_acc[0:1, :] += jnp.sum(gh * unit, 0, keepdims=True)
    norm_acc[1:2, :] += jnp.sum(gh, 0, keepdims=True)
    gx = gx + norm_back(gh, unit, inverse, norm_params[0:1, :])
    hot = jnp.where(codon_col == lax.broadcasted_iota(jnp.int32, (rows, vocab), 1), 1.0, 0.0)
    hot = hot.T.astype(BF16)
    high, middle, low = split_three(gx)
    total = dot(hot, high) + (dot(hot, middle) + dot(hot, low))
    table_acc[...] += total * math.sqrt(width)


def tail_kernel(
    column_ref, x_ref, gx_ref, gproj_ref, norm_ref, project_ref, head_ref, norm_in_ref,
    table_grad_ref, norm_grad_ref,
):
    @pl.when(pl.program_id(0) == 0)
    def _():
        table_grad_ref[...] = head_ref[...]
        norm_grad_ref[...] = norm_in_ref[...]

    tail_part(
        column_ref[:, 0:1], x_ref[...], gx_ref[...], gproj_ref, norm_ref, project_ref,
        table_grad_ref, norm_grad_ref,
    )


def tail_rows(columns, x, gx, gproj, norm_params, project, head, norm_in):
    length, width = x.shape
    rows = 256
    narrow = pl.BlockSpec((rows, width), lambda i: (i, 0))
    return pl.pallas_call(
        tail_kernel,
        out_shape=(
            jax.ShapeDtypeStruct(head.shape, F32),
            jax.ShapeDtypeStruct(norm_in.shape, F32),
        ),
        grid=(length // rows,),
        in_specs=[
            pl.BlockSpec((rows, columns.shape[1]), lambda i: (i, 0)),
            narrow, narrow, pl.BlockSpec((3, rows, width), lambda i: (0, i, 0)),
            whole(norm_params.shape), whole(project.shape), whole(head.shape), whole(norm_in.shape),
        ],
        out_specs=(whole(head.shape), whole(norm_in.shape)),
        compiler_params=params(),
        name="tail_rows",
    )(columns, x, gx, gproj, norm_params, project, head, norm_in)


def weight_grad_kernel(
    place_ref, h_one, att, h_two, active, gproj, d_one, ghid, d_two, out_ref,
    left, right, turned, buf, left_sem, right_sem, out_sem, *, sizes, edge,
):
    width, shards, shard_width, hidden_width = sizes
    model = width // edge
    wide = shard_width // edge
    tall = hidden_width // shards // edge
    starts = [0, 3 * wide * model, 4 * wide * model, 4 * wide * model + model * tall]
    blocks = starts[3] + tall * model
    part = hidden_width // shards
    columns = lambda ref, t: ref.at[:, pl.ds(t * part, part)]
    lefts = [h_one, att, h_two] + [columns(active, t) for t in range(shards)]
    rights = [gproj.at[i] for i in range(3)] + [d_one] + [columns(ghid, t) for t in range(shards)] + [d_two]
    plan = [(0, 0), (0, 1), (0, 2), (1, 3)]
    plan += [(2, 4 + t) for t in range(shards)]
    plan += [(3 + t, 4 + shards) for t in range(shards)]
    step = pl.program_id(0)
    slot = step % 2
    count = buf.shape[1]

    def fetches(n):
        found = []
        if n == 0 or plan[n][0] != plan[n - 1][0]:
            which = plan[n][0] % 2
            found.append(pltpu.make_async_copy(lefts[plan[n][0]], left.at[which], left_sem.at[which]))
        if n == 0 or plan[n][1] != plan[n - 1][1]:
            which = plan[n][1] % 2
            found.append(pltpu.make_async_copy(rights[plan[n][1]], right.at[which], right_sem.at[which]))
        return found

    def drain(which):
        pltpu.make_async_copy(buf.at[which], out_ref.at[pl.ds(0, count)], out_sem.at[which]).wait()

    for n in range(len(plan)):

        @pl.when(step == n)
        def _():
            if n == 0:
                for copy in fetches(0):
                    copy.start()
            for copy in fetches(n):
                copy.wait()
            if n + 1 < len(plan):
                for copy in fetches(n + 1):
                    copy.start()
            if n == 0 or plan[n][0] != plan[n - 1][0]:
                turned[...] = left[plan[n][0] % 2].T

    @pl.when(step >= 2)
    def _():
        drain(slot)

    which = jnp.minimum(step, 4 + shards) % 2
    rows = turned.shape[0] // 2
    for half in range(2):
        result = dot(turned[half * rows : (half + 1) * rows], right[which])
        for i in range(rows // edge):
            r = half * (rows // edge) + i
            for c in range(model):
                block = result[i * edge : (i + 1) * edge, c * edge : (c + 1) * edge]
                upper, lower = to_dense(block)
                buf[slot, r * model + c, : edge // 2] = upper
                buf[slot, r * model + c, edge // 2 :] = lower
            for c in range(model):
                index = block_index(c // wide, r * 3 * wide + step * wide + c % wide, blocks)
                index = jnp.where(
                    step == 3, block_index(r // wide, starts[1] + r % wide * model + c, blocks), index
                )
                index = jnp.where(
                    step >= 4, block_index(step - 4, starts[2] + r * tall + c, blocks), index
                )
                index = jnp.where(
                    step >= 4 + shards,
                    block_index(step - 4 - shards, starts[3] + r * model + c, blocks),
                    index,
                )
                k = r * model + c
                pltpu.make_async_copy(
                    buf.at[slot, k], out_ref.at[place_ref[index]], out_sem.at[slot]
                ).start()

    @pl.when(step == len(plan) - 1)
    def _():
        drain(1 - slot)
        drain(slot)


def weight_grads(place, h_one, att, h_two, active, gproj, d_one, ghid, d_two, sizes, blocks, edge):
    length, width = h_one.shape
    shards = sizes[1]
    count = (width // edge) ** 2
    anywhere = pl.BlockSpec(memory_space=pl.ANY)
    return pl.pallas_call(
        functools.partial(weight_grad_kernel, sizes=sizes, edge=edge),
        out_shape=jax.ShapeDtypeStruct((blocks, dense_rows(edge), LANES), F32),
        grid_spec=pltpu.PrefetchScalarGridSpec(
            num_scalar_prefetch=1,
            grid=(4 + 2 * shards,),
            in_specs=[anywhere] * 8,
            out_specs=anywhere,
            scratch_shapes=[
                pltpu.VMEM((2, length, width), BF16),
                pltpu.VMEM((2, length, width), BF16),
                pltpu.VMEM((width, length), BF16),
                pltpu.VMEM((2, count, dense_rows(edge), LANES), F32),
                pltpu.SemaphoreType.DMA((2,)),
                pltpu.SemaphoreType.DMA((2,)),
                pltpu.SemaphoreType.DMA((2,)),
            ],
        ),
        compiler_params=params(),
        name="weight_gradients",
    )(place, h_one, att, h_two, active, gproj, d_one, ghid, d_two)


CORE, NEAR_Y, NEAR_X, NEAR_Z, FAR_Z = range(5)
AXIS_STRIDE = {CORE: 1, NEAR_Y: 2, NEAR_X: 4, NEAR_Z: 8, FAR_Z: 16}
NATURAL = (FAR_Z, NEAR_Z, NEAR_X, NEAR_Y)
CHUNK_AXES = (
    (NEAR_X, NEAR_Y, NEAR_Z, FAR_Z),
    (NEAR_Y, NEAR_X, NEAR_Z, FAR_Z),
    (NEAR_X, NEAR_Y, NEAR_Z, FAR_Z),
    (NEAR_Y, NEAR_X, NEAR_Z, FAR_Z),
    (NEAR_Z, NEAR_X, NEAR_Y, FAR_Z),
    (NEAR_Z, NEAR_Y, NEAR_X, FAR_Z),
)
PACK_GROUPS = 6
SUM_CHUNKS = PACK_GROUPS * PACK
SUM_SLOTS = 6
SUM_ORDER = (
    0, 2000, 10, 20, 2010, 30, 40, 50, 2020, 1000, 2001, 2030, 60, 1010, 2011, 2040, 70, 1020, 2021, 2050, 80, 1030,
    2031, 2060, 90, 1040, 2041, 2070, 100, 1050, 2051, 2080, 110, 1060, 2090, 120, 1070, 2100, 130, 1080, 2061,
    2110, 140, 1090, 2071, 2120, 150, 1100, 1001, 2130, 160, 1110, 1011, 2140, 170, 2012, 1120, 2150, 180, 2002,
    1130, 2101, 2160, 190, 1140, 1021, 2170, 200, 2111, 1150, 1031, 1041, 2180, 210, 1160, 2190, 220, 2032, 1170,
    1051, 2200, 230, 2022, 1180, 2042, 2210, 1190, 2052, 1012, 2220, 1200, 1002, 1061, 2230, 1210, 1071, 2072, 1220,
    2062, 1230, 2081, 2003, 1032, 2091, 2013, 1022, 1101, 1042, 2023, 1052, 2053, 1111, 2033, 2043, 1003, 2004,
    2161, 1072, 2102, 1013, 2014, 1062, 2112, 1023, 2024, 2063, 1053, 2054, 1004, 1043, 2044, 2121, 1033, 2034,
    2131, 2141, 1014, 2151, 1081, 1024, 2073, 1091, 1102, 1054, 1112, 1063, 2064, 1044, 2171, 1034, 1073, 2074,
    1064, 2221, 2092, 2082, 2113, 2103, 1161, 1121, 1074, 1131, 1141, 2132, 1151, 2122, 2152, 1113, 2114, 2142,
    1103, 2104, 1092, 2093, 1082, 2162, 2191, 1171, 2181, 2083, 1114, 1132, 2172, 2133, 1104, 1122, 1152, 1093,
    2094, 2123, 1142, 1221, 2201, 2143, 1083, 2084, 1162, 2163, 1133, 2134, 2153, 1094, 2231, 1172, 2211, 1123,
    2124, 1084, 2173, 1143, 2144, 1163, 2164, 1134, 1191, 1181, 2182, 2192, 1153, 2154, 2222, 1124, 1173, 2174,
    1144, 1201, 2202, 1164, 1154, 1211, 2212, 1231, 2232, 1182, 2183, 1174, 1192, 2193, 1222, 2223, 1202, 2203,
    1212, 2213, 1183, 2184, 1193, 2194, 1223, 1232, 2233, 2224, 1203, 1213, 2204, 2214, 1184, 1233, 2234, 1194,
    1224, 1204, 1214, 1234,
)
SMALL_ROWS = 1024
SMALL_AXES = (CORE, NEAR_X, NEAR_Y, NEAR_Z, FAR_Z)
MESH = pl.DeviceIdType.MESH


def on_known_slice(owners, shards, slots):
    return owners == 8 and shards == 4 and slots % PACK == 0 and slots == PACK * PACK_GROUPS


def bits_of(owner, shard):
    return {
        CORE: shard % 2,
        NEAR_Y: shard // 2,
        NEAR_X: owner % 2,
        NEAR_Z: owner // 2 % 2,
        FAR_Z: owner // 4,
    }


def own_bits():
    owner, shard = lax.axis_index("dp"), lax.axis_index("tensor")
    return owner, shard, bits_of(owner, shard)


def partner_of(axis, owner, shard, bits):
    if axis == CORE:
        return (owner, shard + 1 - 2 * bits[CORE])
    if axis == NEAR_Y:
        return (owner, shard + 2 - 4 * bits[NEAR_Y])
    step = {NEAR_X: 1, NEAR_Z: 2, FAR_Z: 4}[axis]
    return (owner + step - 2 * step * bits[axis], shard)


def axis_partners(owner, shard, bits):
    return [partner_of(axis, owner, shard, bits) for axis in range(5)]


def group_partners(owner, shard):
    same_owner = [(owner, (shard + i) % 4) for i in range(1, 4)]
    same_shard = [((owner + i) % 8, shard) for i in range(1, 8)]
    return same_owner, same_shard


def greet(partners):
    for partner in partners:
        pl.semaphore_signal(
            pltpu.get_barrier_semaphore(), inc=1, device_id=partner, device_id_type=MESH
        )


def await_greetings(count):
    pl.semaphore_wait(pltpu.get_barrier_semaphore(), count)


def total_of(values):
    return jnp.sum(jnp.sum(values, 1, keepdims=True), 0, keepdims=True)


def statistics(square_sum, loss_sum, count):
    norm = jnp.sqrt(square_sum)
    factor = CLIP_LEVEL / jnp.maximum(norm, CLIP_LEVEL)
    row = lax.broadcasted_iota(jnp.int32, (8, LANES), 0)
    return jnp.where(row == 0, factor, jnp.where(row == 1, norm, loss_sum / count))


def sum_kernel(
    grads_ref, table_ref, norm_ref, count_ref,
    owned_ref, table_out, norm_out, stats_out,
    inbuf, r0, r1, r2, r3, r4, small, s0, s1, s2, s3, s4, spread, square, near_squares, far_squares,
    in_sem, send_sem, recv_sem, small_send, small_recv, square_send, square_recv,
):
    owner, shard, bits = own_bits()
    received = (r0, r1, r2, r3, r4)

    def axes_of(c):
        return CHUNK_AXES[c % len(CHUNK_AXES)]

    def half_of(ref, c, k, bit):
        left = [axis for axis in NATURAL if axis not in axes_of(c)[:k]]
        place = left.index(axes_of(c)[k])
        return ref.at[(c,) + (slice(None),) * place + (bit,)]

    def fetch(c):
        slot = c % SUM_SLOTS
        return pltpu.make_async_copy(
            grads_ref.at[c, :, :, :, :, bits[CORE]], inbuf.at[slot], in_sem.at[slot]
        )

    same_owner, same_shard = group_partners(owner, shard)
    greet(same_owner + same_shard)
    await_greetings(len(same_owner) + len(same_shard))

    def chunk_send(c, k):
        if k == 0:
            axis, source = CORE, grads_ref.at[c, :, :, :, :, 1 - bits[CORE]]
        else:
            axis = axes_of(c)[k - 1]
            source = half_of(received[k - 1], c, k - 1, 1 - bits[axis])
        return pltpu.make_async_remote_copy(
            src_ref=source,
            dst_ref=received[k].at[c],
            send_sem=send_sem.at[c, k],
            recv_sem=recv_sem.at[c, k],
            device_id=partner_of(axis, owner, shard, bits),
            device_id_type=MESH,
        )

    def merge(c, k):
        chunk_send(c, k).wait_recv()
        if k == 0:
            fetch(c).wait()

            def add(e, carry):
                for y in range(2):
                    place = (e // 4, e // 2 % 2, e % 2, y)
                    r0[(c,) + place] = r0[(c,) + place] + inbuf[(c % SUM_SLOTS,) + place]
                return carry

            lax.fori_loop(0, 8, add, 0)
            return
        own = half_of(received[k - 1], c, k - 1, bits[axes_of(c)[k - 1]])
        if k < 4:

            def add(e, carry):
                received[k][c, e] = received[k][c, e] + own[e]
                return carry

            lax.fori_loop(0, 2, add, 0)
            return
        dense = r4[c] + own[...]
        quarter = owned_ref.shape[1] // 4
        for i, rows in enumerate(from_dense(dense)):
            owned_ref[c, i * quarter : (i + 1) * quarter, :] = rows
        parts = dense * dense
        total = square[...]
        for r in range(dense.shape[0] // 8):
            total = total + parts[r * 8 : (r + 1) * 8]
        square[...] = total

    vocab, width = table_ref.shape
    vectors = norm_ref.shape[0]
    columns = width // LANES
    small_parts = (s0, s1, s2, s3, s4)

    def small_fill():
        for c in range(columns):
            lanes = slice(c * LANES, (c + 1) * LANES)
            small[c * vocab : (c + 1) * vocab] = table_ref[:, lanes]
            start = columns * vocab + c * vectors
            small[start : start + vectors] = norm_ref[:, lanes]
        used = columns * (vocab + vectors)
        small[used:] = jnp.zeros((SMALL_ROWS - used, LANES), F32)

    def small_base(k):
        base = 0
        for i in range(k):
            base = base + (SMALL_ROWS >> (i + 1)) * bits[SMALL_AXES[i]]
        return base

    def small_copy(k):
        rows = SMALL_ROWS >> (k + 1)
        start = pl.multiple_of(small_base(k) + rows * (1 - bits[SMALL_AXES[k]]), 8)
        return pltpu.make_async_remote_copy(
            src_ref=small.at[pl.ds(start, rows)],
            dst_ref=small_parts[k],
            send_sem=small_send.at[k],
            recv_sem=small_recv.at[k],
            device_id=partner_of(SMALL_AXES[k], owner, shard, bits),
            device_id_type=MESH,
        )

    def small_merge(k):
        small_copy(k).wait_recv()
        rows = SMALL_ROWS >> (k + 1)
        mine = pl.ds(pl.multiple_of(small_base(k + 1), 8), rows)
        if k < 4:
            small[mine, :] = small[mine, :] + small_parts[k][...]
            small_copy(k + 1).start()
        else:
            spread[mine, :] = small[mine, :] + small_parts[k][...]
            spread_copy(4).start()

    def spread_copy(k):
        rows = SMALL_ROWS >> (k + 1)
        here = pl.ds(pl.multiple_of(small_base(k + 1), 8), rows)
        return pltpu.make_async_remote_copy(
            src_ref=spread.at[here],
            dst_ref=spread.at[here],
            send_sem=small_send.at[5 + k],
            recv_sem=small_recv.at[5 + k],
            device_id=partner_of(SMALL_AXES[k], owner, shard, bits),
            device_id_type=MESH,
        )

    def spread_next(k):
        spread_copy(k).wait_recv()
        if k > 0:
            spread_copy(k - 1).start()
        else:
            for c in range(columns):
                lanes = slice(c * LANES, (c + 1) * LANES)
                table_out[:, lanes] = spread[c * vocab : (c + 1) * vocab]
                start = columns * vocab + c * vectors
                norm_out[:, lanes] = spread[start : start + vectors]

    square[...] = jnp.zeros_like(square)
    small_fill()
    small_copy(0).start()
    extra = []
    extra += [functools.partial(small_merge, k) for k in range(5)]
    extra += [functools.partial(spread_next, k) for k in range(4, -1, -1)]
    for position, code in enumerate(SUM_ORDER):
        c, k = code % 1000 // 10, code % 10
        if code < 1000:
            fetch(c).start()
        elif code < 2000:
            merge(c, k)
        else:
            chunk_send(c, k).start()
        if position >= 70 and position % 16 == 0 and extra:
            extra.pop(0)()
    while extra:
        extra.pop(0)()

    def exchange(partners, mine, slots, first):
        slots[mine] = square[...]
        copies = [
            pltpu.make_async_remote_copy(
                src_ref=square,
                dst_ref=slots.at[mine],
                send_sem=square_send.at[first + i],
                recv_sem=square_recv.at[first + i],
                device_id=partner,
                device_id_type=MESH,
            )
            for i, partner in enumerate(partners)
        ]
        for copy in copies:
            copy.start()
        for copy in copies:
            copy.wait()
        value = slots[0]
        for i in range(1, slots.shape[0]):
            value = value + slots[i]
        return value

    square[...] = exchange(same_owner, shard, near_squares, 0)
    value = exchange(same_shard, owner, far_squares, 3)
    table_sum, vectors_sum = table_out[...], norm_out[0:6, :]
    stats_out[...] = statistics(
        total_of(value) + total_of(table_sum * table_sum) + total_of(vectors_sum * vectors_sum),
        total_of(norm_out[6:7, :]),
        count_ref[0:1, 0:1],
    )

    for c in range(SUM_CHUNKS):
        for k in range(5):
            chunk_send(c, k).wait_send()
    for k in range(5):
        small_copy(k).wait_send()
        spread_copy(k).wait_send()


def sum_everywhere(grads, table_grad, norm_grad, count):
    chunks = grads.shape[0]
    block = grads.shape[-2:]
    edge = math.isqrt(block[0] * block[1])
    group = lambda count: pltpu.VMEM((chunks,) + (2,) * count + block, F32)
    small = lambda rows: pltpu.VMEM((rows, LANES), F32)
    anywhere, inside = pl.BlockSpec(memory_space=pl.ANY), pl.BlockSpec(memory_space=pltpu.VMEM)
    return pl.pallas_call(
        sum_kernel,
        out_shape=(
            jax.ShapeDtypeStruct((chunks, edge, edge), F32),
            jax.ShapeDtypeStruct(table_grad.shape, F32),
            jax.ShapeDtypeStruct(norm_grad.shape, F32),
            jax.ShapeDtypeStruct((8, LANES), F32),
        ),
        in_specs=[anywhere, inside, inside, inside],
        out_specs=(inside,) * 4,
        scratch_shapes=[
            pltpu.VMEM((SUM_SLOTS,) + (2,) * 4 + block, F32),
            group(4), group(3), group(2), group(1), group(0),
            small(SMALL_ROWS), small(512), small(256), small(128), small(64), small(32), small(SMALL_ROWS),
            pltpu.VMEM((8, LANES), F32),
            pltpu.VMEM((4, 8, LANES), F32),
            pltpu.VMEM((8, 8, LANES), F32),
            pltpu.SemaphoreType.DMA((SUM_SLOTS,)),
            pltpu.SemaphoreType.DMA((SUM_CHUNKS, 5)),
            pltpu.SemaphoreType.DMA((SUM_CHUNKS, 5)),
            pltpu.SemaphoreType.DMA((10,)),
            pltpu.SemaphoreType.DMA((10,)),
            pltpu.SemaphoreType.DMA((10,)),
            pltpu.SemaphoreType.DMA((10,)),
        ],
        compiler_params=pltpu.CompilerParams(
            vmem_limit_bytes=66_000_000, collective_id=1, has_side_effects=True
        ),
        name="sum_gradients",
    )(grads, table_grad, norm_grad, count)


GATHER_AXES = (
    (NEAR_Z, NEAR_Y, NEAR_X, FAR_Z),
    (NEAR_X, NEAR_Y, NEAR_Z, FAR_Z),
    (NEAR_Y, NEAR_X, FAR_Z, NEAR_Z),
    (NEAR_Z, NEAR_Y, FAR_Z, NEAR_X),
    (NEAR_X, NEAR_Z, FAR_Z, NEAR_Y),
    (NEAR_Y, NEAR_X, FAR_Z, NEAR_Z),
)
HALVES = 2
GATHER_CHUNKS = PACK_GROUPS * HALVES
GATHER_ORDER = (
    2030, 2090, 2100, 2040, 2080, 2060, 2020, 2070, 2110, 2010, 1080, 1030, 1100, 1090, 1040, 1060, 2061, 2050,
    2081, 1020, 1070, 2071, 1110, 1010, 2021, 1061, 2062, 1050, 2011, 1081, 2082, 2031, 1071, 2072, 1062, 2063,
    1021, 2022, 2101, 1011, 2012, 1082, 2083, 1072, 2073, 1031, 2032, 2111, 1022, 1101, 2000, 2023, 2091, 1012,
    2013, 1111, 2112, 1000, 2001, 2041, 1073, 2074, 2102, 1063, 2064, 1091, 2092, 1074, 2051, 1032, 1064, 1041,
    1001, 2033, 1112, 2113, 1102, 2103, 1051, 2052, 1083, 2084, 1013, 2014, 2002, 1084, 2042, 1092, 1014, 1033,
    2034, 1023, 2024, 2093, 1052, 2053, 1034, 1042, 2043, 1024, 1103, 2104, 1002, 2003, 1104, 1093, 2094, 1113,
    2114, 1043, 2044, 1094, 1114, 1053, 2054, 1044, 1003, 2004, 1054, 1004,
)


def gather_entry(group, bits):
    first, second, third, fourth = GATHER_AXES[group]
    return 16 * bits[CORE] + 8 * bits[first] + 4 * bits[second] + 2 * bits[third] + bits[fourth]


def gather_kernel(
    place_ref, own_ref, codon_ref, target_ref, mask_ref, segments_ref,
    project_out, outward_out, expand_out, contract_out,
    count_ref, column_ref, seg_row_ref, cos_ref, sin_ref, low_ref, half_ref,
    packed, held, store, project, outward, expand, contract, counts,
    own_sem, send_sem, recv_sem, count_send, count_recv, out_sem, *, sizes,
):
    owner, shard, bits = own_bits()
    edge = own_ref.shape[1]
    rows = edge // HALVES
    devices = held.shape[1]

    def place(c):
        return gather_entry(c % PACK_GROUPS, bits)

    def own_part(c):
        return packed.at[c % PACK_GROUPS, pl.ds(c // PACK_GROUPS * rows, rows)]

    def keep(c):
        return pltpu.make_async_copy(own_part(c), held.at[c, place(c)], own_sem.at[c])

    def move(c, k):
        axis = CORE if k == 4 else GATHER_AXES[c % PACK_GROUPS][3 - k]
        if k == 0:
            source = own_part(c)
            target = held.at[c, place(c)]
        else:
            size = 1 << k
            base = place(c) // size * size
            source = held.at[c, pl.ds(base, size)]
            target = source
        return pltpu.make_async_remote_copy(
            src_ref=source,
            dst_ref=target,
            send_sem=send_sem.at[c, k],
            recv_sem=recv_sem.at[c, k],
            device_id=partner_of(axis, owner, shard, bits),
            device_id_type=MESH,
        )

    def count_copy(k):
        return pltpu.make_async_remote_copy(
            src_ref=counts.at[k],
            dst_ref=counts.at[5 + k],
            send_sem=count_send.at[k],
            recv_sem=count_recv.at[k],
            device_id=partner_of(SMALL_AXES[k], owner, shard, bits),
            device_id_type=MESH,
        )

    greet(axis_partners(owner, shard, bits))
    for g in range(PACK_GROUPS):
        blocks = [own_ref[g * PACK + b].astype(BF16) for b in range(PACK)]
        packed[g] = jnp.concatenate(blocks, axis=1)
    total = jnp.broadcast_to(jnp.sum(mask_ref[...].astype(F32), keepdims=True), count_ref.shape)
    counts[0] = total
    await_greetings(5)
    for c in range(GATHER_CHUNKS):
        keep(c).start()

    def unpack(c):
        group = c % PACK_GROUPS
        offset = c // PACK_GROUPS * rows

        def body(e, carry):
            unpack_rows(store, (group * devices + e) * PACK, held[c, e], offset, edge)
            return carry

        lax.fori_loop(0, devices, body, 0, unroll=2)

    def describe_rows():
        length = codon_ref.shape[1]
        segment = segments_ref[pl.ds(shard, 1), :]
        stacked = jnp.concatenate([codon_ref[...], target_ref[...], mask_ref[...], segment], axis=0)
        filler = jnp.zeros((LANES - stacked.shape[0], LANES), jnp.int32)
        for i in range(length // LANES):
            lanes = slice(i * LANES, (i + 1) * LANES)
            column_ref[lanes, :] = jnp.concatenate([stacked[:, lanes], filler], axis=0).T
            seg_row_ref[i] = segment[:, lanes]
        for i in range(length // ROWS):
            first = segment[:, i * ROWS : i * ROWS + 1]
            final = segment[:, (i + 1) * ROWS - 1 : (i + 1) * ROWS]
            before = jnp.sum(jnp.where(segment < first, 1.0, 0.0)).astype(jnp.int32)
            until = jnp.sum(jnp.where(segment <= final, 1.0, 0.0)).astype(jnp.int32)
            low_ref[i], half_ref[i] = span_of(before, until, length // TILE)

    def rotary_rows(i, carry):
        rows = pl.ds(pl.multiple_of(i * LANES, LANES), LANES)
        place = lax.broadcasted_iota(jnp.int32, (LANES, LANES), 0) + i * LANES
        lane = lax.broadcasted_iota(jnp.int32, (LANES, LANES), 1)
        cos_ref[rows, :], sin_ref[rows, :] = rotary_of(place, lane)
        return carry

    stage = 0
    for position, code in enumerate(GATHER_ORDER):
        c, k = code % 1000 // 10, code % 10
        if code >= 2000:
            if k == 1:
                keep(c).wait()
            move(c, k).start()
        else:
            move(c, k).wait_recv()
            if k == 4:
                unpack(c)
        if position == 10:
            describe_rows()
        if position == 30:
            lax.fori_loop(0, cos_ref.shape[0] // LANES, rotary_rows, 0)
        if position == 0:
            count_copy(0).start()
        elif position % 12 == 0 and stage < 5:
            count_copy(stage).wait_recv()
            total = counts[stage] + counts[5 + stage]
            stage += 1
            if stage < 5:
                counts[stage] = total
                count_copy(stage).start()
    count_ref[...] = jnp.maximum(total, 1.0)

    steps = project.shape[0] // edge
    staged = ((project, project_out), (outward, outward_out), (expand, expand_out), (contract, contract_out))

    def body(row, carry):
        tables = matrix_rows(row, *sizes, edge)
        targets, copies = [], []
        for n, (inside, outside) in enumerate(staged):
            size = inside.shape[0] // steps
            part = pl.ds(pl.multiple_of(row * size, size), size)
            targets.append(inside.at[part])
            copies.append(pltpu.make_async_copy(inside.at[part], outside.at[part], out_sem.at[n]))
        assemble_rows(tables, place_ref, store, targets, edge)
        for copy in copies:
            copy.start()
        return carry

    lax.fori_loop(0, steps, body, 0)
    for c in range(GATHER_CHUNKS):
        for k in range(5):
            move(c, k).wait_send()
    for k in range(5):
        count_copy(k).wait_send()
    for n, (inside, outside) in enumerate(staged):
        pltpu.make_async_copy(inside, outside, out_sem.at[n]).wait()


def gather_everywhere(place, own, codons, targets, mask, segments, devices, sizes):
    slots, edge, _ = own.shape
    width, _, _, hidden_width = sizes
    strip = PACK * edge
    shapes = matrix_shapes(width, hidden_width)
    length = codons.shape[1]
    inside, scalars = pl.BlockSpec(memory_space=pltpu.VMEM), pl.BlockSpec(memory_space=pltpu.SMEM)
    return pl.pallas_call(
        functools.partial(gather_kernel, sizes=sizes),
        out_shape=shapes
        + (
            jax.ShapeDtypeStruct((8, LANES), F32),
            jax.ShapeDtypeStruct((length, LANES), jnp.int32),
            jax.ShapeDtypeStruct((length // TILE, 1, TILE), jnp.int32),
            jax.ShapeDtypeStruct((length, LANES), F32),
            jax.ShapeDtypeStruct((length, LANES), F32),
            jax.ShapeDtypeStruct((length // ROWS,), jnp.int32),
            jax.ShapeDtypeStruct((length // ROWS,), jnp.int32),
        ),
        in_specs=[scalars] + [inside] * 5,
        out_specs=(pl.BlockSpec(memory_space=pl.ANY),) * 4 + (inside,) * 5 + (scalars,) * 2,
        scratch_shapes=[
            pltpu.VMEM((PACK_GROUPS, edge, strip), BF16),
            pltpu.VMEM((GATHER_CHUNKS, devices, edge // HALVES, strip), BF16),
            pltpu.VMEM((devices * slots, edge, LANES), BF16),
            *[pltpu.VMEM(shape.shape, shape.dtype) for shape in shapes],
            pltpu.VMEM((10, 8, LANES), F32),
            pltpu.SemaphoreType.DMA((GATHER_CHUNKS,)),
            pltpu.SemaphoreType.DMA((GATHER_CHUNKS, 5)),
            pltpu.SemaphoreType.DMA((GATHER_CHUNKS, 5)),
            pltpu.SemaphoreType.DMA((5,)),
            pltpu.SemaphoreType.DMA((5,)),
            pltpu.SemaphoreType.DMA((4,)),
        ],
        compiler_params=params(collective_id=2, has_side_effects=True),
        name="gather_weights",
    )(place, own, codons, targets, mask, segments)


def split_two(values):
    high = values.astype(BF16)
    return high, (values - high.astype(F32)).astype(BF16)


def dot_split(left, right, dims):
    product = lambda a, b: lax.dot_general(a, b, (dims, ((), ())), preferred_element_type=F32)
    return product(left[0], right[0]) + (product(left[0], right[1]) + product(left[1], right[0]))


def shampoo_parts(grad, left, right, left_root, right_root, weight):
    parts = split_two(grad)
    new_left = STAT_DECAY * left + (1.0 - STAT_DECAY) * dot_split(parts, parts, ((1,), (1,)))
    new_right = STAT_DECAY * right + (1.0 - STAT_DECAY) * dot_split(parts, parts, ((0,), (0,)))
    half = dot_split(split_two(left_root), parts, ((1,), (0,)))
    precond = dot_split(split_two(half), split_two(right_root), ((1,), (0,)))
    scale = 1.0 / (grad.shape[0] * grad.shape[1])
    mean = jnp.sum(jnp.sum(precond * precond, 1, keepdims=True), 0, keepdims=True) * scale
    scale_back = lax.rsqrt(mean + ROOT_EPSILON)
    new_weight = weight * (1.0 - MATRIX_RATE * WEIGHT_DECAY) - MATRIX_RATE * precond * scale_back
    return new_left, new_right, new_weight


def block_update_kernel(
    stats_ref, grad_ref, left_ref, right_ref, left_root_ref, right_root_ref, weight_ref,
    grad_out, left_out, right_out, weight_out,
):
    factor = stats_ref[0:1, 0:1]
    for b in range(grad_ref.shape[0]):
        grad = grad_ref[b] * factor
        grad_out[b] = grad
        left_out[b], right_out[b], weight_out[b] = shampoo_parts(
            grad, left_ref[b], right_ref[b], left_root_ref[b], right_root_ref[b], weight_ref[b]
        )


def update_blocks(stats, grads, left, right, left_root, right_root, weight):
    count, edge, _ = grads.shape
    per_step = PACK if count % PACK == 0 else 1
    spec = pl.BlockSpec((per_step, edge, edge), lambda i: (i, 0, 0))
    out = jax.ShapeDtypeStruct(grads.shape, F32)
    return pl.pallas_call(
        block_update_kernel,
        out_shape=(out,) * 4,
        grid=(count // per_step,),
        in_specs=[whole(stats.shape)] + [spec] * 6,
        out_specs=(spec,) * 4,
        compiler_params=params(),
        name="update_blocks",
    )(stats, grads, left, right, left_root, right_root, weight)


def table_update_kernel(
    step_ref, stats_ref, grad_ref, left_ref, right_ref, left_root_ref, right_root_ref, weight_ref,
    norm_grad_ref, moment_ref, second_ref, norm_ref,
    grad_out, left_out, right_out, weight_out, norm_grad_out, moment_out, second_out, norm_out,
    grad_parts, precond,
):
    factor = stats_ref[0:1, 0:1]
    grad = grad_ref[...] * factor
    grad_out[...] = grad
    parts = split_two(grad)
    left_out[...] = STAT_DECAY * left_ref[...] + (1.0 - STAT_DECAY) * dot_split(parts, parts, ((1,), (1,)))
    half = split_two(dot_split(split_two(left_root_ref[...]), parts, ((1,), (0,))))
    for n in range(2):
        grad_parts[n] = parts[n]
    width = grad.shape[1]
    strip = width // 3

    def strip_body(i, carry):
        cols = pl.ds(pl.multiple_of(i * strip, strip), strip)
        own = (grad_parts[0, :, cols], grad_parts[1, :, cols])
        right_out[cols, :] = STAT_DECAY * right_ref[cols, :] + (1.0 - STAT_DECAY) * dot_split(
            own, parts, ((0,), (0,))
        )
        precond[:, cols] = dot_split(half, split_two(right_root_ref[:, cols]), ((1,), (0,)))
        return carry

    lax.fori_loop(0, 3, strip_body, 0)
    turned = precond[...]
    mean = total_of(turned * turned) * (1.0 / (grad.shape[0] * width))
    weight_out[...] = weight_ref[...] * (1.0 - MATRIX_RATE * WEIGHT_DECAY) - MATRIX_RATE * turned * lax.rsqrt(
        mean + ROOT_EPSILON
    )
    rows = norm_ref.shape[0]
    clipped = norm_grad_ref[0:rows, :] * factor
    norm_grad_out[...] = clipped
    moment = FIRST_BETA * moment_ref[...] + (1.0 - FIRST_BETA) * clipped
    second = SECOND_BETA * second_ref[...] + (1.0 - SECOND_BETA) * clipped * clipped
    moment_out[...] = moment
    second_out[...] = second
    one = moment / step_ref[0:1, 0:1]
    two = second / step_ref[0:1, 1:2]
    weight = norm_ref[...]
    norm_out[...] = weight - VECTOR_RATE * (one / (jnp.sqrt(two) + ADAM_EPSILON) + WEIGHT_DECAY * weight)


def update_table(corrections, stats, grad, left, right, left_root, right_root, weight, norm_grad, moment, second, norms):
    like = lambda array: jax.ShapeDtypeStruct(array.shape, F32)
    return pl.pallas_call(
        table_update_kernel,
        out_shape=(like(grad), like(left), like(right), like(weight)) + (like(norms),) * 4,
        scratch_shapes=[pltpu.VMEM((2,) + grad.shape, BF16), pltpu.VMEM(grad.shape, F32)],
        compiler_params=params(),
        name="update_table",
    )(corrections, stats, grad, left, right, left_root, right_root, weight, norm_grad, moment, second, norms)


def rotary_of(place, lane):
    half = HS // 2
    freqs = jnp.exp(-math.log(ROTARY_BASE) * (2.0 * (lane % half).astype(F32) / HS))
    angles = place.astype(F32) * freqs
    sine = jnp.sin(angles)
    return jnp.cos(angles), jnp.where(lane % HS < half, -sine, sine)


def span_of(before, until, tiles):
    low, high = before // TILE, (until + TILE - 1) // TILE
    half = jnp.maximum((high - low + 1) // 2, SHORTEST)
    return jnp.minimum(low, tiles - 2 * half), half


def pack_blocks(blocks):
    count, edge, _ = blocks.shape
    groups = blocks.reshape(count // PACK, PACK, edge, edge).transpose(0, 2, 1, 3)
    return groups.reshape(count // PACK, edge, PACK * edge)


def gather_weights(own, codons, targets, mask, segments, owner_map, known, sizes):
    everyone = ("dp", "tensor")
    slots, edge, _ = own.shape
    shards = sizes[1]
    owner, slot = owner_map[None, :] // slots, owner_map[None, :] % slots
    shard = jnp.arange(shards, dtype=jnp.int32)[:, None]
    if known:
        bits = bits_of(owner, shard)
        group = slot // PACK
        entry = gather_entry(0, bits)
        for g in range(1, PACK_GROUPS):
            entry = jnp.where(group == g, gather_entry(g, bits), entry)
        place = ((group * 32 + entry) * PACK + slot % PACK).reshape(-1)
        return gather_everywhere(place, own, codons, targets, mask, segments, 32, sizes)
    packed = pack_blocks(lax.all_gather(own.astype(BF16), everyone, axis=0, tiled=True))
    count = jnp.maximum(lax.psum(jnp.sum(mask.astype(F32)), everyone), 1.0)
    place = ((owner * shards + shard) * slots + slot).reshape(-1)
    length = codons.shape[1]
    tiles = length // TILE
    segment = lax.dynamic_index_in_dim(segments, lax.axis_index("tensor"), 0, keepdims=False)
    columns = jnp.stack([codons[0], targets[0], mask[0], segment], 1)
    tiled = segment.reshape(length // ROWS, ROWS)
    before = jnp.sum((segment[None, :] < tiled[:, :1]).astype(jnp.int32), -1)
    until = jnp.sum((segment[None, :] <= tiled[:, -1:]).astype(jnp.int32), -1)
    spans = span_of(before, until, tiles)
    cosine, sine = rotary_of(
        jnp.arange(length, dtype=jnp.int32)[:, None], jnp.arange(LANES, dtype=jnp.int32)[None, :]
    )
    return assemble(place, packed, sizes) + (
        jnp.broadcast_to(count, (8, LANES)), columns, segment.reshape(tiles, 1, TILE), cosine, sine,
    ) + spans


def body(
    codons,
    segments,
    targets,
    loss_mask,
    owner_map,
    step_count,
    block_weight,
    block_left,
    block_right,
    block_left_root,
    block_right_root,
    embedding_weight,
    table_left,
    table_right,
    table_left_root,
    table_right_root,
    norm_params,
    norm_moment,
    norm_second,
):
    everyone = ("dp", "tensor")
    vocab, width = embedding_weight.shape
    shards = lax.axis_size("tensor")
    owners = lax.axis_size("dp")
    slots = block_weight.shape[1]
    edge = block_weight.shape[-1]
    blocks = owner_map.shape[0]
    shard_width = width // shards

    known = on_known_slice(owners, shards, slots)
    sizes = (width, shards, shard_width, FF)
    project, outward, expand, contract, count, columns, seg_row, cosine, sine, *spans = gather_weights(
        block_weight[0], codons, targets, loss_mask, segments, owner_map, known, sizes
    )

    x0, h1, query, keys, values = front(columns, embedding_weight, norm_params, project, cosine, sine)
    attended, lse = attend(*spans, query, keys, values, columns, seg_row)
    (h2, active, d_two, ghid, d_one, gatt, gx, head_grad, norm_grad) = middle_rows(
        x0, attended, columns, count, norm_params, embedding_weight,
        outward, expand, contract,
    )
    gproj = attend_back(
        *spans, query, keys, values, gatt, lse, columns, seg_row, cosine, sine
    )
    table_grad, norm_grad = tail_rows(
        columns, x0, gx, gproj, norm_params, project, head_grad, norm_grad
    )
    owner, slot = owner_map[None, :] // slots, owner_map[None, :] % slots
    device = owner * shards + jnp.arange(shards, dtype=jnp.int32)[:, None]
    if known:
        home = slot * (owners * shards) + device
    else:
        home = device * slots + slot
    grads = weight_grads(
        home.reshape(-1), h1, attended, h2, active, gproj, d_one, ghid, d_two, sizes, shards * blocks, edge
    )
    if known:
        owned, table_grad, norm_grad, stats = sum_everywhere(
            grads.reshape((slots,) + (2,) * 5 + grads.shape[1:]),
            table_grad, norm_grad, count,
        )
    else:
        owned = lax.psum_scatter(grads, everyone, scatter_dimension=0, tiled=True)
        owned = jnp.stack([jnp.concatenate(from_dense(owned[b]), 0) for b in range(slots)])
        table_grad, norm_grad, square_sum = lax.psum((table_grad, norm_grad), everyone) + (
            lax.psum(jnp.sum(owned * owned), everyone),
        )
        vectors = norm_grad[:6]
        square_sum = square_sum + jnp.sum(table_grad * table_grad) + jnp.sum(vectors * vectors)
        stats = statistics(square_sum, jnp.sum(norm_grad[6]), count[:1, :1])
    loss_value, grad_norm = stats[2, 0], stats[1, 0]
    step_value = step_count.astype(F32)
    corrections = jnp.stack([1.0 - FIRST_BETA**step_value, 1.0 - SECOND_BETA**step_value]).reshape(1, 2)
    block_grad, new_left, new_right, new_weight = update_blocks(
        stats, owned, block_left[0], block_right[0], block_left_root[0], block_right_root[0], block_weight[0]
    )
    (
        table_clipped, table_left_new, table_right_new, table_weight_new,
        norm_clipped, moment_new, second_new, params_new,
    ) = update_table(
        corrections, stats, table_grad, table_left, table_right, table_left_root, table_right_root,
        embedding_weight, norm_grad, norm_moment, norm_second, norm_params,
    )
    return (
        loss_value,
        grad_norm,
        block_grad[None],
        new_left[None],
        new_right[None],
        new_weight[None],
        table_clipped,
        table_left_new,
        table_right_new,
        table_weight_new,
        norm_clipped,
        moment_new,
        second_new,
        params_new,
    )


def solution(mesh):
    in_specs = (
        P(("dp", "tensor"), None),
        P("dp", None),
        P(("dp", "tensor"), None),
        P(("dp", "tensor"), None),
        P(),
        P(),
        P("tensor", "dp", None, None),
        P("tensor", "dp", None, None),
        P("tensor", "dp", None, None),
        P("tensor", "dp", None, None),
        P("tensor", "dp", None, None),
        P(),
        P(),
        P(),
        P(),
        P(),
        P(),
        P(),
        P(),
    )
    out_specs = (
        P(),
        P(),
        P("tensor", "dp", None, None),
        P("tensor", "dp", None, None),
        P("tensor", "dp", None, None),
        P("tensor", "dp", None, None),
        P(),
        P(),
        P(),
        P(),
        P(),
        P(),
        P(),
        P(),
    )
    return jax.shard_map(body, mesh=mesh, in_specs=in_specs, out_specs=out_specs, check_vma=False)
```

```python
import functools
import math

import jax
import jax.numpy as jnp
from jax import lax
from jax.experimental import pallas as pl
from jax.experimental.pallas import tpu as pltpu
from jax.sharding import PartitionSpec as P

FF = 3072
HS = 64

CLIP_LEVEL = 0.005
STAT_DECAY = 0.5
MATRIX_RATE = 0.03
WEIGHT_DECAY = 0.01
VECTOR_RATE = 0.2
FIRST_BETA = 0.9
SECOND_BETA = 0.999
ADAM_EPSILON = 1e-08
NORM_EPSILON = 1e-05
ROOT_EPSILON = 1e-06
MASK_VALUE = -1e30
ROTARY_BASE = 10000.0

LANES = 128
PACK = 4
VMEM_LIMIT = 60 * 1024 * 1024
BF16 = jnp.bfloat16
F32 = jnp.float32


def dot(left, right):
    return lax.dot_general(left, right, (((1,), (0,)), ((), ())), preferred_element_type=F32)


def dot_nt(left, right):
    return lax.dot_general(left, right, (((1,), (1,)), ((), ())), preferred_element_type=F32)


def dot_tn(left, right):
    return lax.dot_general(left, right, (((0,), (0,)), ((), ())), preferred_element_type=F32)


def split_three(values):
    high = values.astype(BF16)
    rest = values - high.astype(F32)
    middle = rest.astype(BF16)
    low = (rest - middle.astype(F32)).astype(BF16)
    return high, middle, low


def params(**more):
    return pltpu.CompilerParams(vmem_limit_bytes=VMEM_LIMIT, **more)


def whole(shape):
    return pl.BlockSpec(shape, lambda *_: (0,) * len(shape))


def dense_rows(edge):
    return edge * edge // LANES


def to_dense(block):
    half, quarter = block.shape[0] // 2, block.shape[0] // 4
    wide, slim = LANES // 2, LANES // 4
    return (
        jnp.concatenate([block[:half, :wide], block[half:, :wide]], axis=1),
        jnp.concatenate(
            [block[i * quarter : (i + 1) * quarter, wide : wide + slim] for i in range(4)], axis=1
        ),
    )


def from_dense(dense):
    half = dense.shape[0] * 2 // 3
    quarter = half // 2
    wide, slim = LANES // 2, LANES // 4
    quarters = []
    for i in range(4):
        start = i % 2 * quarter
        lanes = slice(i // 2 * wide, (i // 2 + 1) * wide)
        quarters.append(
            jnp.concatenate(
                [dense[start : start + quarter, lanes], dense[half:, i * slim : (i + 1) * slim]], axis=1
            )
        )
    return quarters


def unpack_group(group, edge):
    return [group[:, edge * j : edge * (j + 1)] for j in range(PACK)]


def block_index(shard, block, blocks):
    return shard * blocks + block


def matrix_rows(row, width, shards, shard_width, hidden_width, edge):
    model = width // edge
    wide = shard_width // edge
    tall = hidden_width // shards // edge
    starts = [0, 3 * wide * model, 4 * wide * model, 4 * wide * model + model * tall]
    blocks = starts[3] + tall * model
    project = [
        block_index(c % (shards * wide) // wide, row * 3 * wide + c // (shards * wide) * wide + c % wide, blocks)
        for c in range(3 * model)
    ]
    outward = [
        block_index(row // wide, starts[1] + row % wide * model + c, blocks) for c in range(model)
    ]
    expand = [
        block_index(c // tall, starts[2] + row * tall + c % tall, blocks) for c in range(shards * tall)
    ]
    steps = model
    each = shards * tall // steps
    contract = []
    for q in range(each):
        r = row * each + q
        contract.append(
            [block_index(r // tall, starts[3] + r % tall * model + c, blocks) for c in range(model)]
        )
    return [project], [outward], [expand], contract


def assemble_rows(tables, place_ref, store, targets, edge):
    strip = PACK * edge
    for block_rows, target in zip(tables, targets):
        for r, places in enumerate(block_rows):
            for c in range(len(places) // PACK):
                blocks = [store[place_ref[places[c * PACK + j]]][:, :edge] for j in range(PACK)]
                target[r * edge : (r + 1) * edge, c * strip : (c + 1) * strip] = jnp.concatenate(
                    blocks, axis=1
                )


def unpack_rows(store, first, group, offset, edge):
    pieces = unpack_group(group, edge)
    for j in range(PACK):
        store[first + j, offset : offset + group.shape[0], :edge] = pieces[j]


def assemble_kernel(
    place_ref, in_ref, project_ref, outward_ref, expand_ref, contract_ref, store, *, load_steps, sizes
):
    step = pl.program_id(0)
    per_step, edge, _ = in_ref.shape

    @pl.when(step < load_steps)
    def _():
        def unpack(g, carry):
            unpack_rows(store, (step * per_step + g) * PACK, in_ref[g], 0, edge)
            return carry

        lax.fori_loop(0, per_step, unpack, 0)

    @pl.when(step >= load_steps)
    def _():
        tables = matrix_rows(step - load_steps, *sizes, edge)
        assemble_rows(tables, place_ref, store, (project_ref, outward_ref, expand_ref, contract_ref), edge)


def matrix_shapes(width, hidden_width):
    return (
        jax.ShapeDtypeStruct((width, 3 * width), BF16),
        jax.ShapeDtypeStruct((width, width), BF16),
        jax.ShapeDtypeStruct((width, hidden_width), BF16),
        jax.ShapeDtypeStruct((hidden_width, width), BF16),
    )


def assemble(place, packed, sizes):
    groups, edge, strip = packed.shape
    width, _, _, hidden_width = sizes
    per_step = 16
    load_steps = groups // per_step
    fill_steps = width // edge
    tall = hidden_width // fill_steps

    def late(step, *_):
        return (jnp.maximum(step - load_steps, 0), 0)

    return pl.pallas_call(
        functools.partial(assemble_kernel, load_steps=load_steps, sizes=sizes),
        out_shape=matrix_shapes(width, hidden_width),
        grid_spec=pltpu.PrefetchScalarGridSpec(
            num_scalar_prefetch=1,
            grid=(load_steps + fill_steps,),
            in_specs=[
                pl.BlockSpec(
                    (per_step, edge, strip), lambda s, *_: (jnp.minimum(s, load_steps - 1), 0, 0)
                )
            ],
            out_specs=[
                pl.BlockSpec((edge, 3 * width), late),
                pl.BlockSpec((edge, width), late),
                pl.BlockSpec((edge, hidden_width), late),
                pl.BlockSpec((tall, width), late),
            ],
            scratch_shapes=[pltpu.VMEM((groups * PACK, edge, LANES), BF16)],
        ),
        compiler_params=params(),
        name="assemble_weights",
    )(place, packed)


def norm_parts(values):
    scale = 1.0 / values.shape[-1]
    center = values - jnp.sum(values, -1, keepdims=True) * scale
    spread = jnp.sum(center * center, -1, keepdims=True) * scale
    inverse = lax.rsqrt(spread + NORM_EPSILON)
    return center * inverse, inverse


def norm_back(grad, unit, inverse, gain):
    scale = 1.0 / grad.shape[-1]
    inner = grad * gain
    mean_one = jnp.sum(inner, -1, keepdims=True) * scale
    mean_two = jnp.sum(inner * unit, -1, keepdims=True) * scale
    return (inner - mean_one - unit * mean_two) * inverse


def turn(values, cosine, sine):
    lane = lax.broadcasted_iota(jnp.int32, values.shape, 1)
    half = HS // 2
    ahead = pltpu.roll(values, LANES - half, 1)
    behind = pltpu.roll(values, half, 1)
    other = jnp.where(lane % HS < half, ahead, behind)
    return values * cosine + other * sine


def embed_rows(codon_col, table, gain, bias):
    rows, (vocab, width) = codon_col.shape[0], table.shape
    index = lax.broadcasted_iota(jnp.int32, (rows, vocab), 1)
    hot = jnp.where(codon_col == index, 1.0, 0.0).astype(BF16)
    high, middle, low = split_three(table)
    embedded = ((dot(hot, high) + dot(hot, middle)) + dot(hot, low)) * math.sqrt(width)
    unit, _ = norm_parts(embedded)
    return embedded, (unit * gain + bias).astype(BF16)


def front_kernel(h_ref, project_ref, cos_ref, sin_ref, q_ref, k_ref, v_ref):
    width = h_ref.shape[1]
    normed = h_ref[...]
    cosine = cos_ref[...]
    sine = sin_ref[...]
    for part, out_ref in ((0, q_ref), (1, k_ref), (2, v_ref)):
        values = dot(normed, project_ref[:, part * width : (part + 1) * width])
        for c in range(width // LANES):
            piece = values[:, c * LANES : (c + 1) * LANES]
            if part < 2:
                piece = turn(piece, cosine, sine)
            if part == 0:
                piece = piece * HS ** (-0.5)
            out_ref[:, c * LANES : (c + 1) * LANES] = piece.astype(BF16)


def front(normed, project, cosine, sine):
    length, width = normed.shape
    rows = 256
    spec = pl.BlockSpec((rows, width), lambda i: (i, 0))
    narrow = pl.BlockSpec((rows, LANES), lambda i: (i, 0))
    return pl.pallas_call(
        front_kernel,
        out_shape=(jax.ShapeDtypeStruct((length, width), BF16),) * 3,
        grid=(length // rows,),
        in_specs=[spec, whole(project.shape), narrow, narrow],
        out_specs=(spec,) * 3,
        compiler_params=params(),
        name="project_rotate",
    )(normed, project, cosine, sine)


ROWS = 512
TILE = 128
SHORTEST = 3


def head_masks(rows):
    lane = lax.broadcasted_iota(jnp.int32, (rows, LANES), 1)
    return [lane // HS == h for h in range(LANES // HS)]


def same_segment(seg_col, seg_row_ref, first, count):
    row = jnp.concatenate([seg_row_ref[first + i] for i in range(count)], axis=1)
    return seg_col == row


def attend_kernel(low_ref, half_ref, q_ref, k_ref, v_ref, column_ref, seg_row_ref, o_ref, lse_ref):
    part = pl.program_id(1)
    first, half = low_ref[part], half_ref[part]
    masks = head_masks(ROWS)

    def run(count):
        query = q_ref[...]
        zero = jnp.zeros_like(query)
        span = pl.ds(pl.multiple_of(first * TILE, TILE), count * TILE)
        keys = k_ref[span, :]
        values = v_ref[span, :]
        same = same_segment(column_ref[:, 3:4], seg_row_ref, first, count)
        outs, logs = [], []
        for mask in masks:
            scores = jnp.where(same, dot_nt(jnp.where(mask, query, zero), keys), MASK_VALUE)
            top = jnp.max(scores, -1, keepdims=True)
            exps = jnp.exp(scores - top)
            total = jnp.sum(exps, -1, keepdims=True)
            probs = (exps * (1.0 / total)).astype(BF16)
            outs.append(dot(probs, values))
            logs.append(top + jnp.log(total))
        o_ref[...] = jnp.where(masks[0], outs[0], outs[1]).astype(BF16)
        lse_ref[...] = jnp.where(masks[0], logs[0], logs[1])

    for n in range(SHORTEST, k_ref.shape[0] // TILE // 2 + 1):
        pl.when(half == n)(functools.partial(run, 2 * n))


def attend(low, half, query, keys, values, columns, seg_row):
    length, width = query.shape
    tiles = length // TILE
    pairs = width // LANES
    column = pl.BlockSpec((ROWS, LANES), lambda p, i, *_: (i, p))
    full = pl.BlockSpec((length, LANES), lambda p, i, *_: (0, p))
    return pl.pallas_call(
        attend_kernel,
        out_shape=(
            jax.ShapeDtypeStruct((length, width), BF16),
            jax.ShapeDtypeStruct((length, width), F32),
        ),
        grid_spec=pltpu.PrefetchScalarGridSpec(
            num_scalar_prefetch=2,
            grid=(pairs, length // ROWS),
            in_specs=[
                column,
                full,
                full,
                pl.BlockSpec((ROWS, columns.shape[1]), lambda p, i, *_: (i, 0)),
                whole((tiles, 1, TILE)),
            ],
            out_specs=(column, column),
        ),
        compiler_params=params(),
        name="attend_forward",
    )(low, half, query, keys, values, columns, seg_row)


def attend_back_kernel(
    low_ref, half_ref, q_ref, k_ref, v_ref, g_ref, lse_ref, column_ref, seg_row_ref, cos_ref, sin_ref,
    out_ref, dk_acc, dv_acc,
):
    part = pl.program_id(1)
    parts = pl.num_programs(1)
    heads = LANES // HS
    first, half = low_ref[part], half_ref[part]
    masks = head_masks(ROWS)

    @pl.when(part == 0)
    def _():
        dk_acc[...] = jnp.zeros_like(dk_acc)
        dv_acc[...] = jnp.zeros_like(dv_acc)

    def run(count):
        query = q_ref[...]
        grad = g_ref[...]
        zero = jnp.zeros_like(query)
        span = pl.ds(pl.multiple_of(first * TILE, TILE), count * TILE)
        keys = k_ref[span, :]
        values = v_ref[span, :]
        same = same_segment(column_ref[:, 3:4], seg_row_ref, first, count)
        dq, dk, dv = [], [], []
        query_turned, grad_turned = query.T, grad.T
        for h, mask in enumerate(masks):
            own_query = jnp.where(mask, query, zero)
            own_grad = jnp.where(mask, grad, zero)
            scores = jnp.where(same, dot_nt(own_query, keys), MASK_VALUE)
            probs = jnp.exp(scores - lse_ref[:, h * HS : h * HS + 1])
            grad_probs = dot_nt(own_grad, values)
            delta = jnp.sum(probs * grad_probs, -1, keepdims=True)
            grad_scores = (probs * (grad_probs - delta)).astype(BF16)
            dq.append(dot(grad_scores, keys))
            rows = slice(h * HS, (h + 1) * HS)
            dk.append(dot(query_turned[rows], grad_scores))
            dv.append(dot(grad_turned[rows], probs.astype(BF16)))
        dk, dv = jnp.concatenate(dk, axis=0), jnp.concatenate(dv, axis=0)
        for i in range(count):
            lanes = slice(i * TILE, (i + 1) * TILE)
            dk_acc[first + i] += dk[:, lanes]
            dv_acc[first + i] += dv[:, lanes]
        rows = pl.ds(pl.multiple_of(part * ROWS, ROWS), ROWS)
        turned = turn(
            jnp.where(masks[0], dq[0], dq[1]) * HS ** (-0.5), cos_ref[rows, :], -sin_ref[rows, :]
        )
        out_ref[0, rows, :] = turned.astype(BF16)

    for n in range(SHORTEST, k_ref.shape[0] // TILE // 2 + 1):
        pl.when(half == n)(functools.partial(run, 2 * n))

    @pl.when(part == parts - 1)
    def _():
        for j in range(dk_acc.shape[0]):
            rows = slice(j * TILE, (j + 1) * TILE)
            out_ref[1, rows, :] = turn(dk_acc[j].T, cos_ref[rows, :], -sin_ref[rows, :]).astype(BF16)
            out_ref[2, rows, :] = dv_acc[j].T.astype(BF16)


def attend_back(low, half, query, keys, values, grad, lse, columns, seg_row, cosine, sine):
    length, width = query.shape
    tiles = length // TILE
    pairs = width // LANES
    column = pl.BlockSpec((ROWS, LANES), lambda p, i, *_: (i, p))
    full = pl.BlockSpec((length, LANES), lambda p, i, *_: (0, p))
    return pl.pallas_call(
        attend_back_kernel,
        out_shape=jax.ShapeDtypeStruct((3, length, width), BF16),
        grid_spec=pltpu.PrefetchScalarGridSpec(
            num_scalar_prefetch=2,
            grid=(pairs, length // ROWS),
            in_specs=[
                column,
                full,
                full,
                column,
                column,
                pl.BlockSpec((ROWS, columns.shape[1]), lambda p, i, *_: (i, 0)),
                whole((tiles, 1, TILE)),
                whole((length, LANES)),
                whole((length, LANES)),
            ],
            out_specs=pl.BlockSpec((3, length, LANES), lambda p, i, *_: (0, 0, p)),
            scratch_shapes=[
                pltpu.VMEM((tiles, LANES, TILE), F32),
                pltpu.VMEM((tiles, LANES, TILE), F32),
            ],
        ),
        compiler_params=params(),
        name="attend_backward",
    )(low, half, query, keys, values, grad, lse, columns, seg_row, cosine, sine)


INV_SQRT_TWO = 2.0 ** (-0.5)
INV_SQRT_TWO_PI = (2.0 * math.pi) ** (-0.5)


def middle_kernel(
    x_ref, att_ref, column_ref, count_ref, norm_ref, table_ref,
    outward_ref, expand_in, contract_in,
    h_ref, active_ref, d_two_ref, ghid_ref, d_one_ref, gatt_ref, gx_ref, head_ref, norm_grad_ref,
    slope, expand_ref, contract_ref, weight_sem,
):
    step = pl.program_id(0)
    rows, width = x_ref.shape
    vocab = table_ref.shape[0]
    ff = expand_ref.shape[1]
    part = width

    fetches = (
        pltpu.make_async_copy(expand_in, expand_ref, weight_sem.at[0]),
        pltpu.make_async_copy(contract_in, contract_ref, weight_sem.at[1]),
    )

    @pl.when(step == 0)
    def _():
        for fetch in fetches:
            fetch.start()
        head_ref[...] = jnp.zeros_like(head_ref)
        norm_grad_ref[...] = jnp.zeros_like(norm_grad_ref)

    middle = x_ref[...] + dot(att_ref[...], outward_ref[...])
    unit_two, inverse_two = norm_parts(middle)
    gain_two = norm_ref[2:3, :]
    normed_two = (unit_two * gain_two + norm_ref[3:4, :]).astype(BF16)
    h_ref[...] = normed_two

    @pl.when(step == 0)
    def _():
        for fetch in fetches:
            fetch.wait()

    def forward(c, total):
        cols = pl.ds(pl.multiple_of(c * part, part), part)
        hidden = dot(normed_two, expand_ref[:, cols])
        cumulative = 0.5 + 0.5 * lax.erf(hidden * INV_SQRT_TWO)
        active = (hidden * cumulative).astype(BF16)
        density = jnp.exp(-0.5 * hidden * hidden) * INV_SQRT_TWO_PI
        slope[:, cols] = cumulative + hidden * density
        active_ref[:, cols] = active
        return total + dot(active, contract_ref[cols, :])

    branch = lax.fori_loop(0, ff // part, forward, jnp.zeros((rows, width), F32))
    unit, inverse = norm_parts(middle + branch)
    gain = norm_ref[4:5, :]
    final = (unit * gain + norm_ref[5:6, :]).astype(BF16)
    table = table_ref[...].astype(BF16)
    logits = dot_nt(final, table)
    shifted = logits - jnp.max(logits, -1, keepdims=True)
    exps = jnp.exp(shifted)
    sums = jnp.sum(exps, -1, keepdims=True)
    hot = column_ref[:, 1:2] == lax.broadcasted_iota(jnp.int32, (rows, vocab), 1)
    mask = column_ref[:, 2:3].astype(F32)
    log_probs = shifted - jnp.log(sums)
    picked = jnp.sum(jnp.where(hot, log_probs, 0.0) * mask, 0, keepdims=True)
    norm_grad_ref[6:7, 0:vocab] -= picked
    glogits = ((jnp.exp(log_probs) - jnp.where(hot, 1.0, 0.0)) * (mask / count_ref[0:1, 0:1])).astype(BF16)
    head_ref[...] += dot_tn(glogits, final)
    gfinal = dot(glogits, table)
    norm_grad_ref[4:5, :] += jnp.sum(gfinal * unit, 0, keepdims=True)
    norm_grad_ref[5:6, :] += jnp.sum(gfinal, 0, keepdims=True)
    gx_two = norm_back(gfinal, unit, inverse, gain)
    d_two = gx_two.astype(BF16)
    d_two_ref[...] = d_two

    def backward(c, total):
        cols = pl.ds(pl.multiple_of(c * part, part), part)
        gactive = dot_nt(d_two, contract_ref[cols, :])
        ghid = (gactive * slope[:, cols]).astype(BF16)
        ghid_ref[:, cols] = ghid
        return total + dot_nt(ghid, expand_ref[:, cols])

    gh = lax.fori_loop(0, ff // part, backward, jnp.zeros((rows, width), F32))
    norm_grad_ref[2:3, :] += jnp.sum(gh * unit_two, 0, keepdims=True)
    norm_grad_ref[3:4, :] += jnp.sum(gh, 0, keepdims=True)
    gx_one = gx_two + norm_back(gh, unit_two, inverse_two, gain_two)
    gx_ref[...] = gx_one
    d_one = gx_one.astype(BF16)
    d_one_ref[...] = d_one
    gatt_ref[...] = dot_nt(d_one, outward_ref[...]).astype(BF16)


def middle_rows(x, att, columns, count, norm_params, table, outward, expand, contract):
    length, width = x.shape
    vocab = table.shape[0]
    ff = expand.shape[1]
    rows = 512
    narrow = pl.BlockSpec((rows, width), lambda i: (i, 0))
    broad = pl.BlockSpec((rows, ff), lambda i: (i, 0))
    column = pl.BlockSpec((rows, columns.shape[1]), lambda i: (i, 0))
    low = jax.ShapeDtypeStruct((length, width), BF16)
    low_broad = jax.ShapeDtypeStruct((length, ff), BF16)
    return pl.pallas_call(
        middle_kernel,
        out_shape=(
            low, low_broad, low, low_broad, low, low,
            jax.ShapeDtypeStruct((length, width), F32),
            jax.ShapeDtypeStruct((vocab, width), F32),
            jax.ShapeDtypeStruct((8, width), F32),
        ),
        grid=(length // rows,),
        in_specs=[
            narrow, narrow, column, whole(count.shape), whole(norm_params.shape), whole(table.shape),
            whole(outward.shape), pl.BlockSpec(memory_space=pl.ANY), pl.BlockSpec(memory_space=pl.ANY),
        ],
        out_specs=(
            narrow, broad, narrow, broad, narrow, narrow, narrow,
            whole((vocab, width)), whole((8, width)),
        ),
        scratch_shapes=[
            pltpu.VMEM((rows, ff), F32),
            pltpu.VMEM(expand.shape, BF16),
            pltpu.VMEM(contract.shape, BF16),
            pltpu.SemaphoreType.DMA((2,)),
        ],
        compiler_params=params(),
        name="middle_rows",
    )(x, att, columns, count, norm_params, table, outward, expand, contract)


def tail_part(codon_col, x, gx, gprojs, norm_params, project, table_acc, norm_acc):
    rows, width = x.shape
    vocab = table_acc.shape[0]
    gh = dot_nt(gprojs[0], project[:, 0:width])
    gh = gh + dot_nt(gprojs[1], project[:, width : 2 * width])
    gh = gh + dot_nt(gprojs[2], project[:, 2 * width : 3 * width])
    unit, inverse = norm_parts(x)
    norm_acc[0:1, :] += jnp.sum(gh * unit, 0, keepdims=True)
    norm_acc[1:2, :] += jnp.sum(gh, 0, keepdims=True)
    gx = gx + norm_back(gh, unit, inverse, norm_params[0:1, :])
    hot = jnp.where(codon_col == lax.broadcasted_iota(jnp.int32, (rows, vocab), 1), 1.0, 0.0)
    hot = hot.T.astype(BF16)
    high, middle, low = split_three(gx)
    total = dot(hot, high) + (dot(hot, middle) + dot(hot, low))
    table_acc[...] += total * math.sqrt(width)


def tail_kernel(
    column_ref, x_ref, gx_ref, gproj_ref, norm_ref, project_ref, head_ref, norm_in_ref,
    table_grad_ref, norm_grad_ref,
):
    @pl.when(pl.program_id(0) == 0)
    def _():
        table_grad_ref[...] = head_ref[...]
        norm_grad_ref[...] = norm_in_ref[...]

    tail_part(
        column_ref[:, 0:1], x_ref[...], gx_ref[...], gproj_ref, norm_ref, project_ref,
        table_grad_ref, norm_grad_ref,
    )


def tail_rows(columns, x, gx, gproj, norm_params, project, head, norm_in):
    length, width = x.shape
    rows = 256
    narrow = pl.BlockSpec((rows, width), lambda i: (i, 0))
    return pl.pallas_call(
        tail_kernel,
        out_shape=(
            jax.ShapeDtypeStruct(head.shape, F32),
            jax.ShapeDtypeStruct(norm_in.shape, F32),
        ),
        grid=(length // rows,),
        in_specs=[
            pl.BlockSpec((rows, columns.shape[1]), lambda i: (i, 0)),
            narrow, narrow, pl.BlockSpec((3, rows, width), lambda i: (0, i, 0)),
            whole(norm_params.shape), whole(project.shape), whole(head.shape), whole(norm_in.shape),
        ],
        out_specs=(whole(head.shape), whole(norm_in.shape)),
        compiler_params=params(),
        name="tail_rows",
    )(columns, x, gx, gproj, norm_params, project, head, norm_in)


def weight_grad_kernel(
    place_ref, h_one, att, h_two, active, gproj, d_one, ghid, d_two, out_ref,
    left, right, turned, buf, left_sem, right_sem, out_sem, *, sizes, edge,
):
    width, shards, shard_width, hidden_width = sizes
    model = width // edge
    wide = shard_width // edge
    tall = hidden_width // shards // edge
    starts = [0, 3 * wide * model, 4 * wide * model, 4 * wide * model + model * tall]
    blocks = starts[3] + tall * model
    part = hidden_width // shards
    columns = lambda ref, t: ref.at[:, pl.ds(t * part, part)]
    lefts = [h_one, att, h_two] + [columns(active, t) for t in range(shards)]
    rights = [gproj.at[i] for i in range(3)] + [d_one] + [columns(ghid, t) for t in range(shards)] + [d_two]
    plan = [(0, 0), (0, 1), (0, 2), (1, 3)]
    plan += [(2, 4 + t) for t in range(shards)]
    plan += [(3 + t, 4 + shards) for t in range(shards)]
    step = pl.program_id(0)
    slot = step % 2
    count = buf.shape[1]

    def fetches(n):
        found = []
        if n == 0 or plan[n][0] != plan[n - 1][0]:
            which = plan[n][0] % 2
            found.append(pltpu.make_async_copy(lefts[plan[n][0]], left.at[which], left_sem.at[which]))
        if n == 0 or plan[n][1] != plan[n - 1][1]:
            which = plan[n][1] % 2
            found.append(pltpu.make_async_copy(rights[plan[n][1]], right.at[which], right_sem.at[which]))
        return found

    def drain(which):
        pltpu.make_async_copy(buf.at[which], out_ref.at[pl.ds(0, count)], out_sem.at[which]).wait()

    for n in range(len(plan)):

        @pl.when(step == n)
        def _():
            if n == 0:
                for copy in fetches(0):
                    copy.start()
            for copy in fetches(n):
                copy.wait()
            if n + 1 < len(plan):
                for copy in fetches(n + 1):
                    copy.start()
            if n == 0 or plan[n][0] != plan[n - 1][0]:
                turned[...] = left[plan[n][0] % 2].T

    @pl.when(step >= 2)
    def _():
        drain(slot)

    which = jnp.minimum(step, 4 + shards) % 2
    rows = turned.shape[0] // 2
    for half in range(2):
        result = dot(turned[half * rows : (half + 1) * rows], right[which])
        for i in range(rows // edge):
            r = half * (rows // edge) + i
            for c in range(model):
                block = result[i * edge : (i + 1) * edge, c * edge : (c + 1) * edge]
                upper, lower = to_dense(block)
                buf[slot, r * model + c, : edge // 2] = upper
                buf[slot, r * model + c, edge // 2 :] = lower
            for c in range(model):
                index = block_index(c // wide, r * 3 * wide + step * wide + c % wide, blocks)
                index = jnp.where(
                    step == 3, block_index(r // wide, starts[1] + r % wide * model + c, blocks), index
                )
                index = jnp.where(
                    step >= 4, block_index(step - 4, starts[2] + r * tall + c, blocks), index
                )
                index = jnp.where(
                    step >= 4 + shards,
                    block_index(step - 4 - shards, starts[3] + r * model + c, blocks),
                    index,
                )
                k = r * model + c
                pltpu.make_async_copy(
                    buf.at[slot, k], out_ref.at[place_ref[index]], out_sem.at[slot]
                ).start()

    @pl.when(step == len(plan) - 1)
    def _():
        drain(1 - slot)
        drain(slot)


def weight_grads(place, h_one, att, h_two, active, gproj, d_one, ghid, d_two, sizes, blocks, edge):
    length, width = h_one.shape
    shards = sizes[1]
    count = (width // edge) ** 2
    anywhere = pl.BlockSpec(memory_space=pl.ANY)
    return pl.pallas_call(
        functools.partial(weight_grad_kernel, sizes=sizes, edge=edge),
        out_shape=jax.ShapeDtypeStruct((blocks, dense_rows(edge), LANES), F32),
        grid_spec=pltpu.PrefetchScalarGridSpec(
            num_scalar_prefetch=1,
            grid=(4 + 2 * shards,),
            in_specs=[anywhere] * 8,
            out_specs=anywhere,
            scratch_shapes=[
                pltpu.VMEM((2, length, width), BF16),
                pltpu.VMEM((2, length, width), BF16),
                pltpu.VMEM((width, length), BF16),
                pltpu.VMEM((2, count, dense_rows(edge), LANES), F32),
                pltpu.SemaphoreType.DMA((2,)),
                pltpu.SemaphoreType.DMA((2,)),
                pltpu.SemaphoreType.DMA((2,)),
            ],
        ),
        compiler_params=params(),
        name="weight_gradients",
    )(place, h_one, att, h_two, active, gproj, d_one, ghid, d_two)


CORE, NEAR_Y, NEAR_X, NEAR_Z, FAR_Z = range(5)
AXIS_STRIDE = {CORE: 1, NEAR_Y: 2, NEAR_X: 4, NEAR_Z: 8, FAR_Z: 16}
NATURAL = (FAR_Z, NEAR_Z, NEAR_X, NEAR_Y)
CHUNK_AXES = (
    (NEAR_X, NEAR_Y, NEAR_Z, FAR_Z),
    (NEAR_Y, NEAR_X, NEAR_Z, FAR_Z),
    (NEAR_X, NEAR_Y, NEAR_Z, FAR_Z),
    (NEAR_Y, NEAR_X, NEAR_Z, FAR_Z),
    (NEAR_Z, NEAR_X, NEAR_Y, FAR_Z),
    (NEAR_Z, NEAR_Y, NEAR_X, FAR_Z),
)
PACK_GROUPS = 6
SUM_CHUNKS = PACK_GROUPS * PACK
SUM_SLOTS = 6
SUM_ORDER = (
    0, 2000, 10, 20, 2010, 30, 40, 50, 2020, 1000, 2001, 2030, 60, 1010, 2011, 2040, 70, 1020, 2021, 2050, 80, 1030,
    2031, 2060, 90, 1040, 2041, 2070, 100, 1050, 2051, 2080, 110, 1060, 2090, 120, 1070, 2100, 130, 1080, 2061,
    2110, 140, 1090, 2071, 2120, 150, 1100, 1001, 2130, 160, 1110, 1011, 2140, 170, 2012, 1120, 2150, 180, 2002,
    1130, 2101, 2160, 190, 1140, 1021, 2170, 200, 2111, 1150, 1031, 1041, 2180, 210, 1160, 2190, 220, 2032, 1170,
    1051, 2200, 230, 2022, 1180, 2042, 2210, 1190, 2052, 1012, 2220, 1200, 1002, 1061, 2230, 1210, 1071, 2072, 1220,
    2062, 1230, 2081, 2003, 1032, 2091, 2013, 1022, 1101, 1042, 2023, 1052, 2053, 1111, 2033, 2043, 1003, 2004,
    2161, 1072, 2102, 1013, 2014, 1062, 2112, 1023, 2024, 2063, 1053, 2054, 1004, 1043, 2044, 2121, 1033, 2034,
    2131, 2141, 1014, 2151, 1081, 1024, 2073, 1091, 1102, 1054, 1112, 1063, 2064, 1044, 2171, 1034, 1073, 2074,
    1064, 2221, 2092, 2082, 2113, 2103, 1161, 1121, 1074, 1131, 1141, 2132, 1151, 2122, 2152, 1113, 2114, 2142,
    1103, 2104, 1092, 2093, 1082, 2162, 2191, 1171, 2181, 2083, 1114, 1132, 2172, 2133, 1104, 1122, 1152, 1093,
    2094, 2123, 1142, 1221, 2201, 2143, 1083, 2084, 1162, 2163, 1133, 2134, 2153, 1094, 2231, 1172, 2211, 1123,
    2124, 1084, 2173, 1143, 2144, 1163, 2164, 1134, 1191, 1181, 2182, 2192, 1153, 2154, 2222, 1124, 1173, 2174,
    1144, 1201, 2202, 1164, 1154, 1211, 2212, 1231, 2232, 1182, 2183, 1174, 1192, 2193, 1222, 2223, 1202, 2203,
    1212, 2213, 1183, 2184, 1193, 2194, 1223, 1232, 2233, 2224, 1203, 1213, 2204, 2214, 1184, 1233, 2234, 1194,
    1224, 1204, 1214, 1234,
)
SMALL_ROWS = 1024
SMALL_AXES = (CORE, NEAR_X, NEAR_Y, NEAR_Z, FAR_Z)
MESH = pl.DeviceIdType.MESH


def on_known_slice(owners, shards, slots):
    return owners == 8 and shards == 4 and slots % PACK == 0 and slots == PACK * PACK_GROUPS


def bits_of(owner, shard):
    return {
        CORE: shard % 2,
        NEAR_Y: shard // 2,
        NEAR_X: owner % 2,
        NEAR_Z: owner // 2 % 2,
        FAR_Z: owner // 4,
    }


def own_bits():
    owner, shard = lax.axis_index("dp"), lax.axis_index("tensor")
    return owner, shard, bits_of(owner, shard)


def partner_of(axis, owner, shard, bits):
    if axis == CORE:
        return (owner, shard + 1 - 2 * bits[CORE])
    if axis == NEAR_Y:
        return (owner, shard + 2 - 4 * bits[NEAR_Y])
    step = {NEAR_X: 1, NEAR_Z: 2, FAR_Z: 4}[axis]
    return (owner + step - 2 * step * bits[axis], shard)


def axis_partners(owner, shard, bits):
    return [partner_of(axis, owner, shard, bits) for axis in range(5)]


def group_partners(owner, shard):
    same_owner = [(owner, (shard + i) % 4) for i in range(1, 4)]
    same_shard = [((owner + i) % 8, shard) for i in range(1, 8)]
    return same_owner, same_shard


def greet(partners):
    for partner in partners:
        pl.semaphore_signal(
            pltpu.get_barrier_semaphore(), inc=1, device_id=partner, device_id_type=MESH
        )


def await_greetings(count):
    pl.semaphore_wait(pltpu.get_barrier_semaphore(), count)


def total_of(values):
    return jnp.sum(jnp.sum(values, 1, keepdims=True), 0, keepdims=True)


def statistics(square_sum, loss_sum, count):
    norm = jnp.sqrt(square_sum)
    factor = CLIP_LEVEL / jnp.maximum(norm, CLIP_LEVEL)
    row = lax.broadcasted_iota(jnp.int32, (8, LANES), 0)
    return jnp.where(row == 0, factor, jnp.where(row == 1, norm, loss_sum / count))


def sum_kernel(
    grads_ref, table_ref, norm_ref, count_ref,
    owned_ref, table_out, norm_out, stats_out,
    inbuf, r0, r1, r2, r3, r4, small, s0, s1, s2, s3, s4, spread, square, near_squares, far_squares,
    in_sem, send_sem, recv_sem, small_send, small_recv, square_send, square_recv,
):
    owner, shard, bits = own_bits()
    received = (r0, r1, r2, r3, r4)

    def axes_of(c):
        return CHUNK_AXES[c % len(CHUNK_AXES)]

    def half_of(ref, c, k, bit):
        left = [axis for axis in NATURAL if axis not in axes_of(c)[:k]]
        place = left.index(axes_of(c)[k])
        return ref.at[(c,) + (slice(None),) * place + (bit,)]

    def fetch(c):
        slot = c % SUM_SLOTS
        return pltpu.make_async_copy(
            grads_ref.at[c, :, :, :, :, bits[CORE]], inbuf.at[slot], in_sem.at[slot]
        )

    same_owner, same_shard = group_partners(owner, shard)
    greet(same_owner + same_shard)
    await_greetings(len(same_owner) + len(same_shard))

    def chunk_send(c, k):
        if k == 0:
            axis, source = CORE, grads_ref.at[c, :, :, :, :, 1 - bits[CORE]]
        else:
            axis = axes_of(c)[k - 1]
            source = half_of(received[k - 1], c, k - 1, 1 - bits[axis])
        return pltpu.make_async_remote_copy(
            src_ref=source,
            dst_ref=received[k].at[c],
            send_sem=send_sem.at[c, k],
            recv_sem=recv_sem.at[c, k],
            device_id=partner_of(axis, owner, shard, bits),
            device_id_type=MESH,
        )

    def merge(c, k):
        chunk_send(c, k).wait_recv()
        if k == 0:
            fetch(c).wait()

            def add(e, carry):
                for y in range(2):
                    place = (e // 4, e // 2 % 2, e % 2, y)
                    r0[(c,) + place] = r0[(c,) + place] + inbuf[(c % SUM_SLOTS,) + place]
                return carry

            lax.fori_loop(0, 8, add, 0)
            return
        own = half_of(received[k - 1], c, k - 1, bits[axes_of(c)[k - 1]])
        if k < 4:

            def add(e, carry):
                received[k][c, e] = received[k][c, e] + own[e]
                return carry

            lax.fori_loop(0, 2, add, 0)
            return
        dense = r4[c] + own[...]
        quarter = owned_ref.shape[1] // 4
        for i, rows in enumerate(from_dense(dense)):
            owned_ref[c, i * quarter : (i + 1) * quarter, :] = rows
        parts = dense * dense
        total = square[...]
        for r in range(dense.shape[0] // 8):
            total = total + parts[r * 8 : (r + 1) * 8]
        square[...] = total

    vocab, width = table_ref.shape
    vectors = norm_ref.shape[0]
    columns = width // LANES
    small_parts = (s0, s1, s2, s3, s4)

    def small_fill():
        for c in range(columns):
            lanes = slice(c * LANES, (c + 1) * LANES)
            small[c * vocab : (c + 1) * vocab] = table_ref[:, lanes]
            start = columns * vocab + c * vectors
            small[start : start + vectors] = norm_ref[:, lanes]
        used = columns * (vocab + vectors)
        small[used:] = jnp.zeros((SMALL_ROWS - used, LANES), F32)

    def small_base(k):
        base = 0
        for i in range(k):
            base = base + (SMALL_ROWS >> (i + 1)) * bits[SMALL_AXES[i]]
        return base

    def small_copy(k):
        rows = SMALL_ROWS >> (k + 1)
        start = pl.multiple_of(small_base(k) + rows * (1 - bits[SMALL_AXES[k]]), 8)
        return pltpu.make_async_remote_copy(
            src_ref=small.at[pl.ds(start, rows)],
            dst_ref=small_parts[k],
            send_sem=small_send.at[k],
            recv_sem=small_recv.at[k],
            device_id=partner_of(SMALL_AXES[k], owner, shard, bits),
            device_id_type=MESH,
        )

    def small_merge(k):
        small_copy(k).wait_recv()
        rows = SMALL_ROWS >> (k + 1)
        mine = pl.ds(pl.multiple_of(small_base(k + 1), 8), rows)
        if k < 4:
            small[mine, :] = small[mine, :] + small_parts[k][...]
            small_copy(k + 1).start()
        else:
            spread[mine, :] = small[mine, :] + small_parts[k][...]
            spread_copy(4).start()

    def spread_copy(k):
        rows = SMALL_ROWS >> (k + 1)
        here = pl.ds(pl.multiple_of(small_base(k + 1), 8), rows)
        return pltpu.make_async_remote_copy(
            src_ref=spread.at[here],
            dst_ref=spread.at[here],
            send_sem=small_send.at[5 + k],
            recv_sem=small_recv.at[5 + k],
            device_id=partner_of(SMALL_AXES[k], owner, shard, bits),
            device_id_type=MESH,
        )

    def spread_next(k):
        spread_copy(k).wait_recv()
        if k > 0:
            spread_copy(k - 1).start()
        else:
            for c in range(columns):
                lanes = slice(c * LANES, (c + 1) * LANES)
                table_out[:, lanes] = spread[c * vocab : (c + 1) * vocab]
                start = columns * vocab + c * vectors
                norm_out[:, lanes] = spread[start : start + vectors]

    square[...] = jnp.zeros_like(square)
    small_fill()
    small_copy(0).start()
    extra = []
    extra += [functools.partial(small_merge, k) for k in range(5)]
    extra += [functools.partial(spread_next, k) for k in range(4, -1, -1)]
    for position, code in enumerate(SUM_ORDER):
        c, k = code % 1000 // 10, code % 10
        if code < 1000:
            fetch(c).start()
        elif code < 2000:
            merge(c, k)
        else:
            chunk_send(c, k).start()
        if position >= 70 and position % 16 == 0 and extra:
            extra.pop(0)()
    while extra:
        extra.pop(0)()

    def exchange(partners, mine, slots, first):
        slots[mine] = square[...]
        copies = [
            pltpu.make_async_remote_copy(
                src_ref=square,
                dst_ref=slots.at[mine],
                send_sem=square_send.at[first + i],
                recv_sem=square_recv.at[first + i],
                device_id=partner,
                device_id_type=MESH,
            )
            for i, partner in enumerate(partners)
        ]
        for copy in copies:
            copy.start()
        for copy in copies:
            copy.wait()
        value = slots[0]
        for i in range(1, slots.shape[0]):
            value = value + slots[i]
        return value

    square[...] = exchange(same_owner, shard, near_squares, 0)
    value = exchange(same_shard, owner, far_squares, 3)
    table_sum, vectors_sum = table_out[...], norm_out[0:6, :]
    stats_out[...] = statistics(
        total_of(value) + total_of(table_sum * table_sum) + total_of(vectors_sum * vectors_sum),
        total_of(norm_out[6:7, :]),
        count_ref[0:1, 0:1],
    )

    for c in range(SUM_CHUNKS):
        for k in range(5):
            chunk_send(c, k).wait_send()
    for k in range(5):
        small_copy(k).wait_send()
        spread_copy(k).wait_send()


def sum_everywhere(grads, table_grad, norm_grad, count):
    chunks = grads.shape[0]
    block = grads.shape[-2:]
    edge = math.isqrt(block[0] * block[1])
    group = lambda count: pltpu.VMEM((chunks,) + (2,) * count + block, F32)
    small = lambda rows: pltpu.VMEM((rows, LANES), F32)
    anywhere, inside = pl.BlockSpec(memory_space=pl.ANY), pl.BlockSpec(memory_space=pltpu.VMEM)
    return pl.pallas_call(
        sum_kernel,
        out_shape=(
            jax.ShapeDtypeStruct((chunks, edge, edge), F32),
            jax.ShapeDtypeStruct(table_grad.shape, F32),
            jax.ShapeDtypeStruct(norm_grad.shape, F32),
            jax.ShapeDtypeStruct((8, LANES), F32),
        ),
        in_specs=[anywhere, inside, inside, inside],
        out_specs=(inside,) * 4,
        scratch_shapes=[
            pltpu.VMEM((SUM_SLOTS,) + (2,) * 4 + block, F32),
            group(4), group(3), group(2), group(1), group(0),
            small(SMALL_ROWS), small(512), small(256), small(128), small(64), small(32), small(SMALL_ROWS),
            pltpu.VMEM((8, LANES), F32),
            pltpu.VMEM((4, 8, LANES), F32),
            pltpu.VMEM((8, 8, LANES), F32),
            pltpu.SemaphoreType.DMA((SUM_SLOTS,)),
            pltpu.SemaphoreType.DMA((SUM_CHUNKS, 5)),
            pltpu.SemaphoreType.DMA((SUM_CHUNKS, 5)),
            pltpu.SemaphoreType.DMA((10,)),
            pltpu.SemaphoreType.DMA((10,)),
            pltpu.SemaphoreType.DMA((10,)),
            pltpu.SemaphoreType.DMA((10,)),
        ],
        compiler_params=pltpu.CompilerParams(
            vmem_limit_bytes=66_000_000, collective_id=1, has_side_effects=True
        ),
        name="sum_gradients",
    )(grads, table_grad, norm_grad, count)


GATHER_AXES = (
    (NEAR_Z, NEAR_Y, NEAR_X, FAR_Z),
    (NEAR_X, NEAR_Y, NEAR_Z, FAR_Z),
    (NEAR_Y, NEAR_X, FAR_Z, NEAR_Z),
    (NEAR_Z, NEAR_Y, FAR_Z, NEAR_X),
    (NEAR_X, NEAR_Z, FAR_Z, NEAR_Y),
    (NEAR_Y, NEAR_X, FAR_Z, NEAR_Z),
)
EMBED_ROWS = 256
HALVES = 2
GATHER_CHUNKS = PACK_GROUPS * HALVES
GATHER_ORDER = (
    2030, 2090, 2100, 2040, 2080, 2060, 2020, 2070, 2110, 2010, 1080, 1030, 1100, 1090, 1040, 1060, 2061, 2050,
    2081, 1020, 1070, 2071, 1110, 1010, 2021, 1061, 2062, 1050, 2011, 1081, 2082, 2031, 1071, 2072, 1062, 2063,
    1021, 2022, 2101, 1011, 2012, 1082, 2083, 1072, 2073, 1031, 2032, 2111, 1022, 1101, 2000, 2023, 2091, 1012,
    2013, 1111, 2112, 1000, 2001, 2041, 1073, 2074, 2102, 1063, 2064, 1091, 2092, 1074, 2051, 1032, 1064, 1041,
    1001, 2033, 1112, 2113, 1102, 2103, 1051, 2052, 1083, 2084, 1013, 2014, 2002, 1084, 2042, 1092, 1014, 1033,
    2034, 1023, 2024, 2093, 1052, 2053, 1034, 1042, 2043, 1024, 1103, 2104, 1002, 2003, 1104, 1093, 2094, 1113,
    2114, 1043, 2044, 1094, 1114, 1053, 2054, 1044, 1003, 2004, 1054, 1004,
)


def gather_entry(group, bits):
    first, second, third, fourth = GATHER_AXES[group]
    return 16 * bits[CORE] + 8 * bits[first] + 4 * bits[second] + 2 * bits[third] + bits[fourth]


def gather_kernel(
    place_ref, own_ref, codon_ref, target_ref, mask_ref, segments_ref, table_ref, norm_ref,
    project_out, outward_out, expand_out, contract_out, x_out, h_out,
    count_ref, column_ref, seg_row_ref, cos_ref, sin_ref, low_ref, half_ref,
    packed, held, store, project, outward, expand, contract, x_rows, h_rows, counts,
    own_sem, send_sem, recv_sem, count_send, count_recv, out_sem, row_sem, *, sizes,
):
    owner, shard, bits = own_bits()
    edge = own_ref.shape[1]
    rows = edge // HALVES
    devices = held.shape[1]

    def place(c):
        return gather_entry(c % PACK_GROUPS, bits)

    def own_part(c):
        return packed.at[c % PACK_GROUPS, pl.ds(c // PACK_GROUPS * rows, rows)]

    def keep(c):
        return pltpu.make_async_copy(own_part(c), held.at[c, place(c)], own_sem.at[c])

    def move(c, k):
        axis = CORE if k == 4 else GATHER_AXES[c % PACK_GROUPS][3 - k]
        if k == 0:
            source = own_part(c)
            target = held.at[c, place(c)]
        else:
            size = 1 << k
            base = place(c) // size * size
            source = held.at[c, pl.ds(base, size)]
            target = source
        return pltpu.make_async_remote_copy(
            src_ref=source,
            dst_ref=target,
            send_sem=send_sem.at[c, k],
            recv_sem=recv_sem.at[c, k],
            device_id=partner_of(axis, owner, shard, bits),
            device_id_type=MESH,
        )

    def count_copy(k):
        return pltpu.make_async_remote_copy(
            src_ref=counts.at[k],
            dst_ref=counts.at[5 + k],
            send_sem=count_send.at[k],
            recv_sem=count_recv.at[k],
            device_id=partner_of(SMALL_AXES[k], owner, shard, bits),
            device_id_type=MESH,
        )

    greet(axis_partners(owner, shard, bits))
    for g in range(PACK_GROUPS):
        blocks = [own_ref[g * PACK + b].astype(BF16) for b in range(PACK)]
        packed[g] = jnp.concatenate(blocks, axis=1)
    total = jnp.broadcast_to(jnp.sum(mask_ref[...].astype(F32), keepdims=True), count_ref.shape)
    counts[0] = total
    await_greetings(5)
    for c in range(GATHER_CHUNKS):
        keep(c).start()

    def unpack(c):
        group = c % PACK_GROUPS
        offset = c // PACK_GROUPS * rows

        def body(e, carry):
            unpack_rows(store, (group * devices + e) * PACK, held[c, e], offset, edge)
            return carry

        lax.fori_loop(0, devices, body, 0, unroll=4)

    def describe_rows():
        length = codon_ref.shape[1]
        segment = segments_ref[pl.ds(shard, 1), :]
        stacked = jnp.concatenate([codon_ref[...], target_ref[...], mask_ref[...], segment], axis=0)
        filler = jnp.zeros((LANES - stacked.shape[0], LANES), jnp.int32)
        for i in range(length // LANES):
            lanes = slice(i * LANES, (i + 1) * LANES)
            column_ref[lanes, :] = jnp.concatenate([stacked[:, lanes], filler], axis=0).T
            seg_row_ref[i] = segment[:, lanes]
        for i in range(length // ROWS):
            first = segment[:, i * ROWS : i * ROWS + 1]
            final = segment[:, (i + 1) * ROWS - 1 : (i + 1) * ROWS]
            before = jnp.sum(jnp.where(segment < first, 1.0, 0.0)).astype(jnp.int32)
            until = jnp.sum(jnp.where(segment <= final, 1.0, 0.0)).astype(jnp.int32)
            low_ref[i], half_ref[i] = span_of(before, until, length // TILE)

    def rotary_rows(i, carry):
        rows = pl.ds(pl.multiple_of(i * LANES, LANES), LANES)
        place = lax.broadcasted_iota(jnp.int32, (LANES, LANES), 0) + i * LANES
        lane = lax.broadcasted_iota(jnp.int32, (LANES, LANES), 1)
        cos_ref[rows, :], sin_ref[rows, :] = rotary_of(place, lane)
        return carry

    def embed(i, carry):
        rows = pl.ds(pl.multiple_of(i * EMBED_ROWS, EMBED_ROWS), EMBED_ROWS)
        x_rows[rows, :], h_rows[rows, :] = embed_rows(
            column_ref[rows, 0:1], table_ref[...], norm_ref[0:1, :], norm_ref[1:2, :]
        )
        return carry

    row_copies = (
        pltpu.make_async_copy(x_rows, x_out, row_sem.at[0]),
        pltpu.make_async_copy(h_rows, h_out, row_sem.at[1]),
    )
    stage = 0
    for position, code in enumerate(GATHER_ORDER):
        c, k = code % 1000 // 10, code % 10
        if code >= 2000:
            if k == 1:
                keep(c).wait()
            move(c, k).start()
        else:
            move(c, k).wait_recv()
            if k == 4:
                unpack(c)
        if position == 10:
            describe_rows()
        if position == 30:
            lax.fori_loop(0, cos_ref.shape[0] // LANES, rotary_rows, 0)
        if position == 55:
            lax.fori_loop(0, x_rows.shape[0] // EMBED_ROWS, embed, 0)
            for copy in row_copies:
                copy.start()
        if position == 0:
            count_copy(0).start()
        elif position % 12 == 0 and stage < 5:
            count_copy(stage).wait_recv()
            total = counts[stage] + counts[5 + stage]
            stage += 1
            if stage < 5:
                counts[stage] = total
                count_copy(stage).start()
    count_ref[...] = jnp.maximum(total, 1.0)

    steps = project.shape[0] // edge
    staged = ((project, project_out), (outward, outward_out), (expand, expand_out), (contract, contract_out))

    def body(row, carry):
        tables = matrix_rows(row, *sizes, edge)
        targets, copies = [], []
        for n, (inside, outside) in enumerate(staged):
            size = inside.shape[0] // steps
            part = pl.ds(pl.multiple_of(row * size, size), size)
            targets.append(inside.at[part])
            copies.append(pltpu.make_async_copy(inside.at[part], outside.at[part], out_sem.at[n]))
        assemble_rows(tables, place_ref, store, targets, edge)
        for copy in copies:
            copy.start()
        return carry

    lax.fori_loop(0, steps, body, 0)
    for c in range(GATHER_CHUNKS):
        for k in range(5):
            move(c, k).wait_send()
    for k in range(5):
        count_copy(k).wait_send()
    for n, (inside, outside) in enumerate(staged):
        pltpu.make_async_copy(inside, outside, out_sem.at[n]).wait()
    for copy in row_copies:
        copy.wait()


def gather_everywhere(place, own, rows, table, norm_params, devices, sizes):
    slots, edge, _ = own.shape
    width, _, _, hidden_width = sizes
    strip = PACK * edge
    shapes = matrix_shapes(width, hidden_width)
    length = rows[0].shape[1]
    inside, scalars = pl.BlockSpec(memory_space=pltpu.VMEM), pl.BlockSpec(memory_space=pltpu.SMEM)
    return pl.pallas_call(
        functools.partial(gather_kernel, sizes=sizes),
        out_shape=shapes
        + (
            jax.ShapeDtypeStruct((length, width), F32),
            jax.ShapeDtypeStruct((length, width), BF16),
            jax.ShapeDtypeStruct((8, LANES), F32),
            jax.ShapeDtypeStruct((length, LANES), jnp.int32),
            jax.ShapeDtypeStruct((length // TILE, 1, TILE), jnp.int32),
            jax.ShapeDtypeStruct((length, LANES), F32),
            jax.ShapeDtypeStruct((length, LANES), F32),
            jax.ShapeDtypeStruct((length // ROWS,), jnp.int32),
            jax.ShapeDtypeStruct((length // ROWS,), jnp.int32),
        ),
        in_specs=[scalars] + [inside] * 7,
        out_specs=(pl.BlockSpec(memory_space=pl.ANY),) * 6 + (inside,) * 5 + (scalars,) * 2,
        scratch_shapes=[
            pltpu.VMEM((PACK_GROUPS, edge, strip), BF16),
            pltpu.VMEM((GATHER_CHUNKS, devices, edge // HALVES, strip), BF16),
            pltpu.VMEM((devices * slots, edge, LANES), BF16),
            *[pltpu.VMEM(shape.shape, shape.dtype) for shape in shapes],
            pltpu.VMEM((length, width), F32),
            pltpu.VMEM((length, width), BF16),
            pltpu.VMEM((10, 8, LANES), F32),
            pltpu.SemaphoreType.DMA((GATHER_CHUNKS,)),
            pltpu.SemaphoreType.DMA((GATHER_CHUNKS, 5)),
            pltpu.SemaphoreType.DMA((GATHER_CHUNKS, 5)),
            pltpu.SemaphoreType.DMA((5,)),
            pltpu.SemaphoreType.DMA((5,)),
            pltpu.SemaphoreType.DMA((4,)),
            pltpu.SemaphoreType.DMA((2,)),
        ],
        compiler_params=params(collective_id=2, has_side_effects=True),
        name="gather_weights",
    )(place, own, *rows, table, norm_params)


def split_two(values):
    high = values.astype(BF16)
    return high, (values - high.astype(F32)).astype(BF16)


def dot_split(left, right, dims):
    product = lambda a, b: lax.dot_general(a, b, (dims, ((), ())), preferred_element_type=F32)
    return product(left[0], right[0]) + (product(left[0], right[1]) + product(left[1], right[0]))


def shampoo_parts(grad, left, right, left_root, right_root, weight):
    parts = split_two(grad)
    new_left = STAT_DECAY * left + (1.0 - STAT_DECAY) * dot_split(parts, parts, ((1,), (1,)))
    new_right = STAT_DECAY * right + (1.0 - STAT_DECAY) * dot_split(parts, parts, ((0,), (0,)))
    half = dot_split(split_two(left_root), parts, ((1,), (0,)))
    precond = dot_split(split_two(half), split_two(right_root), ((1,), (0,)))
    scale = 1.0 / (grad.shape[0] * grad.shape[1])
    mean = jnp.sum(jnp.sum(precond * precond, 1, keepdims=True), 0, keepdims=True) * scale
    scale_back = lax.rsqrt(mean + ROOT_EPSILON)
    new_weight = weight * (1.0 - MATRIX_RATE * WEIGHT_DECAY) - MATRIX_RATE * precond * scale_back
    return new_left, new_right, new_weight


TABLE_STEP = 3


def update_kernel(
    corrections_ref, stats_ref, table_grad_ref, table_left_ref, table_left_root_ref, table_ref,
    norm_grad_ref, moment_ref, second_ref, norm_ref, table_right_in, table_right_root_in,
    grad_ref, left_ref, right_ref, left_root_ref, right_root_ref, weight_ref,
    table_grad_out, table_left_out, table_right_out, table_out,
    norm_grad_out, moment_out, second_out, norm_out,
    grad_out, left_out, right_out, weight_out,
    grad_parts, precond, table_right, table_right_root, sem,
):
    step, steps = pl.program_id(0), pl.num_programs(0)
    factor = stats_ref[0:1, 0:1]
    fetches = (
        pltpu.make_async_copy(table_right_in, table_right, sem.at[0]),
        pltpu.make_async_copy(table_right_root_in, table_right_root, sem.at[1]),
    )
    keep = pltpu.make_async_copy(table_right, table_right_out, sem.at[2])

    @pl.when(step == 0)
    def _():
        for fetch in fetches:
            fetch.start()

    for b in range(grad_ref.shape[0]):
        grad = grad_ref[b] * factor
        grad_out[b] = grad
        left_out[b], right_out[b], weight_out[b] = shampoo_parts(
            grad, left_ref[b], right_ref[b], left_root_ref[b], right_root_ref[b], weight_ref[b]
        )

    @pl.when(step == jnp.minimum(TABLE_STEP, steps - 1))
    def _():
        for fetch in fetches:
            fetch.wait()
        grad = table_grad_ref[...] * factor
        table_grad_out[...] = grad
        parts = split_two(grad)
        table_left_out[...] = STAT_DECAY * table_left_ref[...] + (1.0 - STAT_DECAY) * dot_split(
            parts, parts, ((1,), (1,))
        )
        half = split_two(dot_split(split_two(table_left_root_ref[...]), parts, ((1,), (0,))))
        for n in range(2):
            grad_parts[n] = parts[n]
        width = grad.shape[1]
        strip = width // 3

        def strip_body(i, carry):
            cols = pl.ds(pl.multiple_of(i * strip, strip), strip)
            own = (grad_parts[0, :, cols], grad_parts[1, :, cols])
            table_right[cols, :] = STAT_DECAY * table_right[cols, :] + (1.0 - STAT_DECAY) * dot_split(
                own, parts, ((0,), (0,))
            )
            precond[:, cols] = dot_split(half, split_two(table_right_root[:, cols]), ((1,), (0,)))
            return carry

        lax.fori_loop(0, 3, strip_body, 0)
        keep.start()
        turned = precond[...]
        mean = total_of(turned * turned) * (1.0 / (grad.shape[0] * width))
        table_out[...] = table_ref[...] * (
            1.0 - MATRIX_RATE * WEIGHT_DECAY
        ) - MATRIX_RATE * turned * lax.rsqrt(mean + ROOT_EPSILON)
        clipped = norm_grad_ref[0 : norm_ref.shape[0], :] * factor
        norm_grad_out[...] = clipped
        moment = FIRST_BETA * moment_ref[...] + (1.0 - FIRST_BETA) * clipped
        second = SECOND_BETA * second_ref[...] + (1.0 - SECOND_BETA) * clipped * clipped
        moment_out[...] = moment
        second_out[...] = second
        one = moment / corrections_ref[0:1, 0:1]
        two = second / corrections_ref[0:1, 1:2]
        weight = norm_ref[...]
        norm_out[...] = weight - VECTOR_RATE * (
            one / (jnp.sqrt(two) + ADAM_EPSILON) + WEIGHT_DECAY * weight
        )

    @pl.when(step == steps - 1)
    def _():
        keep.wait()


def update_all(small, right, right_root, blocks):
    corrections, stats, table_grad, table_left, table_left_root, table, norm_grad, moment, second, norms = small
    count, edge, _ = blocks[0].shape
    per_step = PACK if count % PACK == 0 else 1
    spec = pl.BlockSpec((per_step, edge, edge), lambda i: (i, 0, 0))
    anywhere = pl.BlockSpec(memory_space=pl.ANY)
    like = lambda array: jax.ShapeDtypeStruct(array.shape, F32)
    return pl.pallas_call(
        update_kernel,
        out_shape=(like(table_grad), like(table_left), like(right), like(table))
        + (like(norms),) * 4
        + (like(blocks[0]),) * 4,
        grid=(count // per_step,),
        in_specs=[whole(array.shape) for array in small] + [anywhere] * 2 + [spec] * 6,
        out_specs=(whole(table_grad.shape), whole(table_left.shape), anywhere, whole(table.shape))
        + (whole(norms.shape),) * 4
        + (spec,) * 4,
        scratch_shapes=[
            pltpu.VMEM((2,) + table_grad.shape, BF16),
            pltpu.VMEM(table_grad.shape, F32),
            pltpu.VMEM(right.shape, F32),
            pltpu.VMEM(right.shape, F32),
            pltpu.SemaphoreType.DMA((3,)),
        ],
        compiler_params=params(),
        name="update_all",
    )(*small, right, right_root, *blocks)


def rotary_of(place, lane):
    half = HS // 2
    freqs = jnp.exp(-math.log(ROTARY_BASE) * (2.0 * (lane % half).astype(F32) / HS))
    angles = place.astype(F32) * freqs
    sine = jnp.sin(angles)
    return jnp.cos(angles), jnp.where(lane % HS < half, -sine, sine)


def span_of(before, until, tiles):
    low, high = before // TILE, (until + TILE - 1) // TILE
    half = jnp.maximum((high - low + 1) // 2, SHORTEST)
    return jnp.minimum(low, tiles - 2 * half), half


def pack_blocks(blocks):
    count, edge, _ = blocks.shape
    groups = blocks.reshape(count // PACK, PACK, edge, edge).transpose(0, 2, 1, 3)
    return groups.reshape(count // PACK, edge, PACK * edge)


def gather_weights(own, rows, table, norm_params, owner_map, known, sizes):
    everyone = ("dp", "tensor")
    codons, targets, mask, segments = rows
    slots, edge, _ = own.shape
    shards = sizes[1]
    owner, slot = owner_map[None, :] // slots, owner_map[None, :] % slots
    shard = jnp.arange(shards, dtype=jnp.int32)[:, None]
    if known:
        bits = bits_of(owner, shard)
        group = slot // PACK
        entry = gather_entry(0, bits)
        for g in range(1, PACK_GROUPS):
            entry = jnp.where(group == g, gather_entry(g, bits), entry)
        place = ((group * 32 + entry) * PACK + slot % PACK).reshape(-1)
        return gather_everywhere(place, own, rows, table, norm_params, 32, sizes)
    packed = pack_blocks(lax.all_gather(own.astype(BF16), everyone, axis=0, tiled=True))
    count = jnp.maximum(lax.psum(jnp.sum(mask.astype(F32)), everyone), 1.0)
    place = ((owner * shards + shard) * slots + slot).reshape(-1)
    length = codons.shape[1]
    tiles = length // TILE
    segment = lax.dynamic_index_in_dim(segments, lax.axis_index("tensor"), 0, keepdims=False)
    columns = jnp.stack([codons[0], targets[0], mask[0], segment], 1)
    tiled = segment.reshape(length // ROWS, ROWS)
    before = jnp.sum((segment[None, :] < tiled[:, :1]).astype(jnp.int32), -1)
    until = jnp.sum((segment[None, :] <= tiled[:, -1:]).astype(jnp.int32), -1)
    spans = span_of(before, until, tiles)
    cosine, sine = rotary_of(
        jnp.arange(length, dtype=jnp.int32)[:, None], jnp.arange(LANES, dtype=jnp.int32)[None, :]
    )
    return assemble(place, packed, sizes) + embed_rows(columns[:, :1], table, norm_params[0:1], norm_params[1:2]) + (
        jnp.broadcast_to(count, (8, LANES)), columns, segment.reshape(tiles, 1, TILE), cosine, sine,
    ) + spans


def body(
    codons,
    segments,
    targets,
    loss_mask,
    owner_map,
    step_count,
    block_weight,
    block_left,
    block_right,
    block_left_root,
    block_right_root,
    embedding_weight,
    table_left,
    table_right,
    table_left_root,
    table_right_root,
    norm_params,
    norm_moment,
    norm_second,
):
    everyone = ("dp", "tensor")
    vocab, width = embedding_weight.shape
    shards = lax.axis_size("tensor")
    owners = lax.axis_size("dp")
    slots = block_weight.shape[1]
    edge = block_weight.shape[-1]
    blocks = owner_map.shape[0]
    shard_width = width // shards

    known = on_known_slice(owners, shards, slots)
    sizes = (width, shards, shard_width, FF)
    project, outward, expand, contract, x0, h1, count, columns, seg_row, cosine, sine, *spans = gather_weights(
        block_weight[0], (codons, targets, loss_mask, segments), embedding_weight, norm_params, owner_map, known, sizes
    )
    query, keys, values = front(h1, project, cosine, sine)
    attended, lse = attend(*spans, query, keys, values, columns, seg_row)
    (h2, active, d_two, ghid, d_one, gatt, gx, head_grad, norm_grad) = middle_rows(
        x0, attended, columns, count, norm_params, embedding_weight,
        outward, expand, contract,
    )
    gproj = attend_back(
        *spans, query, keys, values, gatt, lse, columns, seg_row, cosine, sine
    )
    table_grad, norm_grad = tail_rows(
        columns, x0, gx, gproj, norm_params, project, head_grad, norm_grad
    )
    owner, slot = owner_map[None, :] // slots, owner_map[None, :] % slots
    device = owner * shards + jnp.arange(shards, dtype=jnp.int32)[:, None]
    if known:
        home = slot * (owners * shards) + device
    else:
        home = device * slots + slot
    grads = weight_grads(
        home.reshape(-1), h1, attended, h2, active, gproj, d_one, ghid, d_two, sizes, shards * blocks, edge
    )
    if known:
        owned, table_grad, norm_grad, stats = sum_everywhere(
            grads.reshape((slots,) + (2,) * 5 + grads.shape[1:]),
            table_grad, norm_grad, count,
        )
    else:
        owned = lax.psum_scatter(grads, everyone, scatter_dimension=0, tiled=True)
        owned = jnp.stack([jnp.concatenate(from_dense(owned[b]), 0) for b in range(slots)])
        table_grad, norm_grad, square_sum = lax.psum((table_grad, norm_grad), everyone) + (
            lax.psum(jnp.sum(owned * owned), everyone),
        )
        vectors = norm_grad[:6]
        square_sum = square_sum + jnp.sum(table_grad * table_grad) + jnp.sum(vectors * vectors)
        stats = statistics(square_sum, jnp.sum(norm_grad[6]), count[:1, :1])
    loss_value, grad_norm = stats[2, 0], stats[1, 0]
    step_value = step_count.astype(F32)
    corrections = jnp.stack([1.0 - FIRST_BETA**step_value, 1.0 - SECOND_BETA**step_value]).reshape(1, 2)
    (
        table_clipped, table_left_new, table_right_new, table_weight_new,
        norm_clipped, moment_new, second_new, params_new,
        block_grad, new_left, new_right, new_weight,
    ) = update_all(
        (
            corrections, stats, table_grad, table_left, table_left_root, embedding_weight,
            norm_grad, norm_moment, norm_second, norm_params,
        ),
        table_right,
        table_right_root,
        (owned, block_left[0], block_right[0], block_left_root[0], block_right_root[0], block_weight[0]),
    )
    return (
        loss_value,
        grad_norm,
        block_grad[None],
        new_left[None],
        new_right[None],
        new_weight[None],
        table_clipped,
        table_left_new,
        table_right_new,
        table_weight_new,
        norm_clipped,
        moment_new,
        second_new,
        params_new,
    )


def solution(mesh):
    in_specs = (
        P(("dp", "tensor"), None),
        P("dp", None),
        P(("dp", "tensor"), None),
        P(("dp", "tensor"), None),
        P(),
        P(),
        P("tensor", "dp", None, None),
        P("tensor", "dp", None, None),
        P("tensor", "dp", None, None),
        P("tensor", "dp", None, None),
        P("tensor", "dp", None, None),
        P(),
        P(),
        P(),
        P(),
        P(),
        P(),
        P(),
        P(),
    )
    out_specs = (
        P(),
        P(),
        P("tensor", "dp", None, None),
        P("tensor", "dp", None, None),
        P("tensor", "dp", None, None),
        P("tensor", "dp", None, None),
        P(),
        P(),
        P(),
        P(),
        P(),
        P(),
        P(),
        P(),
    )
    return jax.shard_map(body, mesh=mesh, in_specs=in_specs, out_specs=out_specs, check_vma=False)
```

```python
import functools
import math

import jax
import jax.numpy as jnp
from jax import lax
from jax.experimental import pallas as pl
from jax.experimental.pallas import tpu as pltpu
from jax.sharding import PartitionSpec as P

FF = 3072
HS = 64

CLIP_LEVEL = 0.005
STAT_DECAY = 0.5
MATRIX_RATE = 0.03
WEIGHT_DECAY = 0.01
VECTOR_RATE = 0.2
FIRST_BETA = 0.9
SECOND_BETA = 0.999
ADAM_EPSILON = 1e-08
NORM_EPSILON = 1e-05
ROOT_EPSILON = 1e-06
MASK_VALUE = -1e30
ROTARY_BASE = 10000.0

LANES = 128
PACK = 4
VMEM_LIMIT = 60 * 1024 * 1024
BF16 = jnp.bfloat16
F32 = jnp.float32


def dot(left, right):
    return lax.dot_general(left, right, (((1,), (0,)), ((), ())), preferred_element_type=F32)


def dot_nt(left, right):
    return lax.dot_general(left, right, (((1,), (1,)), ((), ())), preferred_element_type=F32)


def dot_tn(left, right):
    return lax.dot_general(left, right, (((0,), (0,)), ((), ())), preferred_element_type=F32)


def split_three(values):
    high = values.astype(BF16)
    rest = values - high.astype(F32)
    middle = rest.astype(BF16)
    low = (rest - middle.astype(F32)).astype(BF16)
    return high, middle, low


def params(**more):
    return pltpu.CompilerParams(vmem_limit_bytes=VMEM_LIMIT, **more)


def whole(shape):
    return pl.BlockSpec(shape, lambda *_: (0,) * len(shape))


def dense_rows(edge):
    return edge * edge // LANES


def to_dense(block):
    half, quarter = block.shape[0] // 2, block.shape[0] // 4
    wide, slim = LANES // 2, LANES // 4
    return (
        jnp.concatenate([block[:half, :wide], block[half:, :wide]], axis=1),
        jnp.concatenate(
            [block[i * quarter : (i + 1) * quarter, wide : wide + slim] for i in range(4)], axis=1
        ),
    )


def from_dense(dense):
    half = dense.shape[0] * 2 // 3
    quarter = half // 2
    wide, slim = LANES // 2, LANES // 4
    quarters = []
    for i in range(4):
        start = i % 2 * quarter
        lanes = slice(i // 2 * wide, (i // 2 + 1) * wide)
        quarters.append(
            jnp.concatenate(
                [dense[start : start + quarter, lanes], dense[half:, i * slim : (i + 1) * slim]], axis=1
            )
        )
    return quarters


def unpack_group(group, edge):
    return [group[:, edge * j : edge * (j + 1)] for j in range(PACK)]


def block_index(shard, block, blocks):
    return shard * blocks + block


def matrix_rows(row, width, shards, shard_width, hidden_width, edge):
    model = width // edge
    wide = shard_width // edge
    tall = hidden_width // shards // edge
    starts = [0, 3 * wide * model, 4 * wide * model, 4 * wide * model + model * tall]
    blocks = starts[3] + tall * model
    project = [
        block_index(c % (shards * wide) // wide, row * 3 * wide + c // (shards * wide) * wide + c % wide, blocks)
        for c in range(3 * model)
    ]
    outward = [
        block_index(row // wide, starts[1] + row % wide * model + c, blocks) for c in range(model)
    ]
    expand = [
        block_index(c // tall, starts[2] + row * tall + c % tall, blocks) for c in range(shards * tall)
    ]
    steps = model
    each = shards * tall // steps
    contract = []
    for q in range(each):
        r = row * each + q
        contract.append(
            [block_index(r // tall, starts[3] + r % tall * model + c, blocks) for c in range(model)]
        )
    return [project], [outward], [expand], contract


def assemble_rows(tables, place_ref, store, targets, edge):
    strip = PACK * edge
    for block_rows, target in zip(tables, targets):
        for r, places in enumerate(block_rows):
            for c in range(len(places) // PACK):
                blocks = [store[place_ref[places[c * PACK + j]]][:, :edge] for j in range(PACK)]
                target[r * edge : (r + 1) * edge, c * strip : (c + 1) * strip] = jnp.concatenate(
                    blocks, axis=1
                )


def unpack_rows(store, first, group, offset, edge):
    pieces = unpack_group(group, edge)
    for j in range(PACK):
        store[first + j, offset : offset + group.shape[0], :edge] = pieces[j]


def assemble_kernel(
    place_ref, in_ref, project_ref, outward_ref, expand_ref, contract_ref, store, *, load_steps, sizes
):
    step = pl.program_id(0)
    per_step, edge, _ = in_ref.shape

    @pl.when(step < load_steps)
    def _():
        def unpack(g, carry):
            unpack_rows(store, (step * per_step + g) * PACK, in_ref[g], 0, edge)
            return carry

        lax.fori_loop(0, per_step, unpack, 0)

    @pl.when(step >= load_steps)
    def _():
        tables = matrix_rows(step - load_steps, *sizes, edge)
        assemble_rows(tables, place_ref, store, (project_ref, outward_ref, expand_ref, contract_ref), edge)


def matrix_shapes(width, hidden_width):
    return (
        jax.ShapeDtypeStruct((width, 3 * width), BF16),
        jax.ShapeDtypeStruct((width, width), BF16),
        jax.ShapeDtypeStruct((width, hidden_width), BF16),
        jax.ShapeDtypeStruct((hidden_width, width), BF16),
    )


def assemble(place, packed, sizes):
    groups, edge, strip = packed.shape
    width, _, _, hidden_width = sizes
    per_step = 16
    load_steps = groups // per_step
    fill_steps = width // edge
    tall = hidden_width // fill_steps

    def late(step, *_):
        return (jnp.maximum(step - load_steps, 0), 0)

    return pl.pallas_call(
        functools.partial(assemble_kernel, load_steps=load_steps, sizes=sizes),
        out_shape=matrix_shapes(width, hidden_width),
        grid_spec=pltpu.PrefetchScalarGridSpec(
            num_scalar_prefetch=1,
            grid=(load_steps + fill_steps,),
            in_specs=[
                pl.BlockSpec(
                    (per_step, edge, strip), lambda s, *_: (jnp.minimum(s, load_steps - 1), 0, 0)
                )
            ],
            out_specs=[
                pl.BlockSpec((edge, 3 * width), late),
                pl.BlockSpec((edge, width), late),
                pl.BlockSpec((edge, hidden_width), late),
                pl.BlockSpec((tall, width), late),
            ],
            scratch_shapes=[pltpu.VMEM((groups * PACK, edge, LANES), BF16)],
        ),
        compiler_params=params(),
        name="assemble_weights",
    )(place, packed)


def norm_parts(values):
    scale = 1.0 / values.shape[-1]
    center = values - jnp.sum(values, -1, keepdims=True) * scale
    spread = jnp.sum(center * center, -1, keepdims=True) * scale
    inverse = lax.rsqrt(spread + NORM_EPSILON)
    return center * inverse, inverse


def norm_back(grad, unit, inverse, gain):
    scale = 1.0 / grad.shape[-1]
    inner = grad * gain
    mean_one = jnp.sum(inner, -1, keepdims=True) * scale
    mean_two = jnp.sum(inner * unit, -1, keepdims=True) * scale
    return (inner - mean_one - unit * mean_two) * inverse


def turn(values, cosine, sine):
    lane = lax.broadcasted_iota(jnp.int32, values.shape, 1)
    half = HS // 2
    ahead = pltpu.roll(values, LANES - half, 1)
    behind = pltpu.roll(values, half, 1)
    other = jnp.where(lane % HS < half, ahead, behind)
    return values * cosine + other * sine


def embed_rows(codon_col, table, gain, bias):
    rows, (vocab, width) = codon_col.shape[0], table.shape
    index = lax.broadcasted_iota(jnp.int32, (rows, vocab), 1)
    hot = jnp.where(codon_col == index, 1.0, 0.0).astype(BF16)
    high, middle, low = split_three(table)
    embedded = ((dot(hot, high) + dot(hot, middle)) + dot(hot, low)) * math.sqrt(width)
    unit, _ = norm_parts(embedded)
    return embedded, (unit * gain + bias).astype(BF16)


def front_kernel(h_ref, project_ref, cos_ref, sin_ref, q_ref, k_ref, v_ref):
    width = h_ref.shape[1]
    normed = h_ref[...]
    cosine = cos_ref[...]
    sine = sin_ref[...]
    for part, out_ref in ((0, q_ref), (1, k_ref), (2, v_ref)):
        values = dot(normed, project_ref[:, part * width : (part + 1) * width])
        for c in range(width // LANES):
            piece = values[:, c * LANES : (c + 1) * LANES]
            if part < 2:
                piece = turn(piece, cosine, sine)
            if part == 0:
                piece = piece * HS ** (-0.5)
            out_ref[:, c * LANES : (c + 1) * LANES] = piece.astype(BF16)


def front(normed, project, cosine, sine):
    length, width = normed.shape
    rows = 256
    spec = pl.BlockSpec((rows, width), lambda i: (i, 0))
    narrow = pl.BlockSpec((rows, LANES), lambda i: (i, 0))
    return pl.pallas_call(
        front_kernel,
        out_shape=(jax.ShapeDtypeStruct((length, width), BF16),) * 3,
        grid=(length // rows,),
        in_specs=[spec, whole(project.shape), narrow, narrow],
        out_specs=(spec,) * 3,
        compiler_params=params(),
        name="project_rotate",
    )(normed, project, cosine, sine)


ROWS = 512
TILE = 128
SHORTEST = 3


def head_masks(rows):
    lane = lax.broadcasted_iota(jnp.int32, (rows, LANES), 1)
    return [lane // HS == h for h in range(LANES // HS)]


def same_segment(seg_col, seg_row_ref, first, count):
    row = jnp.concatenate([seg_row_ref[first + i] for i in range(count)], axis=1)
    return seg_col == row


def attend_kernel(low_ref, half_ref, q_ref, k_ref, v_ref, column_ref, seg_row_ref, o_ref, lse_ref):
    part = pl.program_id(1)
    first, half = low_ref[part], half_ref[part]
    masks = head_masks(ROWS)

    def run(count):
        query = q_ref[...]
        zero = jnp.zeros_like(query)
        span = pl.ds(pl.multiple_of(first * TILE, TILE), count * TILE)
        keys = k_ref[span, :]
        values = v_ref[span, :]
        same = same_segment(column_ref[:, 3:4], seg_row_ref, first, count)
        outs, logs = [], []
        for mask in masks:
            scores = jnp.where(same, dot_nt(jnp.where(mask, query, zero), keys), MASK_VALUE)
            top = jnp.max(scores, -1, keepdims=True)
            exps = jnp.exp(scores - top)
            total = jnp.sum(exps, -1, keepdims=True)
            probs = (exps * (1.0 / total)).astype(BF16)
            outs.append(dot(probs, values))
            logs.append(top + jnp.log(total))
        o_ref[...] = jnp.where(masks[0], outs[0], outs[1]).astype(BF16)
        lse_ref[...] = jnp.where(masks[0], logs[0], logs[1])

    for n in range(SHORTEST, k_ref.shape[0] // TILE // 2 + 1):
        pl.when(half == n)(functools.partial(run, 2 * n))


def attend(low, half, query, keys, values, columns, seg_row):
    length, width = query.shape
    tiles = length // TILE
    pairs = width // LANES
    column = pl.BlockSpec((ROWS, LANES), lambda p, i, *_: (i, p))
    full = pl.BlockSpec((length, LANES), lambda p, i, *_: (0, p))
    return pl.pallas_call(
        attend_kernel,
        out_shape=(
            jax.ShapeDtypeStruct((length, width), BF16),
            jax.ShapeDtypeStruct((length, width), F32),
        ),
        grid_spec=pltpu.PrefetchScalarGridSpec(
            num_scalar_prefetch=2,
            grid=(pairs, length // ROWS),
            in_specs=[
                column,
                full,
                full,
                pl.BlockSpec((ROWS, columns.shape[1]), lambda p, i, *_: (i, 0)),
                whole((tiles, 1, TILE)),
            ],
            out_specs=(column, column),
        ),
        compiler_params=params(),
        name="attend_forward",
    )(low, half, query, keys, values, columns, seg_row)


def attend_back_kernel(
    low_ref, half_ref, q_ref, k_ref, v_ref, g_ref, lse_ref, column_ref, seg_row_ref, cos_ref, sin_ref,
    out_ref, dk_acc, dv_acc,
):
    part = pl.program_id(1)
    parts = pl.num_programs(1)
    heads = LANES // HS
    first, half = low_ref[part], half_ref[part]
    masks = head_masks(ROWS)

    @pl.when(part == 0)
    def _():
        dk_acc[...] = jnp.zeros_like(dk_acc)
        dv_acc[...] = jnp.zeros_like(dv_acc)

    def run(count):
        query = q_ref[...]
        grad = g_ref[...]
        zero = jnp.zeros_like(query)
        span = pl.ds(pl.multiple_of(first * TILE, TILE), count * TILE)
        keys = k_ref[span, :]
        values = v_ref[span, :]
        same = same_segment(column_ref[:, 3:4], seg_row_ref, first, count)
        dq, dk, dv = [], [], []
        query_turned, grad_turned = query.T, grad.T
        for h, mask in enumerate(masks):
            own_query = jnp.where(mask, query, zero)
            own_grad = jnp.where(mask, grad, zero)
            scores = jnp.where(same, dot_nt(own_query, keys), MASK_VALUE)
            probs = jnp.exp(scores - lse_ref[:, h * HS : h * HS + 1])
            grad_probs = dot_nt(own_grad, values)
            delta = jnp.sum(probs * grad_probs, -1, keepdims=True)
            grad_scores = (probs * (grad_probs - delta)).astype(BF16)
            dq.append(dot(grad_scores, keys))
            rows = slice(h * HS, (h + 1) * HS)
            dk.append(dot(query_turned[rows], grad_scores))
            dv.append(dot(grad_turned[rows], probs.astype(BF16)))
        dk, dv = jnp.concatenate(dk, axis=0), jnp.concatenate(dv, axis=0)
        for i in range(count):
            lanes = slice(i * TILE, (i + 1) * TILE)
            dk_acc[first + i] += dk[:, lanes]
            dv_acc[first + i] += dv[:, lanes]
        rows = pl.ds(pl.multiple_of(part * ROWS, ROWS), ROWS)
        turned = turn(
            jnp.where(masks[0], dq[0], dq[1]) * HS ** (-0.5), cos_ref[rows, :], -sin_ref[rows, :]
        )
        out_ref[0, rows, :] = turned.astype(BF16)

    for n in range(SHORTEST, k_ref.shape[0] // TILE // 2 + 1):
        pl.when(half == n)(functools.partial(run, 2 * n))

    @pl.when(part == parts - 1)
    def _():
        for j in range(dk_acc.shape[0]):
            rows = slice(j * TILE, (j + 1) * TILE)
            out_ref[1, rows, :] = turn(dk_acc[j].T, cos_ref[rows, :], -sin_ref[rows, :]).astype(BF16)
            out_ref[2, rows, :] = dv_acc[j].T.astype(BF16)


def attend_back(low, half, query, keys, values, grad, lse, columns, seg_row, cosine, sine):
    length, width = query.shape
    tiles = length // TILE
    pairs = width // LANES
    column = pl.BlockSpec((ROWS, LANES), lambda p, i, *_: (i, p))
    full = pl.BlockSpec((length, LANES), lambda p, i, *_: (0, p))
    return pl.pallas_call(
        attend_back_kernel,
        out_shape=jax.ShapeDtypeStruct((3, length, width), BF16),
        grid_spec=pltpu.PrefetchScalarGridSpec(
            num_scalar_prefetch=2,
            grid=(pairs, length // ROWS),
            in_specs=[
                column,
                full,
                full,
                column,
                column,
                pl.BlockSpec((ROWS, columns.shape[1]), lambda p, i, *_: (i, 0)),
                whole((tiles, 1, TILE)),
                whole((length, LANES)),
                whole((length, LANES)),
            ],
            out_specs=pl.BlockSpec((3, length, LANES), lambda p, i, *_: (0, 0, p)),
            scratch_shapes=[
                pltpu.VMEM((tiles, LANES, TILE), F32),
                pltpu.VMEM((tiles, LANES, TILE), F32),
            ],
        ),
        compiler_params=params(),
        name="attend_backward",
    )(low, half, query, keys, values, grad, lse, columns, seg_row, cosine, sine)


INV_SQRT_TWO = 2.0 ** (-0.5)
INV_SQRT_TWO_PI = (2.0 * math.pi) ** (-0.5)


def middle_kernel(
    x_ref, att_ref, column_ref, count_ref, norm_ref, table_ref,
    outward_ref, expand_in, contract_in,
    h_ref, active_ref, d_two_ref, ghid_ref, d_one_ref, gatt_ref, gx_ref, head_ref, norm_grad_ref,
    slope, expand_ref, contract_ref, weight_sem,
):
    step = pl.program_id(0)
    rows, width = x_ref.shape
    vocab = table_ref.shape[0]
    ff = expand_ref.shape[1]
    part = width

    fetches = (
        pltpu.make_async_copy(expand_in, expand_ref, weight_sem.at[0]),
        pltpu.make_async_copy(contract_in, contract_ref, weight_sem.at[1]),
    )

    @pl.when(step == 0)
    def _():
        for fetch in fetches:
            fetch.start()
        head_ref[...] = jnp.zeros_like(head_ref)
        norm_grad_ref[...] = jnp.zeros_like(norm_grad_ref)

    middle = x_ref[...] + dot(att_ref[...], outward_ref[...])
    unit_two, inverse_two = norm_parts(middle)
    gain_two = norm_ref[2:3, :]
    normed_two = (unit_two * gain_two + norm_ref[3:4, :]).astype(BF16)
    h_ref[...] = normed_two

    @pl.when(step == 0)
    def _():
        for fetch in fetches:
            fetch.wait()

    def forward(c, total):
        cols = pl.ds(pl.multiple_of(c * part, part), part)
        hidden = dot(normed_two, expand_ref[:, cols])
        cumulative = 0.5 + 0.5 * lax.erf(hidden * INV_SQRT_TWO)
        active = (hidden * cumulative).astype(BF16)
        density = jnp.exp(-0.5 * hidden * hidden) * INV_SQRT_TWO_PI
        slope[:, cols] = cumulative + hidden * density
        active_ref[:, cols] = active
        return total + dot(active, contract_ref[cols, :])

    branch = lax.fori_loop(0, ff // part, forward, jnp.zeros((rows, width), F32))
    unit, inverse = norm_parts(middle + branch)
    gain = norm_ref[4:5, :]
    final = (unit * gain + norm_ref[5:6, :]).astype(BF16)
    table = table_ref[...].astype(BF16)
    logits = dot_nt(final, table)
    shifted = logits - jnp.max(logits, -1, keepdims=True)
    exps = jnp.exp(shifted)
    sums = jnp.sum(exps, -1, keepdims=True)
    hot = column_ref[:, 1:2] == lax.broadcasted_iota(jnp.int32, (rows, vocab), 1)
    mask = column_ref[:, 2:3].astype(F32)
    log_probs = shifted - jnp.log(sums)
    picked = jnp.sum(jnp.where(hot, log_probs, 0.0) * mask, 0, keepdims=True)
    norm_grad_ref[6:7, 0:vocab] -= picked
    glogits = ((jnp.exp(log_probs) - jnp.where(hot, 1.0, 0.0)) * (mask / count_ref[0:1, 0:1])).astype(BF16)
    head_ref[...] += dot_tn(glogits, final)
    gfinal = dot(glogits, table)
    norm_grad_ref[4:5, :] += jnp.sum(gfinal * unit, 0, keepdims=True)
    norm_grad_ref[5:6, :] += jnp.sum(gfinal, 0, keepdims=True)
    gx_two = norm_back(gfinal, unit, inverse, gain)
    d_two = gx_two.astype(BF16)
    d_two_ref[...] = d_two

    def backward(c, total):
        cols = pl.ds(pl.multiple_of(c * part, part), part)
        gactive = dot_nt(d_two, contract_ref[cols, :])
        ghid = (gactive * slope[:, cols]).astype(BF16)
        ghid_ref[:, cols] = ghid
        return total + dot_nt(ghid, expand_ref[:, cols])

    gh = lax.fori_loop(0, ff // part, backward, jnp.zeros((rows, width), F32))
    norm_grad_ref[2:3, :] += jnp.sum(gh * unit_two, 0, keepdims=True)
    norm_grad_ref[3:4, :] += jnp.sum(gh, 0, keepdims=True)
    gx_one = gx_two + norm_back(gh, unit_two, inverse_two, gain_two)
    gx_ref[...] = gx_one
    d_one = gx_one.astype(BF16)
    d_one_ref[...] = d_one
    gatt_ref[...] = dot_nt(d_one, outward_ref[...]).astype(BF16)


def middle_rows(x, att, columns, count, norm_params, table, outward, expand, contract):
    length, width = x.shape
    vocab = table.shape[0]
    ff = expand.shape[1]
    rows = 512
    narrow = pl.BlockSpec((rows, width), lambda i: (i, 0))
    broad = pl.BlockSpec((rows, ff), lambda i: (i, 0))
    column = pl.BlockSpec((rows, columns.shape[1]), lambda i: (i, 0))
    low = jax.ShapeDtypeStruct((length, width), BF16)
    low_broad = jax.ShapeDtypeStruct((length, ff), BF16)
    return pl.pallas_call(
        middle_kernel,
        out_shape=(
            low, low_broad, low, low_broad, low, low,
            jax.ShapeDtypeStruct((length, width), F32),
            jax.ShapeDtypeStruct((vocab, width), F32),
            jax.ShapeDtypeStruct((8, width), F32),
        ),
        grid=(length // rows,),
        in_specs=[
            narrow, narrow, column, whole(count.shape), whole(norm_params.shape), whole(table.shape),
            whole(outward.shape), pl.BlockSpec(memory_space=pl.ANY), pl.BlockSpec(memory_space=pl.ANY),
        ],
        out_specs=(
            narrow, broad, narrow, broad, narrow, narrow, narrow,
            whole((vocab, width)), whole((8, width)),
        ),
        scratch_shapes=[
            pltpu.VMEM((rows, ff), F32),
            pltpu.VMEM(expand.shape, BF16),
            pltpu.VMEM(contract.shape, BF16),
            pltpu.SemaphoreType.DMA((2,)),
        ],
        compiler_params=params(),
        name="middle_rows",
    )(x, att, columns, count, norm_params, table, outward, expand, contract)


def tail_part(codon_col, x, gx, gprojs, norm_params, project, table_acc, norm_acc):
    rows, width = x.shape
    vocab = table_acc.shape[0]
    gh = dot_nt(gprojs[0], project[:, 0:width])
    gh = gh + dot_nt(gprojs[1], project[:, width : 2 * width])
    gh = gh + dot_nt(gprojs[2], project[:, 2 * width : 3 * width])
    unit, inverse = norm_parts(x)
    norm_acc[0:1, :] += jnp.sum(gh * unit, 0, keepdims=True)
    norm_acc[1:2, :] += jnp.sum(gh, 0, keepdims=True)
    gx = gx + norm_back(gh, unit, inverse, norm_params[0:1, :])
    hot = jnp.where(codon_col == lax.broadcasted_iota(jnp.int32, (rows, vocab), 1), 1.0, 0.0)
    hot = hot.T.astype(BF16)
    high, middle, low = split_three(gx)
    total = dot(hot, high) + (dot(hot, middle) + dot(hot, low))
    table_acc[...] += total * math.sqrt(width)


def tail_kernel(
    column_ref, x_ref, gx_ref, gproj_ref, norm_ref, project_ref, head_ref, norm_in_ref,
    table_grad_ref, norm_grad_ref,
):
    @pl.when(pl.program_id(0) == 0)
    def _():
        table_grad_ref[...] = head_ref[...]
        norm_grad_ref[...] = norm_in_ref[...]

    tail_part(
        column_ref[:, 0:1], x_ref[...], gx_ref[...], gproj_ref, norm_ref, project_ref,
        table_grad_ref, norm_grad_ref,
    )


def tail_rows(columns, x, gx, gproj, norm_params, project, head, norm_in):
    length, width = x.shape
    rows = 256
    narrow = pl.BlockSpec((rows, width), lambda i: (i, 0))
    return pl.pallas_call(
        tail_kernel,
        out_shape=(
            jax.ShapeDtypeStruct(head.shape, F32),
            jax.ShapeDtypeStruct(norm_in.shape, F32),
        ),
        grid=(length // rows,),
        in_specs=[
            pl.BlockSpec((rows, columns.shape[1]), lambda i: (i, 0)),
            narrow, narrow, pl.BlockSpec((3, rows, width), lambda i: (0, i, 0)),
            whole(norm_params.shape), whole(project.shape), whole(head.shape), whole(norm_in.shape),
        ],
        out_specs=(whole(head.shape), whole(norm_in.shape)),
        compiler_params=params(),
        name="tail_rows",
    )(columns, x, gx, gproj, norm_params, project, head, norm_in)


def weight_grad_kernel(
    place_ref, h_one, att, h_two, active, gproj, d_one, ghid, d_two, out_ref,
    left, right, turned, buf, left_sem, right_sem, out_sem, *, sizes, edge,
):
    width, shards, shard_width, hidden_width = sizes
    model = width // edge
    wide = shard_width // edge
    tall = hidden_width // shards // edge
    starts = [0, 3 * wide * model, 4 * wide * model, 4 * wide * model + model * tall]
    blocks = starts[3] + tall * model
    part = hidden_width // shards
    columns = lambda ref, t: ref.at[:, pl.ds(t * part, part)]
    lefts = [h_one, att, h_two] + [columns(active, t) for t in range(shards)]
    rights = [gproj.at[i] for i in range(3)] + [d_one] + [columns(ghid, t) for t in range(shards)] + [d_two]
    plan = [(0, 0), (0, 1), (0, 2), (1, 3)]
    plan += [(2, 4 + t) for t in range(shards)]
    plan += [(3 + t, 4 + shards) for t in range(shards)]
    step = pl.program_id(0)
    slot = step % 2
    count = buf.shape[1]

    def fetches(n):
        found = []
        if n == 0 or plan[n][0] != plan[n - 1][0]:
            which = plan[n][0] % 2
            found.append(pltpu.make_async_copy(lefts[plan[n][0]], left.at[which], left_sem.at[which]))
        if n == 0 or plan[n][1] != plan[n - 1][1]:
            which = plan[n][1] % 2
            found.append(pltpu.make_async_copy(rights[plan[n][1]], right.at[which], right_sem.at[which]))
        return found

    def drain(which):
        pltpu.make_async_copy(buf.at[which], out_ref.at[pl.ds(0, count)], out_sem.at[which]).wait()

    for n in range(len(plan)):

        @pl.when(step == n)
        def _():
            if n == 0:
                for copy in fetches(0):
                    copy.start()
            for copy in fetches(n):
                copy.wait()
            if n + 1 < len(plan):
                for copy in fetches(n + 1):
                    copy.start()
            if n == 0 or plan[n][0] != plan[n - 1][0]:
                turned[...] = left[plan[n][0] % 2].T

    @pl.when(step >= 2)
    def _():
        drain(slot)

    which = jnp.minimum(step, 4 + shards) % 2
    rows = turned.shape[0] // 2
    for half in range(2):
        result = dot(turned[half * rows : (half + 1) * rows], right[which])
        for i in range(rows // edge):
            r = half * (rows // edge) + i
            for c in range(model):
                block = result[i * edge : (i + 1) * edge, c * edge : (c + 1) * edge]
                upper, lower = to_dense(block)
                buf[slot, r * model + c, : edge // 2] = upper
                buf[slot, r * model + c, edge // 2 :] = lower
            for c in range(model):
                index = block_index(c // wide, r * 3 * wide + step * wide + c % wide, blocks)
                index = jnp.where(
                    step == 3, block_index(r // wide, starts[1] + r % wide * model + c, blocks), index
                )
                index = jnp.where(
                    step >= 4, block_index(step - 4, starts[2] + r * tall + c, blocks), index
                )
                index = jnp.where(
                    step >= 4 + shards,
                    block_index(step - 4 - shards, starts[3] + r * model + c, blocks),
                    index,
                )
                k = r * model + c
                pltpu.make_async_copy(
                    buf.at[slot, k], out_ref.at[place_ref[index]], out_sem.at[slot]
                ).start()

    @pl.when(step == len(plan) - 1)
    def _():
        drain(1 - slot)
        drain(slot)


def weight_grads(place, h_one, att, h_two, active, gproj, d_one, ghid, d_two, sizes, blocks, edge):
    length, width = h_one.shape
    shards = sizes[1]
    count = (width // edge) ** 2
    anywhere = pl.BlockSpec(memory_space=pl.ANY)
    return pl.pallas_call(
        functools.partial(weight_grad_kernel, sizes=sizes, edge=edge),
        out_shape=jax.ShapeDtypeStruct((blocks, dense_rows(edge), LANES), F32),
        grid_spec=pltpu.PrefetchScalarGridSpec(
            num_scalar_prefetch=1,
            grid=(4 + 2 * shards,),
            in_specs=[anywhere] * 8,
            out_specs=anywhere,
            scratch_shapes=[
                pltpu.VMEM((2, length, width), BF16),
                pltpu.VMEM((2, length, width), BF16),
                pltpu.VMEM((width, length), BF16),
                pltpu.VMEM((2, count, dense_rows(edge), LANES), F32),
                pltpu.SemaphoreType.DMA((2,)),
                pltpu.SemaphoreType.DMA((2,)),
                pltpu.SemaphoreType.DMA((2,)),
            ],
        ),
        compiler_params=params(),
        name="weight_gradients",
    )(place, h_one, att, h_two, active, gproj, d_one, ghid, d_two)


CORE, NEAR_Y, NEAR_X, NEAR_Z, FAR_Z = range(5)
AXIS_STRIDE = {CORE: 1, NEAR_Y: 2, NEAR_X: 4, NEAR_Z: 8, FAR_Z: 16}
NATURAL = (FAR_Z, NEAR_Z, NEAR_X, NEAR_Y)
CHUNK_AXES = (
    (NEAR_X, NEAR_Y, NEAR_Z, FAR_Z),
    (NEAR_Y, NEAR_X, NEAR_Z, FAR_Z),
    (NEAR_X, NEAR_Y, NEAR_Z, FAR_Z),
    (NEAR_Y, NEAR_X, NEAR_Z, FAR_Z),
    (NEAR_Z, NEAR_X, NEAR_Y, FAR_Z),
    (NEAR_Z, NEAR_Y, NEAR_X, FAR_Z),
)
PACK_GROUPS = 6
SUM_CHUNKS = PACK_GROUPS * PACK
SUM_SLOTS = 6
SUM_ORDER = (
    0, 2000, 10, 20, 2010, 30, 40, 50, 2020, 1000, 2001, 2030, 60, 1010, 2011, 2040, 70, 1020, 2021, 2050, 80, 1030,
    2031, 2060, 90, 1040, 2041, 2070, 100, 1050, 2051, 2080, 110, 1060, 2090, 120, 1070, 2100, 130, 1080, 2061,
    2110, 140, 1090, 2071, 2120, 150, 1100, 1001, 2130, 160, 1110, 1011, 2140, 170, 2012, 1120, 2150, 180, 2002,
    1130, 2101, 2160, 190, 1140, 1021, 2170, 200, 2111, 1150, 1031, 1041, 2180, 210, 1160, 2190, 220, 2032, 1170,
    1051, 2200, 230, 2022, 1180, 2042, 2210, 1190, 2052, 1012, 2220, 1200, 1002, 1061, 2230, 1210, 1071, 2072, 1220,
    2062, 1230, 2081, 2003, 1032, 2091, 2013, 1022, 1101, 1042, 2023, 1052, 2053, 1111, 2033, 2043, 1003, 2004,
    2161, 1072, 2102, 1013, 2014, 1062, 2112, 1023, 2024, 2063, 1053, 2054, 1004, 1043, 2044, 2121, 1033, 2034,
    2131, 2141, 1014, 2151, 1081, 1024, 2073, 1091, 1102, 1054, 1112, 1063, 2064, 1044, 2171, 1034, 1073, 2074,
    1064, 2221, 2092, 2082, 2113, 2103, 1161, 1121, 1074, 1131, 1141, 2132, 1151, 2122, 2152, 1113, 2114, 2142,
    1103, 2104, 1092, 2093, 1082, 2162, 2191, 1171, 2181, 2083, 1114, 1132, 2172, 2133, 1104, 1122, 1152, 1093,
    2094, 2123, 1142, 1221, 2201, 2143, 1083, 2084, 1162, 2163, 1133, 2134, 2153, 1094, 2231, 1172, 2211, 1123,
    2124, 1084, 2173, 1143, 2144, 1163, 2164, 1134, 1191, 1181, 2182, 2192, 1153, 2154, 2222, 1124, 1173, 2174,
    1144, 1201, 2202, 1164, 1154, 1211, 2212, 1231, 2232, 1182, 2183, 1174, 1192, 2193, 1222, 2223, 1202, 2203,
    1212, 2213, 1183, 2184, 1193, 2194, 1223, 1232, 2233, 2224, 1203, 1213, 2204, 2214, 1184, 1233, 2234, 1194,
    1224, 1204, 1214, 1234,
)
SMALL_ROWS = 1024
SMALL_AXES = (CORE, NEAR_X, NEAR_Y, NEAR_Z, FAR_Z)
MESH = pl.DeviceIdType.MESH


def on_known_slice(owners, shards, slots):
    return owners == 8 and shards == 4 and slots % PACK == 0 and slots == PACK * PACK_GROUPS


def bits_of(owner, shard):
    return {
        CORE: shard % 2,
        NEAR_Y: shard // 2,
        NEAR_X: owner % 2,
        NEAR_Z: owner // 2 % 2,
        FAR_Z: owner // 4,
    }


def own_bits():
    owner, shard = lax.axis_index("dp"), lax.axis_index("tensor")
    return owner, shard, bits_of(owner, shard)


def partner_of(axis, owner, shard, bits):
    if axis == CORE:
        return (owner, shard + 1 - 2 * bits[CORE])
    if axis == NEAR_Y:
        return (owner, shard + 2 - 4 * bits[NEAR_Y])
    step = {NEAR_X: 1, NEAR_Z: 2, FAR_Z: 4}[axis]
    return (owner + step - 2 * step * bits[axis], shard)


def axis_partners(owner, shard, bits):
    return [partner_of(axis, owner, shard, bits) for axis in range(5)]


def group_partners(owner, shard):
    same_owner = [(owner, (shard + i) % 4) for i in range(1, 4)]
    same_shard = [((owner + i) % 8, shard) for i in range(1, 8)]
    return same_owner, same_shard


def greet(partners):
    for partner in partners:
        pl.semaphore_signal(
            pltpu.get_barrier_semaphore(), inc=1, device_id=partner, device_id_type=MESH
        )


def await_greetings(count):
    pl.semaphore_wait(pltpu.get_barrier_semaphore(), count)


def total_of(values):
    return jnp.sum(jnp.sum(values, 1, keepdims=True), 0, keepdims=True)


def statistics(square_sum, loss_sum, count):
    norm = jnp.sqrt(square_sum)
    factor = CLIP_LEVEL / jnp.maximum(norm, CLIP_LEVEL)
    row = lax.broadcasted_iota(jnp.int32, (8, LANES), 0)
    return jnp.where(row == 0, factor, jnp.where(row == 1, norm, loss_sum / count))


def sum_kernel(
    grads_ref, table_ref, norm_ref, count_ref,
    owned_ref, table_out, norm_out, stats_out,
    inbuf, r0, r1, r2, r3, r4, small, s0, s1, s2, s3, s4, spread, square, near_squares, far_squares,
    in_sem, send_sem, recv_sem, small_send, small_recv, square_send, square_recv,
):
    owner, shard, bits = own_bits()
    received = (r0, r1, r2, r3, r4)

    def axes_of(c):
        return CHUNK_AXES[c % len(CHUNK_AXES)]

    def half_of(ref, c, k, bit):
        left = [axis for axis in NATURAL if axis not in axes_of(c)[:k]]
        place = left.index(axes_of(c)[k])
        return ref.at[(c,) + (slice(None),) * place + (bit,)]

    def fetch(c):
        slot = c % SUM_SLOTS
        return pltpu.make_async_copy(
            grads_ref.at[c, :, :, :, :, bits[CORE]], inbuf.at[slot], in_sem.at[slot]
        )

    same_owner, same_shard = group_partners(owner, shard)
    greet(same_owner + same_shard)
    await_greetings(len(same_owner) + len(same_shard))

    def chunk_send(c, k):
        if k == 0:
            axis, source = CORE, grads_ref.at[c, :, :, :, :, 1 - bits[CORE]]
        else:
            axis = axes_of(c)[k - 1]
            source = half_of(received[k - 1], c, k - 1, 1 - bits[axis])
        return pltpu.make_async_remote_copy(
            src_ref=source,
            dst_ref=received[k].at[c],
            send_sem=send_sem.at[c, k],
            recv_sem=recv_sem.at[c, k],
            device_id=partner_of(axis, owner, shard, bits),
            device_id_type=MESH,
        )

    def merge(c, k):
        chunk_send(c, k).wait_recv()
        if k == 0:
            fetch(c).wait()

            def add(e, carry):
                for y in range(2):
                    place = (e // 4, e // 2 % 2, e % 2, y)
                    r0[(c,) + place] = r0[(c,) + place] + inbuf[(c % SUM_SLOTS,) + place]
                return carry

            lax.fori_loop(0, 8, add, 0)
            return
        own = half_of(received[k - 1], c, k - 1, bits[axes_of(c)[k - 1]])
        if k < 4:

            def add(e, carry):
                received[k][c, e] = received[k][c, e] + own[e]
                return carry

            lax.fori_loop(0, 2, add, 0)
            return
        dense = r4[c] + own[...]
        quarter = owned_ref.shape[1] // 4
        for i, rows in enumerate(from_dense(dense)):
            owned_ref[c, i * quarter : (i + 1) * quarter, :] = rows
        parts = dense * dense
        total = square[...]
        for r in range(dense.shape[0] // 8):
            total = total + parts[r * 8 : (r + 1) * 8]
        square[...] = total

    vocab, width = table_ref.shape
    vectors = norm_ref.shape[0]
    columns = width // LANES
    small_parts = (s0, s1, s2, s3, s4)

    def small_fill():
        for c in range(columns):
            lanes = slice(c * LANES, (c + 1) * LANES)
            small[c * vocab : (c + 1) * vocab] = table_ref[:, lanes]
            start = columns * vocab + c * vectors
            small[start : start + vectors] = norm_ref[:, lanes]
        used = columns * (vocab + vectors)
        small[used:] = jnp.zeros((SMALL_ROWS - used, LANES), F32)

    def small_base(k):
        base = 0
        for i in range(k):
            base = base + (SMALL_ROWS >> (i + 1)) * bits[SMALL_AXES[i]]
        return base

    def small_copy(k):
        rows = SMALL_ROWS >> (k + 1)
        start = pl.multiple_of(small_base(k) + rows * (1 - bits[SMALL_AXES[k]]), 8)
        return pltpu.make_async_remote_copy(
            src_ref=small.at[pl.ds(start, rows)],
            dst_ref=small_parts[k],
            send_sem=small_send.at[k],
            recv_sem=small_recv.at[k],
            device_id=partner_of(SMALL_AXES[k], owner, shard, bits),
            device_id_type=MESH,
        )

    def small_merge(k):
        small_copy(k).wait_recv()
        rows = SMALL_ROWS >> (k + 1)
        mine = pl.ds(pl.multiple_of(small_base(k + 1), 8), rows)
        if k < 4:
            small[mine, :] = small[mine, :] + small_parts[k][...]
            small_copy(k + 1).start()
        else:
            spread[mine, :] = small[mine, :] + small_parts[k][...]
            spread_copy(4).start()

    def spread_copy(k):
        rows = SMALL_ROWS >> (k + 1)
        here = pl.ds(pl.multiple_of(small_base(k + 1), 8), rows)
        return pltpu.make_async_remote_copy(
            src_ref=spread.at[here],
            dst_ref=spread.at[here],
            send_sem=small_send.at[5 + k],
            recv_sem=small_recv.at[5 + k],
            device_id=partner_of(SMALL_AXES[k], owner, shard, bits),
            device_id_type=MESH,
        )

    def spread_next(k):
        spread_copy(k).wait_recv()
        if k > 0:
            spread_copy(k - 1).start()
        else:
            for c in range(columns):
                lanes = slice(c * LANES, (c + 1) * LANES)
                table_out[:, lanes] = spread[c * vocab : (c + 1) * vocab]
                start = columns * vocab + c * vectors
                norm_out[:, lanes] = spread[start : start + vectors]

    square[...] = jnp.zeros_like(square)
    small_fill()
    small_copy(0).start()
    extra = []
    extra += [functools.partial(small_merge, k) for k in range(5)]
    extra += [functools.partial(spread_next, k) for k in range(4, -1, -1)]
    for position, code in enumerate(SUM_ORDER):
        c, k = code % 1000 // 10, code % 10
        if code < 1000:
            fetch(c).start()
        elif code < 2000:
            merge(c, k)
        else:
            chunk_send(c, k).start()
        if position >= 70 and position % 16 == 0 and extra:
            extra.pop(0)()
    while extra:
        extra.pop(0)()

    def exchange(partners, mine, slots, first):
        slots[mine] = square[...]
        copies = [
            pltpu.make_async_remote_copy(
                src_ref=square,
                dst_ref=slots.at[mine],
                send_sem=square_send.at[first + i],
                recv_sem=square_recv.at[first + i],
                device_id=partner,
                device_id_type=MESH,
            )
            for i, partner in enumerate(partners)
        ]
        for copy in copies:
            copy.start()
        for copy in copies:
            copy.wait()
        value = slots[0]
        for i in range(1, slots.shape[0]):
            value = value + slots[i]
        return value

    square[...] = exchange(same_owner, shard, near_squares, 0)
    value = exchange(same_shard, owner, far_squares, 3)
    table_sum, vectors_sum = table_out[...], norm_out[0:6, :]
    stats_out[...] = statistics(
        total_of(value) + total_of(table_sum * table_sum) + total_of(vectors_sum * vectors_sum),
        total_of(norm_out[6:7, :]),
        count_ref[0:1, 0:1],
    )

    for c in range(SUM_CHUNKS):
        for k in range(5):
            chunk_send(c, k).wait_send()
    for k in range(5):
        small_copy(k).wait_send()
        spread_copy(k).wait_send()


def sum_everywhere(grads, table_grad, norm_grad, count):
    chunks = grads.shape[0]
    block = grads.shape[-2:]
    edge = math.isqrt(block[0] * block[1])
    group = lambda count: pltpu.VMEM((chunks,) + (2,) * count + block, F32)
    small = lambda rows: pltpu.VMEM((rows, LANES), F32)
    anywhere, inside = pl.BlockSpec(memory_space=pl.ANY), pl.BlockSpec(memory_space=pltpu.VMEM)
    return pl.pallas_call(
        sum_kernel,
        out_shape=(
            jax.ShapeDtypeStruct((chunks, edge, edge), F32),
            jax.ShapeDtypeStruct(table_grad.shape, F32),
            jax.ShapeDtypeStruct(norm_grad.shape, F32),
            jax.ShapeDtypeStruct((8, LANES), F32),
        ),
        in_specs=[anywhere, inside, inside, inside],
        out_specs=(inside,) * 4,
        scratch_shapes=[
            pltpu.VMEM((SUM_SLOTS,) + (2,) * 4 + block, F32),
            group(4), group(3), group(2), group(1), group(0),
            small(SMALL_ROWS), small(512), small(256), small(128), small(64), small(32), small(SMALL_ROWS),
            pltpu.VMEM((8, LANES), F32),
            pltpu.VMEM((4, 8, LANES), F32),
            pltpu.VMEM((8, 8, LANES), F32),
            pltpu.SemaphoreType.DMA((SUM_SLOTS,)),
            pltpu.SemaphoreType.DMA((SUM_CHUNKS, 5)),
            pltpu.SemaphoreType.DMA((SUM_CHUNKS, 5)),
            pltpu.SemaphoreType.DMA((10,)),
            pltpu.SemaphoreType.DMA((10,)),
            pltpu.SemaphoreType.DMA((10,)),
            pltpu.SemaphoreType.DMA((10,)),
        ],
        compiler_params=pltpu.CompilerParams(
            vmem_limit_bytes=66_000_000, collective_id=1, has_side_effects=True
        ),
        name="sum_gradients",
    )(grads, table_grad, norm_grad, count)


GATHER_AXES = (
    (NEAR_Z, NEAR_Y, NEAR_X, FAR_Z),
    (NEAR_X, NEAR_Y, NEAR_Z, FAR_Z),
    (NEAR_Y, NEAR_X, FAR_Z, NEAR_Z),
    (NEAR_Z, NEAR_Y, FAR_Z, NEAR_X),
    (NEAR_X, NEAR_Z, FAR_Z, NEAR_Y),
    (NEAR_Y, NEAR_X, FAR_Z, NEAR_Z),
)
EMBED_ROWS = 256
HALVES = 2
GATHER_CHUNKS = PACK_GROUPS * HALVES
GATHER_ORDER = (
    2030, 2090, 2100, 2040, 2080, 2060, 2020, 2070, 2110, 2010, 1080, 1030, 1100, 1090, 1040, 1060, 2061, 2050,
    2081, 1020, 1070, 2071, 1110, 1010, 2021, 1061, 2062, 1050, 2011, 1081, 2082, 2031, 1071, 2072, 1062, 2063,
    1021, 2022, 2101, 1011, 2012, 1082, 2083, 1072, 2073, 1031, 2032, 2111, 1022, 1101, 2000, 2023, 2091, 1012,
    2013, 1111, 2112, 1000, 2001, 2041, 1073, 2074, 2102, 1063, 2064, 1091, 2092, 1074, 2051, 1032, 1064, 1041,
    1001, 2033, 1112, 2113, 1102, 2103, 1051, 2052, 1083, 2084, 1013, 2014, 2002, 1084, 2042, 1092, 1014, 1033,
    2034, 1023, 2024, 2093, 1052, 2053, 1034, 1042, 2043, 1024, 1103, 2104, 1002, 2003, 1104, 1093, 2094, 1113,
    2114, 1043, 2044, 1094, 1114, 1053, 2054, 1044, 1003, 2004, 1054, 1004,
)


def gather_entry(group, bits):
    first, second, third, fourth = GATHER_AXES[group]
    return 16 * bits[CORE] + 8 * bits[first] + 4 * bits[second] + 2 * bits[third] + bits[fourth]


def gather_kernel(
    place_ref, own_ref, codon_ref, target_ref, mask_ref, segments_ref, table_ref, norm_ref,
    project_out, outward_out, expand_out, contract_out, x_out, h_out,
    count_ref, column_ref, seg_row_ref, cos_ref, sin_ref, low_ref, half_ref,
    packed, held, store, project, outward, expand, contract, x_rows, h_rows, counts,
    own_sem, send_sem, recv_sem, count_send, count_recv, out_sem, row_sem, *, sizes,
):
    owner, shard, bits = own_bits()
    edge = own_ref.shape[1]
    rows = edge // HALVES
    devices = held.shape[1]

    def place(c):
        return gather_entry(c % PACK_GROUPS, bits)

    def own_part(c):
        return packed.at[c % PACK_GROUPS, pl.ds(c // PACK_GROUPS * rows, rows)]

    def keep(c):
        return pltpu.make_async_copy(own_part(c), held.at[c, place(c)], own_sem.at[c])

    def move(c, k):
        axis = CORE if k == 4 else GATHER_AXES[c % PACK_GROUPS][3 - k]
        if k == 0:
            source = own_part(c)
            target = held.at[c, place(c)]
        else:
            size = 1 << k
            base = place(c) // size * size
            source = held.at[c, pl.ds(base, size)]
            target = source
        return pltpu.make_async_remote_copy(
            src_ref=source,
            dst_ref=target,
            send_sem=send_sem.at[c, k],
            recv_sem=recv_sem.at[c, k],
            device_id=partner_of(axis, owner, shard, bits),
            device_id_type=MESH,
        )

    def count_copy(k):
        return pltpu.make_async_remote_copy(
            src_ref=counts.at[k],
            dst_ref=counts.at[5 + k],
            send_sem=count_send.at[k],
            recv_sem=count_recv.at[k],
            device_id=partner_of(SMALL_AXES[k], owner, shard, bits),
            device_id_type=MESH,
        )

    greet(axis_partners(owner, shard, bits))
    for g in range(PACK_GROUPS):
        blocks = [own_ref[g * PACK + b].astype(BF16) for b in range(PACK)]
        packed[g] = jnp.concatenate(blocks, axis=1)
    total = jnp.broadcast_to(jnp.sum(mask_ref[...].astype(F32), keepdims=True), count_ref.shape)
    counts[0] = total
    await_greetings(5)
    for c in range(GATHER_CHUNKS):
        keep(c).start()

    def unpack(c):
        group = c % PACK_GROUPS
        offset = c // PACK_GROUPS * rows

        def body(e, carry):
            unpack_rows(store, (group * devices + e) * PACK, held[c, e], offset, edge)
            return carry

        lax.fori_loop(0, devices, body, 0, unroll=4)

    def describe_rows():
        length = codon_ref.shape[1]
        segment = segments_ref[pl.ds(shard, 1), :]
        stacked = jnp.concatenate([codon_ref[...], target_ref[...], mask_ref[...], segment], axis=0)
        filler = jnp.zeros((LANES - stacked.shape[0], LANES), jnp.int32)
        for i in range(length // LANES):
            lanes = slice(i * LANES, (i + 1) * LANES)
            column_ref[lanes, :] = jnp.concatenate([stacked[:, lanes], filler], axis=0).T
            seg_row_ref[i] = segment[:, lanes]
        for i in range(length // ROWS):
            first = segment[:, i * ROWS : i * ROWS + 1]
            final = segment[:, (i + 1) * ROWS - 1 : (i + 1) * ROWS]
            before = jnp.sum(jnp.where(segment < first, 1.0, 0.0)).astype(jnp.int32)
            until = jnp.sum(jnp.where(segment <= final, 1.0, 0.0)).astype(jnp.int32)
            low_ref[i], half_ref[i] = span_of(before, until, length // TILE)

    def rotary_rows(i, carry):
        rows = pl.ds(pl.multiple_of(i * LANES, LANES), LANES)
        place = lax.broadcasted_iota(jnp.int32, (LANES, LANES), 0) + i * LANES
        lane = lax.broadcasted_iota(jnp.int32, (LANES, LANES), 1)
        cos_ref[rows, :], sin_ref[rows, :] = rotary_of(place, lane)
        return carry

    def embed(i, carry):
        rows = pl.ds(pl.multiple_of(i * EMBED_ROWS, EMBED_ROWS), EMBED_ROWS)
        x_rows[rows, :], h_rows[rows, :] = embed_rows(
            column_ref[rows, 0:1], table_ref[...], norm_ref[0:1, :], norm_ref[1:2, :]
        )
        return carry

    row_copies = (
        pltpu.make_async_copy(x_rows, x_out, row_sem.at[0]),
        pltpu.make_async_copy(h_rows, h_out, row_sem.at[1]),
    )
    stage = 0
    for position, code in enumerate(GATHER_ORDER):
        c, k = code % 1000 // 10, code % 10
        if code >= 2000:
            if k == 1:
                keep(c).wait()
            move(c, k).start()
        else:
            move(c, k).wait_recv()
            if k == 4:
                unpack(c)
        if position == 16:
            describe_rows()
        if position == 45:
            lax.fori_loop(0, cos_ref.shape[0] // LANES, rotary_rows, 0)
        if position == 80:
            lax.fori_loop(0, x_rows.shape[0] // EMBED_ROWS, embed, 0)
            for copy in row_copies:
                copy.start()
        if position == 0:
            count_copy(0).start()
        elif position % 12 == 0 and stage < 5:
            count_copy(stage).wait_recv()
            total = counts[stage] + counts[5 + stage]
            stage += 1
            if stage < 5:
                counts[stage] = total
                count_copy(stage).start()
    count_ref[...] = jnp.maximum(total, 1.0)

    steps = project.shape[0] // edge
    staged = ((project, project_out), (outward, outward_out), (expand, expand_out), (contract, contract_out))

    def body(row, carry):
        tables = matrix_rows(row, *sizes, edge)
        targets, copies = [], []
        for n, (inside, outside) in enumerate(staged):
            size = inside.shape[0] // steps
            part = pl.ds(pl.multiple_of(row * size, size), size)
            targets.append(inside.at[part])
            copies.append(pltpu.make_async_copy(inside.at[part], outside.at[part], out_sem.at[n]))
        assemble_rows(tables, place_ref, store, targets, edge)
        for copy in copies:
            copy.start()
        return carry

    lax.fori_loop(0, steps, body, 0)
    for c in range(GATHER_CHUNKS):
        for k in range(5):
            move(c, k).wait_send()
    for k in range(5):
        count_copy(k).wait_send()
    for n, (inside, outside) in enumerate(staged):
        pltpu.make_async_copy(inside, outside, out_sem.at[n]).wait()
    for copy in row_copies:
        copy.wait()


def gather_everywhere(place, own, rows, table, norm_params, devices, sizes):
    slots, edge, _ = own.shape
    width, _, _, hidden_width = sizes
    strip = PACK * edge
    shapes = matrix_shapes(width, hidden_width)
    length = rows[0].shape[1]
    inside, scalars = pl.BlockSpec(memory_space=pltpu.VMEM), pl.BlockSpec(memory_space=pltpu.SMEM)
    return pl.pallas_call(
        functools.partial(gather_kernel, sizes=sizes),
        out_shape=shapes
        + (
            jax.ShapeDtypeStruct((length, width), F32),
            jax.ShapeDtypeStruct((length, width), BF16),
            jax.ShapeDtypeStruct((8, LANES), F32),
            jax.ShapeDtypeStruct((length, LANES), jnp.int32),
            jax.ShapeDtypeStruct((length // TILE, 1, TILE), jnp.int32),
            jax.ShapeDtypeStruct((length, LANES), F32),
            jax.ShapeDtypeStruct((length, LANES), F32),
            jax.ShapeDtypeStruct((length // ROWS,), jnp.int32),
            jax.ShapeDtypeStruct((length // ROWS,), jnp.int32),
        ),
        in_specs=[scalars] + [inside] * 7,
        out_specs=(pl.BlockSpec(memory_space=pl.ANY),) * 6 + (inside,) * 5 + (scalars,) * 2,
        scratch_shapes=[
            pltpu.VMEM((PACK_GROUPS, edge, strip), BF16),
            pltpu.VMEM((GATHER_CHUNKS, devices, edge // HALVES, strip), BF16),
            pltpu.VMEM((devices * slots, edge, LANES), BF16),
            *[pltpu.VMEM(shape.shape, shape.dtype) for shape in shapes],
            pltpu.VMEM((length, width), F32),
            pltpu.VMEM((length, width), BF16),
            pltpu.VMEM((10, 8, LANES), F32),
            pltpu.SemaphoreType.DMA((GATHER_CHUNKS,)),
            pltpu.SemaphoreType.DMA((GATHER_CHUNKS, 5)),
            pltpu.SemaphoreType.DMA((GATHER_CHUNKS, 5)),
            pltpu.SemaphoreType.DMA((5,)),
            pltpu.SemaphoreType.DMA((5,)),
            pltpu.SemaphoreType.DMA((4,)),
            pltpu.SemaphoreType.DMA((2,)),
        ],
        compiler_params=params(collective_id=2, has_side_effects=True),
        name="gather_weights",
    )(place, own, *rows, table, norm_params)


def split_two(values):
    high = values.astype(BF16)
    return high, (values - high.astype(F32)).astype(BF16)


def dot_split(left, right, dims):
    product = lambda a, b: lax.dot_general(a, b, (dims, ((), ())), preferred_element_type=F32)
    return product(left[0], right[0]) + (product(left[0], right[1]) + product(left[1], right[0]))


def shampoo_parts(grad, left, right, left_root, right_root, weight):
    parts = split_two(grad)
    new_left = STAT_DECAY * left + (1.0 - STAT_DECAY) * dot_split(parts, parts, ((1,), (1,)))
    new_right = STAT_DECAY * right + (1.0 - STAT_DECAY) * dot_split(parts, parts, ((0,), (0,)))
    half = dot_split(split_two(left_root), parts, ((1,), (0,)))
    precond = dot_split(split_two(half), split_two(right_root), ((1,), (0,)))
    scale = 1.0 / (grad.shape[0] * grad.shape[1])
    mean = jnp.sum(jnp.sum(precond * precond, 1, keepdims=True), 0, keepdims=True) * scale
    scale_back = lax.rsqrt(mean + ROOT_EPSILON)
    new_weight = weight * (1.0 - MATRIX_RATE * WEIGHT_DECAY) - MATRIX_RATE * precond * scale_back
    return new_left, new_right, new_weight


TABLE_STEP = 3


def update_kernel(
    corrections_ref, stats_ref, table_grad_ref, table_left_ref, table_left_root_ref, table_ref,
    norm_grad_ref, moment_ref, second_ref, norm_ref, table_right_in, table_right_root_in,
    grad_ref, left_ref, right_ref, left_root_ref, right_root_ref, weight_ref,
    table_grad_out, table_left_out, table_right_out, table_out,
    norm_grad_out, moment_out, second_out, norm_out,
    grad_out, left_out, right_out, weight_out,
    grad_parts, precond, table_right, table_right_root, sem,
):
    step, steps = pl.program_id(0), pl.num_programs(0)
    factor = stats_ref[0:1, 0:1]
    fetches = (
        pltpu.make_async_copy(table_right_in, table_right, sem.at[0]),
        pltpu.make_async_copy(table_right_root_in, table_right_root, sem.at[1]),
    )
    keep = pltpu.make_async_copy(table_right, table_right_out, sem.at[2])

    @pl.when(step == 0)
    def _():
        for fetch in fetches:
            fetch.start()

    for b in range(grad_ref.shape[0]):
        grad = grad_ref[b] * factor
        grad_out[b] = grad
        left_out[b], right_out[b], weight_out[b] = shampoo_parts(
            grad, left_ref[b], right_ref[b], left_root_ref[b], right_root_ref[b], weight_ref[b]
        )

    @pl.when(step == jnp.minimum(TABLE_STEP, steps - 1))
    def _():
        for fetch in fetches:
            fetch.wait()
        grad = table_grad_ref[...] * factor
        table_grad_out[...] = grad
        parts = split_two(grad)
        table_left_out[...] = STAT_DECAY * table_left_ref[...] + (1.0 - STAT_DECAY) * dot_split(
            parts, parts, ((1,), (1,))
        )
        half = split_two(dot_split(split_two(table_left_root_ref[...]), parts, ((1,), (0,))))
        for n in range(2):
            grad_parts[n] = parts[n]
        width = grad.shape[1]
        strip = width // 3

        def strip_body(i, carry):
            cols = pl.ds(pl.multiple_of(i * strip, strip), strip)
            own = (grad_parts[0, :, cols], grad_parts[1, :, cols])
            table_right[cols, :] = STAT_DECAY * table_right[cols, :] + (1.0 - STAT_DECAY) * dot_split(
                own, parts, ((0,), (0,))
            )
            precond[:, cols] = dot_split(half, split_two(table_right_root[:, cols]), ((1,), (0,)))
            return carry

        lax.fori_loop(0, 3, strip_body, 0)
        keep.start()
        turned = precond[...]
        mean = total_of(turned * turned) * (1.0 / (grad.shape[0] * width))
        table_out[...] = table_ref[...] * (
            1.0 - MATRIX_RATE * WEIGHT_DECAY
        ) - MATRIX_RATE * turned * lax.rsqrt(mean + ROOT_EPSILON)
        clipped = norm_grad_ref[0 : norm_ref.shape[0], :] * factor
        norm_grad_out[...] = clipped
        moment = FIRST_BETA * moment_ref[...] + (1.0 - FIRST_BETA) * clipped
        second = SECOND_BETA * second_ref[...] + (1.0 - SECOND_BETA) * clipped * clipped
        moment_out[...] = moment
        second_out[...] = second
        one = moment / corrections_ref[0:1, 0:1]
        two = second / corrections_ref[0:1, 1:2]
        weight = norm_ref[...]
        norm_out[...] = weight - VECTOR_RATE * (
            one / (jnp.sqrt(two) + ADAM_EPSILON) + WEIGHT_DECAY * weight
        )

    @pl.when(step == steps - 1)
    def _():
        keep.wait()


def update_all(small, right, right_root, blocks):
    corrections, stats, table_grad, table_left, table_left_root, table, norm_grad, moment, second, norms = small
    count, edge, _ = blocks[0].shape
    per_step = PACK if count % PACK == 0 else 1
    spec = pl.BlockSpec((per_step, edge, edge), lambda i: (i, 0, 0))
    anywhere = pl.BlockSpec(memory_space=pl.ANY)
    like = lambda array: jax.ShapeDtypeStruct(array.shape, F32)
    return pl.pallas_call(
        update_kernel,
        out_shape=(like(table_grad), like(table_left), like(right), like(table))
        + (like(norms),) * 4
        + (like(blocks[0]),) * 4,
        grid=(count // per_step,),
        in_specs=[whole(array.shape) for array in small] + [anywhere] * 2 + [spec] * 6,
        out_specs=(whole(table_grad.shape), whole(table_left.shape), anywhere, whole(table.shape))
        + (whole(norms.shape),) * 4
        + (spec,) * 4,
        scratch_shapes=[
            pltpu.VMEM((2,) + table_grad.shape, BF16),
            pltpu.VMEM(table_grad.shape, F32),
            pltpu.VMEM(right.shape, F32),
            pltpu.VMEM(right.shape, F32),
            pltpu.SemaphoreType.DMA((3,)),
        ],
        compiler_params=params(),
        name="update_all",
    )(*small, right, right_root, *blocks)


def rotary_of(place, lane):
    half = HS // 2
    freqs = jnp.exp(-math.log(ROTARY_BASE) * (2.0 * (lane % half).astype(F32) / HS))
    angles = place.astype(F32) * freqs
    sine = jnp.sin(angles)
    return jnp.cos(angles), jnp.where(lane % HS < half, -sine, sine)


def span_of(before, until, tiles):
    low, high = before // TILE, (until + TILE - 1) // TILE
    half = jnp.maximum((high - low + 1) // 2, SHORTEST)
    return jnp.minimum(low, tiles - 2 * half), half


def pack_blocks(blocks):
    count, edge, _ = blocks.shape
    groups = blocks.reshape(count // PACK, PACK, edge, edge).transpose(0, 2, 1, 3)
    return groups.reshape(count // PACK, edge, PACK * edge)


def gather_weights(own, rows, table, norm_params, owner_map, known, sizes):
    everyone = ("dp", "tensor")
    codons, targets, mask, segments = rows
    slots, edge, _ = own.shape
    shards = sizes[1]
    owner, slot = owner_map[None, :] // slots, owner_map[None, :] % slots
    shard = jnp.arange(shards, dtype=jnp.int32)[:, None]
    if known:
        bits = bits_of(owner, shard)
        group = slot // PACK
        entry = gather_entry(0, bits)
        for g in range(1, PACK_GROUPS):
            entry = jnp.where(group == g, gather_entry(g, bits), entry)
        place = ((group * 32 + entry) * PACK + slot % PACK).reshape(-1)
        return gather_everywhere(place, own, rows, table, norm_params, 32, sizes)
    packed = pack_blocks(lax.all_gather(own.astype(BF16), everyone, axis=0, tiled=True))
    count = jnp.maximum(lax.psum(jnp.sum(mask.astype(F32)), everyone), 1.0)
    place = ((owner * shards + shard) * slots + slot).reshape(-1)
    length = codons.shape[1]
    tiles = length // TILE
    segment = lax.dynamic_index_in_dim(segments, lax.axis_index("tensor"), 0, keepdims=False)
    columns = jnp.stack([codons[0], targets[0], mask[0], segment], 1)
    tiled = segment.reshape(length // ROWS, ROWS)
    before = jnp.sum((segment[None, :] < tiled[:, :1]).astype(jnp.int32), -1)
    until = jnp.sum((segment[None, :] <= tiled[:, -1:]).astype(jnp.int32), -1)
    spans = span_of(before, until, tiles)
    cosine, sine = rotary_of(
        jnp.arange(length, dtype=jnp.int32)[:, None], jnp.arange(LANES, dtype=jnp.int32)[None, :]
    )
    return assemble(place, packed, sizes) + embed_rows(columns[:, :1], table, norm_params[0:1], norm_params[1:2]) + (
        jnp.broadcast_to(count, (8, LANES)), columns, segment.reshape(tiles, 1, TILE), cosine, sine,
    ) + spans


def body(
    codons,
    segments,
    targets,
    loss_mask,
    owner_map,
    step_count,
    block_weight,
    block_left,
    block_right,
    block_left_root,
    block_right_root,
    embedding_weight,
    table_left,
    table_right,
    table_left_root,
    table_right_root,
    norm_params,
    norm_moment,
    norm_second,
):
    everyone = ("dp", "tensor")
    vocab, width = embedding_weight.shape
    shards = lax.axis_size("tensor")
    owners = lax.axis_size("dp")
    slots = block_weight.shape[1]
    edge = block_weight.shape[-1]
    blocks = owner_map.shape[0]
    shard_width = width // shards

    known = on_known_slice(owners, shards, slots)
    sizes = (width, shards, shard_width, FF)
    project, outward, expand, contract, x0, h1, count, columns, seg_row, cosine, sine, *spans = gather_weights(
        block_weight[0], (codons, targets, loss_mask, segments), embedding_weight, norm_params, owner_map, known, sizes
    )
    query, keys, values = front(h1, project, cosine, sine)
    attended, lse = attend(*spans, query, keys, values, columns, seg_row)
    (h2, active, d_two, ghid, d_one, gatt, gx, head_grad, norm_grad) = middle_rows(
        x0, attended, columns, count, norm_params, embedding_weight,
        outward, expand, contract,
    )
    gproj = attend_back(
        *spans, query, keys, values, gatt, lse, columns, seg_row, cosine, sine
    )
    table_grad, norm_grad = tail_rows(
        columns, x0, gx, gproj, norm_params, project, head_grad, norm_grad
    )
    owner, slot = owner_map[None, :] // slots, owner_map[None, :] % slots
    device = owner * shards + jnp.arange(shards, dtype=jnp.int32)[:, None]
    if known:
        home = slot * (owners * shards) + device
    else:
        home = device * slots + slot
    grads = weight_grads(
        home.reshape(-1), h1, attended, h2, active, gproj, d_one, ghid, d_two, sizes, shards * blocks, edge
    )
    if known:
        owned, table_grad, norm_grad, stats = sum_everywhere(
            grads.reshape((slots,) + (2,) * 5 + grads.shape[1:]),
            table_grad, norm_grad, count,
        )
    else:
        owned = lax.psum_scatter(grads, everyone, scatter_dimension=0, tiled=True)
        owned = jnp.stack([jnp.concatenate(from_dense(owned[b]), 0) for b in range(slots)])
        table_grad, norm_grad, square_sum = lax.psum((table_grad, norm_grad), everyone) + (
            lax.psum(jnp.sum(owned * owned), everyone),
        )
        vectors = norm_grad[:6]
        square_sum = square_sum + jnp.sum(table_grad * table_grad) + jnp.sum(vectors * vectors)
        stats = statistics(square_sum, jnp.sum(norm_grad[6]), count[:1, :1])
    loss_value, grad_norm = stats[2, 0], stats[1, 0]
    step_value = step_count.astype(F32)
    corrections = jnp.stack([1.0 - FIRST_BETA**step_value, 1.0 - SECOND_BETA**step_value]).reshape(1, 2)
    (
        table_clipped, table_left_new, table_right_new, table_weight_new,
        norm_clipped, moment_new, second_new, params_new,
        block_grad, new_left, new_right, new_weight,
    ) = update_all(
        (
            corrections, stats, table_grad, table_left, table_left_root, embedding_weight,
            norm_grad, norm_moment, norm_second, norm_params,
        ),
        table_right,
        table_right_root,
        (owned, block_left[0], block_right[0], block_left_root[0], block_right_root[0], block_weight[0]),
    )
    return (
        loss_value,
        grad_norm,
        block_grad[None],
        new_left[None],
        new_right[None],
        new_weight[None],
        table_clipped,
        table_left_new,
        table_right_new,
        table_weight_new,
        norm_clipped,
        moment_new,
        second_new,
        params_new,
    )


def solution(mesh):
    in_specs = (
        P(("dp", "tensor"), None),
        P("dp", None),
        P(("dp", "tensor"), None),
        P(("dp", "tensor"), None),
        P(),
        P(),
        P("tensor", "dp", None, None),
        P("tensor", "dp", None, None),
        P("tensor", "dp", None, None),
        P("tensor", "dp", None, None),
        P("tensor", "dp", None, None),
        P(),
        P(),
        P(),
        P(),
        P(),
        P(),
        P(),
        P(),
    )
    out_specs = (
        P(),
        P(),
        P("tensor", "dp", None, None),
        P("tensor", "dp", None, None),
        P("tensor", "dp", None, None),
        P("tensor", "dp", None, None),
        P(),
        P(),
        P(),
        P(),
        P(),
        P(),
        P(),
        P(),
    )
    return jax.shard_map(body, mesh=mesh, in_specs=in_specs, out_specs=out_specs, check_vma=False)
```
